32 devices in a mesh: ctx: 8 (over y, x, core), fsdp: 4 (over z).
Axes of the slice: x: 2, y: 2, z: 4, core: 2. Of those that a mesh axis runs over, the one named last changes fastest.
Arguments:
- patches: bfloat16 [4, 2048, 1024], P('fsdp', 'ctx'), may hold values from -6 to 6
- cotangent: bfloat16 [4, 2048, 1024], P('fsdp', 'ctx'), may hold values from -6 to 6
- deal_table: int32 [16], replicated, may hold values from 0 to 15, each once
- prompt_len: int32 [4], P('fsdp'), may hold values from 256 to 1024, as said below
- w_query: bfloat16 [1024, 1024], P('fsdp'), may hold values from -0.375 to 0.375
- w_key: bfloat16 [1024, 1024], P('fsdp'), may hold values from -0.1875 to 0.1875
- w_value: bfloat16 [1024, 1024], P('fsdp'), may hold values from -0.1875 to 0.1875
- w_output: bfloat16 [1024, 1024], P('fsdp'), may hold values from -1.5 to 1.5
- w_gate: bfloat16 [1024, 2816], P('fsdp'), may hold values from -0.1875 to 0.1875
- w_up: bfloat16 [1024, 2816], P('fsdp'), may hold values from -0.1875 to 0.1875
- w_down: bfloat16 [2816, 1024], P('fsdp'), may hold values from -0.109375 to 0.109375
- gain_attn: bfloat16 [1024], P('fsdp'), may hold values from 0.5 to 1.5
- gain_ffn: bfloat16 [1024], P('fsdp'), may hold values from 0.5 to 1.5
Outputs:
- layer_out: bfloat16 [4, 2048, 1024], P('fsdp', 'ctx')
- grad_patches: float32 [4, 2048, 1024], P('fsdp', 'ctx')
- grad_w_query: float32 [1024, 1024], P('fsdp')
- grad_w_key: float32 [1024, 1024], P('fsdp')
- grad_w_value: float32 [1024, 1024], P('fsdp')
- grad_w_output: float32 [1024, 1024], P('fsdp')
- grad_w_gate: float32 [1024, 2816], P('fsdp')
- grad_w_up: float32 [1024, 2816], P('fsdp')
- grad_w_down: float32 [2816, 1024], P('fsdp')
- grad_gain_attn: float32 [1024], P('fsdp')
- grad_gain_ffn: float32 [1024], P('fsdp')
The draws below stay inside these ranges and needn't reach their ends.
Inputs may be any that keep to these rules, and one draw needn't show every extreme that they name: A permutation: stored block s of every group holds the group's patch block deal_table[s]. `prompt_len`: one group's continuations see its whole prompt.
All inputs are finite; a program needn't handle non-finite values.
Results may differ from the reference program's by a relative error of at most 0.025.
Values may be sent and summed in bfloat16 or wider, within the bound.
A program may use at most 384 MiB of HBM per device.

```python
import math
import jax
import jax.numpy as jnp
from jax import lax

D = 1024
HEADS = 16
HEAD = 64
FF = 2816
TOK_DEV = 256
CONT_LEN = 1024
GROUPS = 4
GROUP_TOK = 2048
NCONT = 1
PROMPT = 1024
SLOTS = 16
N_CTX = 8


def draw_prompt_len(key, part):
    lengths = jax.random.randint(jax.random.fold_in(key, 11), (GROUPS,), PROMPT // 4, PROMPT + 1, dtype=jnp.int32)
    chosen = jax.random.randint(jax.random.fold_in(key, 12), (), 0, GROUPS, dtype=jnp.int32)
    return jnp.where(jnp.arange(GROUPS, dtype=jnp.int32) == chosen, PROMPT, lengths).astype(jnp.int32)


def levels(stream_key, dims, pieces, smallest, largest):
    level, own = 1.0, jax.random.fold_in(stream_key, 6)
    for dim, shards_of in pieces:
        steps = jnp.exp(jax.random.uniform(jax.random.fold_in(own, dim), (shards_of,), jnp.float32, smallest / len(pieces), largest / len(pieces)))
        level = level * jnp.repeat(steps, dims[dim] // shards_of).reshape([-1 if axis == dim else 1 for axis in range(len(dims))])
    return level


def scatter_about(own_key, dims, spread, reach, cuts=(), kind=jnp.bfloat16):
    drawn = jax.random.normal(own_key, dims, jnp.float32) * spread
    if len(cuts) > 0:
        drawn = levels(own_key, dims, cuts, -0.22, 0.18) * drawn
    return jnp.clip(drawn, min=-reach, max=reach).astype(kind)


def setup_inputs(seed: int = 0) -> dict:
    streams_of = jax.random.split(jax.random.key(seed), 14)
    patches = scatter_about(streams_of[0], (GROUPS, GROUP_TOK, D), 1.0, 6.0, ((0, 4), (1, 8)))
    cotangent = scatter_about(streams_of[1], (GROUPS, GROUP_TOK, D), 1.0, 6.0, ((0, 4), (1, 8)))
    deal_table = jax.random.permutation(streams_of[2], SLOTS).astype(jnp.int32)
    prompt_len = draw_prompt_len(jax.random.fold_in(streams_of[13], 71), 0)
    w_query = scatter_about(streams_of[4], (D, D), (D // 4) ** -0.5, 0.375, ((0, 4),))
    w_key = scatter_about(streams_of[5], (D, D), D ** -0.5, 0.1875, ((0, 4),))
    w_value = scatter_about(streams_of[6], (D, D), D ** -0.5, 0.1875, ((0, 4),))
    w_output = scatter_about(streams_of[7], (D, D), (D // 64) ** -0.5, 1.5, ((0, 4),))
    w_gate = scatter_about(streams_of[8], (D, FF), D ** -0.5, 0.1875, ((0, 4),))
    w_up = scatter_about(streams_of[9], (D, FF), D ** -0.5, 0.1875, ((0, 4),))
    w_down = scatter_about(streams_of[10], (FF, D), FF ** -0.5, 0.109375, ((0, 4),))
    gain_attn = jnp.clip(1.0 + 0.1 * jax.random.normal(streams_of[11], (D,), jnp.float32), 0.5, 1.5).astype(jnp.bfloat16)
    gain_ffn = jnp.clip(1.0 + 0.1 * jax.random.normal(streams_of[12], (D,), jnp.float32), 0.5, 1.5).astype(jnp.bfloat16)
    return {"patches": patches, "cotangent": cotangent, "deal_table": deal_table, "prompt_len": prompt_len, "w_query": w_query, "w_key": w_key, "w_value": w_value, "w_output": w_output, "w_gate": w_gate, "w_up": w_up, "w_down": w_down, "gain_attn": gain_attn, "gain_ffn": gain_ffn}


epsilon = 1e-05
score_scale = 0.125
masked_value = -1e+30
highest = lax.Precision.HIGHEST

@jax.custom_vjp
def low(v):
    return lax.optimization_barrier(v.astype(jnp.bfloat16)).astype(jnp.float32)

@jax.custom_vjp
def low_back(v):
    return v

def low_keep(v):
    return (low(v), None)

def low_pass(kept, grad):
    return (grad,)

def back_keep(v):
    return (v, None)

def back_low(kept, grad):
    return (low(grad),)
low.defvjp(low_keep, low_pass)
low_back.defvjp(back_keep, back_low)

def segment_of(position):
    return jnp.where(position < PROMPT, -1, (position - PROMPT) // CONT_LEN)

def visible(query_pos, key_pos, length):
    same = (segment_of(query_pos)[:, None] == segment_of(key_pos)[None, :]) & (key_pos[None, :] <= query_pos[:, None])
    shared = (query_pos[:, None] >= PROMPT) & (key_pos[None, :] < length)
    return same | shared

def rms_norm(values, gain):
    return values * lax.rsqrt(lax.optimization_barrier(jnp.mean(values * values, axis=-1, keepdims=True)) + epsilon) * gain

def attend(queries, query_pos, keys, values, key_pos, length):
    scores = jnp.einsum('qhe,khe->hqk', queries, keys, precision=highest) * score_scale
    scores = low_back(scores)
    scores = jnp.where(visible(query_pos, key_pos, length)[None], scores, masked_value)
    weights = low(jax.nn.softmax(scores, axis=-1))
    return jnp.einsum('hqk,khe->qhe', weights, values, precision=highest)

def attend_rows(queries, query_pos, keys, values, key_pos, length):
    row_count = queries.shape[0]
    block_rows = math.gcd(math.gcd(512, CONT_LEN), PROMPT)
    blocks = (queries.reshape(row_count // block_rows, block_rows, HEADS, HEAD), query_pos.reshape(row_count // block_rows, block_rows))
    block_step = jax.checkpoint(lambda block_pair: attend(block_pair[0], block_pair[1], keys, values, key_pos, length))
    return lax.map(block_step, blocks).reshape(row_count, HEADS, HEAD)

def group_forward(group_rows, length, params):
    w_query, w_key, w_value, w_output, w_gate, w_up, w_down, gain_attn, gain_ffn = params
    normed = low(rms_norm(group_rows, gain_attn))

    def project(weight):
        return low(low_back(jnp.dot(normed, weight, precision=highest))).reshape(GROUP_TOK, HEADS, HEAD)
    queries = project(w_query)
    keys = project(w_key)
    values = project(w_value)
    position = jnp.arange(GROUP_TOK, dtype=jnp.int32)
    prompt_out = attend_rows(queries[:PROMPT], position[:PROMPT], keys[:PROMPT], values[:PROMPT], position[:PROMPT], length)

    def continuation(index):
        start = (PROMPT + index * CONT_LEN).astype(jnp.int32)
        cont_keys = jnp.concatenate([keys[:PROMPT], lax.dynamic_slice_in_dim(keys, start, CONT_LEN, 0)], 0)
        cont_values = jnp.concatenate([values[:PROMPT], lax.dynamic_slice_in_dim(values, start, CONT_LEN, 0)], 0)
        cont_pos = start + jnp.arange(CONT_LEN, dtype=jnp.int32)
        key_pos = jnp.concatenate([position[:PROMPT], cont_pos], 0)
        cont_queries = lax.dynamic_slice_in_dim(queries, start, CONT_LEN, 0)
        return attend_rows(cont_queries, cont_pos, cont_keys, cont_values, key_pos, length)
    cont_out = lax.map(continuation, jnp.arange(NCONT, dtype=jnp.int32)).reshape(NCONT * CONT_LEN, HEADS, HEAD)
    attn = jnp.concatenate([prompt_out, cont_out], 0).reshape(GROUP_TOK, D)
    attn = low(low_back(attn))
    hidden = group_rows + low_back(jnp.dot(attn, w_output, precision=highest))
    normed_ffn = low(rms_norm(hidden, gain_ffn))
    gate = low_back(jnp.dot(normed_ffn, w_gate, precision=highest))
    up_proj = low_back(jnp.dot(normed_ffn, w_up, precision=highest))
    inner = low(jax.nn.silu(gate) * up_proj)
    return hidden + low_back(jnp.dot(inner, w_down, precision=highest))

def reference(patches, cotangent, deal_table, prompt_len, w_query, w_key, w_value, w_output, w_gate, w_up, w_down, gain_attn, gain_ffn):
    slot_count = 2 * N_CTX
    block_len = TOK_DEV // 2

    def to_logical(array):
        shaped = array.astype(jnp.float32).reshape(GROUPS, slot_count, block_len, D)
        return jnp.zeros_like(shaped).at[:, deal_table].set(shaped).reshape(GROUPS, GROUP_TOK, D)

    def to_slots(array):
        return array.reshape(GROUPS, slot_count, block_len, D)[:, deal_table].reshape(GROUPS, GROUP_TOK, D)
    params = tuple((weight.astype(jnp.float32) for weight in (w_query, w_key, w_value, w_output, w_gate, w_up, w_down, gain_attn, gain_ffn)))

    def forward(rows_all, weights_all):
        return lax.map(jax.checkpoint(lambda group_pair: group_forward(group_pair[0], group_pair[1], weights_all)), (rows_all, prompt_len))
    layer_logical, pullback = jax.vjp(forward, to_logical(patches), params)
    grad_rows, grad_params = pullback(to_logical(cotangent))
    return (to_slots(layer_logical).astype(jnp.bfloat16), to_slots(grad_rows), grad_params[0], grad_params[1], grad_params[2], grad_params[3], grad_params[4], grad_params[5], grad_params[6], grad_params[7], grad_params[8])
```

```python
import functools
import math

import jax
import jax.numpy as jnp
from jax import lax
from jax.experimental import pallas as pl
from jax.experimental.pallas import tpu as pltpu
from jax.sharding import PartitionSpec as P

HEADS = 16
HEAD = 64
CONT_LEN = 1024


epsilon = 1e-05
score_scale = 0.125
masked_value = -1e30


def rms_forward(values, gain):
    factor = lax.rsqrt(jnp.mean(values * values, axis=-1, keepdims=True) + epsilon)
    return (values * factor * gain, factor)


def rms_backward(values, factor, gain, grad_normed):
    scaled = grad_normed * gain
    grad_gain = jnp.sum(grad_normed * values * factor, axis=0)
    cubed = factor * factor * factor
    grad_values = factor * scaled - values * cubed * jnp.mean(
        scaled * values, axis=-1, keepdims=True
    )
    return (grad_values, grad_gain)


def segment_of(position, prompt):
    return jnp.where(position < prompt, -1, (position - prompt) // CONT_LEN)


def visible(query_pos, key_pos, prompt, length):
    same = (segment_of(query_pos, prompt)[:, None] == segment_of(key_pos, prompt)[None, :]) & (
        key_pos[None, :] <= query_pos[:, None]
    )
    shared = (query_pos[:, None] >= prompt) & (key_pos[None, :] < length)
    return same | shared


def rows_plan(
    patches,
    cotangent,
    deal_table,
    prompt_len,
    w_query,
    w_key,
    w_value,
    w_output,
    w_gate,
    w_up,
    w_down,
    gain_attn,
    gain_ffn,
):
    local_rows = patches.shape[1]
    width = patches.shape[2]
    devices_ctx = lax.axis_size("ctx")
    group_tok = local_rows * devices_ctx
    cont_count = group_tok // (2 * CONT_LEN)
    prompt = group_tok - cont_count * CONT_LEN
    block_len = local_rows // 2
    slot_count = 2 * devices_ctx
    key_rows = math.gcd(512, group_tok)
    block_count = group_tok // key_rows
    length = prompt_len[0]

    def positions_of(first_row, count):
        stored = first_row + jnp.arange(count, dtype=jnp.int32)
        slot_ids = stored // block_len
        picked = jnp.where(
            slot_ids[:, None] == jnp.arange(slot_count, dtype=jnp.int32)[None, :],
            deal_table[None, :],
            0,
        )
        return jnp.sum(picked, axis=1) * block_len + stored % block_len

    query_pos = positions_of(lax.axis_index("ctx") * local_rows, local_rows)
    key_pos = positions_of(0, group_tok).reshape(block_count, key_rows)
    (
        full_query,
        full_key,
        full_value,
        full_output,
        full_gate,
        full_up,
        full_down,
        full_gain_attn,
        full_gain_ffn,
    ) = (
        lax.all_gather(w_query, "fsdp", axis=0, tiled=True),
        lax.all_gather(w_key, "fsdp", axis=0, tiled=True),
        lax.all_gather(w_value, "fsdp", axis=0, tiled=True),
        lax.all_gather(w_output, "fsdp", axis=0, tiled=True),
        lax.all_gather(w_gate, "fsdp", axis=0, tiled=True),
        lax.all_gather(w_up, "fsdp", axis=0, tiled=True),
        lax.all_gather(w_down, "fsdp", axis=0, tiled=True),
        lax.all_gather(gain_attn, "fsdp", axis=0, tiled=True),
        lax.all_gather(gain_ffn, "fsdp", axis=0, tiled=True),
    )
    rows_f32 = patches[0].astype(jnp.float32)
    gain_one = full_gain_attn.astype(jnp.float32)
    normed, factor_attn = rms_forward(rows_f32, gain_one)
    normed_low = normed.astype(jnp.bfloat16)
    queries = jnp.dot(normed_low, full_query, preferred_element_type=jnp.float32).astype(
        jnp.bfloat16
    )
    keys_local = jnp.dot(normed_low, full_key, preferred_element_type=jnp.float32).astype(
        jnp.bfloat16
    )
    values_local = jnp.dot(normed_low, full_value, preferred_element_type=jnp.float32).astype(
        jnp.bfloat16
    )
    key_all, value_all = (
        lax.all_gather(keys_local, "ctx", axis=0, tiled=True),
        lax.all_gather(values_local, "ctx", axis=0, tiled=True),
    )
    query_heads = queries.reshape(local_rows, HEADS, HEAD)

    def split_blocks(array):
        return array.reshape(block_count, key_rows, HEADS, HEAD)

    def forward_block(state, block):
        key_block, value_block, block_pos = block
        visible_mask = visible(query_pos, block_pos, prompt, length)

        def forward_update(inner_state):
            maxima, totals, accum = inner_state
            scores = (
                jnp.einsum(
                    "qhe,khe->hqk", query_heads, key_block, preferred_element_type=jnp.float32
                )
                * score_scale
            )
            scores = jnp.where(visible_mask[None], scores, masked_value)
            new_max = jnp.maximum(maxima, jnp.max(scores, axis=-1))
            rescale = jnp.exp(maxima - new_max)
            probs = jnp.where(visible_mask[None], jnp.exp(scores - new_max[:, :, None]), 0.0)
            totals = totals * rescale + jnp.sum(probs, axis=-1)
            accum = accum * rescale.T[:, :, None] + jnp.einsum(
                "hqk,khe->qhe",
                probs.astype(jnp.bfloat16),
                value_block,
                preferred_element_type=jnp.float32,
            )
            return (new_max, totals, accum)

        return (
            lax.cond(jnp.any(visible_mask), forward_update, lambda inner_state: inner_state, state),
            None,
        )

    start_state = (
        jnp.full((HEADS, local_rows), masked_value, jnp.float32),
        jnp.zeros((HEADS, local_rows), jnp.float32),
        jnp.zeros((local_rows, HEADS, HEAD), jnp.float32),
    )
    (maxima, totals, accum), unused = lax.scan(
        forward_block, start_state, (split_blocks(key_all), split_blocks(value_all), key_pos)
    )
    attn_f32 = accum / totals.T[:, :, None]
    log_total = maxima + jnp.log(totals)
    attn_low = attn_f32.astype(jnp.bfloat16).reshape(local_rows, width)
    hidden = rows_f32 + jnp.dot(attn_low, full_output, preferred_element_type=jnp.float32)
    gain_two = full_gain_ffn.astype(jnp.float32)
    normed_ffn, factor_ffn = rms_forward(hidden, gain_two)
    ffn_low = normed_ffn.astype(jnp.bfloat16)
    gate = jnp.dot(ffn_low, full_gate, preferred_element_type=jnp.float32)
    up_proj = jnp.dot(ffn_low, full_up, preferred_element_type=jnp.float32)
    sigmoid = jax.nn.sigmoid(gate)
    activated = gate * sigmoid
    inner_low = (activated * up_proj).astype(jnp.bfloat16)
    layer = hidden + jnp.dot(inner_low, full_down, preferred_element_type=jnp.float32)
    grad_out = cotangent[0].astype(jnp.float32)
    grad_down_in = cotangent[0]
    grad_w_down = jnp.dot(inner_low.T, grad_down_in, preferred_element_type=jnp.float32)
    grad_inner = jnp.dot(grad_down_in, full_down.T, preferred_element_type=jnp.float32)
    grad_gate = (grad_inner * up_proj * sigmoid * (1.0 + gate * (1.0 - sigmoid))).astype(
        jnp.bfloat16
    )
    grad_up = (grad_inner * activated).astype(jnp.bfloat16)
    grad_w_gate = jnp.dot(ffn_low.T, grad_gate, preferred_element_type=jnp.float32)
    grad_w_up = jnp.dot(ffn_low.T, grad_up, preferred_element_type=jnp.float32)
    grad_normed_ffn = jnp.dot(grad_gate, full_gate.T, preferred_element_type=jnp.float32) + jnp.dot(
        grad_up, full_up.T, preferred_element_type=jnp.float32
    )
    grad_hidden_norm, grad_gain_ffn = rms_backward(hidden, factor_ffn, gain_two, grad_normed_ffn)
    grad_hidden = grad_out + grad_hidden_norm
    grad_branch = grad_hidden.astype(jnp.bfloat16)
    grad_w_output = jnp.dot(attn_low.T, grad_branch, preferred_element_type=jnp.float32)
    grad_attn = (
        jnp.dot(grad_branch, full_output.T, preferred_element_type=jnp.float32)
        .astype(jnp.bfloat16)
        .reshape(local_rows, HEADS, HEAD)
    )
    delta = jnp.einsum("qhe,qhe->hq", grad_attn.astype(jnp.float32), attn_f32)
    key_back, value_back = (key_all, value_all)

    def backward_block(grad_query, block):
        key_block, value_block, block_pos = block
        visible_mask = visible(query_pos, block_pos, prompt, length)

        def backward_update(grad_state):
            scores = (
                jnp.einsum(
                    "qhe,khe->hqk", query_heads, key_block, preferred_element_type=jnp.float32
                )
                * score_scale
            )
            probs = jnp.where(visible_mask[None], jnp.exp(scores - log_total[:, :, None]), 0.0)
            grad_probs = jnp.einsum(
                "qhe,khe->hqk", grad_attn, value_block, preferred_element_type=jnp.float32
            )
            grad_scores = (probs * (grad_probs - delta[:, :, None])).astype(jnp.bfloat16)
            grad_state = (
                grad_state
                + jnp.einsum(
                    "hqk,khe->qhe", grad_scores, key_block, preferred_element_type=jnp.float32
                )
                * score_scale
            )
            grad_keys = (
                jnp.einsum(
                    "hqk,qhe->khe", grad_scores, query_heads, preferred_element_type=jnp.float32
                )
                * score_scale
            )
            grad_values = jnp.einsum(
                "hqk,qhe->khe",
                probs.astype(jnp.bfloat16),
                grad_attn,
                preferred_element_type=jnp.float32,
            )
            return (grad_state, (grad_keys, grad_values))

        def skipped(grad_state):
            empty = jnp.zeros((key_rows, HEADS, HEAD), jnp.float32)
            return (grad_state, (empty, empty))

        return lax.cond(jnp.any(visible_mask), backward_update, skipped, grad_query)

    zero_query = jnp.zeros((local_rows, HEADS, HEAD), jnp.float32)
    grad_query, (grad_key_blocks, grad_value_blocks) = lax.scan(
        backward_block, zero_query, (split_blocks(key_back), split_blocks(value_back), key_pos)
    )
    grad_key_sum, grad_value_sum = (
        lax.psum_scatter(
            grad_key_blocks.reshape(group_tok, width).astype(jnp.bfloat16),
            "ctx",
            scatter_dimension=0,
            tiled=True,
        ).astype(jnp.float32),
        lax.psum_scatter(
            grad_value_blocks.reshape(group_tok, width).astype(jnp.bfloat16),
            "ctx",
            scatter_dimension=0,
            tiled=True,
        ).astype(jnp.float32),
    )
    grad_key_low = grad_key_sum.astype(jnp.bfloat16)
    grad_value_low = grad_value_sum.astype(jnp.bfloat16)
    grad_query_low = grad_query.reshape(local_rows, width).astype(jnp.bfloat16)
    grad_w_query = jnp.dot(normed_low.T, grad_query_low, preferred_element_type=jnp.float32)
    grad_w_key = jnp.dot(normed_low.T, grad_key_low, preferred_element_type=jnp.float32)
    grad_w_value = jnp.dot(normed_low.T, grad_value_low, preferred_element_type=jnp.float32)
    grad_normed = (
        jnp.dot(grad_query_low, full_query.T, preferred_element_type=jnp.float32)
        + jnp.dot(grad_key_low, full_key.T, preferred_element_type=jnp.float32)
        + jnp.dot(grad_value_low, full_value.T, preferred_element_type=jnp.float32)
    )
    grad_rows_norm, grad_gain_attn = rms_backward(rows_f32, factor_attn, gain_one, grad_normed)
    grad_rows = grad_hidden + grad_rows_norm
    shards = (
        lax.psum_scatter(
            grad_w_query.astype(jnp.bfloat16), "fsdp", scatter_dimension=0, tiled=True
        ).astype(jnp.float32),
        lax.psum_scatter(
            grad_w_key.astype(jnp.bfloat16), "fsdp", scatter_dimension=0, tiled=True
        ).astype(jnp.float32),
        lax.psum_scatter(
            grad_w_value.astype(jnp.bfloat16), "fsdp", scatter_dimension=0, tiled=True
        ).astype(jnp.float32),
        lax.psum_scatter(
            grad_w_output.astype(jnp.bfloat16), "fsdp", scatter_dimension=0, tiled=True
        ).astype(jnp.float32),
        lax.psum_scatter(
            grad_w_gate.astype(jnp.bfloat16), "fsdp", scatter_dimension=0, tiled=True
        ).astype(jnp.float32),
        lax.psum_scatter(
            grad_w_up.astype(jnp.bfloat16), "fsdp", scatter_dimension=0, tiled=True
        ).astype(jnp.float32),
        lax.psum_scatter(
            grad_w_down.astype(jnp.bfloat16), "fsdp", scatter_dimension=0, tiled=True
        ).astype(jnp.float32),
        lax.psum_scatter(
            grad_gain_attn.astype(jnp.bfloat16), "fsdp", scatter_dimension=0, tiled=True
        ).astype(jnp.float32),
        lax.psum_scatter(
            grad_gain_ffn.astype(jnp.bfloat16), "fsdp", scatter_dimension=0, tiled=True
        ).astype(jnp.float32),
    )
    summed = (
        lax.psum(shards[0].astype(jnp.bfloat16), "ctx").astype(jnp.float32),
        lax.psum(shards[1].astype(jnp.bfloat16), "ctx").astype(jnp.float32),
        lax.psum(shards[2].astype(jnp.bfloat16), "ctx").astype(jnp.float32),
        lax.psum(shards[3].astype(jnp.bfloat16), "ctx").astype(jnp.float32),
        lax.psum(shards[4].astype(jnp.bfloat16), "ctx").astype(jnp.float32),
        lax.psum(shards[5].astype(jnp.bfloat16), "ctx").astype(jnp.float32),
        lax.psum(shards[6].astype(jnp.bfloat16), "ctx").astype(jnp.float32),
        lax.psum(shards[7].astype(jnp.bfloat16), "ctx").astype(jnp.float32),
        lax.psum(shards[8].astype(jnp.bfloat16), "ctx").astype(jnp.float32),
    )
    return (
        layer.astype(jnp.bfloat16)[None],
        grad_rows[None],
        summed[0],
        summed[1],
        summed[2],
        summed[3],
        summed[4],
        summed[5],
        summed[6],
        summed[7],
        summed[8],
    )


TILE = 256


def dot_f32(left, right, left_dim, right_dim):
    return lax.dot_general(
        left,
        right,
        (((left_dim,), (right_dim,)), ((), ())),
        preferred_element_type=jnp.float32,
    )


def head_masks():
    lane = lax.broadcasted_iota(jnp.int32, (TILE, 2 * HEAD), 1)
    first = (lane < HEAD).astype(jnp.bfloat16)
    return first, (1 - first).astype(jnp.bfloat16)


def stack_heads(tile, masks):
    return jnp.concatenate([tile * masks[0], tile * masks[1]], axis=0)


def tile_mask(kind, tile, length):
    row = lax.broadcasted_iota(jnp.int32, (TILE, 2 * TILE), 0)
    if kind == "diagonal":
        column = lax.broadcasted_iota(jnp.int32, (TILE, 2 * TILE), 1)
        return row <= jnp.where(column < TILE, column, column - TILE)
    return row + tile * TILE < length


def over_keys(tile, per_segment, step, state):
    base = tile // per_segment * per_segment
    state = lax.fori_loop(0, base, lambda key, kept: step(key, kept, "prompt"), state)
    state = lax.fori_loop(base, tile, lambda key, kept: step(key, kept, "full"), state)
    return step(tile, state, "diagonal")


def to_logical(slot_of, source, column, target, blocks, block_len, scale=None):
    for block in range(blocks):
        first = pl.multiple_of(slot_of[block] * block_len, block_len)
        picked = source[pl.ds(first, block_len), column : column + 2 * HEAD]
        if scale is not None:
            picked = picked * scale
        target[block * block_len : (block + 1) * block_len, :] = picked


def to_stored(block_of, source, target, column, blocks, block_len):
    for slot in range(blocks):
        first = pl.multiple_of(block_of[slot] * block_len, block_len)
        target[slot * block_len : (slot + 1) * block_len, column : column + 2 * HEAD] = source[
            pl.ds(first, block_len), :
        ]


def attend_forward(
    per_segment, slot_of, block_of, length_ref, qkv, attn, attn_t, lse, query, key, value_t, kept
):
    rows = qkv.shape[0]
    blocks = slot_of.shape[0]
    block_len = rows // blocks
    length = length_ref[0]
    to_logical(slot_of, qkv, 0, query, blocks, block_len, jnp.bfloat16(score_scale))
    to_logical(slot_of, qkv, 2 * HEAD, key, blocks, block_len)
    to_logical(slot_of, qkv, 4 * HEAD, kept, blocks, block_len)
    for tile in range(rows // TILE):
        value_t[tile] = kept[tile * TILE : (tile + 1) * TILE, :].T
    masks = head_masks()

    def one_tile(tile, unused):
        rows_at = pl.ds(pl.multiple_of(tile * TILE, TILE), TILE)
        both = stack_heads(query[rows_at, :], masks)

        def step(key_tile, state, kind):
            maxima, totals, accum = state
            keys_at = pl.ds(pl.multiple_of(key_tile * TILE, TILE), TILE)
            scores = dot_f32(key[keys_at, :], both, 1, 1)
            if kind != "full":
                scores = jnp.where(tile_mask(kind, key_tile, length), scores, masked_value)
            new_max = jnp.maximum(maxima, jnp.max(scores, axis=0, keepdims=True))
            probs = jnp.exp(scores - new_max)
            rescale = jnp.exp(maxima - new_max)
            totals = totals * rescale + jnp.sum(probs, axis=0, keepdims=True)
            accum = accum * rescale + dot_f32(
                value_t[key_tile], probs.astype(jnp.bfloat16), 1, 0
            )
            return new_max, totals, accum

        maxima, totals, accum = over_keys(
            tile,
            per_segment,
            step,
            (
                jnp.full((1, 2 * TILE), masked_value, jnp.float32),
                jnp.zeros((1, 2 * TILE), jnp.float32),
                jnp.zeros((2 * HEAD, 2 * TILE), jnp.float32),
            ),
        )
        accum = accum / totals
        feature = lax.broadcasted_iota(jnp.int32, (2 * HEAD, TILE), 0)
        picked = jnp.where(feature < HEAD, accum[:, :TILE], accum[:, TILE:])
        attn_t[tile] = picked
        lse[tile] = maxima + jnp.log(totals)
        kept[rows_at, :] = picked.T.astype(jnp.bfloat16)
        return unused

    lax.fori_loop(0, rows // TILE, one_tile, 0)
    to_stored(block_of, kept, attn, 0, blocks, block_len)


def attend_backward(
    per_segment,
    slot_of,
    block_of,
    length_ref,
    qkv,
    grad_attn,
    attn_t,
    lse,
    grad_qkv,
    query,
    key,
    value,
    grad,
    key_t,
    grad_key,
    grad_value,
):
    rows = qkv.shape[0]
    blocks = slot_of.shape[0]
    block_len = rows // blocks
    length = length_ref[0]
    to_logical(slot_of, qkv, 0, query, blocks, block_len, jnp.bfloat16(score_scale))
    to_logical(slot_of, qkv, 2 * HEAD, key, blocks, block_len)
    to_logical(slot_of, qkv, 4 * HEAD, value, blocks, block_len)
    to_logical(slot_of, grad_attn, 0, grad, blocks, block_len)
    for tile in range(rows // TILE):
        key_t[tile] = key[tile * TILE : (tile + 1) * TILE, :].T
    grad_key[...] = jnp.zeros_like(grad_key)
    grad_value[...] = jnp.zeros_like(grad_value)
    masks = head_masks()

    def one_tile(tile, unused):
        rows_at = pl.ds(pl.multiple_of(tile * TILE, TILE), TILE)
        both = stack_heads(query[rows_at, :], masks)
        grad_tile = grad[rows_at, :]
        both_grad = stack_heads(grad_tile, masks)
        product = grad_tile.astype(jnp.float32).T * attn_t[tile]
        delta = jnp.concatenate(
            [
                jnp.sum(product[:HEAD], axis=0, keepdims=True),
                jnp.sum(product[HEAD:], axis=0, keepdims=True),
            ],
            axis=1,
        )
        log_total = lse[tile]

        def step(key_tile, grad_query, kind):
            keys_at = pl.ds(pl.multiple_of(key_tile * TILE, TILE), TILE)
            scores = dot_f32(key[keys_at, :], both, 1, 1)
            if kind != "full":
                scores = jnp.where(tile_mask(kind, key_tile, length), scores, masked_value)
            probs = jnp.exp(scores - log_total)
            grad_probs = dot_f32(value[keys_at, :], both_grad, 1, 1)
            grad_scores = (probs * (grad_probs - delta)).astype(jnp.bfloat16)
            grad_value[keys_at, :] += dot_f32(probs.astype(jnp.bfloat16), both_grad, 1, 0)
            grad_key[keys_at, :] += dot_f32(grad_scores, both, 1, 0)
            return grad_query + dot_f32(key_t[key_tile], grad_scores, 1, 0)

        grad_query = over_keys(
            tile, per_segment, step, jnp.zeros((2 * HEAD, 2 * TILE), jnp.float32)
        )
        feature = lax.broadcasted_iota(jnp.int32, (2 * HEAD, TILE), 0)
        picked = jnp.where(feature < HEAD, grad_query[:, :TILE], grad_query[:, TILE:])
        query[rows_at, :] = (picked * score_scale).T.astype(jnp.bfloat16)
        return unused

    lax.fori_loop(0, rows // TILE, one_tile, 0)
    key[...] = grad_key[...].astype(jnp.bfloat16)
    value[...] = grad_value[...].astype(jnp.bfloat16)
    to_stored(block_of, query, grad_qkv, 0, blocks, block_len)
    to_stored(block_of, key, grad_qkv, 2 * HEAD, blocks, block_len)
    to_stored(block_of, value, grad_qkv, 4 * HEAD, blocks, block_len)


def heads_plan(
    patches,
    cotangent,
    deal_table,
    prompt_len,
    w_query,
    w_key,
    w_value,
    w_output,
    w_gate,
    w_up,
    w_down,
    gain_attn,
    gain_ffn,
):
    local_rows = patches.shape[1]
    width = patches.shape[2]
    devices_ctx = lax.axis_size("ctx")
    devices_fsdp = lax.axis_size("fsdp")
    me = lax.axis_index("ctx")
    group_tok = local_rows * devices_ctx
    slot_count = deal_table.shape[0]
    cols = width // devices_ctx
    part = w_down.shape[0] // devices_ctx
    hidden_units = part * devices_fsdp
    slots = jnp.arange(slot_count, dtype=jnp.int32)
    slot_of = jnp.sum(
        jnp.where(deal_table[None, :] == slots[:, None], slots[None, :], 0), axis=1
    ).astype(jnp.int32)

    def columns_of(weight):
        return lax.dynamic_slice_in_dim(weight, me * cols, cols, 1)

    def units_of(weight):
        split = weight.reshape(weight.shape[0], devices_fsdp, devices_ctx, part)
        return lax.dynamic_index_in_dim(split, me, 2, keepdims=False).reshape(
            weight.shape[0], hidden_units
        )

    def rows_gathered(array):
        return lax.all_gather(array, "fsdp", axis=0, tiled=True)

    w_qkv = rows_gathered(
        jnp.concatenate([columns_of(w_query), columns_of(w_key), columns_of(w_value)], axis=1)
    )
    full_output = rows_gathered(w_output)
    gate_up = rows_gathered(jnp.concatenate([units_of(w_gate), units_of(w_up)], axis=1))
    my_gate, my_up = gate_up[:, :hidden_units], gate_up[:, hidden_units:]
    my_down = rows_gathered(lax.dynamic_slice_in_dim(w_down, me * part, part, 0))
    gains = lax.all_gather(jnp.stack([gain_attn, gain_ffn]), "fsdp", axis=1, tiled=True)
    gain_one = gains[0].astype(jnp.float32)
    gain_two = gains[1].astype(jnp.float32)

    rows_f32 = patches[0].astype(jnp.float32)
    all_rows = lax.all_gather(patches[0], "ctx", axis=0, tiled=True)
    normed, unused = rms_forward(all_rows.astype(jnp.float32), gain_one)
    normed_low = normed.astype(jnp.bfloat16)
    qkv = jnp.dot(normed_low, w_qkv, preferred_element_type=jnp.float32).astype(jnp.bfloat16)

    tiles = group_tok // TILE
    per_segment = CONT_LEN // TILE
    smem = pl.BlockSpec(memory_space=pltpu.SMEM)
    vmem = pl.BlockSpec(memory_space=pltpu.VMEM)
    attn, attn_t, lse = pl.pallas_call(
        functools.partial(attend_forward, per_segment),
        out_shape=(
            jax.ShapeDtypeStruct((group_tok, cols), jnp.bfloat16),
            jax.ShapeDtypeStruct((tiles, cols, TILE), jnp.float32),
            jax.ShapeDtypeStruct((tiles, 1, 2 * TILE), jnp.float32),
        ),
        in_specs=[smem, smem, smem, vmem],
        out_specs=(vmem, vmem, vmem),
        scratch_shapes=[
            pltpu.VMEM((group_tok, cols), jnp.bfloat16),
            pltpu.VMEM((group_tok, cols), jnp.bfloat16),
            pltpu.VMEM((tiles, cols, TILE), jnp.bfloat16),
            pltpu.VMEM((group_tok, cols), jnp.bfloat16),
        ],
        name="attend_forward",
    )(slot_of, deal_table, prompt_len, qkv)

    def to_rows(array):
        moved = lax.all_to_all(
            array.reshape(devices_ctx, local_rows, cols), "ctx", split_axis=0, concat_axis=0
        )
        return moved.transpose(1, 0, 2).reshape(local_rows, width)

    def to_heads(array):
        moved = array.reshape(local_rows, devices_ctx, cols).transpose(1, 0, 2)
        return lax.all_to_all(moved, "ctx", split_axis=0, concat_axis=0).reshape(group_tok, cols)

    attn_rows = to_rows(attn)
    hidden = rows_f32 + jnp.dot(attn_rows, full_output, preferred_element_type=jnp.float32)
    normed_ffn, factor_ffn = rms_forward(hidden, gain_two)
    ffn_low = lax.all_gather(normed_ffn.astype(jnp.bfloat16), "ctx", axis=0, tiled=True)
    grad_down_in = lax.all_gather(cotangent[0], "ctx", axis=0, tiled=True)
    gate = jnp.dot(ffn_low, my_gate, preferred_element_type=jnp.float32)
    up_proj = jnp.dot(ffn_low, my_up, preferred_element_type=jnp.float32)
    sigmoid = jax.nn.sigmoid(gate)
    activated = gate * sigmoid
    inner_low = (activated * up_proj).astype(jnp.bfloat16)

    def summed_rows(array):
        return lax.psum_scatter(
            array.astype(jnp.bfloat16), "ctx", scatter_dimension=0, tiled=True
        ).astype(jnp.float32)

    grad_inner = jnp.dot(grad_down_in, my_down.T, preferred_element_type=jnp.float32)
    grad_gate = (grad_inner * up_proj * sigmoid * (1.0 + gate * (1.0 - sigmoid))).astype(
        jnp.bfloat16
    )
    grad_up = (grad_inner * activated).astype(jnp.bfloat16)
    grad_normed_ffn = summed_rows(
        jnp.dot(grad_gate, my_gate.T, preferred_element_type=jnp.float32)
        + jnp.dot(grad_up, my_up.T, preferred_element_type=jnp.float32)
    )
    layer = hidden + summed_rows(jnp.dot(inner_low, my_down, preferred_element_type=jnp.float32))
    grad_w_gate = jnp.dot(ffn_low.T, grad_gate, preferred_element_type=jnp.float32)
    grad_w_up = jnp.dot(ffn_low.T, grad_up, preferred_element_type=jnp.float32)
    grad_w_down = jnp.dot(inner_low.T, grad_down_in, preferred_element_type=jnp.float32)

    grad_hidden_norm, grad_gain_ffn = rms_backward(hidden, factor_ffn, gain_two, grad_normed_ffn)
    grad_hidden = cotangent[0].astype(jnp.float32) + grad_hidden_norm
    grad_branch = grad_hidden.astype(jnp.bfloat16)
    grad_w_output = jnp.dot(attn_rows.T, grad_branch, preferred_element_type=jnp.float32)
    grad_attn = to_heads(
        jnp.dot(grad_branch, full_output.T, preferred_element_type=jnp.float32).astype(
            jnp.bfloat16
        )
    )
    grad_qkv = pl.pallas_call(
        functools.partial(attend_backward, per_segment),
        out_shape=jax.ShapeDtypeStruct((group_tok, 3 * cols), jnp.bfloat16),
        in_specs=[smem, smem, smem, vmem, vmem, vmem, vmem],
        out_specs=vmem,
        scratch_shapes=[
            pltpu.VMEM((group_tok, cols), jnp.bfloat16),
            pltpu.VMEM((group_tok, cols), jnp.bfloat16),
            pltpu.VMEM((group_tok, cols), jnp.bfloat16),
            pltpu.VMEM((group_tok, cols), jnp.bfloat16),
            pltpu.VMEM((tiles, cols, TILE), jnp.bfloat16),
            pltpu.VMEM((group_tok, cols), jnp.float32),
            pltpu.VMEM((group_tok, cols), jnp.float32),
        ],
        name="attend_backward",
    )(slot_of, deal_table, prompt_len, qkv, grad_attn, attn_t, lse)
    grad_w_qkv = jnp.dot(normed_low.T, grad_qkv, preferred_element_type=jnp.float32)
    grad_normed = summed_rows(jnp.dot(grad_qkv, w_qkv.T, preferred_element_type=jnp.float32))
    factor_attn = lax.rsqrt(jnp.mean(rows_f32 * rows_f32, axis=-1, keepdims=True) + epsilon)
    grad_rows_norm, grad_gain_attn = rms_backward(rows_f32, factor_attn, gain_one, grad_normed)
    grad_rows = grad_hidden + grad_rows_norm

    def scattered(array, axis=0):
        return lax.psum_scatter(
            array.astype(jnp.bfloat16), "fsdp", scatter_dimension=axis, tiled=True
        )

    def spread(array):
        return lax.all_gather(array, "ctx", axis=0, tiled=False)

    qkv_shard = spread(scattered(grad_w_qkv))

    def columns_back(index):
        piece = qkv_shard[:, :, index * cols : (index + 1) * cols]
        return piece.transpose(1, 0, 2).reshape(-1, width).astype(jnp.float32)

    gate_up_shard = spread(scattered(jnp.concatenate([grad_w_gate, grad_w_up], axis=1)))

    def units_back(index):
        piece = gate_up_shard[:, :, index * hidden_units : (index + 1) * hidden_units]
        piece = piece.reshape(devices_ctx, -1, devices_fsdp, part).transpose(1, 2, 0, 3)
        return piece.reshape(-1, devices_fsdp * devices_ctx * part).astype(jnp.float32)

    down_shard = spread(scattered(grad_w_down)).reshape(-1, width).astype(jnp.float32)
    output_part = lax.psum_scatter(
        grad_w_output.astype(jnp.bfloat16), "ctx", scatter_dimension=1, tiled=True
    )
    output_shard = spread(scattered(output_part)).transpose(1, 0, 2).reshape(-1, width)
    gains_sum = lax.psum(
        lax.psum_scatter(
            jnp.stack([grad_gain_attn, grad_gain_ffn]), "fsdp", scatter_dimension=1, tiled=True
        ),
        "ctx",
    )
    return (
        layer.astype(jnp.bfloat16)[None],
        grad_rows[None],
        columns_back(0),
        columns_back(1),
        columns_back(2),
        output_shard.astype(jnp.float32),
        units_back(0),
        units_back(1),
        down_shard,
        gains_sum[0],
        gains_sum[1],
    )


def solution(mesh):
    if HEADS % mesh.shape["ctx"] == 0:
        per_device = heads_plan
    else:
        per_device = rows_plan
    placed = (
        P("fsdp", "ctx", None),
        P("fsdp", "ctx", None),
        P(),
        P("fsdp"),
        P("fsdp", None),
        P("fsdp", None),
        P("fsdp", None),
        P("fsdp", None),
        P("fsdp", None),
        P("fsdp", None),
        P("fsdp", None),
        P("fsdp"),
        P("fsdp"),
    )
    return jax.shard_map(
        per_device,
        mesh=mesh,
        in_specs=placed,
        out_specs=(
            P("fsdp", "ctx", None),
            P("fsdp", "ctx", None),
            P("fsdp", None),
            P("fsdp", None),
            P("fsdp", None),
            P("fsdp", None),
            P("fsdp", None),
            P("fsdp", None),
            P("fsdp", None),
            P("fsdp"),
            P("fsdp"),
        ),
        check_vma=False,
    )
```

```python
import functools
import math

import jax
import jax.numpy as jnp
from jax import lax
from jax.experimental import pallas as pl
from jax.experimental.pallas import tpu as pltpu
from jax.sharding import PartitionSpec as P

HEADS = 16
HEAD = 64
CONT_LEN = 1024


epsilon = 1e-05
score_scale = 0.125
masked_value = -1e30


def rms_forward(values, gain):
    factor = lax.rsqrt(jnp.mean(values * values, axis=-1, keepdims=True) + epsilon)
    return (values * factor * gain, factor)


def rms_backward(values, factor, gain, grad_normed):
    scaled = grad_normed * gain
    grad_gain = jnp.sum(grad_normed * values * factor, axis=0)
    cubed = factor * factor * factor
    grad_values = factor * scaled - values * cubed * jnp.mean(
        scaled * values, axis=-1, keepdims=True
    )
    return (grad_values, grad_gain)


def segment_of(position, prompt):
    return jnp.where(position < prompt, -1, (position - prompt) // CONT_LEN)


def visible(query_pos, key_pos, prompt, length):
    same = (segment_of(query_pos, prompt)[:, None] == segment_of(key_pos, prompt)[None, :]) & (
        key_pos[None, :] <= query_pos[:, None]
    )
    shared = (query_pos[:, None] >= prompt) & (key_pos[None, :] < length)
    return same | shared


def rows_plan(
    patches,
    cotangent,
    deal_table,
    prompt_len,
    w_query,
    w_key,
    w_value,
    w_output,
    w_gate,
    w_up,
    w_down,
    gain_attn,
    gain_ffn,
):
    local_rows = patches.shape[1]
    width = patches.shape[2]
    devices_ctx = lax.axis_size("ctx")
    group_tok = local_rows * devices_ctx
    cont_count = group_tok // (2 * CONT_LEN)
    prompt = group_tok - cont_count * CONT_LEN
    block_len = local_rows // 2
    slot_count = 2 * devices_ctx
    key_rows = math.gcd(512, group_tok)
    block_count = group_tok // key_rows
    length = prompt_len[0]

    def positions_of(first_row, count):
        stored = first_row + jnp.arange(count, dtype=jnp.int32)
        slot_ids = stored // block_len
        picked = jnp.where(
            slot_ids[:, None] == jnp.arange(slot_count, dtype=jnp.int32)[None, :],
            deal_table[None, :],
            0,
        )
        return jnp.sum(picked, axis=1) * block_len + stored % block_len

    query_pos = positions_of(lax.axis_index("ctx") * local_rows, local_rows)
    key_pos = positions_of(0, group_tok).reshape(block_count, key_rows)
    (
        full_query,
        full_key,
        full_value,
        full_output,
        full_gate,
        full_up,
        full_down,
        full_gain_attn,
        full_gain_ffn,
    ) = (
        lax.all_gather(w_query, "fsdp", axis=0, tiled=True),
        lax.all_gather(w_key, "fsdp", axis=0, tiled=True),
        lax.all_gather(w_value, "fsdp", axis=0, tiled=True),
        lax.all_gather(w_output, "fsdp", axis=0, tiled=True),
        lax.all_gather(w_gate, "fsdp", axis=0, tiled=True),
        lax.all_gather(w_up, "fsdp", axis=0, tiled=True),
        lax.all_gather(w_down, "fsdp", axis=0, tiled=True),
        lax.all_gather(gain_attn, "fsdp", axis=0, tiled=True),
        lax.all_gather(gain_ffn, "fsdp", axis=0, tiled=True),
    )
    rows_f32 = patches[0].astype(jnp.float32)
    gain_one = full_gain_attn.astype(jnp.float32)
    normed, factor_attn = rms_forward(rows_f32, gain_one)
    normed_low = normed.astype(jnp.bfloat16)
    queries = jnp.dot(normed_low, full_query, preferred_element_type=jnp.float32).astype(
        jnp.bfloat16
    )
    keys_local = jnp.dot(normed_low, full_key, preferred_element_type=jnp.float32).astype(
        jnp.bfloat16
    )
    values_local = jnp.dot(normed_low, full_value, preferred_element_type=jnp.float32).astype(
        jnp.bfloat16
    )
    key_all, value_all = (
        lax.all_gather(keys_local, "ctx", axis=0, tiled=True),
        lax.all_gather(values_local, "ctx", axis=0, tiled=True),
    )
    query_heads = queries.reshape(local_rows, HEADS, HEAD)

    def split_blocks(array):
        return array.reshape(block_count, key_rows, HEADS, HEAD)

    def forward_block(state, block):
        key_block, value_block, block_pos = block
        visible_mask = visible(query_pos, block_pos, prompt, length)

        def forward_update(inner_state):
            maxima, totals, accum = inner_state
            scores = (
                jnp.einsum(
                    "qhe,khe->hqk", query_heads, key_block, preferred_element_type=jnp.float32
                )
                * score_scale
            )
            scores = jnp.where(visible_mask[None], scores, masked_value)
            new_max = jnp.maximum(maxima, jnp.max(scores, axis=-1))
            rescale = jnp.exp(maxima - new_max)
            probs = jnp.where(visible_mask[None], jnp.exp(scores - new_max[:, :, None]), 0.0)
            totals = totals * rescale + jnp.sum(probs, axis=-1)
            accum = accum * rescale.T[:, :, None] + jnp.einsum(
                "hqk,khe->qhe",
                probs.astype(jnp.bfloat16),
                value_block,
                preferred_element_type=jnp.float32,
            )
            return (new_max, totals, accum)

        return (
            lax.cond(jnp.any(visible_mask), forward_update, lambda inner_state: inner_state, state),
            None,
        )

    start_state = (
        jnp.full((HEADS, local_rows), masked_value, jnp.float32),
        jnp.zeros((HEADS, local_rows), jnp.float32),
        jnp.zeros((local_rows, HEADS, HEAD), jnp.float32),
    )
    (maxima, totals, accum), unused = lax.scan(
        forward_block, start_state, (split_blocks(key_all), split_blocks(value_all), key_pos)
    )
    attn_f32 = accum / totals.T[:, :, None]
    log_total = maxima + jnp.log(totals)
    attn_low = attn_f32.astype(jnp.bfloat16).reshape(local_rows, width)
    hidden = rows_f32 + jnp.dot(attn_low, full_output, preferred_element_type=jnp.float32)
    gain_two = full_gain_ffn.astype(jnp.float32)
    normed_ffn, factor_ffn = rms_forward(hidden, gain_two)
    ffn_low = normed_ffn.astype(jnp.bfloat16)
    gate = jnp.dot(ffn_low, full_gate, preferred_element_type=jnp.float32)
    up_proj = jnp.dot(ffn_low, full_up, preferred_element_type=jnp.float32)
    sigmoid = jax.nn.sigmoid(gate)
    activated = gate * sigmoid
    inner_low = (activated * up_proj).astype(jnp.bfloat16)
    layer = hidden + jnp.dot(inner_low, full_down, preferred_element_type=jnp.float32)
    grad_out = cotangent[0].astype(jnp.float32)
    grad_down_in = cotangent[0]
    grad_w_down = jnp.dot(inner_low.T, grad_down_in, preferred_element_type=jnp.float32)
    grad_inner = jnp.dot(grad_down_in, full_down.T, preferred_element_type=jnp.float32)
    grad_gate = (grad_inner * up_proj * sigmoid * (1.0 + gate * (1.0 - sigmoid))).astype(
        jnp.bfloat16
    )
    grad_up = (grad_inner * activated).astype(jnp.bfloat16)
    grad_w_gate = jnp.dot(ffn_low.T, grad_gate, preferred_element_type=jnp.float32)
    grad_w_up = jnp.dot(ffn_low.T, grad_up, preferred_element_type=jnp.float32)
    grad_normed_ffn = jnp.dot(grad_gate, full_gate.T, preferred_element_type=jnp.float32) + jnp.dot(
        grad_up, full_up.T, preferred_element_type=jnp.float32
    )
    grad_hidden_norm, grad_gain_ffn = rms_backward(hidden, factor_ffn, gain_two, grad_normed_ffn)
    grad_hidden = grad_out + grad_hidden_norm
    grad_branch = grad_hidden.astype(jnp.bfloat16)
    grad_w_output = jnp.dot(attn_low.T, grad_branch, preferred_element_type=jnp.float32)
    grad_attn = (
        jnp.dot(grad_branch, full_output.T, preferred_element_type=jnp.float32)
        .astype(jnp.bfloat16)
        .reshape(local_rows, HEADS, HEAD)
    )
    delta = jnp.einsum("qhe,qhe->hq", grad_attn.astype(jnp.float32), attn_f32)
    key_back, value_back = (key_all, value_all)

    def backward_block(grad_query, block):
        key_block, value_block, block_pos = block
        visible_mask = visible(query_pos, block_pos, prompt, length)

        def backward_update(grad_state):
            scores = (
                jnp.einsum(
                    "qhe,khe->hqk", query_heads, key_block, preferred_element_type=jnp.float32
                )
                * score_scale
            )
            probs = jnp.where(visible_mask[None], jnp.exp(scores - log_total[:, :, None]), 0.0)
            grad_probs = jnp.einsum(
                "qhe,khe->hqk", grad_attn, value_block, preferred_element_type=jnp.float32
            )
            grad_scores = (probs * (grad_probs - delta[:, :, None])).astype(jnp.bfloat16)
            grad_state = (
                grad_state
                + jnp.einsum(
                    "hqk,khe->qhe", grad_scores, key_block, preferred_element_type=jnp.float32
                )
                * score_scale
            )
            grad_keys = (
                jnp.einsum(
                    "hqk,qhe->khe", grad_scores, query_heads, preferred_element_type=jnp.float32
                )
                * score_scale
            )
            grad_values = jnp.einsum(
                "hqk,qhe->khe",
                probs.astype(jnp.bfloat16),
                grad_attn,
                preferred_element_type=jnp.float32,
            )
            return (grad_state, (grad_keys, grad_values))

        def skipped(grad_state):
            empty = jnp.zeros((key_rows, HEADS, HEAD), jnp.float32)
            return (grad_state, (empty, empty))

        return lax.cond(jnp.any(visible_mask), backward_update, skipped, grad_query)

    zero_query = jnp.zeros((local_rows, HEADS, HEAD), jnp.float32)
    grad_query, (grad_key_blocks, grad_value_blocks) = lax.scan(
        backward_block, zero_query, (split_blocks(key_back), split_blocks(value_back), key_pos)
    )
    grad_key_sum, grad_value_sum = (
        lax.psum_scatter(
            grad_key_blocks.reshape(group_tok, width).astype(jnp.bfloat16),
            "ctx",
            scatter_dimension=0,
            tiled=True,
        ).astype(jnp.float32),
        lax.psum_scatter(
            grad_value_blocks.reshape(group_tok, width).astype(jnp.bfloat16),
            "ctx",
            scatter_dimension=0,
            tiled=True,
        ).astype(jnp.float32),
    )
    grad_key_low = grad_key_sum.astype(jnp.bfloat16)
    grad_value_low = grad_value_sum.astype(jnp.bfloat16)
    grad_query_low = grad_query.reshape(local_rows, width).astype(jnp.bfloat16)
    grad_w_query = jnp.dot(normed_low.T, grad_query_low, preferred_element_type=jnp.float32)
    grad_w_key = jnp.dot(normed_low.T, grad_key_low, preferred_element_type=jnp.float32)
    grad_w_value = jnp.dot(normed_low.T, grad_value_low, preferred_element_type=jnp.float32)
    grad_normed = (
        jnp.dot(grad_query_low, full_query.T, preferred_element_type=jnp.float32)
        + jnp.dot(grad_key_low, full_key.T, preferred_element_type=jnp.float32)
        + jnp.dot(grad_value_low, full_value.T, preferred_element_type=jnp.float32)
    )
    grad_rows_norm, grad_gain_attn = rms_backward(rows_f32, factor_attn, gain_one, grad_normed)
    grad_rows = grad_hidden + grad_rows_norm
    shards = (
        lax.psum_scatter(
            grad_w_query.astype(jnp.bfloat16), "fsdp", scatter_dimension=0, tiled=True
        ).astype(jnp.float32),
        lax.psum_scatter(
            grad_w_key.astype(jnp.bfloat16), "fsdp", scatter_dimension=0, tiled=True
        ).astype(jnp.float32),
        lax.psum_scatter(
            grad_w_value.astype(jnp.bfloat16), "fsdp", scatter_dimension=0, tiled=True
        ).astype(jnp.float32),
        lax.psum_scatter(
            grad_w_output.astype(jnp.bfloat16), "fsdp", scatter_dimension=0, tiled=True
        ).astype(jnp.float32),
        lax.psum_scatter(
            grad_w_gate.astype(jnp.bfloat16), "fsdp", scatter_dimension=0, tiled=True
        ).astype(jnp.float32),
        lax.psum_scatter(
            grad_w_up.astype(jnp.bfloat16), "fsdp", scatter_dimension=0, tiled=True
        ).astype(jnp.float32),
        lax.psum_scatter(
            grad_w_down.astype(jnp.bfloat16), "fsdp", scatter_dimension=0, tiled=True
        ).astype(jnp.float32),
        lax.psum_scatter(
            grad_gain_attn.astype(jnp.bfloat16), "fsdp", scatter_dimension=0, tiled=True
        ).astype(jnp.float32),
        lax.psum_scatter(
            grad_gain_ffn.astype(jnp.bfloat16), "fsdp", scatter_dimension=0, tiled=True
        ).astype(jnp.float32),
    )
    summed = (
        lax.psum(shards[0].astype(jnp.bfloat16), "ctx").astype(jnp.float32),
        lax.psum(shards[1].astype(jnp.bfloat16), "ctx").astype(jnp.float32),
        lax.psum(shards[2].astype(jnp.bfloat16), "ctx").astype(jnp.float32),
        lax.psum(shards[3].astype(jnp.bfloat16), "ctx").astype(jnp.float32),
        lax.psum(shards[4].astype(jnp.bfloat16), "ctx").astype(jnp.float32),
        lax.psum(shards[5].astype(jnp.bfloat16), "ctx").astype(jnp.float32),
        lax.psum(shards[6].astype(jnp.bfloat16), "ctx").astype(jnp.float32),
        lax.psum(shards[7].astype(jnp.bfloat16), "ctx").astype(jnp.float32),
        lax.psum(shards[8].astype(jnp.bfloat16), "ctx").astype(jnp.float32),
    )
    return (
        layer.astype(jnp.bfloat16)[None],
        grad_rows[None],
        summed[0],
        summed[1],
        summed[2],
        summed[3],
        summed[4],
        summed[5],
        summed[6],
        summed[7],
        summed[8],
    )


TILE = 256


def dot_f32(left, right, left_dim, right_dim):
    return lax.dot_general(
        left,
        right,
        (((left_dim,), (right_dim,)), ((), ())),
        preferred_element_type=jnp.float32,
    )


def head_masks():
    lane = lax.broadcasted_iota(jnp.int32, (TILE, 2 * HEAD), 1)
    first = (lane < HEAD).astype(jnp.bfloat16)
    return first, (1 - first).astype(jnp.bfloat16)


def stack_heads(tile, masks):
    return jnp.concatenate([tile * masks[0], tile * masks[1]], axis=0)


def tile_mask(kind, tile, length):
    row = lax.broadcasted_iota(jnp.int32, (TILE, 2 * TILE), 0)
    if kind == "diagonal":
        column = lax.broadcasted_iota(jnp.int32, (TILE, 2 * TILE), 1)
        return row <= jnp.where(column < TILE, column, column - TILE)
    return row + tile * TILE < length


def over_keys(tile, per_segment, step, state):
    base = tile // per_segment * per_segment
    state = lax.fori_loop(0, base, lambda key, kept: step(key, kept, "prompt"), state)
    state = lax.fori_loop(base, tile, lambda key, kept: step(key, kept, "full"), state)
    return step(tile, state, "diagonal")


def load_tile(ref, tile):
    held = TILE // ref.shape[1]
    return ref[pl.ds(tile * held, held)].reshape(TILE, ref.shape[2])


def store_tile(ref, tile, values):
    held = TILE // ref.shape[1]
    ref[pl.ds(tile * held, held)] = values.reshape(held, ref.shape[1], ref.shape[2])


def to_logical(slot_of, source, column, target, scale=None):
    for block in range(target.shape[0]):
        picked = source[slot_of[block], :, column : column + 2 * HEAD]
        if scale is not None:
            picked = picked * scale
        target[block] = picked


def to_stored(block_of, source, target, column):
    block_len = source.shape[1]
    for slot in range(source.shape[0]):
        target[slot * block_len : (slot + 1) * block_len, column : column + 2 * HEAD] = source[
            block_of[slot]
        ]


def tiles_between(count, one_tile, between):
    first = 0
    for stop in sorted(between):
        lax.fori_loop(first, stop, one_tile, 0)
        between[stop]()
        first = stop
    lax.fori_loop(first, count, one_tile, 0)


def attend_forward(
    per_segment,
    slot_of,
    block_of,
    length_ref,
    qkv,
    attn,
    attn_t,
    lse,
    query,
    key,
    value_t,
    kept,
    between,
):
    rows = qkv.shape[0] * qkv.shape[1]
    length = length_ref[0]
    to_logical(slot_of, qkv, 0, query, jnp.bfloat16(score_scale))
    to_logical(slot_of, qkv, 2 * HEAD, key)
    to_logical(slot_of, qkv, 4 * HEAD, kept)
    for tile in range(rows // TILE):
        value_t[tile] = load_tile(kept, tile).T
    masks = head_masks()

    def one_tile(tile, unused):
        both = stack_heads(load_tile(query, tile), masks)

        def step(key_tile, state, kind):
            maxima, totals, accum = state
            scores = dot_f32(load_tile(key, key_tile), both, 1, 1)
            if kind != "full":
                scores = jnp.where(tile_mask(kind, key_tile, length), scores, masked_value)
            new_max = jnp.maximum(maxima, jnp.max(scores, axis=0, keepdims=True))
            probs = jnp.exp(scores - new_max)
            rescale = jnp.exp(maxima - new_max)
            totals = totals * rescale + jnp.sum(probs, axis=0, keepdims=True)
            accum = accum * rescale + dot_f32(
                value_t[key_tile], probs.astype(jnp.bfloat16), 1, 0
            )
            return new_max, totals, accum

        maxima, totals, accum = over_keys(
            tile,
            per_segment,
            step,
            (
                jnp.full((1, 2 * TILE), masked_value, jnp.float32),
                jnp.zeros((1, 2 * TILE), jnp.float32),
                jnp.zeros((2 * HEAD, 2 * TILE), jnp.float32),
            ),
        )
        accum = accum / totals
        feature = lax.broadcasted_iota(jnp.int32, (2 * HEAD, TILE), 0)
        picked = jnp.where(feature < HEAD, accum[:, :TILE], accum[:, TILE:])
        attn_t[tile] = picked
        lse[tile] = maxima + jnp.log(totals)
        store_tile(kept, tile, picked.T.astype(jnp.bfloat16))
        return unused

    tiles_between(rows // TILE, one_tile, between)
    to_stored(block_of, kept, attn, 0)


def attend_backward(
    per_segment,
    slot_of,
    block_of,
    length_ref,
    qkv,
    grad_attn,
    attn_t,
    lse,
    grad_qkv,
    query,
    key,
    value,
    grad,
    key_t,
    grad_key,
    grad_value,
    between,
):
    rows = qkv.shape[0] * qkv.shape[1]
    length = length_ref[0]
    to_logical(slot_of, qkv, 0, query, jnp.bfloat16(score_scale))
    to_logical(slot_of, qkv, 2 * HEAD, key)
    to_logical(slot_of, qkv, 4 * HEAD, value)
    to_logical(slot_of, grad_attn, 0, grad)
    for tile in range(rows // TILE):
        key_t[tile] = load_tile(key, tile).T
    grad_key[...] = jnp.zeros_like(grad_key)
    grad_value[...] = jnp.zeros_like(grad_value)
    masks = head_masks()

    def one_tile(tile, unused):
        both = stack_heads(load_tile(query, tile), masks)
        grad_tile = load_tile(grad, tile)
        both_grad = stack_heads(grad_tile, masks)
        product = grad_tile.astype(jnp.float32).T * attn_t[tile]
        delta = jnp.concatenate(
            [
                jnp.sum(product[:HEAD], axis=0, keepdims=True),
                jnp.sum(product[HEAD:], axis=0, keepdims=True),
            ],
            axis=1,
        )
        log_total = lse[tile]

        def step(key_tile, grad_query, kind):
            keys_at = pl.ds(pl.multiple_of(key_tile * TILE, TILE), TILE)
            scores = dot_f32(load_tile(key, key_tile), both, 1, 1)
            if kind != "full":
                scores = jnp.where(tile_mask(kind, key_tile, length), scores, masked_value)
            probs = jnp.exp(scores - log_total)
            grad_probs = dot_f32(load_tile(value, key_tile), both_grad, 1, 1)
            grad_scores = (probs * (grad_probs - delta)).astype(jnp.bfloat16)
            grad_value[keys_at, :] += dot_f32(probs.astype(jnp.bfloat16), both_grad, 1, 0)
            grad_key[keys_at, :] += dot_f32(grad_scores, both, 1, 0)
            return grad_query + dot_f32(key_t[key_tile], grad_scores, 1, 0)

        grad_query = over_keys(
            tile, per_segment, step, jnp.zeros((2 * HEAD, 2 * TILE), jnp.float32)
        )
        feature = lax.broadcasted_iota(jnp.int32, (2 * HEAD, TILE), 0)
        picked = jnp.where(feature < HEAD, grad_query[:, :TILE], grad_query[:, TILE:])
        store_tile(query, tile, (picked * score_scale).T.astype(jnp.bfloat16))
        return unused

    tiles_between(rows // TILE, one_tile, between)
    key[...] = grad_key[...].astype(jnp.bfloat16).reshape(key.shape)
    value[...] = grad_value[...].astype(jnp.bfloat16).reshape(value.shape)
    to_stored(block_of, query, grad_qkv, 0)
    to_stored(block_of, key, grad_qkv, 2 * HEAD)
    to_stored(block_of, value, grad_qkv, 4 * HEAD)


def dma(count):
    return pltpu.SemaphoreType.DMA((count,))


def flipped(bit, flip):
    return bit + flip - 2 * bit * flip


class Place:
    def __init__(self, devices_fsdp):
        self.me = lax.axis_index("ctx")
        self.core = lax.rem(self.me, 2)
        self.column = lax.rem(self.me // 2, 2)
        self.row = self.me // 4
        self.group = lax.axis_index("fsdp")
        self.groups = devices_fsdp

    def peer(self, flip):
        low, middle, high = flip % 2, flip // 2 % 2, flip // 4
        return (
            flipped(self.row, high) * 4
            + flipped(self.column, middle) * 2
            + flipped(self.core, low)
        )

    def other_group(self, step):
        return lax.rem(self.group + step, self.groups)

    def meet(self):
        barrier = pltpu.get_barrier_semaphore()
        for flip in range(1, 8):
            pl.semaphore_signal(barrier, inc=1, device_id={"ctx": self.peer(flip)})
        for step in range(1, self.groups):
            pl.semaphore_signal(barrier, inc=1, device_id={"fsdp": self.other_group(step)})
        pl.semaphore_wait(barrier, 7 + self.groups - 1)


def remote(source, target, send, recv, device):
    return pltpu.make_async_remote_copy(
        src_ref=source,
        dst_ref=target,
        send_sem=send,
        recv_sem=recv,
        device_id=device,
        device_id_type=pl.DeviceIdType.MESH,
    )


class Spread:
    def __init__(self, place, own, region, send, recv):
        me, peer = place.me, place.peer

        def copy(index, source, target, flip):
            return remote(source, target, send.at[index], recv.at[index], {"ctx": peer(flip)})

        self.copies = [
            copy(0, own(None), region(me, None), 1),
            copy(1, own(0), region(me, 0), 2),
            copy(2, own(1), region(me, 1), 2),
            copy(3, own(1), region(me, 1), 4),
            copy(4, own(0), region(me, 0), 4),
            copy(5, region(peer(2), 0), region(peer(2), 0), 4),
            copy(6, region(peer(4), 1), region(peer(4), 1), 2),
            copy(7, region(peer(2), None), region(peer(2), None), 1),
            copy(8, region(peer(4), None), region(peer(4), None), 1),
            copy(9, region(peer(6), None), region(peer(6), None), 1),
        ]

    def start(self):
        for index in (1, 3, 0, 2, 4):
            self.copies[index].start()

    def arrived(self, *indices):
        for index in indices:
            self.copies[index].wait_recv()

    def relay_first(self):
        self.arrived(1)
        self.copies[5].start()
        self.arrived(3)
        self.copies[6].start()

    def relay_second(self):
        self.arrived(2)
        self.copies[7].start()
        self.arrived(4)
        self.copies[8].start()

    def relay_third(self):
        self.arrived(5, 6)
        self.copies[9].start()

    def sent(self):
        for copy in self.copies:
            copy.wait_send()


class PairSum:
    def __init__(self, place, stage, landed, sums, received, send, recv, out_send, out_recv):
        self.place = place
        self.stage, self.landed, self.sums, self.received = stage, landed, sums, received
        self.send, self.recv, self.out_send, self.out_recv = send, recv, out_send, out_recv

    def mine(self, pair):
        place = self.place
        return (
            flipped(place.row, pair // 2) * 4
            + flipped(place.column, lax.rem(pair, 2)) * 2
            + place.core
        )

    def theirs(self, pair):
        return self.mine(pair) + 1 - 2 * self.place.core

    def exchange(self, pair):
        return remote(
            self.stage.at[pair],
            self.landed.at[pair],
            self.send.at[pair],
            self.recv.at[pair],
            {"ctx": self.place.peer(1)},
        )

    def deliver(self, pair):
        return remote(
            self.sums.at[pair],
            self.received.at[pair],
            self.out_send.at[pair],
            self.out_recv.at[pair],
            {"ctx": self.mine(pair)},
        )

    def sent(self):
        for pair in range(4):
            self.exchange(pair).wait_send()
            if pair:
                self.deliver(pair).wait_send()


def halves(count):
    return lambda half: pl.ds(0 if half in (None, 0) else count // 2, count if half is None else count // 2)


def forward_kernel(
    per_segment,
    devices_fsdp,
    slot_of,
    block_of,
    length_ref,
    patches,
    cotangent,
    w_query,
    w_key,
    w_value,
    w_output,
    w_gate,
    w_up,
    w_down,
    gain_attn,
    gain_ffn,
    qkv,
    normed_out,
    attn_t,
    lse,
    qkv_out,
    gains_out,
    grad_units,
    grad_output,
    layer_sums,
    hidden,
    grad_hidden,
    gain_part,
    grad_attn_out,
    normed,
    grads,
    normed_ffn,
    w_qkv,
    output_all,
    gate_t,
    up_t,
    down,
    down_parts,
    gate_stage,
    up_stage,
    gain_stage,
    gains,
    query,
    key,
    value_t,
    kept,
    attn,
    attn_rows,
    own_ffn,
    inner_t,
    grad_gate_t,
    grad_up_t,
    stage,
    landed,
    own_sum,
    norm_sums,
    norm_received,
    down_tiles,
    grad_branch,
    grad_rows,
    grad_attn,
    local_sem,
    group_send,
    group_recv,
    x_send,
    x_recv,
    g_send,
    g_recv,
    o_send,
    o_recv,
    f_send,
    f_recv,
    a_send,
    a_recv,
    b_send,
    b_recv,
    pair_send,
    pair_recv,
    out_send,
    out_recv,
):
    place = Place(devices_fsdp)
    me, group = place.me, place.group
    local_rows, width = patches.shape
    cols = width // 8
    shard = w_query.shape[0]
    part = w_down.shape[1]
    units = part * devices_fsdp
    place.meet()

    def rows_of(block, count=local_rows):
        return pl.ds(pl.multiple_of(block * count, count), count)

    def rows_half(ref):
        def region(block, half):
            start = block * local_rows + (local_rows // 2 if half == 1 else 0)
            count = local_rows if half is None else local_rows // 2
            return ref.at[pl.ds(pl.multiple_of(start, local_rows // 2), count)]

        return region

    def own_half(ref):
        return lambda half: ref.at[halves(local_rows)(half)]

    spread_x = Spread(place, own_half(patches), rows_half(normed), x_send, x_recv)
    spread_x.start()

    my_cols = rows_of(me, cols)
    my_shard = rows_of(group, shard)
    group_items = [
        (w_query.at[:, my_cols], w_qkv.at[my_shard, 0:cols]),
        (w_key.at[:, my_cols], w_qkv.at[my_shard, cols : 2 * cols]),
        (w_value.at[:, my_cols], w_qkv.at[my_shard, 2 * cols : 3 * cols]),
        (gain_stage, gains.at[:, my_shard]),
        (w_output.at[me], output_all.at[group, me]),
        (gate_stage, gate_t.at[:, my_shard]),
        (up_stage, up_t.at[:, my_shard]),
        (w_down.at[me], down_parts.at[group]),
    ]

    def group_copies(index):
        source, target = group_items[index]
        return [
            remote(
                source,
                target,
                group_send.at[index, step - 1],
                group_recv.at[index, step - 1],
                {"fsdp": place.other_group(step)},
            )
            for step in range(1, devices_fsdp)
        ]

    def local_copy(index):
        source, target = group_items[index]
        return pltpu.make_async_copy(source, target, local_sem.at[index])

    def send_group(index):
        for copy in group_copies(index):
            copy.start()
        local_copy(index).start()

    def group_arrived(index):
        for copy in group_copies(index):
            copy.wait_recv()
        local_copy(index).wait()

    for index in (0, 1, 2):
        send_group(index)
    gain_stage[0:8, :] = jnp.broadcast_to(gain_attn[...].astype(jnp.float32), (8, shard))
    gain_stage[8:16, :] = jnp.broadcast_to(gain_ffn[...].astype(jnp.float32), (8, shard))
    send_group(3)
    send_group(4)

    def pick_units(weight, target):
        span = part * 8
        pieces = []
        for index in range(devices_fsdp):
            low = span * index // 128 * 128
            high = -(-span * (index + 1) // 128) * 128
            unit = lax.broadcasted_iota(jnp.int32, (part, high - low), 0)
            column = lax.broadcasted_iota(jnp.int32, (part, high - low), 1)
            chosen = (column + low == unit + span * index + part * me).astype(jnp.bfloat16)
            pieces.append(dot_f32(chosen, weight[:, low:high], 1, 1))
        target[...] = jnp.concatenate(pieces, axis=0).astype(jnp.bfloat16)

    pick_units(w_gate, gate_stage)
    pick_units(w_up, up_stage)
    send_group(5)
    send_group(6)
    send_group(7)

    normed[rows_of(me), :] = patches[...]
    grads[rows_of(me), :] = cotangent[...]
    spread_x.relay_first()
    spread_x.relay_second()
    spread_g = Spread(place, own_half(cotangent), rows_half(grads), g_send, g_recv)
    spread_g.start()
    spread_x.relay_third()
    spread_x.arrived(0, 7, 8, 9)
    for index in (0, 1, 2, 3):
        group_arrived(index)
    gain_one = gains[0:1, :]

    def project(block, unused):
        at = rows_of(block)
        values = normed[at, :].astype(jnp.float32)
        low = rms_forward(values, gain_one)[0].astype(jnp.bfloat16)
        normed[at, :] = low
        store_tile(qkv, block, dot_f32(low, w_qkv[...], 1, 0).astype(jnp.bfloat16))
        return unused

    spread_x.sent()
    lax.fori_loop(0, 8, project, 0)
    save_normed = pltpu.make_async_copy(normed, normed_out, local_sem.at[8])
    save_normed.start()

    group_arrived(4)

    def output_half(block, half):
        if half is None:
            return output_all.at[:, block]
        lines = output_all.shape[2]
        return output_all.at[:, block, halves(lines)(half)]

    spread_o = Spread(place, lambda half: output_half(me, half), output_half, o_send, o_recv)

    def after_prompt():
        spread_g.relay_first()
        spread_g.relay_second()
        spread_o.start()

    def after_half():
        spread_g.relay_third()
        spread_o.relay_first()
        spread_o.relay_second()

    attend_forward(
        per_segment,
        slot_of,
        block_of,
        length_ref,
        qkv,
        attn,
        attn_t,
        lse,
        query,
        key,
        value_t,
        kept,
        {per_segment: after_prompt, per_segment + per_segment // 2: after_half},
    )

    def swap(source, target, send, recv):
        return [
            remote(source(flip), target, send.at[flip - 1], recv.at[flip - 1], {"ctx": place.peer(flip)})
            for flip in range(1, 8)
        ]

    to_rows = swap(
        lambda flip: attn.at[rows_of(place.peer(flip))], attn_rows.at[:, my_cols], a_send, a_recv
    )
    for copy in to_rows:
        copy.start()
    attn_rows[:, my_cols] = attn[rows_of(me), :]
    spread_o.relay_third()
    for index in (5, 6, 7):
        group_arrived(index)
    down[...] = jnp.concatenate(
        [down_parts[index].astype(jnp.float32) for index in range(devices_fsdp)], axis=0
    ).astype(jnp.bfloat16)
    spread_g.arrived(0, 7, 8, 9)
    spread_o.arrived(0, 7, 8, 9)
    for copy in to_rows:
        copy.wait_recv()

    full_output = output_all[...].reshape(width, width)
    gain_two = gains[8:9, :]
    hidden[...] = patches[...].astype(jnp.float32) + dot_f32(attn_rows[...], full_output, 1, 0)
    own_ffn[...] = rms_forward(hidden[...], gain_two)[0].astype(jnp.bfloat16)
    spread_f = Spread(place, own_half(own_ffn), rows_half(normed_ffn), f_send, f_recv)
    spread_f.start()
    normed_ffn[rows_of(me), :] = own_ffn[...]

    sums = PairSum(
        place, stage, landed, norm_sums, norm_received, pair_send, pair_recv, out_send, out_recv
    )

    def feed(block):
        at = rows_of(block)
        low = normed_ffn[at, :]
        grad_out = grads[at, :]
        gate = dot_f32(low, gate_t[...], 1, 1)
        up_proj = dot_f32(low, up_t[...], 1, 1)
        grad_inner = dot_f32(grad_out, down[...], 1, 1)
        sigmoid = jax.nn.sigmoid(gate)
        activated = gate * sigmoid
        inner = activated * up_proj
        inner_low = inner.astype(jnp.bfloat16)
        grad_gate = grad_inner * up_proj * sigmoid * (1.0 + gate * (1.0 - sigmoid))
        grad_up = grad_inner * activated
        gate_low = grad_gate.astype(jnp.bfloat16)
        up_low = grad_up.astype(jnp.bfloat16)
        inner_t[:, at] = inner.T.astype(jnp.bfloat16)
        grad_gate_t[:, at] = grad_gate.T.astype(jnp.bfloat16)
        grad_up_t[:, at] = grad_up.T.astype(jnp.bfloat16)
        return (
            dot_f32(inner_low, down[...], 1, 0),
            dot_f32(gate_low, gate_t[...], 1, 0) + dot_f32(up_low, up_t[...], 1, 0),
        )

    def one_pair(pair, unused):
        @pl.when(pair == 0)
        def _():
            spread_f.arrived(0)

        @pl.when(pair == 1)
        def _():
            spread_f.relay_first()
            spread_f.relay_second()
            spread_f.arrived(7)

        @pl.when(pair == 2)
        def _():
            spread_f.arrived(8)

        @pl.when(pair == 3)
        def _():
            spread_f.relay_third()
            spread_f.arrived(9)

        layer, norm = feed(sums.theirs(pair))
        stage[pair, 0] = layer.astype(jnp.bfloat16)
        stage[pair, 1] = norm.astype(jnp.bfloat16)
        sums.exchange(pair).start()
        layer, norm = feed(sums.mine(pair))
        own_sum[0] = layer
        own_sum[1] = norm
        sums.exchange(pair).wait_recv()
        layer_sums[pair] = (own_sum[0] + landed[pair, 0].astype(jnp.float32)).astype(jnp.bfloat16)
        norm_sums[pair] = (own_sum[1] + landed[pair, 1].astype(jnp.float32)).astype(jnp.bfloat16)

        @pl.when(pair > 0)
        def _():
            sums.deliver(pair).start()

        return unused

    lax.fori_loop(0, 4, one_pair, 0)

    def units_tile(tile, unused):
        at = rows_of(tile, shard)
        low = normed_ffn[:, at]
        grad_units[tile, 0:units, :] = dot_f32(grad_gate_t[...], low, 1, 0).astype(jnp.bfloat16)
        grad_units[tile, units : 2 * units, :] = dot_f32(grad_up_t[...], low, 1, 0).astype(
            jnp.bfloat16
        )
        down_tiles[tile] = dot_f32(inner_t[...], grads[:, at], 1, 0)
        return unused

    lax.fori_loop(0, devices_fsdp, units_tile, 0)
    for index in range(devices_fsdp):
        grad_units[index, 2 * units : 3 * units, :] = jnp.concatenate(
            [
                down_tiles[tile, index * part : (index + 1) * part, :]
                for tile in range(devices_fsdp)
            ],
            axis=0,
        ).astype(jnp.bfloat16)

    total = norm_sums[0].astype(jnp.float32)
    for pair in range(1, 4):
        sums.deliver(pair).wait_recv()
        total = total + norm_received[pair].astype(jnp.float32)
    values = hidden[...]
    factor = lax.rsqrt(jnp.mean(values * values, axis=-1, keepdims=True) + epsilon)
    scaled = total * gain_two
    gain_part[...] = jnp.sum(total * values * factor, axis=0, keepdims=True)
    whole = (
        cotangent[...].astype(jnp.float32)
        + factor * scaled
        - values * (factor * factor * factor) * jnp.mean(scaled * values, axis=-1, keepdims=True)
    )
    grad_hidden[...] = whole
    grad_branch[...] = whole.astype(jnp.bfloat16)
    grad_rows[...] = dot_f32(grad_branch[...], output_all[...].reshape(width, width), 1, 1).astype(
        jnp.bfloat16
    )
    to_heads = swap(
        lambda flip: grad_rows.at[:, rows_of(place.peer(flip), cols)],
        grad_attn.at[rows_of(me)],
        b_send,
        b_recv,
    )
    for copy in to_heads:
        copy.start()
    grad_attn[rows_of(me), :] = grad_rows[:, my_cols]

    for index in range(devices_fsdp):
        piece = attn_rows[:, index * shard : (index + 1) * shard].T
        grad_output[index] = (
            dot_f32(piece, grad_branch[...], 1, 0)
            .astype(jnp.bfloat16)
            .reshape(8, shard // 8, width)
        )
    qkv_out[...] = w_qkv[...]
    gains_out[...] = gains[...]
    for copy in to_heads:
        copy.wait_recv()
    grad_attn_out[...] = grad_attn[...].reshape(grad_attn_out.shape)

    save_normed.wait()
    for index in range(8):
        for copy in group_copies(index):
            copy.wait_send()
    spread_g.sent()
    spread_o.sent()
    spread_f.sent()
    for copy in to_rows + to_heads:
        copy.wait_send()
    sums.sent()


def backward_kernel(
    per_segment,
    devices_fsdp,
    slot_of,
    block_of,
    length_ref,
    qkv,
    grad_attn,
    attn_t,
    lse,
    normed,
    w_qkv,
    gains,
    patches,
    grad_hidden,
    hidden,
    layer_sums,
    grad_units,
    grad_output,
    gain_part,
    layer,
    grad_patches,
    units_out,
    columns_out,
    gains_out,
    grad_qkv,
    query,
    key,
    value,
    grad,
    key_t,
    grad_key,
    grad_value,
    units_landed,
    units_stage,
    units_all,
    layer_received,
    output_stage,
    output_landed,
    output_sums,
    output_received,
    output_total,
    output_group,
    stage,
    landed,
    own_sum,
    norm_sums,
    norm_received,
    grad_qkv_t,
    qkv_parts,
    qkv_landed,
    columns_stage,
    columns_all,
    gain_stage,
    gain_landed,
    gain_total,
    gain_all,
    local_sem,
    units_send,
    units_recv,
    layer_send,
    layer_recv,
    wo_send,
    wo_recv,
    wo_out_send,
    wo_out_recv,
    group_send,
    group_recv,
    pair_send,
    pair_recv,
    out_send,
    out_recv,
    u_send,
    u_recv,
    c_send,
    c_recv,
    gain_send,
    gain_recv,
    gain_out_send,
    gain_out_recv,
):
    place = Place(devices_fsdp)
    me, group = place.me, place.group
    local_rows, width = patches.shape
    shard = width // devices_fsdp
    cols = width // 8
    units = grad_units.shape[1] // 3
    place.meet()

    def rows_of(block, count=local_rows):
        return pl.ds(pl.multiple_of(block * count, count), count)

    def over_groups(source, target, send, recv):
        return [
            remote(
                source(place.other_group(step)),
                target.at[group],
                send.at[step - 1],
                recv.at[step - 1],
                {"fsdp": place.other_group(step)},
            )
            for step in range(1, devices_fsdp)
        ]

    units_copies = over_groups(lambda to: grad_units.at[to], units_landed, units_send, units_recv)
    for copy in units_copies:
        copy.start()
    sums = PairSum(
        place, stage, landed, norm_sums, norm_received, pair_send, pair_recv, out_send, out_recv
    )
    output_pairs = PairSum(
        place,
        output_stage,
        output_landed,
        output_sums,
        output_received,
        wo_send,
        wo_recv,
        wo_out_send,
        wo_out_recv,
    )
    for pair in range(4):
        output_stage[pair] = grad_output[:, output_pairs.theirs(pair)]
        output_pairs.exchange(pair).start()
    layer_copies = [
        remote(
            layer_sums.at[pair],
            layer_received.at[pair],
            layer_send.at[pair],
            layer_recv.at[pair],
            {"ctx": sums.mine(pair)},
        )
        for pair in range(1, 4)
    ]
    for copy in layer_copies:
        copy.start()

    def after_prompt():
        for pair in range(4):
            output_pairs.exchange(pair).wait_recv()
            output_sums[pair] = (
                grad_output[:, output_pairs.mine(pair)].astype(jnp.float32)
                + output_landed[pair].astype(jnp.float32)
            ).astype(jnp.bfloat16)
            if pair:
                output_pairs.deliver(pair).start()

    attend_backward(
        per_segment,
        slot_of,
        block_of,
        length_ref,
        qkv,
        grad_attn,
        attn_t,
        lse,
        grad_qkv,
        query,
        key,
        value,
        grad,
        key_t,
        grad_key,
        grad_value,
        {per_segment: after_prompt},
    )

    def one_pair(pair, unused):
        stage[pair] = dot_f32(grad_qkv[rows_of(sums.theirs(pair)), :], w_qkv[...], 1, 1).astype(
            jnp.bfloat16
        )
        sums.exchange(pair).start()
        return unused

    lax.fori_loop(0, 4, one_pair, 0)

    def sum_pair(step, unused):
        pair = 3 - step
        own_sum[...] = dot_f32(grad_qkv[rows_of(sums.mine(pair)), :], w_qkv[...], 1, 1)
        sums.exchange(pair).wait_recv()
        norm_sums[pair] = (own_sum[...] + landed[pair].astype(jnp.float32)).astype(jnp.bfloat16)

        @pl.when(pair > 0)
        def _():
            sums.deliver(pair).start()

        return unused

    lax.fori_loop(0, 4, sum_pair, 0)

    def turn(tile, unused):
        at = rows_of(tile, TILE)
        grad_qkv_t[:, at] = grad_qkv[at, :].T
        return unused

    lax.fori_loop(0, grad_qkv.shape[0] // TILE, turn, 0)

    def weight_tile(tile, unused):
        qkv_parts[tile] = dot_f32(grad_qkv_t[...], normed[:, rows_of(tile, shard)], 1, 0).astype(
            jnp.bfloat16
        )
        return unused

    lax.fori_loop(0, devices_fsdp, weight_tile, 0)
    qkv_copies = over_groups(
        lambda to: qkv_parts.at[to], qkv_landed, group_send.at[0], group_recv.at[0]
    )
    for copy in qkv_copies:
        copy.start()

    total = output_sums[0].astype(jnp.float32)
    for pair in range(1, 4):
        output_pairs.deliver(pair).wait_recv()
        total = total + output_received[pair].astype(jnp.float32)
    output_total[...] = total.astype(jnp.bfloat16)
    output_copies = over_groups(
        lambda to: output_total.at[to], output_group, group_send.at[1], group_recv.at[1]
    )
    for copy in output_copies:
        copy.start()

    def group_sum(own, landed_ref, copies):
        landed_ref[group] = own
        for copy in copies:
            copy.wait_recv()
        total = landed_ref[0].astype(jnp.float32)
        for index in range(1, devices_fsdp):
            total = total + landed_ref[index].astype(jnp.float32)
        return total

    units_stage[...] = group_sum(grad_units[group], units_landed, units_copies).astype(
        jnp.bfloat16
    )

    def half_of(ref, lines):
        def region(block, half):
            return ref.at[block] if half is None else ref.at[block, halves(lines)(half)]

        return region

    def own_of(ref, lines):
        return lambda half: ref if half is None else ref.at[halves(lines)(half)]

    spread_u = Spread(
        place,
        own_of(units_stage, 3 * units),
        half_of(units_all, 3 * units),
        u_send,
        u_recv,
    )
    spread_u.start()
    units_all[me] = units_stage[...]

    total = layer_sums[0].astype(jnp.float32)
    for pair, copy in enumerate(layer_copies):
        copy.wait_recv()
        total = total + layer_received[pair + 1].astype(jnp.float32)
    layer[...] = (hidden[...] + total).astype(jnp.bfloat16)

    total = norm_sums[0].astype(jnp.float32)
    for pair in range(1, 4):
        sums.deliver(pair).wait_recv()
        total = total + norm_received[pair].astype(jnp.float32)
    values = patches[...].astype(jnp.float32)
    gain_one = gains[0:1, :]
    factor = lax.rsqrt(jnp.mean(values * values, axis=-1, keepdims=True) + epsilon)
    scaled = total * gain_one
    gain_stage[...] = jnp.zeros_like(gain_stage)
    attn_part = jnp.sum(total * values * factor, axis=0, keepdims=True)
    ffn_part = gain_part[...]
    for index in range(devices_fsdp):
        at = slice(index * shard, (index + 1) * shard)
        gain_stage[index, 0:1, :] = attn_part[:, at]
        gain_stage[index, 1:2, :] = ffn_part[:, at]
    gain_copies = over_groups(lambda to: gain_stage.at[to], gain_landed, gain_send, gain_recv)
    for copy in gain_copies:
        copy.start()
    grad_patches[...] = (
        grad_hidden[...]
        + factor * scaled
        - values * (factor * factor * factor) * jnp.mean(scaled * values, axis=-1, keepdims=True)
    )
    spread_u.relay_first()
    spread_u.relay_second()
    gain_total[...] = group_sum(gain_stage[group], gain_landed, gain_copies)
    gain_out = [
        remote(
            gain_total,
            gain_all.at[me],
            gain_out_send.at[flip - 1],
            gain_out_recv.at[flip - 1],
            {"ctx": place.peer(flip)},
        )
        for flip in range(1, 8)
    ]
    for copy in gain_out:
        copy.start()
    gain_all[me] = gain_total[...]

    turned = group_sum(qkv_parts[group], qkv_landed, qkv_copies).T.astype(jnp.bfloat16)
    for index in range(3):
        columns_stage[index * shard : (index + 1) * shard, :] = turned[
            :, index * cols : (index + 1) * cols
        ]
    summed = group_sum(output_total[group], output_group, output_copies).astype(jnp.bfloat16)
    lines = shard // 8
    for index in range(8):
        columns_stage[3 * shard + index * lines : 3 * shard + (index + 1) * lines, :] = summed[
            :, index * cols : (index + 1) * cols
        ]
    spread_c = Spread(
        place, own_of(columns_stage, 4 * shard), half_of(columns_all, 4 * shard), c_send, c_recv
    )
    spread_c.start()
    columns_all[me] = columns_stage[...]
    spread_u.relay_third()
    for copy in gain_out:
        copy.wait_recv()
    gain_sum = gain_all[0]
    for index in range(1, 8):
        gain_sum = gain_sum + gain_all[index]
    gains_out[...] = gain_sum
    spread_c.relay_first()
    spread_c.relay_second()
    spread_u.arrived(0, 7, 8, 9)
    save_units = pltpu.make_async_copy(units_all, units_out, local_sem.at[0])
    save_units.start()
    spread_c.relay_third()
    spread_c.arrived(0, 7, 8, 9)
    save_columns = pltpu.make_async_copy(columns_all, columns_out, local_sem.at[1])
    save_columns.start()
    for copy in units_copies + layer_copies + qkv_copies + output_copies + gain_copies + gain_out:
        copy.wait_send()
    sums.sent()
    output_pairs.sent()
    spread_u.sent()
    spread_c.sent()
    save_units.wait()
    save_columns.wait()


def place_kernel(
    devices_fsdp,
    units_all,
    columns_all,
    out_query,
    out_key,
    out_value,
    out_output,
    out_gate,
    out_up,
    out_down,
    columns,
    outputs,
    natural,
    gate,
    up,
    down,
    sems,
):
    shard = out_query.shape[0]
    cols = columns_all.shape[2]
    lines = shard // 8
    units = units_all.shape[1] // 3
    part = units // devices_fsdp
    span = part * 8
    saves = []

    def save(source, target):
        copy = pltpu.make_async_copy(source, target, sems.at[len(saves)])
        copy.start()
        saves.append(copy)

    for index in range(8):
        piece = units_all[index, 2 * units : 3 * units, :].astype(jnp.float32)
        for tile in range(devices_fsdp):
            down[index * part : (index + 1) * part, tile * shard : (tile + 1) * shard] = piece[
                tile * part : (tile + 1) * part, :
            ]
    save(down, out_down)
    for which, (target, out) in enumerate(((gate, out_gate), (up, out_up))):
        for index in range(8):
            piece = units_all[index, which * units : (which + 1) * units, :].astype(jnp.float32)
            for tile in range(devices_fsdp):
                first = tile * span + index * part
                natural[first : first + part, :] = piece[tile * part : (tile + 1) * part, :]
        for first in range(0, span * devices_fsdp, 128):
            target[:, first : first + 128] = natural[first : first + 128, :].T
        save(target, out)
    for index in range(8):
        at = slice(index * cols, (index + 1) * cols)
        for which in range(3):
            columns[which, :, at] = columns_all[
                index, which * shard : (which + 1) * shard, :
            ].astype(jnp.float32)
        for tile in range(8):
            first = 3 * shard + tile * lines
            outputs[index * lines : (index + 1) * lines, tile * cols : (tile + 1) * cols] = (
                columns_all[index, first : first + lines, :].astype(jnp.float32)
            )
    save(columns.at[0], out_query)
    save(columns.at[1], out_key)
    save(columns.at[2], out_value)
    save(outputs, out_output)
    for copy in saves:
        copy.wait()


def heads_plan(
    patches,
    cotangent,
    deal_table,
    prompt_len,
    w_query,
    w_key,
    w_value,
    w_output,
    w_gate,
    w_up,
    w_down,
    gain_attn,
    gain_ffn,
):
    local_rows = patches.shape[1]
    width = patches.shape[2]
    groups = lax.axis_size("fsdp")
    rows = local_rows * 8
    cols = width // 8
    shard = width // groups
    part = w_down.shape[0] // 8
    units = part * groups
    tiles = rows // TILE
    blocks = deal_table.shape[0]
    block_len = rows // blocks
    per_segment = CONT_LEN // TILE
    slots = jnp.arange(deal_table.shape[0], dtype=jnp.int32)
    slot_of = jnp.sum(
        jnp.where(deal_table[None, :] == slots[:, None], slots[None, :], 0), axis=1
    ).astype(jnp.int32)
    smem = pl.BlockSpec(memory_space=pltpu.SMEM)
    vmem = pl.BlockSpec(memory_space=pltpu.VMEM)
    anywhere = pl.BlockSpec(memory_space=pl.ANY)
    low, full = jnp.bfloat16, jnp.float32

    def shaped(kind, *dims):
        return jax.ShapeDtypeStruct(dims, kind)

    def room(kind, *dims):
        return pltpu.VMEM(dims, kind)

    (
        qkv,
        normed,
        attn_t,
        lse,
        w_qkv,
        gains,
        grad_units,
        grad_output,
        layer_sums,
        hidden,
        grad_hidden,
        gain_part,
        grad_attn,
    ) = pl.pallas_call(
        functools.partial(forward_kernel, per_segment, groups),
        out_shape=(
            shaped(low, blocks, block_len, 3 * cols),
            shaped(low, rows, width),
            shaped(full, tiles, cols, TILE),
            shaped(full, tiles, 1, 2 * TILE),
            shaped(low, width, 3 * cols),
            shaped(full, 16, width),
            shaped(low, groups, 3 * units, shard),
            shaped(low, groups, 8, shard // 8, width),
            shaped(low, 4, local_rows, width),
            shaped(full, local_rows, width),
            shaped(full, local_rows, width),
            shaped(full, 1, width),
            shaped(low, blocks, block_len, cols),
        ),
        in_specs=[smem] * 3
        + [vmem] * 2
        + [anywhere] * 4
        + [vmem] * 2
        + [anywhere]
        + [vmem] * 2,
        out_specs=(vmem, anywhere) + (vmem,) * 11,
        scratch_shapes=[
            room(low, rows, width),
            room(low, rows, width),
            room(low, rows, width),
            room(low, width, 3 * cols),
            room(low, groups, 8, shard // 8, width),
            room(low, units, width),
            room(low, units, width),
            room(low, units, width),
            room(low, groups, part, width),
            room(low, units, shard),
            room(low, units, shard),
            room(full, 16, shard),
            room(full, 16, width),
            room(low, blocks, block_len, cols),
            room(low, blocks, block_len, cols),
            room(low, tiles, cols, TILE),
            room(low, blocks, block_len, cols),
            room(low, rows, cols),
            room(low, local_rows, width),
            room(low, local_rows, width),
            room(low, units, rows),
            room(low, units, rows),
            room(low, units, rows),
            room(low, 4, 2, local_rows, width),
            room(low, 4, 2, local_rows, width),
            room(full, 2, local_rows, width),
            room(low, 4, local_rows, width),
            room(low, 4, local_rows, width),
            room(full, groups, units, shard),
            room(low, local_rows, width),
            room(low, local_rows, width),
            room(low, rows, cols),
            dma(9),
            pltpu.SemaphoreType.DMA((8, groups - 1)),
            pltpu.SemaphoreType.DMA((8, groups - 1)),
        ]
        + [dma(10)] * 8
        + [dma(7)] * 4
        + [dma(4)] * 4,
        compiler_params=pltpu.CompilerParams(
            collective_id=0, has_side_effects=True, vmem_limit_bytes=66_000_000
        ),
        name="forward",
    )(
        slot_of,
        deal_table,
        prompt_len,
        patches[0],
        cotangent[0],
        w_query,
        w_key,
        w_value,
        w_output.reshape(8, shard // 8, width),
        w_gate,
        w_up,
        w_down.reshape(8, part, width),
        gain_attn[None],
        gain_ffn[None],
    )

    layer, grad_rows, units_all, columns_all, gains_sum = pl.pallas_call(
        functools.partial(backward_kernel, per_segment, groups),
        out_shape=(
            shaped(low, local_rows, width),
            shaped(full, local_rows, width),
            shaped(low, 8, 3 * units, shard),
            shaped(low, 8, 4 * shard, cols),
            shaped(full, 8, shard),
        ),
        in_specs=[smem] * 3 + [vmem] * 14,
        out_specs=(vmem, vmem, anywhere, anywhere, vmem),
        scratch_shapes=[
            room(low, rows, 3 * cols),
            room(low, blocks, block_len, cols),
            room(low, blocks, block_len, cols),
            room(low, blocks, block_len, cols),
            room(low, blocks, block_len, cols),
            room(low, tiles, cols, TILE),
            room(full, rows, cols),
            room(full, rows, cols),
            room(low, groups, 3 * units, shard),
            room(low, 3 * units, shard),
            room(low, 8, 3 * units, shard),
            room(low, 4, local_rows, width),
            room(low, 4, groups, shard // 8, width),
            room(low, 4, groups, shard // 8, width),
            room(low, 4, groups, shard // 8, width),
            room(low, 4, groups, shard // 8, width),
            room(low, groups, shard // 8, width),
            room(low, groups, shard // 8, width),
            room(low, 4, local_rows, width),
            room(low, 4, local_rows, width),
            room(full, local_rows, width),
            room(low, 4, local_rows, width),
            room(low, 4, local_rows, width),
            room(low, 3 * cols, rows),
            room(low, groups, 3 * cols, shard),
            room(low, groups, 3 * cols, shard),
            room(low, 4 * shard, cols),
            room(low, 8, 4 * shard, cols),
            room(full, groups, 8, shard),
            room(full, groups, 8, shard),
            room(full, 8, shard),
            room(full, 8, 8, shard),
            dma(2),
            dma(groups - 1),
            dma(groups - 1),
            dma(4),
            dma(4),
            dma(4),
            dma(4),
            dma(4),
            dma(4),
            pltpu.SemaphoreType.DMA((2, groups - 1)),
            pltpu.SemaphoreType.DMA((2, groups - 1)),
            dma(4),
            dma(4),
            dma(4),
            dma(4),
            dma(10),
            dma(10),
            dma(10),
            dma(10),
            dma(groups - 1),
            dma(groups - 1),
            dma(7),
            dma(7),
        ],
        compiler_params=pltpu.CompilerParams(
            collective_id=1, has_side_effects=True, vmem_limit_bytes=66_000_000
        ),
        name="backward",
    )(
        slot_of,
        deal_table,
        prompt_len,
        qkv,
        grad_attn,
        attn_t,
        lse,
        normed,
        w_qkv,
        gains,
        patches[0],
        grad_hidden,
        hidden,
        layer_sums,
        grad_units,
        grad_output,
        gain_part,
    )

    weights = pl.pallas_call(
        functools.partial(place_kernel, groups),
        out_shape=tuple(shaped(full, shard, width) for _ in range(4))
        + tuple(shaped(full, shard, 8 * units) for _ in range(2))
        + (shaped(full, 8 * part, width),),
        in_specs=[vmem, vmem],
        out_specs=(anywhere,) * 7,
        scratch_shapes=[
            room(full, 3, shard, width),
            room(full, shard, width),
            room(full, 8 * units, shard),
            room(full, shard, 8 * units),
            room(full, shard, 8 * units),
            room(full, 8 * part, width),
            dma(7),
        ],
        name="place",
    )(units_all, columns_all)
    return (layer[None], grad_rows[None]) + tuple(weights) + (gains_sum[0], gains_sum[1])


def solution(mesh):
    if mesh.shape["ctx"] == 8:
        per_device = heads_plan
    else:
        per_device = rows_plan
    placed = (
        P("fsdp", "ctx", None),
        P("fsdp", "ctx", None),
        P(),
        P("fsdp"),
        P("fsdp", None),
        P("fsdp", None),
        P("fsdp", None),
        P("fsdp", None),
        P("fsdp", None),
        P("fsdp", None),
        P("fsdp", None),
        P("fsdp"),
        P("fsdp"),
    )
    return jax.shard_map(
        per_device,
        mesh=mesh,
        in_specs=placed,
        out_specs=(
            P("fsdp", "ctx", None),
            P("fsdp", "ctx", None),
            P("fsdp", None),
            P("fsdp", None),
            P("fsdp", None),
            P("fsdp", None),
            P("fsdp", None),
            P("fsdp", None),
            P("fsdp", None),
            P("fsdp"),
            P("fsdp"),
        ),
        check_vma=False,
    )
```

```python
import functools
import math

import jax
import jax.numpy as jnp
from jax import lax
from jax.experimental import pallas as pl
from jax.experimental.pallas import tpu as pltpu
from jax.sharding import PartitionSpec as P

HEADS = 16
HEAD = 64
CONT_LEN = 1024


epsilon = 1e-05
score_scale = 0.125
masked_value = -1e30


def rms_forward(values, gain):
    factor = lax.rsqrt(jnp.mean(values * values, axis=-1, keepdims=True) + epsilon)
    return (values * factor * gain, factor)


def rms_backward(values, factor, gain, grad_normed):
    scaled = grad_normed * gain
    grad_gain = jnp.sum(grad_normed * values * factor, axis=0)
    cubed = factor * factor * factor
    grad_values = factor * scaled - values * cubed * jnp.mean(
        scaled * values, axis=-1, keepdims=True
    )
    return (grad_values, grad_gain)


def segment_of(position, prompt):
    return jnp.where(position < prompt, -1, (position - prompt) // CONT_LEN)


def visible(query_pos, key_pos, prompt, length):
    same = (segment_of(query_pos, prompt)[:, None] == segment_of(key_pos, prompt)[None, :]) & (
        key_pos[None, :] <= query_pos[:, None]
    )
    shared = (query_pos[:, None] >= prompt) & (key_pos[None, :] < length)
    return same | shared


def rows_plan(
    patches,
    cotangent,
    deal_table,
    prompt_len,
    w_query,
    w_key,
    w_value,
    w_output,
    w_gate,
    w_up,
    w_down,
    gain_attn,
    gain_ffn,
):
    local_rows = patches.shape[1]
    width = patches.shape[2]
    devices_ctx = lax.axis_size("ctx")
    group_tok = local_rows * devices_ctx
    cont_count = group_tok // (2 * CONT_LEN)
    prompt = group_tok - cont_count * CONT_LEN
    block_len = local_rows // 2
    slot_count = 2 * devices_ctx
    key_rows = math.gcd(512, group_tok)
    block_count = group_tok // key_rows
    length = prompt_len[0]

    def positions_of(first_row, count):
        stored = first_row + jnp.arange(count, dtype=jnp.int32)
        slot_ids = stored // block_len
        picked = jnp.where(
            slot_ids[:, None] == jnp.arange(slot_count, dtype=jnp.int32)[None, :],
            deal_table[None, :],
            0,
        )
        return jnp.sum(picked, axis=1) * block_len + stored % block_len

    query_pos = positions_of(lax.axis_index("ctx") * local_rows, local_rows)
    key_pos = positions_of(0, group_tok).reshape(block_count, key_rows)
    (
        full_query,
        full_key,
        full_value,
        full_output,
        full_gate,
        full_up,
        full_down,
        full_gain_attn,
        full_gain_ffn,
    ) = (
        lax.all_gather(w_query, "fsdp", axis=0, tiled=True),
        lax.all_gather(w_key, "fsdp", axis=0, tiled=True),
        lax.all_gather(w_value, "fsdp", axis=0, tiled=True),
        lax.all_gather(w_output, "fsdp", axis=0, tiled=True),
        lax.all_gather(w_gate, "fsdp", axis=0, tiled=True),
        lax.all_gather(w_up, "fsdp", axis=0, tiled=True),
        lax.all_gather(w_down, "fsdp", axis=0, tiled=True),
        lax.all_gather(gain_attn, "fsdp", axis=0, tiled=True),
        lax.all_gather(gain_ffn, "fsdp", axis=0, tiled=True),
    )
    rows_f32 = patches[0].astype(jnp.float32)
    gain_one = full_gain_attn.astype(jnp.float32)
    normed, factor_attn = rms_forward(rows_f32, gain_one)
    normed_low = normed.astype(jnp.bfloat16)
    queries = jnp.dot(normed_low, full_query, preferred_element_type=jnp.float32).astype(
        jnp.bfloat16
    )
    keys_local = jnp.dot(normed_low, full_key, preferred_element_type=jnp.float32).astype(
        jnp.bfloat16
    )
    values_local = jnp.dot(normed_low, full_value, preferred_element_type=jnp.float32).astype(
        jnp.bfloat16
    )
    key_all, value_all = (
        lax.all_gather(keys_local, "ctx", axis=0, tiled=True),
        lax.all_gather(values_local, "ctx", axis=0, tiled=True),
    )
    query_heads = queries.reshape(local_rows, HEADS, HEAD)

    def split_blocks(array):
        return array.reshape(block_count, key_rows, HEADS, HEAD)

    def forward_block(state, block):
        key_block, value_block, block_pos = block
        visible_mask = visible(query_pos, block_pos, prompt, length)

        def forward_update(inner_state):
            maxima, totals, accum = inner_state
            scores = (
                jnp.einsum(
                    "qhe,khe->hqk", query_heads, key_block, preferred_element_type=jnp.float32
                )
                * score_scale
            )
            scores = jnp.where(visible_mask[None], scores, masked_value)
            new_max = jnp.maximum(maxima, jnp.max(scores, axis=-1))
            rescale = jnp.exp(maxima - new_max)
            probs = jnp.where(visible_mask[None], jnp.exp(scores - new_max[:, :, None]), 0.0)
            totals = totals * rescale + jnp.sum(probs, axis=-1)
            accum = accum * rescale.T[:, :, None] + jnp.einsum(
                "hqk,khe->qhe",
                probs.astype(jnp.bfloat16),
                value_block,
                preferred_element_type=jnp.float32,
            )
            return (new_max, totals, accum)

        return (
            lax.cond(jnp.any(visible_mask), forward_update, lambda inner_state: inner_state, state),
            None,
        )

    start_state = (
        jnp.full((HEADS, local_rows), masked_value, jnp.float32),
        jnp.zeros((HEADS, local_rows), jnp.float32),
        jnp.zeros((local_rows, HEADS, HEAD), jnp.float32),
    )
    (maxima, totals, accum), unused = lax.scan(
        forward_block, start_state, (split_blocks(key_all), split_blocks(value_all), key_pos)
    )
    attn_f32 = accum / totals.T[:, :, None]
    log_total = maxima + jnp.log(totals)
    attn_low = attn_f32.astype(jnp.bfloat16).reshape(local_rows, width)
    hidden = rows_f32 + jnp.dot(attn_low, full_output, preferred_element_type=jnp.float32)
    gain_two = full_gain_ffn.astype(jnp.float32)
    normed_ffn, factor_ffn = rms_forward(hidden, gain_two)
    ffn_low = normed_ffn.astype(jnp.bfloat16)
    gate = jnp.dot(ffn_low, full_gate, preferred_element_type=jnp.float32)
    up_proj = jnp.dot(ffn_low, full_up, preferred_element_type=jnp.float32)
    sigmoid = jax.nn.sigmoid(gate)
    activated = gate * sigmoid
    inner_low = (activated * up_proj).astype(jnp.bfloat16)
    layer = hidden + jnp.dot(inner_low, full_down, preferred_element_type=jnp.float32)
    grad_out = cotangent[0].astype(jnp.float32)
    grad_down_in = cotangent[0]
    grad_w_down = jnp.dot(inner_low.T, grad_down_in, preferred_element_type=jnp.float32)
    grad_inner = jnp.dot(grad_down_in, full_down.T, preferred_element_type=jnp.float32)
    grad_gate = (grad_inner * up_proj * sigmoid * (1.0 + gate * (1.0 - sigmoid))).astype(
        jnp.bfloat16
    )
    grad_up = (grad_inner * activated).astype(jnp.bfloat16)
    grad_w_gate = jnp.dot(ffn_low.T, grad_gate, preferred_element_type=jnp.float32)
    grad_w_up = jnp.dot(ffn_low.T, grad_up, preferred_element_type=jnp.float32)
    grad_normed_ffn = jnp.dot(grad_gate, full_gate.T, preferred_element_type=jnp.float32) + jnp.dot(
        grad_up, full_up.T, preferred_element_type=jnp.float32
    )
    grad_hidden_norm, grad_gain_ffn = rms_backward(hidden, factor_ffn, gain_two, grad_normed_ffn)
    grad_hidden = grad_out + grad_hidden_norm
    grad_branch = grad_hidden.astype(jnp.bfloat16)
    grad_w_output = jnp.dot(attn_low.T, grad_branch, preferred_element_type=jnp.float32)
    grad_attn = (
        jnp.dot(grad_branch, full_output.T, preferred_element_type=jnp.float32)
        .astype(jnp.bfloat16)
        .reshape(local_rows, HEADS, HEAD)
    )
    delta = jnp.einsum("qhe,qhe->hq", grad_attn.astype(jnp.float32), attn_f32)
    key_back, value_back = (key_all, value_all)

    def backward_block(grad_query, block):
        key_block, value_block, block_pos = block
        visible_mask = visible(query_pos, block_pos, prompt, length)

        def backward_update(grad_state):
            scores = (
                jnp.einsum(
                    "qhe,khe->hqk", query_heads, key_block, preferred_element_type=jnp.float32
                )
                * score_scale
            )
            probs = jnp.where(visible_mask[None], jnp.exp(scores - log_total[:, :, None]), 0.0)
            grad_probs = jnp.einsum(
                "qhe,khe->hqk", grad_attn, value_block, preferred_element_type=jnp.float32
            )
            grad_scores = (probs * (grad_probs - delta[:, :, None])).astype(jnp.bfloat16)
            grad_state = (
                grad_state
                + jnp.einsum(
                    "hqk,khe->qhe", grad_scores, key_block, preferred_element_type=jnp.float32
                )
                * score_scale
            )
            grad_keys = (
                jnp.einsum(
                    "hqk,qhe->khe", grad_scores, query_heads, preferred_element_type=jnp.float32
                )
                * score_scale
            )
            grad_values = jnp.einsum(
                "hqk,qhe->khe",
                probs.astype(jnp.bfloat16),
                grad_attn,
                preferred_element_type=jnp.float32,
            )
            return (grad_state, (grad_keys, grad_values))

        def skipped(grad_state):
            empty = jnp.zeros((key_rows, HEADS, HEAD), jnp.float32)
            return (grad_state, (empty, empty))

        return lax.cond(jnp.any(visible_mask), backward_update, skipped, grad_query)

    zero_query = jnp.zeros((local_rows, HEADS, HEAD), jnp.float32)
    grad_query, (grad_key_blocks, grad_value_blocks) = lax.scan(
        backward_block, zero_query, (split_blocks(key_back), split_blocks(value_back), key_pos)
    )
    grad_key_sum, grad_value_sum = (
        lax.psum_scatter(
            grad_key_blocks.reshape(group_tok, width).astype(jnp.bfloat16),
            "ctx",
            scatter_dimension=0,
            tiled=True,
        ).astype(jnp.float32),
        lax.psum_scatter(
            grad_value_blocks.reshape(group_tok, width).astype(jnp.bfloat16),
            "ctx",
            scatter_dimension=0,
            tiled=True,
        ).astype(jnp.float32),
    )
    grad_key_low = grad_key_sum.astype(jnp.bfloat16)
    grad_value_low = grad_value_sum.astype(jnp.bfloat16)
    grad_query_low = grad_query.reshape(local_rows, width).astype(jnp.bfloat16)
    grad_w_query = jnp.dot(normed_low.T, grad_query_low, preferred_element_type=jnp.float32)
    grad_w_key = jnp.dot(normed_low.T, grad_key_low, preferred_element_type=jnp.float32)
    grad_w_value = jnp.dot(normed_low.T, grad_value_low, preferred_element_type=jnp.float32)
    grad_normed = (
        jnp.dot(grad_query_low, full_query.T, preferred_element_type=jnp.float32)
        + jnp.dot(grad_key_low, full_key.T, preferred_element_type=jnp.float32)
        + jnp.dot(grad_value_low, full_value.T, preferred_element_type=jnp.float32)
    )
    grad_rows_norm, grad_gain_attn = rms_backward(rows_f32, factor_attn, gain_one, grad_normed)
    grad_rows = grad_hidden + grad_rows_norm
    shards = (
        lax.psum_scatter(
            grad_w_query.astype(jnp.bfloat16), "fsdp", scatter_dimension=0, tiled=True
        ).astype(jnp.float32),
        lax.psum_scatter(
            grad_w_key.astype(jnp.bfloat16), "fsdp", scatter_dimension=0, tiled=True
        ).astype(jnp.float32),
        lax.psum_scatter(
            grad_w_value.astype(jnp.bfloat16), "fsdp", scatter_dimension=0, tiled=True
        ).astype(jnp.float32),
        lax.psum_scatter(
            grad_w_output.astype(jnp.bfloat16), "fsdp", scatter_dimension=0, tiled=True
        ).astype(jnp.float32),
        lax.psum_scatter(
            grad_w_gate.astype(jnp.bfloat16), "fsdp", scatter_dimension=0, tiled=True
        ).astype(jnp.float32),
        lax.psum_scatter(
            grad_w_up.astype(jnp.bfloat16), "fsdp", scatter_dimension=0, tiled=True
        ).astype(jnp.float32),
        lax.psum_scatter(
            grad_w_down.astype(jnp.bfloat16), "fsdp", scatter_dimension=0, tiled=True
        ).astype(jnp.float32),
        lax.psum_scatter(
            grad_gain_attn.astype(jnp.bfloat16), "fsdp", scatter_dimension=0, tiled=True
        ).astype(jnp.float32),
        lax.psum_scatter(
            grad_gain_ffn.astype(jnp.bfloat16), "fsdp", scatter_dimension=0, tiled=True
        ).astype(jnp.float32),
    )
    summed = (
        lax.psum(shards[0].astype(jnp.bfloat16), "ctx").astype(jnp.float32),
        lax.psum(shards[1].astype(jnp.bfloat16), "ctx").astype(jnp.float32),
        lax.psum(shards[2].astype(jnp.bfloat16), "ctx").astype(jnp.float32),
        lax.psum(shards[3].astype(jnp.bfloat16), "ctx").astype(jnp.float32),
        lax.psum(shards[4].astype(jnp.bfloat16), "ctx").astype(jnp.float32),
        lax.psum(shards[5].astype(jnp.bfloat16), "ctx").astype(jnp.float32),
        lax.psum(shards[6].astype(jnp.bfloat16), "ctx").astype(jnp.float32),
        lax.psum(shards[7].astype(jnp.bfloat16), "ctx").astype(jnp.float32),
        lax.psum(shards[8].astype(jnp.bfloat16), "ctx").astype(jnp.float32),
    )
    return (
        layer.astype(jnp.bfloat16)[None],
        grad_rows[None],
        summed[0],
        summed[1],
        summed[2],
        summed[3],
        summed[4],
        summed[5],
        summed[6],
        summed[7],
        summed[8],
    )


TILE = 256


def dot_f32(left, right, left_dim, right_dim):
    return lax.dot_general(
        left,
        right,
        (((left_dim,), (right_dim,)), ((), ())),
        preferred_element_type=jnp.float32,
    )


def head_masks():
    lane = lax.broadcasted_iota(jnp.int32, (TILE, 2 * HEAD), 1)
    first = (lane < HEAD).astype(jnp.bfloat16)
    return first, (1 - first).astype(jnp.bfloat16)


def stack_heads(tile, masks):
    return jnp.concatenate([tile * masks[0], tile * masks[1]], axis=0)


def tile_mask(kind, tile, length):
    row = lax.broadcasted_iota(jnp.int32, (TILE, 2 * TILE), 0)
    if kind == "diagonal":
        column = lax.broadcasted_iota(jnp.int32, (TILE, 2 * TILE), 1)
        return row <= jnp.where(column < TILE, column, column - TILE)
    return row + tile * TILE < length


def over_keys(tile, per_segment, step, state):
    base = tile // per_segment * per_segment
    state = lax.fori_loop(0, base, lambda key, kept: step(key, kept, "prompt"), state)
    state = lax.fori_loop(base, tile, lambda key, kept: step(key, kept, "full"), state)
    return step(tile, state, "diagonal")


def load_tile(ref, tile):
    held = TILE // ref.shape[1]
    return ref[pl.ds(tile * held, held)].reshape(TILE, ref.shape[2])


def store_tile(ref, tile, values):
    held = TILE // ref.shape[1]
    ref[pl.ds(tile * held, held)] = values.reshape(held, ref.shape[1], ref.shape[2])


def to_logical(slot_of, source, column, target, scale=None):
    for block in range(target.shape[0]):
        picked = source[slot_of[block], :, column : column + 2 * HEAD]
        if scale is not None:
            picked = picked * scale
        target[block] = picked


def to_stored(block_of, source, target, column):
    block_len = source.shape[1]
    for slot in range(source.shape[0]):
        target[slot * block_len : (slot + 1) * block_len, column : column + 2 * HEAD] = source[
            block_of[slot]
        ]


def tiles_between(count, one_tile, between):
    first = 0
    for stop in sorted(between):
        lax.fori_loop(first, stop, one_tile, 0)
        between[stop]()
        first = stop
    lax.fori_loop(first, count, one_tile, 0)


def attend_forward(
    per_segment,
    slot_of,
    length_ref,
    qkv,
    attn_t,
    lse,
    query,
    key,
    value_t,
    kept,
    between,
):
    rows = qkv.shape[0] * qkv.shape[1]
    length = length_ref[0]
    to_logical(slot_of, qkv, 0, query, jnp.bfloat16(score_scale))
    to_logical(slot_of, qkv, 2 * HEAD, key)
    to_logical(slot_of, qkv, 4 * HEAD, kept)
    for tile in range(rows // TILE):
        value_t[tile] = load_tile(kept, tile).T
    masks = head_masks()

    def one_tile(tile, unused):
        both = stack_heads(load_tile(query, tile), masks)

        def step(key_tile, state, kind):
            maxima, totals, accum = state
            scores = dot_f32(load_tile(key, key_tile), both, 1, 1)
            if kind != "full":
                scores = jnp.where(tile_mask(kind, key_tile, length), scores, masked_value)
            new_max = jnp.maximum(maxima, jnp.max(scores, axis=0, keepdims=True))
            probs = jnp.exp(scores - new_max)
            rescale = jnp.exp(maxima - new_max)
            totals = totals * rescale + jnp.sum(probs, axis=0, keepdims=True)
            accum = accum * rescale + dot_f32(
                value_t[key_tile], probs.astype(jnp.bfloat16), 1, 0
            )
            return new_max, totals, accum

        maxima, totals, accum = over_keys(
            tile,
            per_segment,
            step,
            (
                jnp.full((1, 2 * TILE), masked_value, jnp.float32),
                jnp.zeros((1, 2 * TILE), jnp.float32),
                jnp.zeros((2 * HEAD, 2 * TILE), jnp.float32),
            ),
        )
        accum = accum / totals
        feature = lax.broadcasted_iota(jnp.int32, (2 * HEAD, TILE), 0)
        picked = jnp.where(feature < HEAD, accum[:, :TILE], accum[:, TILE:])
        attn_t[tile] = picked
        lse[tile] = maxima + jnp.log(totals)
        store_tile(kept, tile, picked.T.astype(jnp.bfloat16))
        return unused

    tiles_between(rows // TILE, one_tile, between)


def attend_backward(
    per_segment,
    slot_of,
    block_of,
    length_ref,
    qkv,
    grad_attn,
    attn_t,
    lse,
    grad_qkv,
    query,
    key,
    value,
    grad,
    key_t,
    grad_key,
    grad_value,
    between,
):
    rows = qkv.shape[0] * qkv.shape[1]
    length = length_ref[0]
    to_logical(slot_of, qkv, 0, query, jnp.bfloat16(score_scale))
    to_logical(slot_of, qkv, 2 * HEAD, key)
    to_logical(slot_of, qkv, 4 * HEAD, value)
    to_logical(slot_of, grad_attn, 0, grad)
    for tile in range(rows // TILE):
        key_t[tile] = load_tile(key, tile).T
    grad_key[...] = jnp.zeros_like(grad_key)
    grad_value[...] = jnp.zeros_like(grad_value)
    masks = head_masks()

    def one_tile(tile, unused):
        both = stack_heads(load_tile(query, tile), masks)
        grad_tile = load_tile(grad, tile)
        both_grad = stack_heads(grad_tile, masks)
        product = grad_tile.astype(jnp.float32).T * attn_t[tile]
        delta = jnp.concatenate(
            [
                jnp.sum(product[:HEAD], axis=0, keepdims=True),
                jnp.sum(product[HEAD:], axis=0, keepdims=True),
            ],
            axis=1,
        )
        log_total = lse[tile]

        def step(key_tile, grad_query, kind):
            keys_at = pl.ds(pl.multiple_of(key_tile * TILE, TILE), TILE)
            scores = dot_f32(load_tile(key, key_tile), both, 1, 1)
            if kind != "full":
                scores = jnp.where(tile_mask(kind, key_tile, length), scores, masked_value)
            probs = jnp.exp(scores - log_total)
            grad_probs = dot_f32(load_tile(value, key_tile), both_grad, 1, 1)
            grad_scores = (probs * (grad_probs - delta)).astype(jnp.bfloat16)
            grad_value[keys_at, :] += dot_f32(probs.astype(jnp.bfloat16), both_grad, 1, 0)
            grad_key[keys_at, :] += dot_f32(grad_scores, both, 1, 0)
            return grad_query + dot_f32(key_t[key_tile], grad_scores, 1, 0)

        grad_query = over_keys(
            tile, per_segment, step, jnp.zeros((2 * HEAD, 2 * TILE), jnp.float32)
        )
        feature = lax.broadcasted_iota(jnp.int32, (2 * HEAD, TILE), 0)
        picked = jnp.where(feature < HEAD, grad_query[:, :TILE], grad_query[:, TILE:])
        store_tile(query, tile, (picked * score_scale).T.astype(jnp.bfloat16))
        return unused

    tiles_between(rows // TILE, one_tile, between)
    key[...] = grad_key[...].astype(jnp.bfloat16).reshape(key.shape)
    value[...] = grad_value[...].astype(jnp.bfloat16).reshape(value.shape)
    to_stored(block_of, query, grad_qkv, 0)
    to_stored(block_of, key, grad_qkv, 2 * HEAD)
    to_stored(block_of, value, grad_qkv, 4 * HEAD)


def dma(count):
    return pltpu.SemaphoreType.DMA((count,))


def flipped(bit, flip):
    return bit + flip - 2 * bit * flip


class Place:
    def __init__(self, devices_fsdp):
        self.me = lax.axis_index("ctx")
        self.core = lax.rem(self.me, 2)
        self.column = lax.rem(self.me // 2, 2)
        self.row = self.me // 4
        self.group = lax.axis_index("fsdp")
        self.groups = devices_fsdp

    def peer(self, flip):
        low, middle, high = flip % 2, flip // 2 % 2, flip // 4
        return (
            flipped(self.row, high) * 4
            + flipped(self.column, middle) * 2
            + flipped(self.core, low)
        )

    def other_group(self, step):
        return lax.rem(self.group + step, self.groups)

    def at_end(self):
        return lax.rem(self.group, 3) == 0

    def between(self):
        return lax.rem(self.group, 3) != 0

    def near(self, step):
        return self.group != {1: 3, 2: 4, 3: 0}[step]

    def heard(self, step):
        return self.group != {1: 0, 2: 4, 3: 3}[step]

    def meet(self):
        barrier = pltpu.get_barrier_semaphore()
        for flip in range(1, 8):
            pl.semaphore_signal(barrier, inc=1, device_id={"ctx": self.peer(flip)})
        for step in range(1, self.groups):
            pl.semaphore_signal(barrier, inc=1, device_id={"fsdp": self.other_group(step)})
        pl.semaphore_wait(barrier, 7 + self.groups - 1)


def remote(source, target, send, recv, device):
    return pltpu.make_async_remote_copy(
        src_ref=source,
        dst_ref=target,
        send_sem=send,
        recv_sem=recv,
        device_id=device,
        device_id_type=pl.DeviceIdType.MESH,
    )


class Spread:
    def __init__(self, place, own, region, send, recv):
        me, peer = place.me, place.peer

        def copy(index, source, target, flip):
            return remote(source, target, send.at[index], recv.at[index], {"ctx": peer(flip)})

        self.copies = [
            copy(0, own(None), region(me, None), 1),
            copy(1, own(0), region(me, 0), 2),
            copy(2, own(1), region(me, 1), 2),
            copy(3, own(1), region(me, 1), 4),
            copy(4, own(0), region(me, 0), 4),
            copy(5, region(peer(2), 0), region(peer(2), 0), 4),
            copy(6, region(peer(4), 1), region(peer(4), 1), 2),
            copy(7, region(peer(2), None), region(peer(2), None), 1),
            copy(8, region(peer(4), None), region(peer(4), None), 1),
            copy(9, region(peer(6), None), region(peer(6), None), 1),
        ]

    def start(self):
        for index in (1, 3, 0, 2, 4):
            self.copies[index].start()

    def arrived(self, *indices):
        for index in indices:
            self.copies[index].wait_recv()

    def relay_first(self):
        self.arrived(1)
        self.copies[5].start()
        self.arrived(3)
        self.copies[6].start()

    def relay_second(self):
        self.arrived(2)
        self.copies[7].start()
        self.arrived(4)
        self.copies[8].start()

    def relay_third(self):
        self.arrived(5, 6)
        self.copies[9].start()

    def sent(self):
        for copy in self.copies:
            copy.wait_send()


class PairSum:
    def __init__(self, place, stage, landed, sums, received, send, recv, out_send, out_recv):
        self.place = place
        self.stage, self.landed, self.sums, self.received = stage, landed, sums, received
        self.send, self.recv, self.out_send, self.out_recv = send, recv, out_send, out_recv

    def mine(self, pair):
        place = self.place
        return (
            flipped(place.row, pair // 2) * 4
            + flipped(place.column, lax.rem(pair, 2)) * 2
            + place.core
        )

    def theirs(self, pair):
        return self.mine(pair) + 1 - 2 * self.place.core

    def exchange(self, pair):
        return remote(
            self.stage.at[pair],
            self.landed.at[pair],
            self.send.at[pair],
            self.recv.at[pair],
            {"ctx": self.place.peer(1)},
        )

    def deliver(self, pair):
        return remote(
            self.sums.at[pair],
            self.received.at[pair],
            self.out_send.at[pair],
            self.out_recv.at[pair],
            {"ctx": self.mine(pair)},
        )

    def sent(self):
        for pair in range(4):
            self.exchange(pair).wait_send()
            if pair:
                self.deliver(pair).wait_send()


class CrossSum(PairSum):
    def __init__(self, place, stage, landed, sums, received, passed, send, recv, out_send, out_recv):
        super().__init__(place, stage, landed, sums, received, send, recv, out_send, out_recv)
        self.passed = passed

    def half(self, which):
        count = self.sums.shape[1] // 2
        return slice(which * count, (which + 1) * count)

    def far(self, which):
        slot = 3 * which
        return remote(
            self.sums.at[3, self.half(which)],
            self.passed.at[which],
            self.out_send.at[slot],
            self.out_recv.at[slot],
            {"ctx": self.place.peer(2 + 2 * which)},
        )

    def deliver(self, pair):
        return remote(
            self.sums.at[pair],
            self.received.at[pair - 1],
            self.out_send.at[pair],
            self.out_recv.at[pair],
            {"ctx": self.place.peer(2 * pair)},
        )

    def finish(self, pair, total):
        self.sums[pair] = total.astype(jnp.bfloat16)

        @pl.when(pair == 3)
        def _():
            self.far(0).start()
            self.far(1).start()

        for axis in (1, 2):
            which = 2 - axis

            @pl.when(pair == axis)
            def _(axis=axis, which=which):
                at = self.half(which)
                self.far(which).wait_recv()
                self.sums[axis, at, :] = (
                    total[at] + self.passed[which].astype(jnp.float32)
                ).astype(jnp.bfloat16)
                self.deliver(axis).start()

    def collect(self):
        total = self.sums[0].astype(jnp.float32)
        for pair in (1, 2):
            self.deliver(pair).wait_recv()
            total = total + self.received[pair - 1].astype(jnp.float32)
        return total

    def sent(self):
        for pair in range(4):
            self.exchange(pair).wait_send()
        for which in (0, 1):
            self.far(which).wait_send()
            self.deliver(which + 1).wait_send()


def halves(count):
    return lambda half: pl.ds(0 if half in (None, 0) else count // 2, count if half is None else count // 2)


def forward_kernel(
    per_segment,
    devices_fsdp,
    slot_of,
    block_of,
    length_ref,
    patches,
    cotangent,
    w_query,
    w_key,
    w_value,
    w_output,
    w_gate,
    w_up,
    w_down,
    gain_attn,
    gain_ffn,
    qkv,
    normed_out,
    attn_t,
    lse,
    qkv_out,
    gains_out,
    grad_units,
    grad_output,
    layer_sums,
    hidden,
    grad_hidden,
    gain_part,
    grad_attn_out,
    rows_all,
    grads,
    normed_ffn,
    w_qkv,
    output_all,
    gate_t,
    up_t,
    down,
    down_parts,
    gate_stage,
    up_stage,
    gain_stage,
    gains,
    query,
    key,
    value_t,
    kept,
    attn_all,
    attn_rows,
    inner_t,
    grad_gate_t,
    grad_up_t,
    stage,
    landed,
    own_sum,
    norm_sums,
    norm_received,
    norm_passed,
    down_tiles,
    grad_branch,
    grad_rows,
    grad_attn,
    local_sem,
    group_send,
    group_recv,
    pass_send,
    x_send,
    x_recv,
    g_send,
    g_recv,
    o_send,
    o_recv,
    first_send,
    first_recv,
    second_send,
    second_recv,
    third_send,
    third_recv,
    b_send,
    b_recv,
    pair_send,
    pair_recv,
    out_send,
    out_recv,
):
    place = Place(devices_fsdp)
    me, group = place.me, place.group
    local_rows, width = patches.shape
    cols = width // 8
    shard = w_query.shape[0]
    part = w_down.shape[1]
    units = part * devices_fsdp
    place.meet()

    def rows_of(block, count=local_rows):
        return pl.ds(pl.multiple_of(block * count, count), count)

    def rows_half(ref):
        def region(block, half):
            start = block * local_rows + (local_rows // 2 if half == 1 else 0)
            count = local_rows if half is None else local_rows // 2
            return ref.at[pl.ds(pl.multiple_of(start, local_rows // 2), count)]

        return region

    def own_half(ref):
        return lambda half: ref.at[halves(local_rows)(half)]

    spread_x = Spread(place, own_half(patches), rows_half(rows_all), x_send, x_recv)
    spread_x.start()

    my_cols = rows_of(me, cols)
    def shard_of(index):
        return rows_of(index, shard)

    group_items = [
        (w_query.at[:, my_cols], lambda to: w_qkv.at[shard_of(to), 0:cols]),
        (w_key.at[:, my_cols], lambda to: w_qkv.at[shard_of(to), cols : 2 * cols]),
        (w_value.at[:, my_cols], lambda to: w_qkv.at[shard_of(to), 2 * cols : 3 * cols]),
        (gain_stage, lambda to: gains.at[:, shard_of(to)]),
        (w_output.at[me], lambda to: output_all.at[to, me]),
        (gate_stage, lambda to: gate_t.at[:, shard_of(to)]),
        (up_stage, lambda to: up_t.at[:, shard_of(to)]),
        (w_down.at[me], lambda to: down_parts.at[to]),
    ]

    def group_copy(index, step):
        source, target = group_items[index]
        return remote(
            source,
            target(group),
            group_send.at[index, step - 1],
            group_recv.at[index, step - 1],
            {"fsdp": place.other_group(step)},
        )

    def passed_copy(index):
        whose = place.other_group(2)
        held = group_items[index][1](whose)
        return remote(
            held,
            held,
            pass_send.at[index],
            group_recv.at[index, 2 * (group // 2)],
            {"fsdp": devices_fsdp - 1 - whose},
        )

    def local_copy(index):
        source, target = group_items[index]
        return pltpu.make_async_copy(source, target(group), local_sem.at[index])

    def send_group(index):
        group_copy(index, 2).start()
        for step in (1, 3):
            pl.when(place.near(step))(group_copy(index, step).start)
        local_copy(index).start()

    def pass_group(index):
        @pl.when(place.between())
        def _():
            group_copy(index, 2).wait_recv()
            passed_copy(index).start()

    def group_arrived(index):
        pl.when(place.at_end())(group_copy(index, 2).wait_recv)
        for step in (1, 3):
            group_copy(index, step).wait_recv()
        local_copy(index).wait()

    def group_sent(index):
        group_copy(index, 2).wait_send()
        for step in (1, 3):
            pl.when(place.near(step))(group_copy(index, step).wait_send)
        pl.when(place.between())(passed_copy(index).wait_send)

    for index in (0, 1, 2):
        send_group(index)
    gain_stage[0:8, :] = jnp.broadcast_to(gain_attn[...].astype(jnp.float32), (8, shard))
    gain_stage[8:16, :] = jnp.broadcast_to(gain_ffn[...].astype(jnp.float32), (8, shard))
    send_group(3)
    send_group(4)

    def pick_units(weight, target):
        span = part * 8
        pieces = []
        for index in range(devices_fsdp):
            low = span * index // 128 * 128
            high = -(-span * (index + 1) // 128) * 128
            unit = lax.broadcasted_iota(jnp.int32, (part, high - low), 0)
            column = lax.broadcasted_iota(jnp.int32, (part, high - low), 1)
            chosen = (column + low == unit + span * index + part * me).astype(jnp.bfloat16)
            pieces.append(dot_f32(chosen, weight[:, low:high], 1, 1))
        target[...] = jnp.concatenate(pieces, axis=0).astype(jnp.bfloat16)

    pick_units(w_gate, gate_stage)
    pick_units(w_up, up_stage)
    send_group(5)
    send_group(6)
    send_group(7)

    rows_all[rows_of(me), :] = patches[...]
    grads[rows_of(me), :] = cotangent[...]
    for index in (0, 1, 2, 3):
        pass_group(index)
    spread_x.relay_first()
    spread_x.relay_second()
    spread_g = Spread(place, own_half(cotangent), rows_half(grads), g_send, g_recv)
    spread_g.start()
    spread_x.relay_third()
    spread_x.arrived(0, 7, 8, 9)
    for index in (0, 1, 2, 3):
        group_arrived(index)
    gain_one = gains[0:1, :]

    def project(block, unused):
        at = rows_of(block)
        values = rows_all[at, :].astype(jnp.float32)
        low = rms_forward(values, gain_one)[0].astype(jnp.bfloat16)
        normed_ffn[at, :] = low
        store_tile(qkv, block, dot_f32(low, w_qkv[...], 1, 0).astype(jnp.bfloat16))
        return unused

    spread_x.sent()
    lax.fori_loop(0, 8, project, 0)
    save_normed = pltpu.make_async_copy(normed_ffn, normed_out, local_sem.at[8])
    save_normed.start()

    def output_half(block, half):
        if half is None:
            return output_all.at[:, block]
        lines = output_all.shape[2]
        return output_all.at[:, block, halves(lines)(half)]

    pass_group(4)
    group_arrived(4)
    pass_group(5)
    spread_o = Spread(place, lambda half: output_half(me, half), output_half, o_send, o_recv)
    spread_o.start()

    def attn_spread(first, count, send, recv):
        def part(half):
            return slice(
                first + (count // 2 if half == 1 else 0),
                first + (count // 2 if half == 0 else count),
            )

        return Spread(
            place,
            lambda half: kept.at[part(half)],
            lambda block, half: attn_all.at[part(half), :, rows_of(block, cols)],
            send,
            recv,
        )

    half_blocks = kept.shape[0] // 2
    attn_first = attn_spread(0, half_blocks, first_send, first_recv)
    attn_second = attn_spread(half_blocks, half_blocks // 2, second_send, second_recv)
    attn_third = attn_spread(half_blocks * 3 // 2, half_blocks // 2, third_send, third_recv)

    def after_two():
        spread_g.relay_first()

    def after_prompt():
        attn_first.start()
        pass_group(6)

    def after_more():
        spread_g.relay_second()
        spread_o.relay_first()

    def after_half():
        attn_second.start()
        spread_o.relay_second()
        spread_g.relay_third()

    def after_most():
        pass_group(7)
        attn_first.relay_first()
        attn_first.relay_second()
        spread_o.relay_third()

    attend_forward(
        per_segment,
        slot_of,
        length_ref,
        qkv,
        attn_t,
        lse,
        query,
        key,
        value_t,
        kept,
        {
            per_segment // 2: after_two,
            per_segment: after_prompt,
            per_segment + 1: after_more,
            per_segment + per_segment // 2: after_half,
            2 * per_segment - 1: after_most,
        },
    )
    attn_third.start()
    attn_all[:, :, my_cols] = kept[...]
    attn_first.relay_third()
    attn_second.relay_first()
    attn_second.relay_second()
    for index in (5, 6, 7):
        group_arrived(index)
    down[...] = jnp.concatenate(
        [down_parts[index].astype(jnp.float32) for index in range(devices_fsdp)], axis=0
    ).astype(jnp.bfloat16)
    attn_third.relay_first()
    attn_second.relay_third()
    attn_third.relay_second()
    save_normed.wait()
    spread_g.arrived(0, 7, 8, 9)
    spread_o.arrived(0, 7, 8, 9)
    attn_third.relay_third()
    for spread in (attn_first, attn_second, attn_third):
        spread.arrived(0, 7, 8, 9)

    def swap(source, target, send, recv):
        return [
            remote(source(flip), target, send.at[flip - 1], recv.at[flip - 1], {"ctx": place.peer(flip)})
            for flip in range(1, 8)
        ]

    def attn_of(block):
        held = attn_all.shape[0] // 8
        return jnp.concatenate(
            [attn_all[block_of[block * held + index]] for index in range(held)], axis=0
        )

    gain_two = gains[8:9, :]
    sums = CrossSum(
        place,
        stage,
        landed,
        norm_sums,
        norm_received,
        norm_passed,
        pair_send,
        pair_recv,
        out_send,
        out_recv,
    )

    def hidden_of(block, attn):
        return rows_all[rows_of(block), :].astype(jnp.float32) + dot_f32(
            attn, output_all[...].reshape(width, width), 1, 0
        )

    def feed(block):
        at = rows_of(block)
        low = rms_forward(hidden_of(block, attn_of(block)), gain_two)[0].astype(jnp.bfloat16)
        normed_ffn[at, :] = low
        grad_out = grads[at, :]
        gate = dot_f32(low, gate_t[...], 1, 1)
        up_proj = dot_f32(low, up_t[...], 1, 1)
        grad_inner = dot_f32(grad_out, down[...], 1, 1)
        sigmoid = jax.nn.sigmoid(gate)
        activated = gate * sigmoid
        inner = activated * up_proj
        inner_low = inner.astype(jnp.bfloat16)
        grad_gate = grad_inner * up_proj * sigmoid * (1.0 + gate * (1.0 - sigmoid))
        grad_up = grad_inner * activated
        gate_low = grad_gate.astype(jnp.bfloat16)
        up_low = grad_up.astype(jnp.bfloat16)
        inner_t[:, at] = inner.T.astype(jnp.bfloat16)
        grad_gate_t[:, at] = grad_gate.T.astype(jnp.bfloat16)
        grad_up_t[:, at] = grad_up.T.astype(jnp.bfloat16)
        return (
            dot_f32(inner_low, down[...], 1, 0),
            dot_f32(gate_low, gate_t[...], 1, 0) + dot_f32(up_low, up_t[...], 1, 0),
        )

    def one_pair(step, unused):
        pair = 3 - step
        layer, norm = feed(sums.theirs(pair))
        stage[pair, 0] = layer.astype(jnp.bfloat16)
        stage[pair, 1] = norm.astype(jnp.bfloat16)
        sums.exchange(pair).start()
        layer, norm = feed(sums.mine(pair))
        own_sum[0] = layer
        own_sum[1] = norm
        sums.exchange(pair).wait_recv()
        layer_sums[pair] = (own_sum[0] + landed[pair, 0].astype(jnp.float32)).astype(jnp.bfloat16)
        sums.finish(pair, own_sum[1] + landed[pair, 1].astype(jnp.float32))
        return unused

    lax.fori_loop(0, 4, one_pair, 0)
    attn_rows[...] = attn_of(me)
    hidden[...] = hidden_of(me, attn_rows[...])

    def units_tile(tile, unused):
        at = rows_of(tile, shard)
        low = normed_ffn[:, at]
        grad_units[tile, 0:units, :] = dot_f32(grad_gate_t[...], low, 1, 0).astype(jnp.bfloat16)
        grad_units[tile, units : 2 * units, :] = dot_f32(grad_up_t[...], low, 1, 0).astype(
            jnp.bfloat16
        )
        down_tiles[tile] = dot_f32(inner_t[...], grads[:, at], 1, 0)
        return unused

    lax.fori_loop(0, devices_fsdp, units_tile, 0)
    for index in range(devices_fsdp):
        grad_units[index, 2 * units : 3 * units, :] = jnp.concatenate(
            [
                down_tiles[tile, index * part : (index + 1) * part, :]
                for tile in range(devices_fsdp)
            ],
            axis=0,
        ).astype(jnp.bfloat16)

    total = sums.collect()
    values = hidden[...]
    factor = lax.rsqrt(jnp.mean(values * values, axis=-1, keepdims=True) + epsilon)
    scaled = total * gain_two
    gain_part[...] = jnp.sum(total * values * factor, axis=0, keepdims=True)
    whole = (
        cotangent[...].astype(jnp.float32)
        + factor * scaled
        - values * (factor * factor * factor) * jnp.mean(scaled * values, axis=-1, keepdims=True)
    )
    grad_hidden[...] = whole
    grad_branch[...] = whole.astype(jnp.bfloat16)
    grad_rows[...] = dot_f32(grad_branch[...], output_all[...].reshape(width, width), 1, 1).astype(
        jnp.bfloat16
    )
    to_heads = swap(
        lambda flip: grad_rows.at[:, rows_of(place.peer(flip), cols)],
        grad_attn.at[rows_of(me)],
        b_send,
        b_recv,
    )
    for copy in to_heads:
        copy.start()
    grad_attn[rows_of(me), :] = grad_rows[:, my_cols]

    for index in range(devices_fsdp):
        piece = attn_rows[:, index * shard : (index + 1) * shard].T
        grad_output[index] = (
            dot_f32(piece, grad_branch[...], 1, 0)
            .astype(jnp.bfloat16)
            .reshape(8, shard // 8, width)
        )
    qkv_out[...] = w_qkv[...]
    gains_out[...] = gains[...]
    for copy in to_heads:
        copy.wait_recv()
    grad_attn_out[...] = grad_attn[...].reshape(grad_attn_out.shape)

    for index in range(8):
        group_sent(index)
    spread_g.sent()
    spread_o.sent()
    for spread in (attn_first, attn_second, attn_third):
        spread.sent()
    for copy in to_heads:
        copy.wait_send()
    sums.sent()


def backward_kernel(
    per_segment,
    devices_fsdp,
    slot_of,
    block_of,
    length_ref,
    qkv,
    grad_attn,
    attn_t,
    lse,
    normed,
    w_qkv,
    gains,
    patches,
    grad_hidden,
    hidden,
    layer_sums,
    grad_units,
    grad_output,
    gain_part,
    layer,
    grad_patches,
    units_out,
    columns_out,
    gains_out,
    grad_qkv,
    query,
    key,
    value,
    grad,
    key_t,
    grad_key,
    grad_value,
    units_landed,
    units_far,
    units_near,
    units_stage,
    layer_received,
    output_stage,
    output_landed,
    output_sums,
    output_received,
    output_total,
    output_group,
    stage,
    landed,
    own_sum,
    norm_sums,
    norm_received,
    norm_passed,
    grad_qkv_t,
    qkv_parts,
    qkv_landed,
    columns_stage,
    gain_stage,
    gain_landed,
    gain_total,
    gain_all,
    local_sem,
    units_send,
    units_recv,
    far_sem,
    layer_send,
    layer_recv,
    wo_send,
    wo_recv,
    wo_out_send,
    wo_out_recv,
    group_send,
    group_recv,
    pair_send,
    pair_recv,
    out_send,
    out_recv,
    u_send,
    u_recv,
    c_send,
    c_recv,
    gain_send,
    gain_recv,
    gain_out_send,
    gain_out_recv,
):
    place = Place(devices_fsdp)
    me, group = place.me, place.group
    local_rows, width = patches.shape
    shard = width // devices_fsdp
    cols = width // 8
    units = grad_units.shape[1] // 3
    place.meet()

    def rows_of(block, count=local_rows):
        return pl.ds(pl.multiple_of(block * count, count), count)

    def over_groups(source, target, send, recv):
        return [
            remote(
                source(place.other_group(step)),
                target.at[group],
                send.at[step - 1],
                recv.at[step - 1],
                {"fsdp": place.other_group(step)},
            )
            for step in range(1, devices_fsdp)
        ]

    def units_copy(step, source):
        return remote(
            source,
            units_landed.at[group],
            units_send.at[step - 1],
            units_recv.at[step - 1],
            {"fsdp": place.other_group(step)},
        )

    def units_direct(step):
        return units_copy(step, grad_units.at[place.other_group(step)])

    units_far_copy = remote(
        grad_units.at[devices_fsdp - 1 - group],
        units_far,
        far_sem.at[0],
        far_sem.at[1],
        {"fsdp": 1 + group // 3},
    )
    units_sum_copy = units_copy(2, units_near)

    @pl.when(place.at_end())
    def _():
        units_far_copy.start()
        units_direct(2).start()

    for step in (1, 3):
        pl.when(place.near(step))(units_direct(step).start)

    def units_between():
        @pl.when(place.between())
        def _():
            units_far_copy.wait_recv()
            units_near[...] = (
                grad_units[place.other_group(2)].astype(jnp.float32)
                + units_far[...].astype(jnp.float32)
            ).astype(jnp.bfloat16)
            units_sum_copy.start()

    sums = CrossSum(
        place,
        stage,
        landed,
        norm_sums,
        norm_received,
        norm_passed,
        pair_send,
        pair_recv,
        out_send,
        out_recv,
    )
    output_pairs = PairSum(
        place,
        output_stage,
        output_landed,
        output_sums,
        output_received,
        wo_send,
        wo_recv,
        wo_out_send,
        wo_out_recv,
    )
    for pair in range(4):
        output_stage[pair] = grad_output[:, output_pairs.theirs(pair)]
        output_pairs.exchange(pair).start()
    layer_copies = [
        remote(
            layer_sums.at[pair],
            layer_received.at[pair],
            layer_send.at[pair],
            layer_recv.at[pair],
            {"ctx": sums.mine(pair)},
        )
        for pair in range(1, 4)
    ]
    for copy in layer_copies:
        copy.start()

    def after_prompt():
        for pair in range(4):
            output_pairs.exchange(pair).wait_recv()
            output_sums[pair] = (
                grad_output[:, output_pairs.mine(pair)].astype(jnp.float32)
                + output_landed[pair].astype(jnp.float32)
            ).astype(jnp.bfloat16)
            if pair:
                output_pairs.deliver(pair).start()

    attend_backward(
        per_segment,
        slot_of,
        block_of,
        length_ref,
        qkv,
        grad_attn,
        attn_t,
        lse,
        grad_qkv,
        query,
        key,
        value,
        grad,
        key_t,
        grad_key,
        grad_value,
        {per_segment: after_prompt, per_segment + 2: units_between},
    )

    total = output_sums[0].astype(jnp.float32)
    for pair in range(1, 4):
        output_pairs.deliver(pair).wait_recv()
        total = total + output_received[pair].astype(jnp.float32)
    output_total[...] = total.astype(jnp.bfloat16)
    output_copies = over_groups(
        lambda to: output_total.at[to], output_group, group_send.at[1], group_recv.at[1]
    )
    for copy in output_copies:
        copy.start()

    def turn(tile, unused):
        at = rows_of(tile, TILE)
        grad_qkv_t[:, at] = grad_qkv[at, :].T
        return unused

    lax.fori_loop(0, grad_qkv.shape[0] // TILE, turn, 0)

    def weight_tile(tile, unused):
        qkv_parts[tile] = dot_f32(grad_qkv_t[...], normed[:, rows_of(tile, shard)], 1, 0).astype(
            jnp.bfloat16
        )
        return unused

    lax.fori_loop(0, devices_fsdp, weight_tile, 0)
    qkv_copies = over_groups(
        lambda to: qkv_parts.at[to], qkv_landed, group_send.at[0], group_recv.at[0]
    )
    for copy in qkv_copies:
        copy.start()

    def one_pair(step, unused):
        pair = 3 - step
        stage[pair] = dot_f32(grad_qkv[rows_of(sums.theirs(pair)), :], w_qkv[...], 1, 1).astype(
            jnp.bfloat16
        )
        sums.exchange(pair).start()
        return unused

    lax.fori_loop(0, 4, one_pair, 0)

    def sum_pair(step, unused):
        pair = 3 - step
        own_sum[...] = dot_f32(grad_qkv[rows_of(sums.mine(pair)), :], w_qkv[...], 1, 1)
        sums.exchange(pair).wait_recv()
        sums.finish(pair, own_sum[...] + landed[pair].astype(jnp.float32))
        return unused

    lax.fori_loop(0, 4, sum_pair, 0)

    def group_sum(own, landed_ref, copies):
        landed_ref[group] = own
        for copy in copies:
            copy.wait_recv()
        total = landed_ref[0].astype(jnp.float32)
        for index in range(1, devices_fsdp):
            total = total + landed_ref[index].astype(jnp.float32)
        return total

    units_landed[group] = grad_units[group]

    @pl.when(place.at_end())
    def _():
        units_landed[devices_fsdp - 1 - group] = jnp.zeros_like(grad_units[group])

    units_direct(2).wait_recv()
    for step in (1, 3):
        pl.when(place.heard(step))(units_direct(step).wait_recv)
    units_total = units_landed[0].astype(jnp.float32)
    for index in range(1, devices_fsdp):
        units_total = units_total + units_landed[index].astype(jnp.float32)
    units_stage[...] = units_total.astype(jnp.bfloat16)

    def half_of(ref, lines):
        def region(block, half):
            return ref.at[block] if half is None else ref.at[block, halves(lines)(half)]

        return region

    def own_of(ref, lines):
        return lambda half: ref if half is None else ref.at[halves(lines)(half)]

    spread_u = Spread(
        place,
        own_of(units_stage, 3 * units),
        half_of(units_out, 3 * units),
        u_send,
        u_recv,
    )
    spread_u.start()
    save_units = pltpu.make_async_copy(units_stage, units_out.at[me], local_sem.at[0])
    save_units.start()

    total = layer_sums[0].astype(jnp.float32)
    for pair, copy in enumerate(layer_copies):
        copy.wait_recv()
        total = total + layer_received[pair + 1].astype(jnp.float32)
    layer[...] = (hidden[...] + total).astype(jnp.bfloat16)

    total = sums.collect()
    values = patches[...].astype(jnp.float32)
    gain_one = gains[0:1, :]
    factor = lax.rsqrt(jnp.mean(values * values, axis=-1, keepdims=True) + epsilon)
    scaled = total * gain_one
    gain_stage[...] = jnp.zeros_like(gain_stage)
    attn_part = jnp.sum(total * values * factor, axis=0, keepdims=True)
    ffn_part = gain_part[...]
    for index in range(devices_fsdp):
        at = slice(index * shard, (index + 1) * shard)
        gain_stage[index, 0:1, :] = attn_part[:, at]
        gain_stage[index, 1:2, :] = ffn_part[:, at]
    gain_copies = over_groups(lambda to: gain_stage.at[to], gain_landed, gain_send, gain_recv)
    for copy in gain_copies:
        copy.start()
    grad_patches[...] = (
        grad_hidden[...]
        + factor * scaled
        - values * (factor * factor * factor) * jnp.mean(scaled * values, axis=-1, keepdims=True)
    )
    spread_u.relay_first()
    spread_u.relay_second()
    gain_total[...] = group_sum(gain_stage[group], gain_landed, gain_copies)
    gain_out = [
        remote(
            gain_total,
            gain_all.at[me],
            gain_out_send.at[flip - 1],
            gain_out_recv.at[flip - 1],
            {"ctx": place.peer(flip)},
        )
        for flip in range(1, 8)
    ]
    for copy in gain_out:
        copy.start()
    gain_all[me] = gain_total[...]

    turned = group_sum(qkv_parts[group], qkv_landed, qkv_copies).T.astype(jnp.bfloat16)
    for index in range(3):
        columns_stage[index * shard : (index + 1) * shard, :] = turned[
            :, index * cols : (index + 1) * cols
        ]
    summed = group_sum(output_total[group], output_group, output_copies).astype(jnp.bfloat16)
    lines = shard // 8
    for index in range(8):
        columns_stage[3 * shard + index * lines : 3 * shard + (index + 1) * lines, :] = summed[
            :, index * cols : (index + 1) * cols
        ]
    spread_c = Spread(
        place, own_of(columns_stage, 4 * shard), half_of(columns_out, 4 * shard), c_send, c_recv
    )
    spread_c.start()
    save_columns = pltpu.make_async_copy(columns_stage, columns_out.at[me], local_sem.at[1])
    save_columns.start()
    spread_u.relay_third()
    for copy in gain_out:
        copy.wait_recv()
    gain_sum = gain_all[0]
    for index in range(1, 8):
        gain_sum = gain_sum + gain_all[index]
    gains_out[...] = gain_sum
    spread_c.relay_first()
    spread_c.relay_second()
    spread_u.arrived(0, 7, 8, 9)
    spread_c.relay_third()
    spread_c.arrived(0, 7, 8, 9)
    for step in (1, 3):
        pl.when(place.near(step))(units_direct(step).wait_send)
    units_direct(2).wait_send()
    pl.when(place.at_end())(units_far_copy.wait_send)
    for copy in layer_copies + qkv_copies + output_copies + gain_copies + gain_out:
        copy.wait_send()
    sums.sent()
    output_pairs.sent()
    spread_u.sent()
    spread_c.sent()
    save_units.wait()
    save_columns.wait()


def place_kernel(
    devices_fsdp,
    units_all,
    columns_all,
    out_query,
    out_key,
    out_value,
    out_output,
    out_gate,
    out_up,
    out_down,
    columns,
    outputs,
    natural,
    gate,
    up,
    down,
    sems,
):
    shard = out_query.shape[0]
    cols = columns_all.shape[2]
    lines = shard // 8
    units = units_all.shape[1] // 3
    part = units // devices_fsdp
    span = part * 8
    saves = []

    def save(source, target):
        copy = pltpu.make_async_copy(source, target, sems.at[len(saves)])
        copy.start()
        saves.append(copy)

    for index in range(8):
        piece = units_all[index, 2 * units : 3 * units, :].astype(jnp.float32)
        for tile in range(devices_fsdp):
            down[index * part : (index + 1) * part, tile * shard : (tile + 1) * shard] = piece[
                tile * part : (tile + 1) * part, :
            ]
    save(down, out_down)
    for which, (target, out) in enumerate(((gate, out_gate), (up, out_up))):
        for index in range(8):
            piece = units_all[index, which * units : (which + 1) * units, :].astype(jnp.float32)
            for tile in range(devices_fsdp):
                first = tile * span + index * part
                natural[first : first + part, :] = piece[tile * part : (tile + 1) * part, :]
        for first in range(0, span * devices_fsdp, 128):
            target[:, first : first + 128] = natural[first : first + 128, :].T
        save(target, out)
    for index in range(8):
        at = slice(index * cols, (index + 1) * cols)
        for which in range(3):
            columns[which, :, at] = columns_all[
                index, which * shard : (which + 1) * shard, :
            ].astype(jnp.float32)
        for tile in range(8):
            first = 3 * shard + tile * lines
            outputs[index * lines : (index + 1) * lines, tile * cols : (tile + 1) * cols] = (
                columns_all[index, first : first + lines, :].astype(jnp.float32)
            )
    save(columns.at[0], out_query)
    save(columns.at[1], out_key)
    save(columns.at[2], out_value)
    save(outputs, out_output)
    for copy in saves:
        copy.wait()


def heads_plan(
    patches,
    cotangent,
    deal_table,
    prompt_len,
    w_query,
    w_key,
    w_value,
    w_output,
    w_gate,
    w_up,
    w_down,
    gain_attn,
    gain_ffn,
):
    local_rows = patches.shape[1]
    width = patches.shape[2]
    groups = lax.axis_size("fsdp")
    rows = local_rows * 8
    cols = width // 8
    shard = width // groups
    part = w_down.shape[0] // 8
    units = part * groups
    tiles = rows // TILE
    blocks = deal_table.shape[0]
    block_len = rows // blocks
    per_segment = CONT_LEN // TILE
    slots = jnp.arange(deal_table.shape[0], dtype=jnp.int32)
    slot_of = jnp.sum(
        jnp.where(deal_table[None, :] == slots[:, None], slots[None, :], 0), axis=1
    ).astype(jnp.int32)
    smem = pl.BlockSpec(memory_space=pltpu.SMEM)
    vmem = pl.BlockSpec(memory_space=pltpu.VMEM)
    anywhere = pl.BlockSpec(memory_space=pl.ANY)
    low, full = jnp.bfloat16, jnp.float32

    def shaped(kind, *dims):
        return jax.ShapeDtypeStruct(dims, kind)

    def room(kind, *dims):
        return pltpu.VMEM(dims, kind)

    (
        qkv,
        normed,
        attn_t,
        lse,
        w_qkv,
        gains,
        grad_units,
        grad_output,
        layer_sums,
        hidden,
        grad_hidden,
        gain_part,
        grad_attn,
    ) = pl.pallas_call(
        functools.partial(forward_kernel, per_segment, groups),
        out_shape=(
            shaped(low, blocks, block_len, 3 * cols),
            shaped(low, rows, width),
            shaped(full, tiles, cols, TILE),
            shaped(full, tiles, 1, 2 * TILE),
            shaped(low, width, 3 * cols),
            shaped(full, 16, width),
            shaped(low, groups, 3 * units, shard),
            shaped(low, groups, 8, shard // 8, width),
            shaped(low, 4, local_rows, width),
            shaped(full, local_rows, width),
            shaped(full, local_rows, width),
            shaped(full, 1, width),
            shaped(low, blocks, block_len, cols),
        ),
        in_specs=[smem] * 3
        + [vmem] * 2
        + [anywhere] * 4
        + [vmem] * 2
        + [anywhere]
        + [vmem] * 2,
        out_specs=(vmem, anywhere) + (vmem,) * 11,
        scratch_shapes=[
            room(low, rows, width),
            room(low, rows, width),
            room(low, rows, width),
            room(low, width, 3 * cols),
            room(low, groups, 8, shard // 8, width),
            room(low, units, width),
            room(low, units, width),
            room(low, units, width),
            room(low, groups, part, width),
            room(low, units, shard),
            room(low, units, shard),
            room(full, 16, shard),
            room(full, 16, width),
            room(low, blocks, block_len, cols),
            room(low, blocks, block_len, cols),
            room(low, tiles, cols, TILE),
            room(low, blocks, block_len, cols),
            room(low, blocks, block_len, width),
            room(low, local_rows, width),
            room(low, units, rows),
            room(low, units, rows),
            room(low, units, rows),
            room(low, 4, 2, local_rows, width),
            room(low, 4, 2, local_rows, width),
            room(full, 2, local_rows, width),
            room(low, 4, local_rows, width),
            room(low, 2, local_rows, width),
            room(low, 2, local_rows // 2, width),
            room(full, groups, units, shard),
            room(low, local_rows, width),
            room(low, local_rows, width),
            room(low, rows, cols),
            dma(9),
            pltpu.SemaphoreType.DMA((8, groups - 1)),
            pltpu.SemaphoreType.DMA((8, groups - 1)),
            dma(8),
        ]
        + [dma(10)] * 12
        + [dma(7)] * 2
        + [dma(4)] * 4,
        compiler_params=pltpu.CompilerParams(
            collective_id=0, has_side_effects=True, vmem_limit_bytes=66_000_000
        ),
        name="forward",
    )(
        slot_of,
        deal_table,
        prompt_len,
        patches[0],
        cotangent[0],
        w_query,
        w_key,
        w_value,
        w_output.reshape(8, shard // 8, width),
        w_gate,
        w_up,
        w_down.reshape(8, part, width),
        gain_attn[None],
        gain_ffn[None],
    )

    layer, grad_rows, units_all, columns_all, gains_sum = pl.pallas_call(
        functools.partial(backward_kernel, per_segment, groups),
        out_shape=(
            shaped(low, local_rows, width),
            shaped(full, local_rows, width),
            shaped(low, 8, 3 * units, shard),
            shaped(low, 8, 4 * shard, cols),
            shaped(full, 8, shard),
        ),
        in_specs=[smem] * 3 + [vmem] * 14,
        out_specs=(vmem, vmem, anywhere, anywhere, vmem),
        scratch_shapes=[
            room(low, rows, 3 * cols),
            room(low, blocks, block_len, cols),
            room(low, blocks, block_len, cols),
            room(low, blocks, block_len, cols),
            room(low, blocks, block_len, cols),
            room(low, tiles, cols, TILE),
            room(full, rows, cols),
            room(full, rows, cols),
            room(low, groups, 3 * units, shard),
            room(low, 3 * units, shard),
            room(low, 3 * units, shard),
            room(low, 3 * units, shard),
            room(low, 4, local_rows, width),
            room(low, 4, groups, shard // 8, width),
            room(low, 4, groups, shard // 8, width),
            room(low, 4, groups, shard // 8, width),
            room(low, 4, groups, shard // 8, width),
            room(low, groups, shard // 8, width),
            room(low, groups, shard // 8, width),
            room(low, 4, local_rows, width),
            room(low, 4, local_rows, width),
            room(full, local_rows, width),
            room(low, 4, local_rows, width),
            room(low, 2, local_rows, width),
            room(low, 2, local_rows // 2, width),
            room(low, 3 * cols, rows),
            room(low, groups, 3 * cols, shard),
            room(low, groups, 3 * cols, shard),
            room(low, 4 * shard, cols),
            room(full, groups, 8, shard),
            room(full, groups, 8, shard),
            room(full, 8, shard),
            room(full, 8, 8, shard),
            dma(2),
            dma(groups - 1),
            dma(groups - 1),
            dma(2),
            dma(4),
            dma(4),
            dma(4),
            dma(4),
            dma(4),
            dma(4),
            pltpu.SemaphoreType.DMA((2, groups - 1)),
            pltpu.SemaphoreType.DMA((2, groups - 1)),
            dma(4),
            dma(4),
            dma(4),
            dma(4),
            dma(10),
            dma(10),
            dma(10),
            dma(10),
            dma(groups - 1),
            dma(groups - 1),
            dma(7),
            dma(7),
        ],
        compiler_params=pltpu.CompilerParams(
            collective_id=1, has_side_effects=True, vmem_limit_bytes=66_000_000
        ),
        name="backward",
    )(
        slot_of,
        deal_table,
        prompt_len,
        qkv,
        grad_attn,
        attn_t,
        lse,
        normed,
        w_qkv,
        gains,
        patches[0],
        grad_hidden,
        hidden,
        layer_sums,
        grad_units,
        grad_output,
        gain_part,
    )

    weights = pl.pallas_call(
        functools.partial(place_kernel, groups),
        out_shape=tuple(shaped(full, shard, width) for _ in range(4))
        + tuple(shaped(full, shard, 8 * units) for _ in range(2))
        + (shaped(full, 8 * part, width),),
        in_specs=[vmem, vmem],
        out_specs=(anywhere,) * 7,
        scratch_shapes=[
            room(full, 3, shard, width),
            room(full, shard, width),
            room(full, 8 * units, shard),
            room(full, shard, 8 * units),
            room(full, shard, 8 * units),
            room(full, 8 * part, width),
            dma(7),
        ],
        name="place",
    )(units_all, columns_all)
    return (layer[None], grad_rows[None]) + tuple(weights) + (gains_sum[0], gains_sum[1])


def solution(mesh):
    if mesh.shape["ctx"] == 8 and mesh.shape["fsdp"] == 4:
        per_device = heads_plan
    else:
        per_device = rows_plan
    placed = (
        P("fsdp", "ctx", None),
        P("fsdp", "ctx", None),
        P(),
        P("fsdp"),
        P("fsdp", None),
        P("fsdp", None),
        P("fsdp", None),
        P("fsdp", None),
        P("fsdp", None),
        P("fsdp", None),
        P("fsdp", None),
        P("fsdp"),
        P("fsdp"),
    )
    return jax.shard_map(
        per_device,
        mesh=mesh,
        in_specs=placed,
        out_specs=(
            P("fsdp", "ctx", None),
            P("fsdp", "ctx", None),
            P("fsdp", None),
            P("fsdp", None),
            P("fsdp", None),
            P("fsdp", None),
            P("fsdp", None),
            P("fsdp", None),
            P("fsdp", None),
            P("fsdp"),
            P("fsdp"),
        ),
        check_vma=False,
    )
```

```python
import functools
import math

import jax
import jax.numpy as jnp
from jax import lax
from jax.experimental import pallas as pl
from jax.experimental.pallas import tpu as pltpu
from jax.sharding import PartitionSpec as P

HEADS = 16
HEAD = 64
CONT_LEN = 1024


epsilon = 1e-05
score_scale = 0.125
masked_value = -1e30


def rms_forward(values, gain):
    factor = lax.rsqrt(jnp.mean(values * values, axis=-1, keepdims=True) + epsilon)
    return (values * factor * gain, factor)


def rms_backward(values, factor, gain, grad_normed):
    scaled = grad_normed * gain
    grad_gain = jnp.sum(grad_normed * values * factor, axis=0)
    cubed = factor * factor * factor
    grad_values = factor * scaled - values * cubed * jnp.mean(
        scaled * values, axis=-1, keepdims=True
    )
    return (grad_values, grad_gain)


def segment_of(position, prompt):
    return jnp.where(position < prompt, -1, (position - prompt) // CONT_LEN)


def visible(query_pos, key_pos, prompt, length):
    same = (segment_of(query_pos, prompt)[:, None] == segment_of(key_pos, prompt)[None, :]) & (
        key_pos[None, :] <= query_pos[:, None]
    )
    shared = (query_pos[:, None] >= prompt) & (key_pos[None, :] < length)
    return same | shared


def rows_plan(
    patches,
    cotangent,
    deal_table,
    prompt_len,
    w_query,
    w_key,
    w_value,
    w_output,
    w_gate,
    w_up,
    w_down,
    gain_attn,
    gain_ffn,
):
    local_rows = patches.shape[1]
    width = patches.shape[2]
    devices_ctx = lax.axis_size("ctx")
    group_tok = local_rows * devices_ctx
    cont_count = group_tok // (2 * CONT_LEN)
    prompt = group_tok - cont_count * CONT_LEN
    block_len = local_rows // 2
    slot_count = 2 * devices_ctx
    key_rows = math.gcd(512, group_tok)
    block_count = group_tok // key_rows
    length = prompt_len[0]

    def positions_of(first_row, count):
        stored = first_row + jnp.arange(count, dtype=jnp.int32)
        slot_ids = stored // block_len
        picked = jnp.where(
            slot_ids[:, None] == jnp.arange(slot_count, dtype=jnp.int32)[None, :],
            deal_table[None, :],
            0,
        )
        return jnp.sum(picked, axis=1) * block_len + stored % block_len

    query_pos = positions_of(lax.axis_index("ctx") * local_rows, local_rows)
    key_pos = positions_of(0, group_tok).reshape(block_count, key_rows)
    (
        full_query,
        full_key,
        full_value,
        full_output,
        full_gate,
        full_up,
        full_down,
        full_gain_attn,
        full_gain_ffn,
    ) = (
        lax.all_gather(w_query, "fsdp", axis=0, tiled=True),
        lax.all_gather(w_key, "fsdp", axis=0, tiled=True),
        lax.all_gather(w_value, "fsdp", axis=0, tiled=True),
        lax.all_gather(w_output, "fsdp", axis=0, tiled=True),
        lax.all_gather(w_gate, "fsdp", axis=0, tiled=True),
        lax.all_gather(w_up, "fsdp", axis=0, tiled=True),
        lax.all_gather(w_down, "fsdp", axis=0, tiled=True),
        lax.all_gather(gain_attn, "fsdp", axis=0, tiled=True),
        lax.all_gather(gain_ffn, "fsdp", axis=0, tiled=True),
    )
    rows_f32 = patches[0].astype(jnp.float32)
    gain_one = full_gain_attn.astype(jnp.float32)
    normed, factor_attn = rms_forward(rows_f32, gain_one)
    normed_low = normed.astype(jnp.bfloat16)
    queries = jnp.dot(normed_low, full_query, preferred_element_type=jnp.float32).astype(
        jnp.bfloat16
    )
    keys_local = jnp.dot(normed_low, full_key, preferred_element_type=jnp.float32).astype(
        jnp.bfloat16
    )
    values_local = jnp.dot(normed_low, full_value, preferred_element_type=jnp.float32).astype(
        jnp.bfloat16
    )
    key_all, value_all = (
        lax.all_gather(keys_local, "ctx", axis=0, tiled=True),
        lax.all_gather(values_local, "ctx", axis=0, tiled=True),
    )
    query_heads = queries.reshape(local_rows, HEADS, HEAD)

    def split_blocks(array):
        return array.reshape(block_count, key_rows, HEADS, HEAD)

    def forward_block(state, block):
        key_block, value_block, block_pos = block
        visible_mask = visible(query_pos, block_pos, prompt, length)

        def forward_update(inner_state):
            maxima, totals, accum = inner_state
            scores = (
                jnp.einsum(
                    "qhe,khe->hqk", query_heads, key_block, preferred_element_type=jnp.float32
                )
                * score_scale
            )
            scores = jnp.where(visible_mask[None], scores, masked_value)
            new_max = jnp.maximum(maxima, jnp.max(scores, axis=-1))
            rescale = jnp.exp(maxima - new_max)
            probs = jnp.where(visible_mask[None], jnp.exp(scores - new_max[:, :, None]), 0.0)
            totals = totals * rescale + jnp.sum(probs, axis=-1)
            accum = accum * rescale.T[:, :, None] + jnp.einsum(
                "hqk,khe->qhe",
                probs.astype(jnp.bfloat16),
                value_block,
                preferred_element_type=jnp.float32,
            )
            return (new_max, totals, accum)

        return (
            lax.cond(jnp.any(visible_mask), forward_update, lambda inner_state: inner_state, state),
            None,
        )

    start_state = (
        jnp.full((HEADS, local_rows), masked_value, jnp.float32),
        jnp.zeros((HEADS, local_rows), jnp.float32),
        jnp.zeros((local_rows, HEADS, HEAD), jnp.float32),
    )
    (maxima, totals, accum), unused = lax.scan(
        forward_block, start_state, (split_blocks(key_all), split_blocks(value_all), key_pos)
    )
    attn_f32 = accum / totals.T[:, :, None]
    log_total = maxima + jnp.log(totals)
    attn_low = attn_f32.astype(jnp.bfloat16).reshape(local_rows, width)
    hidden = rows_f32 + jnp.dot(attn_low, full_output, preferred_element_type=jnp.float32)
    gain_two = full_gain_ffn.astype(jnp.float32)
    normed_ffn, factor_ffn = rms_forward(hidden, gain_two)
    ffn_low = normed_ffn.astype(jnp.bfloat16)
    gate = jnp.dot(ffn_low, full_gate, preferred_element_type=jnp.float32)
    up_proj = jnp.dot(ffn_low, full_up, preferred_element_type=jnp.float32)
    sigmoid = jax.nn.sigmoid(gate)
    activated = gate * sigmoid
    inner_low = (activated * up_proj).astype(jnp.bfloat16)
    layer = hidden + jnp.dot(inner_low, full_down, preferred_element_type=jnp.float32)
    grad_out = cotangent[0].astype(jnp.float32)
    grad_down_in = cotangent[0]
    grad_w_down = jnp.dot(inner_low.T, grad_down_in, preferred_element_type=jnp.float32)
    grad_inner = jnp.dot(grad_down_in, full_down.T, preferred_element_type=jnp.float32)
    grad_gate = (grad_inner * up_proj * sigmoid * (1.0 + gate * (1.0 - sigmoid))).astype(
        jnp.bfloat16
    )
    grad_up = (grad_inner * activated).astype(jnp.bfloat16)
    grad_w_gate = jnp.dot(ffn_low.T, grad_gate, preferred_element_type=jnp.float32)
    grad_w_up = jnp.dot(ffn_low.T, grad_up, preferred_element_type=jnp.float32)
    grad_normed_ffn = jnp.dot(grad_gate, full_gate.T, preferred_element_type=jnp.float32) + jnp.dot(
        grad_up, full_up.T, preferred_element_type=jnp.float32
    )
    grad_hidden_norm, grad_gain_ffn = rms_backward(hidden, factor_ffn, gain_two, grad_normed_ffn)
    grad_hidden = grad_out + grad_hidden_norm
    grad_branch = grad_hidden.astype(jnp.bfloat16)
    grad_w_output = jnp.dot(attn_low.T, grad_branch, preferred_element_type=jnp.float32)
    grad_attn = (
        jnp.dot(grad_branch, full_output.T, preferred_element_type=jnp.float32)
        .astype(jnp.bfloat16)
        .reshape(local_rows, HEADS, HEAD)
    )
    delta = jnp.einsum("qhe,qhe->hq", grad_attn.astype(jnp.float32), attn_f32)
    key_back, value_back = (key_all, value_all)

    def backward_block(grad_query, block):
        key_block, value_block, block_pos = block
        visible_mask = visible(query_pos, block_pos, prompt, length)

        def backward_update(grad_state):
            scores = (
                jnp.einsum(
                    "qhe,khe->hqk", query_heads, key_block, preferred_element_type=jnp.float32
                )
                * score_scale
            )
            probs = jnp.where(visible_mask[None], jnp.exp(scores - log_total[:, :, None]), 0.0)
            grad_probs = jnp.einsum(
                "qhe,khe->hqk", grad_attn, value_block, preferred_element_type=jnp.float32
            )
            grad_scores = (probs * (grad_probs - delta[:, :, None])).astype(jnp.bfloat16)
            grad_state = (
                grad_state
                + jnp.einsum(
                    "hqk,khe->qhe", grad_scores, key_block, preferred_element_type=jnp.float32
                )
                * score_scale
            )
            grad_keys = (
                jnp.einsum(
                    "hqk,qhe->khe", grad_scores, query_heads, preferred_element_type=jnp.float32
                )
                * score_scale
            )
            grad_values = jnp.einsum(
                "hqk,qhe->khe",
                probs.astype(jnp.bfloat16),
                grad_attn,
                preferred_element_type=jnp.float32,
            )
            return (grad_state, (grad_keys, grad_values))

        def skipped(grad_state):
            empty = jnp.zeros((key_rows, HEADS, HEAD), jnp.float32)
            return (grad_state, (empty, empty))

        return lax.cond(jnp.any(visible_mask), backward_update, skipped, grad_query)

    zero_query = jnp.zeros((local_rows, HEADS, HEAD), jnp.float32)
    grad_query, (grad_key_blocks, grad_value_blocks) = lax.scan(
        backward_block, zero_query, (split_blocks(key_back), split_blocks(value_back), key_pos)
    )
    grad_key_sum, grad_value_sum = (
        lax.psum_scatter(
            grad_key_blocks.reshape(group_tok, width).astype(jnp.bfloat16),
            "ctx",
            scatter_dimension=0,
            tiled=True,
        ).astype(jnp.float32),
        lax.psum_scatter(
            grad_value_blocks.reshape(group_tok, width).astype(jnp.bfloat16),
            "ctx",
            scatter_dimension=0,
            tiled=True,
        ).astype(jnp.float32),
    )
    grad_key_low = grad_key_sum.astype(jnp.bfloat16)
    grad_value_low = grad_value_sum.astype(jnp.bfloat16)
    grad_query_low = grad_query.reshape(local_rows, width).astype(jnp.bfloat16)
    grad_w_query = jnp.dot(normed_low.T, grad_query_low, preferred_element_type=jnp.float32)
    grad_w_key = jnp.dot(normed_low.T, grad_key_low, preferred_element_type=jnp.float32)
    grad_w_value = jnp.dot(normed_low.T, grad_value_low, preferred_element_type=jnp.float32)
    grad_normed = (
        jnp.dot(grad_query_low, full_query.T, preferred_element_type=jnp.float32)
        + jnp.dot(grad_key_low, full_key.T, preferred_element_type=jnp.float32)
        + jnp.dot(grad_value_low, full_value.T, preferred_element_type=jnp.float32)
    )
    grad_rows_norm, grad_gain_attn = rms_backward(rows_f32, factor_attn, gain_one, grad_normed)
    grad_rows = grad_hidden + grad_rows_norm
    shards = (
        lax.psum_scatter(
            grad_w_query.astype(jnp.bfloat16), "fsdp", scatter_dimension=0, tiled=True
        ).astype(jnp.float32),
        lax.psum_scatter(
            grad_w_key.astype(jnp.bfloat16), "fsdp", scatter_dimension=0, tiled=True
        ).astype(jnp.float32),
        lax.psum_scatter(
            grad_w_value.astype(jnp.bfloat16), "fsdp", scatter_dimension=0, tiled=True
        ).astype(jnp.float32),
        lax.psum_scatter(
            grad_w_output.astype(jnp.bfloat16), "fsdp", scatter_dimension=0, tiled=True
        ).astype(jnp.float32),
        lax.psum_scatter(
            grad_w_gate.astype(jnp.bfloat16), "fsdp", scatter_dimension=0, tiled=True
        ).astype(jnp.float32),
        lax.psum_scatter(
            grad_w_up.astype(jnp.bfloat16), "fsdp", scatter_dimension=0, tiled=True
        ).astype(jnp.float32),
        lax.psum_scatter(
            grad_w_down.astype(jnp.bfloat16), "fsdp", scatter_dimension=0, tiled=True
        ).astype(jnp.float32),
        lax.psum_scatter(
            grad_gain_attn.astype(jnp.bfloat16), "fsdp", scatter_dimension=0, tiled=True
        ).astype(jnp.float32),
        lax.psum_scatter(
            grad_gain_ffn.astype(jnp.bfloat16), "fsdp", scatter_dimension=0, tiled=True
        ).astype(jnp.float32),
    )
    summed = (
        lax.psum(shards[0].astype(jnp.bfloat16), "ctx").astype(jnp.float32),
        lax.psum(shards[1].astype(jnp.bfloat16), "ctx").astype(jnp.float32),
        lax.psum(shards[2].astype(jnp.bfloat16), "ctx").astype(jnp.float32),
        lax.psum(shards[3].astype(jnp.bfloat16), "ctx").astype(jnp.float32),
        lax.psum(shards[4].astype(jnp.bfloat16), "ctx").astype(jnp.float32),
        lax.psum(shards[5].astype(jnp.bfloat16), "ctx").astype(jnp.float32),
        lax.psum(shards[6].astype(jnp.bfloat16), "ctx").astype(jnp.float32),
        lax.psum(shards[7].astype(jnp.bfloat16), "ctx").astype(jnp.float32),
        lax.psum(shards[8].astype(jnp.bfloat16), "ctx").astype(jnp.float32),
    )
    return (
        layer.astype(jnp.bfloat16)[None],
        grad_rows[None],
        summed[0],
        summed[1],
        summed[2],
        summed[3],
        summed[4],
        summed[5],
        summed[6],
        summed[7],
        summed[8],
    )


TILE = 256


def dot_f32(left, right, left_dim, right_dim):
    return lax.dot_general(
        left,
        right,
        (((left_dim,), (right_dim,)), ((), ())),
        preferred_element_type=jnp.float32,
    )


def head_masks():
    lane = lax.broadcasted_iota(jnp.int32, (TILE, 2 * HEAD), 1)
    first = (lane < HEAD).astype(jnp.bfloat16)
    return first, (1 - first).astype(jnp.bfloat16)


def stack_heads(tile, masks):
    return jnp.concatenate([tile * masks[0], tile * masks[1]], axis=0)


def tile_mask(kind, tile, length):
    row = lax.broadcasted_iota(jnp.int32, (TILE, 2 * TILE), 0)
    if kind == "diagonal":
        column = lax.broadcasted_iota(jnp.int32, (TILE, 2 * TILE), 1)
        return row <= jnp.where(column < TILE, column, column - TILE)
    return row + tile * TILE < length


def over_keys(tile, per_segment, step, state):
    base = tile // per_segment * per_segment
    state = lax.fori_loop(0, base, lambda key, kept: step(key, kept, "prompt"), state)
    state = lax.fori_loop(base, tile, lambda key, kept: step(key, kept, "full"), state)
    return step(tile, state, "diagonal")


def load_tile(ref, tile):
    held = TILE // ref.shape[1]
    return ref[pl.ds(tile * held, held)].reshape(TILE, ref.shape[2])


def store_tile(ref, tile, values):
    held = TILE // ref.shape[1]
    ref[pl.ds(tile * held, held)] = values.reshape(held, ref.shape[1], ref.shape[2])


def to_logical(slot_of, source, column, target, scale=None):
    for block in range(target.shape[0]):
        picked = source[slot_of[block], :, column : column + 2 * HEAD]
        if scale is not None:
            picked = picked * scale
        target[block] = picked


def to_stored(block_of, source, target, column):
    block_len = source.shape[1]
    for slot in range(source.shape[0]):
        target[slot * block_len : (slot + 1) * block_len, column : column + 2 * HEAD] = source[
            block_of[slot]
        ]


def tiles_between(count, one_tile, between):
    first = 0
    for stop in sorted(between):
        lax.fori_loop(first, stop, one_tile, 0)
        between[stop]()
        first = stop
    lax.fori_loop(first, count, one_tile, 0)


def attend_forward(
    per_segment,
    slot_of,
    length_ref,
    qkv,
    attn_t,
    lse,
    query,
    key,
    value_t,
    kept,
    between,
):
    rows = qkv.shape[0] * qkv.shape[1]
    length = length_ref[0]
    to_logical(slot_of, qkv, 0, query, jnp.bfloat16(score_scale))
    to_logical(slot_of, qkv, 2 * HEAD, key)
    to_logical(slot_of, qkv, 4 * HEAD, kept)
    for tile in range(rows // TILE):
        value_t[tile] = load_tile(kept, tile).T
    masks = head_masks()

    def one_tile(tile, unused):
        both = stack_heads(load_tile(query, tile), masks)

        def step(key_tile, state, kind):
            maxima, totals, accum = state
            scores = dot_f32(load_tile(key, key_tile), both, 1, 1)
            if kind != "full":
                scores = jnp.where(tile_mask(kind, key_tile, length), scores, masked_value)
            new_max = jnp.maximum(maxima, jnp.max(scores, axis=0, keepdims=True))
            probs = jnp.exp(scores - new_max)
            rescale = jnp.exp(maxima - new_max)
            totals = totals * rescale + jnp.sum(probs, axis=0, keepdims=True)
            accum = accum * rescale + dot_f32(
                value_t[key_tile], probs.astype(jnp.bfloat16), 1, 0
            )
            return new_max, totals, accum

        maxima, totals, accum = over_keys(
            tile,
            per_segment,
            step,
            (
                jnp.full((1, 2 * TILE), masked_value, jnp.float32),
                jnp.zeros((1, 2 * TILE), jnp.float32),
                jnp.zeros((2 * HEAD, 2 * TILE), jnp.float32),
            ),
        )
        accum = accum / totals
        feature = lax.broadcasted_iota(jnp.int32, (2 * HEAD, TILE), 0)
        picked = jnp.where(feature < HEAD, accum[:, :TILE], accum[:, TILE:])
        attn_t[tile] = picked
        lse[tile] = maxima + jnp.log(totals)
        store_tile(kept, tile, picked.T.astype(jnp.bfloat16))
        return unused

    tiles_between(rows // TILE, one_tile, between)


def attend_backward(
    per_segment,
    slot_of,
    block_of,
    length_ref,
    qkv,
    grad_attn,
    attn_t,
    lse,
    grad_qkv,
    query,
    key,
    value,
    grad,
    key_t,
    grad_sums,
    between,
):
    rows = qkv.shape[0] * qkv.shape[1]
    length = length_ref[0]
    to_logical(slot_of, qkv, 0, query, jnp.bfloat16(score_scale))
    to_logical(slot_of, qkv, 2 * HEAD, key)
    to_logical(slot_of, qkv, 4 * HEAD, value)
    to_logical(slot_of, grad_attn, 0, grad)
    for tile in range(rows // TILE):
        key_t[tile] = load_tile(key, tile).T
    grad_sums[...] = jnp.zeros_like(grad_sums)
    masks = head_masks()

    def one_tile(tile, unused):
        both = stack_heads(load_tile(query, tile), masks)
        grad_tile = load_tile(grad, tile)
        both_grad = stack_heads(grad_tile, masks)
        product = grad_tile.astype(jnp.float32).T * attn_t[tile]
        delta = jnp.concatenate(
            [
                jnp.sum(product[:HEAD], axis=0, keepdims=True),
                jnp.sum(product[HEAD:], axis=0, keepdims=True),
            ],
            axis=1,
        )
        log_total = lse[tile]

        def step(key_tile, grad_query, kind):
            keys_at = pl.ds(pl.multiple_of(key_tile * 2 * HEAD, 2 * HEAD), 2 * HEAD)
            scores = dot_f32(load_tile(key, key_tile), both, 1, 1)
            if kind != "full":
                scores = jnp.where(tile_mask(kind, key_tile, length), scores, masked_value)
            probs = jnp.exp(scores - log_total)
            grad_probs = dot_f32(load_tile(value, key_tile), both_grad, 1, 1)
            grad_scores = (probs * (grad_probs - delta)).astype(jnp.bfloat16)
            grad_sums[1, :, keys_at] += dot_f32(probs.astype(jnp.bfloat16), both_grad, 1, 0)
            grad_sums[0, :, keys_at] += dot_f32(grad_scores, both, 1, 0)
            return grad_query + dot_f32(key_t[key_tile], grad_scores, 1, 0)

        grad_query = over_keys(
            tile, per_segment, step, jnp.zeros((2 * HEAD, 2 * TILE), jnp.float32)
        )
        feature = lax.broadcasted_iota(jnp.int32, (2 * HEAD, TILE), 0)
        picked = jnp.where(feature < HEAD, grad_query[:, :TILE], grad_query[:, TILE:])
        store_tile(query, tile, (picked * score_scale).T.astype(jnp.bfloat16))
        return unused

    tiles_between(rows // TILE, one_tile, between)
    for tile in range(rows // TILE):
        at = slice(tile * 2 * HEAD, (tile + 1) * 2 * HEAD)
        store_tile(key, tile, grad_sums[0, :, at].astype(jnp.bfloat16))
        store_tile(value, tile, grad_sums[1, :, at].astype(jnp.bfloat16))
    to_stored(block_of, query, grad_qkv, 0)
    to_stored(block_of, key, grad_qkv, 2 * HEAD)
    to_stored(block_of, value, grad_qkv, 4 * HEAD)


def dma(count):
    return pltpu.SemaphoreType.DMA((count,))


def flipped(bit, flip):
    return bit + flip - 2 * bit * flip


class Place:
    def __init__(self, devices_fsdp):
        self.me = lax.axis_index("ctx")
        self.core = lax.rem(self.me, 2)
        self.column = lax.rem(self.me // 2, 2)
        self.row = self.me // 4
        self.group = lax.axis_index("fsdp")
        self.groups = devices_fsdp

    def peer(self, flip):
        low, middle, high = flip % 2, flip // 2 % 2, flip // 4
        return (
            flipped(self.row, high) * 4
            + flipped(self.column, middle) * 2
            + flipped(self.core, low)
        )

    def other_group(self, step):
        return lax.rem(self.group + step, self.groups)

    def at_end(self):
        return lax.rem(self.group, 3) == 0

    def between(self):
        return lax.rem(self.group, 3) != 0

    def near(self, step):
        return self.group != {1: 3, 2: 4, 3: 0}[step]

    def heard(self, step):
        return self.group != {1: 0, 2: 4, 3: 3}[step]

    def meet(self):
        barrier = pltpu.get_barrier_semaphore()
        for flip in range(1, 8):
            pl.semaphore_signal(barrier, inc=1, device_id={"ctx": self.peer(flip)})
        for step in range(1, self.groups):
            pl.semaphore_signal(barrier, inc=1, device_id={"fsdp": self.other_group(step)})
        pl.semaphore_wait(barrier, 7 + self.groups - 1)


def remote(source, target, send, recv, device):
    return pltpu.make_async_remote_copy(
        src_ref=source,
        dst_ref=target,
        send_sem=send,
        recv_sem=recv,
        device_id=device,
        device_id_type=pl.DeviceIdType.MESH,
    )


class Spread:
    def __init__(self, place, own, region, send, recv):
        me, peer = place.me, place.peer

        def copy(index, source, target, flip):
            return remote(source, target, send.at[index], recv.at[index], {"ctx": peer(flip)})

        self.copies = [
            copy(0, own(None), region(me, None), 1),
            copy(1, own(0), region(me, 0), 2),
            copy(2, own(1), region(me, 1), 2),
            copy(3, own(1), region(me, 1), 4),
            copy(4, own(0), region(me, 0), 4),
            copy(5, region(peer(2), 0), region(peer(2), 0), 4),
            copy(6, region(peer(4), 1), region(peer(4), 1), 2),
            copy(7, region(peer(2), None), region(peer(2), None), 1),
            copy(8, region(peer(4), None), region(peer(4), None), 1),
            copy(9, region(peer(6), None), region(peer(6), None), 1),
        ]

    def start(self):
        for index in (1, 3, 0, 2, 4):
            self.copies[index].start()

    def arrived(self, *indices):
        for index in indices:
            self.copies[index].wait_recv()

    def relay_first(self):
        self.arrived(1)
        self.copies[5].start()
        self.arrived(3)
        self.copies[6].start()

    def relay_second(self):
        self.arrived(2)
        self.copies[7].start()
        self.arrived(4)
        self.copies[8].start()

    def relay_third(self):
        self.arrived(5, 6)
        self.copies[9].start()

    def sent(self):
        for copy in self.copies:
            copy.wait_send()


class PairSum:
    def __init__(self, place, stage, landed, sums, received, send, recv, out_send, out_recv):
        self.place = place
        self.slot = lambda pair: pair
        self.stage, self.landed, self.sums, self.received = stage, landed, sums, received
        self.send, self.recv, self.out_send, self.out_recv = send, recv, out_send, out_recv

    def mine(self, pair):
        place = self.place
        return (
            flipped(place.row, pair // 2) * 4
            + flipped(place.column, lax.rem(pair, 2)) * 2
            + place.core
        )

    def theirs(self, pair):
        return self.mine(pair) + 1 - 2 * self.place.core

    def staged(self, pair):
        return self.stage.at[self.slot(pair)]

    def exchange(self, pair):
        return remote(
            self.staged(pair),
            self.landed.at[self.slot(pair)],
            self.send.at[pair],
            self.recv.at[pair],
            {"ctx": self.place.peer(1)},
        )

    def deliver(self, pair):
        return remote(
            self.sums.at[pair],
            self.received.at[pair],
            self.out_send.at[pair],
            self.out_recv.at[pair],
            {"ctx": self.mine(pair)},
        )

    def sent(self):
        for pair in range(4):
            self.exchange(pair).wait_send()
            if pair:
                self.deliver(pair).wait_send()


class OutputSum(PairSum):
    def staged(self, pair):
        return self.stage.at[:, self.theirs(pair)]


class CrossSum(PairSum):
    def __init__(
        self, place, slot, stage, landed, sums, received, passed, send, recv, out_send, out_recv
    ):
        super().__init__(place, stage, landed, sums, received, send, recv, out_send, out_recv)
        self.slot = slot
        self.passed = passed

    def half(self, which):
        count = self.sums.shape[1] // 2
        return slice(which * count, (which + 1) * count)

    def far(self, which):
        slot = 3 * which
        return remote(
            self.sums.at[3, self.half(which)],
            self.passed.at[which],
            self.out_send.at[slot],
            self.out_recv.at[slot],
            {"ctx": self.place.peer(2 + 2 * which)},
        )

    def deliver(self, pair):
        return remote(
            self.sums.at[pair],
            self.received.at[pair - 1],
            self.out_send.at[pair],
            self.out_recv.at[pair],
            {"ctx": self.place.peer(2 * pair)},
        )

    def finish(self, pair, total):
        self.sums[pair] = total.astype(jnp.bfloat16)

        @pl.when(pair == 3)
        def _():
            self.far(0).start()
            self.far(1).start()

        for axis in (1, 2):
            which = 2 - axis

            @pl.when(pair == axis)
            def _(axis=axis, which=which):
                at = self.half(which)
                self.far(which).wait_recv()
                self.sums[axis, at, :] = (
                    total[at] + self.passed[which].astype(jnp.float32)
                ).astype(jnp.bfloat16)
                self.deliver(axis).start()

    def collect(self):
        total = self.sums[0].astype(jnp.float32)
        for pair in (1, 2):
            self.deliver(pair).wait_recv()
            total = total + self.received[pair - 1].astype(jnp.float32)
        return total

    def sent(self):
        for which in (0, 1):
            self.far(which).wait_send()
            self.deliver(which + 1).wait_send()


def halves(count):
    return lambda half: pl.ds(0 if half in (None, 0) else count // 2, count if half is None else count // 2)


def layer_kernel(
    per_segment,
    devices_fsdp,
    slot_of,
    block_of,
    length_ref,
    patches,
    cotangent,
    w_query,
    w_key,
    w_value,
    w_output,
    w_gate,
    w_up,
    w_down,
    gain_attn,
    gain_ffn,
    normed_out,
    layer,
    grad_patches,
    units_out,
    columns_out,
    gains_out,
    qkv,
    attn_t,
    lse,
    grad_units,
    grad_output,
    layer_sums,
    hidden,
    grad_hidden,
    rows_all,
    grads,
    normed_ffn,
    attn_all,
    w_qkv,
    output_all,
    gate_t,
    up_t,
    down,
    down_parts,
    gate_stage,
    up_stage,
    gain_stage,
    gains,
    query,
    key,
    value_t,
    kept,
    grad,
    attn_rows,
    units_t,
    stage,
    landed,
    own_sum,
    norm_sums,
    norm_received,
    norm_passed,
    grad_branch,
    grad_rows,
    grad_attn,
    units_landed,
    units_far,
    units_near,
    units_stage,
    output_landed,
    output_sums,
    output_received,
    output_total,
    output_group,
    qkv_landed,
    columns_stage,
    gain_parts,
    gain_landed,
    gain_total,
    gain_all,
    local_sem,
    save_sem,
    unit_sem,
    group_send,
    group_recv,
    pass_send,
    x_send,
    x_recv,
    g_send,
    g_recv,
    o_send,
    o_recv,
    first_send,
    first_recv,
    second_send,
    second_recv,
    third_send,
    third_recv,
    u_send,
    u_recv,
    c_send,
    c_recv,
    b_send,
    b_recv,
    gain_out_send,
    gain_out_recv,
    pair_send,
    pair_recv,
    out_send,
    out_recv,
    back_pair_send,
    back_pair_recv,
    back_out_send,
    back_out_recv,
    wo_send,
    wo_recv,
    wo_out_send,
    wo_out_recv,
    layer_send,
    layer_recv,
    units_send,
    units_recv,
    gain_send,
    gain_recv,
    far_sem,
    late_send,
    late_recv,
):
    place = Place(devices_fsdp)
    me, group = place.me, place.group
    local_rows, width = patches.shape
    cols = width // 8
    shard = w_query.shape[0]
    part = w_down.shape[1]
    units = part * devices_fsdp
    span = part * 8
    held = qkv.shape[0] // 8

    def unit_range(index):
        return span * index // 128 * 128, -(-span * (index + 1) // 128) * 128

    def unit_copies(weight, target, first):
        copies = []
        for index in range(devices_fsdp):
            low, high = unit_range(index)
            copies.append(
                pltpu.make_async_copy(
                    weight.at[:, low:high],
                    target.at[index // 2, index % 2, :, 0 : high - low],
                    unit_sem.at[first + index],
                )
            )
        return copies

    gate_copies = unit_copies(w_gate, stage, 0)
    up_copies = unit_copies(w_up, landed, devices_fsdp)
    for copy in gate_copies + up_copies:
        copy.start()
    place.meet()

    def rows_of(block, count=local_rows):
        return pl.ds(pl.multiple_of(block * count, count), count)

    def rows_half(ref):
        def region(block, half):
            start = block * local_rows + (local_rows // 2 if half == 1 else 0)
            count = local_rows if half is None else local_rows // 2
            return ref.at[pl.ds(pl.multiple_of(start, local_rows // 2), count)]

        return region

    def own_half(ref):
        return lambda half: ref.at[halves(local_rows)(half)]

    spread_x = Spread(place, own_half(patches), rows_half(rows_all), x_send, x_recv)
    spread_x.start()

    my_cols = rows_of(me, cols)
    def shard_of(index):
        return rows_of(index, shard)

    group_items = [
        (w_query.at[:, my_cols], lambda to: w_qkv.at[shard_of(to), 0:cols]),
        (w_key.at[:, my_cols], lambda to: w_qkv.at[shard_of(to), cols : 2 * cols]),
        (w_value.at[:, my_cols], lambda to: w_qkv.at[shard_of(to), 2 * cols : 3 * cols]),
        (gain_stage, lambda to: gains.at[:, shard_of(to)]),
        (w_output.at[me], lambda to: output_all.at[to, me]),
        (gate_stage, lambda to: gate_t.at[:, shard_of(to)]),
        (up_stage, lambda to: up_t.at[:, shard_of(to)]),
        (w_down.at[me], lambda to: down_parts.at[to]),
    ]

    def group_copy(index, step):
        source, target = group_items[index]
        return remote(
            source,
            target(group),
            group_send.at[index, step - 1],
            group_recv.at[index, step - 1],
            {"fsdp": place.other_group(step)},
        )

    def passed_copy(index):
        whose = place.other_group(2)
        held = group_items[index][1](whose)
        return remote(
            held,
            held,
            pass_send.at[index],
            group_recv.at[index, 2 * (group // 2)],
            {"fsdp": devices_fsdp - 1 - whose},
        )

    def local_copy(index):
        source, target = group_items[index]
        return pltpu.make_async_copy(source, target(group), local_sem.at[index])

    def send_group(index):
        group_copy(index, 2).start()
        for step in (1, 3):
            pl.when(place.near(step))(group_copy(index, step).start)
        local_copy(index).start()

    def pass_group(index):
        @pl.when(place.between())
        def _():
            group_copy(index, 2).wait_recv()
            passed_copy(index).start()

    def group_arrived(index):
        pl.when(place.at_end())(group_copy(index, 2).wait_recv)
        for step in (1, 3):
            group_copy(index, step).wait_recv()
        local_copy(index).wait()

    def group_sent(index):
        group_copy(index, 2).wait_send()
        for step in (1, 3):
            pl.when(place.near(step))(group_copy(index, step).wait_send)
        pl.when(place.between())(passed_copy(index).wait_send)

    for index in (0, 1, 2):
        send_group(index)
    gain_stage[0:8, :] = jnp.broadcast_to(gain_attn[...].astype(jnp.float32), (8, shard))
    gain_stage[8:16, :] = jnp.broadcast_to(gain_ffn[...].astype(jnp.float32), (8, shard))
    send_group(3)
    send_group(4)

    def pick_units(copies, source, target):
        pieces = []
        for index in range(devices_fsdp):
            low, high = unit_range(index)
            unit = lax.broadcasted_iota(jnp.int32, (part, high - low), 0)
            column = lax.broadcasted_iota(jnp.int32, (part, high - low), 1)
            chosen = (column + low == unit + span * index + part * me).astype(jnp.bfloat16)
            copies[index].wait()
            pieces.append(
                dot_f32(chosen, source[index // 2, index % 2, :, 0 : high - low], 1, 1)
            )
        target[...] = jnp.concatenate(pieces, axis=0).astype(jnp.bfloat16)

    pick_units(gate_copies, stage, gate_stage)
    pick_units(up_copies, landed, up_stage)
    send_group(5)
    send_group(6)
    send_group(7)

    rows_all[rows_of(me), :] = patches[...]
    load_grads = pltpu.make_async_copy(cotangent, grads.at[rows_of(me)], save_sem.at[0])
    load_grads.start()
    spread_x.relay_first()
    for index in (0, 1, 2, 3):
        pass_group(index)
    spread_x.relay_second()
    spread_g = Spread(place, own_half(cotangent), rows_half(grads), g_send, g_recv)
    spread_g.start()
    spread_x.relay_third()
    pass_group(4)
    spread_x.arrived(0, 7, 8, 9)
    for index in (0, 1, 2, 3):
        group_arrived(index)
    gain_one = gains[0:1, :]

    def output_half(block, half):
        if half is None:
            return output_all.at[:, block]
        lines = output_all.shape[2]
        return output_all.at[:, block, halves(lines)(half)]

    group_arrived(4)
    spread_o = Spread(place, lambda half: output_half(me, half), output_half, o_send, o_recv)
    spread_o.start()

    def project(block, unused):
        at = rows_of(block)
        values = rows_all[at, :].astype(jnp.float32)
        low = rms_forward(values, gain_one)[0].astype(jnp.bfloat16)
        normed_ffn[at, :] = low
        store_tile(qkv, block, dot_f32(low, w_qkv[...], 1, 0).astype(jnp.bfloat16))
        return unused

    spread_x.sent()
    lax.fori_loop(0, 8, project, 0)
    save_normed = pltpu.make_async_copy(normed_ffn, normed_out, local_sem.at[8])
    save_normed.start()
    spread_g.relay_first()

    def attn_spread(first, count, send, recv):
        def part(half):
            return slice(
                first + (count // 2 if half == 1 else 0),
                first + (count // 2 if half == 0 else count),
            )

        return Spread(
            place,
            lambda half: kept.at[part(half)],
            lambda block, half: attn_all.at[part(half), :, rows_of(block, cols)],
            send,
            recv,
        )

    half_blocks = kept.shape[0] // 2
    attn_first = attn_spread(0, half_blocks, first_send, first_recv)
    attn_second = attn_spread(half_blocks, half_blocks // 2, second_send, second_recv)
    attn_third = attn_spread(half_blocks * 3 // 2, half_blocks // 2, third_send, third_recv)

    def after_two():
        pass_group(5)

    def after_more():
        spread_g.relay_second()
        pass_group(6)

    def after_half():
        attn_second.start()
        spread_o.relay_first()

    def after_most():
        pass_group(7)
        spread_o.relay_second()

    attend_forward(
        per_segment,
        slot_of,
        length_ref,
        qkv,
        attn_t,
        lse,
        query,
        key,
        value_t,
        kept,
        {
            per_segment // 2: after_two,
            per_segment: attn_first.start,
            per_segment + 1: after_more,
            per_segment + per_segment // 2: after_half,
            2 * per_segment - 1: after_most,
        },
    )
    attn_third.start()
    attn_all[:, :, my_cols] = kept[...]
    spread_g.relay_third()
    attn_first.relay_first()
    attn_first.relay_second()
    spread_o.relay_third()
    for index in (5, 6, 7):
        group_arrived(index)
    down[...] = jnp.concatenate(
        [down_parts[index].astype(jnp.float32) for index in range(devices_fsdp)], axis=0
    ).astype(jnp.bfloat16)
    attn_second.relay_first()
    attn_second.relay_second()
    attn_first.relay_third()
    attn_third.relay_first()
    attn_third.relay_second()
    attn_second.relay_third()
    save_normed.wait()
    load_grads.wait()
    spread_g.arrived(0, 7, 8, 9)
    spread_o.arrived(0, 7, 8, 9)
    attn_third.relay_third()
    for spread in (attn_first, attn_second, attn_third):
        spread.arrived(0, 7, 8, 9)

    def swap(source, target, send, recv):
        return [
            remote(source(flip), target, send.at[flip - 1], recv.at[flip - 1], {"ctx": place.peer(flip)})
            for flip in range(1, 8)
        ]

    def attn_of(block):
        return jnp.concatenate(
            [attn_all[block_of[block * held + index]] for index in range(held)], axis=0
        )

    gain_two = gains[8:9, :]
    sums = CrossSum(
        place,
        lambda pair: lax.rem(pair, 2),
        stage,
        landed,
        norm_sums,
        norm_received,
        norm_passed,
        pair_send,
        pair_recv,
        out_send,
        out_recv,
    )

    def hidden_of(block, attn):
        return rows_all[rows_of(block), :].astype(jnp.float32) + dot_f32(
            attn, output_all[...].reshape(width, width), 1, 0
        )

    def feed(block):
        at = rows_of(block)
        low = rms_forward(hidden_of(block, attn_of(block)), gain_two)[0].astype(jnp.bfloat16)
        normed_ffn[at, :] = low
        grad_out = grads[at, :]
        gate = dot_f32(low, gate_t[...], 1, 1)
        up_proj = dot_f32(low, up_t[...], 1, 1)
        grad_inner = dot_f32(grad_out, down[...], 1, 1)
        sigmoid = jax.nn.sigmoid(gate)
        activated = gate * sigmoid
        inner = activated * up_proj
        inner_low = inner.astype(jnp.bfloat16)
        grad_gate = grad_inner * up_proj * sigmoid * (1.0 + gate * (1.0 - sigmoid))
        grad_up = grad_inner * activated
        gate_low = grad_gate.astype(jnp.bfloat16)
        up_low = grad_up.astype(jnp.bfloat16)
        units_t[0:units, at] = inner.T.astype(jnp.bfloat16)
        units_t[units : 2 * units, at] = grad_gate.T.astype(jnp.bfloat16)
        units_t[2 * units : 3 * units, at] = grad_up.T.astype(jnp.bfloat16)
        return (
            dot_f32(inner_low, down[...], 1, 0),
            dot_f32(gate_low, gate_t[...], 1, 0) + dot_f32(up_low, up_t[...], 1, 0),
        )

    def one_pair(step, unused):
        pair = 3 - step
        slot = lax.rem(pair, 2)
        layer, norm = feed(sums.theirs(pair))

        @pl.when(step > 1)
        def _():
            sums.exchange(pair + 2).wait_send()

        stage[slot, 0] = layer.astype(jnp.bfloat16)
        stage[slot, 1] = norm.astype(jnp.bfloat16)
        sums.exchange(pair).start()
        layer, norm = feed(sums.mine(pair))
        own_sum[0] = layer
        own_sum[1] = norm
        sums.exchange(pair).wait_recv()
        layer_sums[pair] = (
            (own_sum[0] + landed[slot, 0].astype(jnp.float32))
            .astype(jnp.bfloat16)
            .reshape(layer_sums.shape[1:])
        )
        sums.finish(pair, own_sum[1] + landed[slot, 1].astype(jnp.float32))
        return unused

    lax.fori_loop(0, 4, one_pair, 0)
    for pair in (1, 0):
        sums.exchange(pair).wait_send()
    attn_rows[...] = attn_of(me)
    hidden[...] = hidden_of(me, attn_rows[...])
    load_normed = pltpu.make_async_copy(normed_out, rows_all, local_sem.at[8])
    load_normed.start()

    def units_tile(tile, unused):
        at = rows_of(tile, shard)
        low = normed_ffn[:, at]
        grad_units[tile, 0 : 2 * units, :] = dot_f32(units_t[units : 3 * units, :], low, 1, 0).astype(
            jnp.bfloat16
        )
        down_tile = dot_f32(units_t[0:units, :], grads[:, at], 1, 0)
        for half in (0, 1):
            own_sum[half, 0 : units // 2, at] = down_tile[half * units // 2 : (half + 1) * units // 2]
        return unused

    lax.fori_loop(0, devices_fsdp, units_tile, 0)
    for index in range(devices_fsdp):
        first = index % 2 * part
        grad_units[index, 2 * units : 3 * units, :] = jnp.concatenate(
            [
                own_sum[index // 2, first : first + part, tile * shard : (tile + 1) * shard]
                for tile in range(devices_fsdp)
            ],
            axis=0,
        ).astype(jnp.bfloat16)

    def units_copy(step, source):
        return remote(
            source,
            units_landed.at[group],
            units_send.at[step - 1],
            units_recv.at[step - 1],
            {"fsdp": place.other_group(step)},
        )

    def units_direct(step):
        return units_copy(step, grad_units.at[place.other_group(step)])

    units_far_copy = remote(
        grad_units.at[devices_fsdp - 1 - group],
        units_far,
        far_sem.at[0],
        far_sem.at[1],
        {"fsdp": 1 + group // 3},
    )
    units_sum_copy = units_copy(2, units_near)

    @pl.when(place.at_end())
    def _():
        units_far_copy.start()
        units_direct(2).start()

    for step in (1, 3):
        pl.when(place.near(step))(units_direct(step).start)

    total = sums.collect()
    values = hidden[...]
    factor = lax.rsqrt(jnp.mean(values * values, axis=-1, keepdims=True) + epsilon)
    scaled = total * gain_two
    gain_part = jnp.sum(total * values * factor, axis=0, keepdims=True)
    whole = (
        grads[rows_of(me), :].astype(jnp.float32)
        + factor * scaled
        - values * (factor * factor * factor) * jnp.mean(scaled * values, axis=-1, keepdims=True)
    )
    grad_hidden[...] = whole
    grad_branch[...] = whole.astype(jnp.bfloat16)
    grad_rows[...] = (
        dot_f32(grad_branch[...], output_all[...].reshape(width, width), 1, 1)
        .astype(jnp.bfloat16)
        .reshape(grad_rows.shape)
    )
    to_heads = swap(
        lambda flip: grad_rows.at[:, :, rows_of(place.peer(flip), cols)],
        grad_attn.at[pl.ds(me * held, held)],
        b_send,
        b_recv,
    )
    for spread in (spread_g, spread_o, attn_first, attn_second, attn_third):
        spread.sent()
    sums.sent()
    for copy in to_heads:
        copy.start()
    grad_attn[pl.ds(me * held, held)] = grad_rows[:, :, my_cols]

    for index in range(devices_fsdp):
        piece = attn_rows[:, index * shard : (index + 1) * shard].T
        grad_output[index] = (
            dot_f32(piece, grad_branch[...], 1, 0)
            .astype(jnp.bfloat16)
            .reshape(8, shard // 8, width)
        )
    for copy in to_heads:
        copy.wait_recv()
    for index in range(8):
        group_sent(index)
    for copy in to_heads:
        copy.wait_send()

    def over_groups(source, target, send, recv):
        return [
            remote(
                source(place.other_group(step)),
                target.at[group],
                send.at[step - 1],
                recv.at[step - 1],
                {"fsdp": place.other_group(step)},
            )
            for step in range(1, devices_fsdp)
        ]

    def units_between():
        @pl.when(place.between())
        def _():
            units_far_copy.wait_recv()
            units_near[...] = (
                grad_units[place.other_group(2)].astype(jnp.float32)
                + units_far[...].astype(jnp.float32)
            ).astype(jnp.bfloat16)
            units_sum_copy.start()

    sums = CrossSum(
        place,
        lambda pair: (pair // 2, lax.rem(pair, 2)),
        stage,
        landed,
        norm_sums,
        norm_received,
        norm_passed,
        back_pair_send,
        back_pair_recv,
        back_out_send,
        back_out_recv,
    )
    output_pairs = OutputSum(
        place,
        grad_output,
        output_landed,
        output_sums,
        output_received,
        wo_send,
        wo_recv,
        wo_out_send,
        wo_out_recv,
    )
    for pair in range(4):
        output_pairs.exchange(pair).start()
    layer_copies = [
        remote(
            layer_sums.at[pair],
            attn_all.at[pair * held : (pair + 1) * held],
            layer_send.at[pair],
            layer_recv.at[pair],
            {"ctx": sums.mine(pair)},
        )
        for pair in range(1, 4)
    ]
    for copy in layer_copies:
        copy.start()

    def after_prompt():
        for pair in range(4):
            output_pairs.exchange(pair).wait_recv()
            output_sums[pair] = (
                grad_output[:, output_pairs.mine(pair)].astype(jnp.float32)
                + output_landed[pair].astype(jnp.float32)
            ).astype(jnp.bfloat16)
            if pair:
                output_pairs.deliver(pair).start()

    attend_backward(
        per_segment,
        slot_of,
        block_of,
        length_ref,
        qkv,
        grad_attn,
        attn_t,
        lse,
        grads,
        query,
        key,
        kept,
        grad,
        value_t,
        own_sum,
        {per_segment // 2: units_between, per_segment: after_prompt},
    )

    total = output_sums[0].astype(jnp.float32)
    for pair in range(1, 4):
        output_pairs.deliver(pair).wait_recv()
        total = total + output_received[pair].astype(jnp.float32)
    output_total[...] = total.astype(jnp.bfloat16)
    output_copies = over_groups(
        lambda to: output_total.at[to], output_group, late_send.at[1], late_recv.at[1]
    )
    for copy in output_copies:
        copy.start()

    def turn(tile, unused):
        at = rows_of(tile, TILE)
        units_t[0 : 3 * cols, at] = grads[at, 0 : 3 * cols].T
        return unused

    lax.fori_loop(0, grads.shape[0] // TILE, turn, 0)
    load_normed.wait()

    def weight_tile(tile, unused):
        at = rows_of(tile, shard)
        normed_ffn[0 : 3 * cols, at] = dot_f32(
            units_t[0 : 3 * cols, :], rows_all[:, at], 1, 0
        ).astype(jnp.bfloat16)
        return unused

    def qkv_parts(to):
        return normed_ffn.at[0 : 3 * cols, rows_of(to, shard)]

    lax.fori_loop(0, devices_fsdp, weight_tile, 0)
    qkv_copies = over_groups(
        qkv_parts, qkv_landed, late_send.at[0], late_recv.at[0]
    )
    for copy in qkv_copies:
        copy.start()

    def one_pair(step, unused):
        pair = 3 - step
        stage[pair // 2, lax.rem(pair, 2)] = dot_f32(
            grads[rows_of(sums.theirs(pair)), 0 : 3 * cols], w_qkv[...], 1, 1
        ).astype(jnp.bfloat16)
        sums.exchange(pair).start()
        return unused

    lax.fori_loop(0, 4, one_pair, 0)

    def sum_pair(step, unused):
        pair = 3 - step
        own_sum[0] = dot_f32(grads[rows_of(sums.mine(pair)), 0 : 3 * cols], w_qkv[...], 1, 1)
        sums.exchange(pair).wait_recv()
        sums.finish(
            pair, own_sum[0] + landed[pair // 2, lax.rem(pair, 2)].astype(jnp.float32)
        )
        return unused

    lax.fori_loop(0, 4, sum_pair, 0)

    def group_sum(own, landed_ref, copies):
        landed_ref[group] = own
        for copy in copies:
            copy.wait_recv()
        total = landed_ref[0].astype(jnp.float32)
        for index in range(1, devices_fsdp):
            total = total + landed_ref[index].astype(jnp.float32)
        return total

    units_landed[group] = grad_units[group]

    @pl.when(place.at_end())
    def _():
        units_landed[devices_fsdp - 1 - group] = jnp.zeros_like(grad_units[group])

    units_direct(2).wait_recv()
    for step in (1, 3):
        pl.when(place.heard(step))(units_direct(step).wait_recv)
    units_total = units_landed[0].astype(jnp.float32)
    for index in range(1, devices_fsdp):
        units_total = units_total + units_landed[index].astype(jnp.float32)
    units_stage[...] = units_total.astype(jnp.bfloat16)

    def half_of(ref, lines):
        def region(block, half):
            return ref.at[block] if half is None else ref.at[block, halves(lines)(half)]

        return region

    def own_of(ref, lines):
        return lambda half: ref if half is None else ref.at[halves(lines)(half)]

    spread_u = Spread(
        place,
        own_of(units_stage, 3 * units),
        half_of(units_out, 3 * units),
        u_send,
        u_recv,
    )
    spread_u.start()
    save_units = pltpu.make_async_copy(units_stage, units_out.at[me], save_sem.at[0])
    save_units.start()

    total = layer_sums[0].astype(jnp.float32)
    for pair, copy in enumerate(layer_copies):
        copy.wait_recv()
        at = slice((pair + 1) * held, (pair + 2) * held)
        total = total + attn_all[at].astype(jnp.float32)
    grad_rows[...] = (hidden[...].reshape(total.shape) + total).astype(jnp.bfloat16)
    save_layer = pltpu.make_async_copy(grad_rows, layer, save_sem.at[2])
    save_layer.start()

    total = sums.collect()
    values = patches[...].astype(jnp.float32)
    factor = lax.rsqrt(jnp.mean(values * values, axis=-1, keepdims=True) + epsilon)
    scaled = total * gain_one
    gain_parts[...] = jnp.zeros_like(gain_parts)
    attn_part = jnp.sum(total * values * factor, axis=0, keepdims=True)
    ffn_part = gain_part
    for index in range(devices_fsdp):
        at = slice(index * shard, (index + 1) * shard)
        gain_parts[index, 0:1, :] = attn_part[:, at]
        gain_parts[index, 1:2, :] = ffn_part[:, at]
    gain_copies = over_groups(lambda to: gain_parts.at[to], gain_landed, gain_send, gain_recv)
    for copy in gain_copies:
        copy.start()
    grad_hidden[...] = (
        grad_hidden[...]
        + factor * scaled
        - values * (factor * factor * factor) * jnp.mean(scaled * values, axis=-1, keepdims=True)
    )
    save_rows = pltpu.make_async_copy(grad_hidden, grad_patches, save_sem.at[3])
    save_rows.start()
    spread_u.relay_first()
    spread_u.relay_second()
    gain_total[...] = group_sum(gain_parts[group], gain_landed, gain_copies)
    gain_out = [
        remote(
            gain_total,
            gain_all.at[me],
            gain_out_send.at[flip - 1],
            gain_out_recv.at[flip - 1],
            {"ctx": place.peer(flip)},
        )
        for flip in range(1, 8)
    ]
    for copy in gain_out:
        copy.start()
    gain_all[me] = gain_total[...]

    turned = group_sum(qkv_parts(group)[...], qkv_landed, qkv_copies).T.astype(jnp.bfloat16)
    for index in range(3):
        columns_stage[index * shard : (index + 1) * shard, :] = turned[
            :, index * cols : (index + 1) * cols
        ]
    summed = group_sum(output_total[group], output_group, output_copies).astype(jnp.bfloat16)
    lines = shard // 8
    for index in range(8):
        columns_stage[3 * shard + index * lines : 3 * shard + (index + 1) * lines, :] = summed[
            :, index * cols : (index + 1) * cols
        ]
    spread_c = Spread(
        place, own_of(columns_stage, 4 * shard), half_of(columns_out, 4 * shard), c_send, c_recv
    )
    spread_c.start()
    save_columns = pltpu.make_async_copy(columns_stage, columns_out.at[me], save_sem.at[1])
    save_columns.start()
    spread_u.relay_third()
    for copy in gain_out:
        copy.wait_recv()
    gain_sum = gain_all[0]
    for index in range(1, 8):
        gain_sum = gain_sum + gain_all[index]
    gains_out[...] = gain_sum
    spread_c.relay_first()
    spread_c.relay_second()
    spread_u.arrived(0, 7, 8, 9)
    spread_c.relay_third()
    spread_c.arrived(0, 7, 8, 9)
    for step in (1, 3):
        pl.when(place.near(step))(units_direct(step).wait_send)
    units_direct(2).wait_send()
    pl.when(place.at_end())(units_far_copy.wait_send)
    for copy in layer_copies + qkv_copies + output_copies + gain_copies + gain_out:
        copy.wait_send()
    for pair in range(4):
        sums.exchange(pair).wait_send()
    sums.sent()
    output_pairs.sent()
    save_layer.wait()
    save_rows.wait()
    spread_u.sent()
    spread_c.sent()
    save_units.wait()
    save_columns.wait()


def place_kernel(
    devices_fsdp,
    units_all,
    columns_all,
    out_query,
    out_key,
    out_value,
    out_output,
    out_gate,
    out_up,
    out_down,
    columns,
    outputs,
    natural,
    gate,
    up,
    down,
    sems,
):
    shard = out_query.shape[0]
    cols = columns_all.shape[2]
    lines = shard // 8
    units = units_all.shape[1] // 3
    part = units // devices_fsdp
    span = part * 8
    saves = []

    def save(source, target):
        copy = pltpu.make_async_copy(source, target, sems.at[len(saves)])
        copy.start()
        saves.append(copy)

    for index in range(8):
        piece = units_all[index, 2 * units : 3 * units, :].astype(jnp.float32)
        for tile in range(devices_fsdp):
            down[index * part : (index + 1) * part, tile * shard : (tile + 1) * shard] = piece[
                tile * part : (tile + 1) * part, :
            ]
    save(down, out_down)
    for which, (target, out) in enumerate(((gate, out_gate), (up, out_up))):
        for index in range(8):
            piece = units_all[index, which * units : (which + 1) * units, :].astype(jnp.float32)
            for tile in range(devices_fsdp):
                first = tile * span + index * part
                natural[first : first + part, :] = piece[tile * part : (tile + 1) * part, :]
        for first in range(0, span * devices_fsdp, 128):
            target[:, first : first + 128] = natural[first : first + 128, :].T
        save(target, out)
    for index in range(8):
        at = slice(index * cols, (index + 1) * cols)
        for which in range(3):
            columns[which, :, at] = columns_all[
                index, which * shard : (which + 1) * shard, :
            ].astype(jnp.float32)
        for tile in range(8):
            first = 3 * shard + tile * lines
            outputs[index * lines : (index + 1) * lines, tile * cols : (tile + 1) * cols] = (
                columns_all[index, first : first + lines, :].astype(jnp.float32)
            )
    save(columns.at[0], out_query)
    save(columns.at[1], out_key)
    save(columns.at[2], out_value)
    save(outputs, out_output)
    for copy in saves:
        copy.wait()


def heads_plan(
    patches,
    cotangent,
    deal_table,
    prompt_len,
    w_query,
    w_key,
    w_value,
    w_output,
    w_gate,
    w_up,
    w_down,
    gain_attn,
    gain_ffn,
):
    local_rows = patches.shape[1]
    width = patches.shape[2]
    groups = lax.axis_size("fsdp")
    rows = local_rows * 8
    cols = width // 8
    shard = width // groups
    part = w_down.shape[0] // 8
    units = part * groups
    tiles = rows // TILE
    blocks = deal_table.shape[0]
    block_len = rows // blocks
    per_segment = CONT_LEN // TILE
    slots = jnp.arange(deal_table.shape[0], dtype=jnp.int32)
    slot_of = jnp.sum(
        jnp.where(deal_table[None, :] == slots[:, None], slots[None, :], 0), axis=1
    ).astype(jnp.int32)
    smem = pl.BlockSpec(memory_space=pltpu.SMEM)
    vmem = pl.BlockSpec(memory_space=pltpu.VMEM)
    anywhere = pl.BlockSpec(memory_space=pl.ANY)
    low, full = jnp.bfloat16, jnp.float32

    def shaped(kind, *dims):
        return jax.ShapeDtypeStruct(dims, kind)

    def room(kind, *dims):
        return pltpu.VMEM(dims, kind)

    unused, layer, grad_rows, units_all, columns_all, gains_sum = pl.pallas_call(
        functools.partial(layer_kernel, per_segment, groups),
        out_shape=(
            shaped(low, rows, width),
            shaped(low, blocks // 8, block_len, width),
            shaped(full, local_rows, width),
            shaped(low, 8, 3 * units, shard),
            shaped(low, 8, 4 * shard, cols),
            shaped(full, 8, shard),
        ),
        in_specs=[smem] * 3 + [vmem] + [anywhere] * 8 + [vmem] * 2,
        out_specs=(anywhere,) * 5 + (vmem,),
        scratch_shapes=[
            room(low, blocks, block_len, 3 * cols),
            room(full, tiles, cols, TILE),
            room(full, tiles, 1, 2 * TILE),
            room(low, groups, 3 * units, shard),
            room(low, groups, 8, shard // 8, width),
            room(low, 4, blocks // 8, block_len, width),
            room(full, local_rows, width),
            room(full, local_rows, width),
            room(low, rows, width),
            room(low, rows, width),
            room(low, rows, width),
            room(low, blocks, block_len, width),
            room(low, width, 3 * cols),
            room(low, groups, 8, shard // 8, width),
            room(low, units, width),
            room(low, units, width),
            room(low, units, width),
            room(low, groups, part, width),
            room(low, units, shard),
            room(low, units, shard),
            room(full, 16, shard),
            room(full, 16, width),
            room(low, blocks, block_len, cols),
            room(low, blocks, block_len, cols),
            room(low, tiles, cols, TILE),
            room(low, blocks, block_len, cols),
            room(low, blocks, block_len, cols),
            room(low, local_rows, width),
            room(low, 3 * units, rows),
            room(low, 2, 2, local_rows, width),
            room(low, 2, 2, local_rows, width),
            room(full, 2, local_rows, width),
            room(low, 4, local_rows, width),
            room(low, 2, local_rows, width),
            room(low, 2, local_rows // 2, width),
            room(low, local_rows, width),
            room(low, blocks // 8, block_len, width),
            room(low, blocks, block_len, cols),
            room(low, groups, 3 * units, shard),
            room(low, 3 * units, shard),
            room(low, 3 * units, shard),
            room(low, 3 * units, shard),
            room(low, 4, groups, shard // 8, width),
            room(low, 4, groups, shard // 8, width),
            room(low, 4, groups, shard // 8, width),
            room(low, groups, shard // 8, width),
            room(low, groups, shard // 8, width),
            room(low, groups, 3 * cols, shard),
            room(low, 4 * shard, cols),
            room(full, groups, 8, shard),
            room(full, groups, 8, shard),
            room(full, 8, shard),
            room(full, 8, 8, shard),
            dma(9),
            dma(4),
            dma(2 * groups),
            pltpu.SemaphoreType.DMA((8, groups - 1)),
            pltpu.SemaphoreType.DMA((8, groups - 1)),
            dma(8),
            dma(10),
            dma(10),
            dma(10),
            dma(10),
            dma(10),
            dma(10),
            dma(10),
            dma(10),
            dma(10),
            dma(10),
            dma(10),
            dma(10),
            dma(10),
            dma(10),
            dma(10),
            dma(10),
            dma(7),
            dma(7),
            dma(7),
            dma(7),
            dma(4),
            dma(4),
            dma(4),
            dma(4),
            dma(4),
            dma(4),
            dma(4),
            dma(4),
            dma(4),
            dma(4),
            dma(4),
            dma(4),
            dma(4),
            dma(4),
            dma(groups - 1),
            dma(groups - 1),
            dma(groups - 1),
            dma(groups - 1),
            dma(2),
            pltpu.SemaphoreType.DMA((2, groups - 1)),
            pltpu.SemaphoreType.DMA((2, groups - 1)),
        ],
        compiler_params=pltpu.CompilerParams(
            collective_id=0, has_side_effects=True, vmem_limit_bytes=67_000_000
        ),
        name="layer",
    )(
        slot_of,
        deal_table,
        prompt_len,
        patches[0],
        cotangent[0],
        w_query,
        w_key,
        w_value,
        w_output.reshape(8, shard // 8, width),
        w_gate,
        w_up,
        w_down.reshape(8, part, width),
        gain_attn[None],
        gain_ffn[None],
    )

    weights = pl.pallas_call(
        functools.partial(place_kernel, groups),
        out_shape=tuple(shaped(full, shard, width) for _ in range(4))
        + tuple(shaped(full, shard, 8 * units) for _ in range(2))
        + (shaped(full, 8 * part, width),),
        in_specs=[vmem, vmem],
        out_specs=(anywhere,) * 7,
        scratch_shapes=[
            room(full, 3, shard, width),
            room(full, shard, width),
            room(full, 8 * units, shard),
            room(full, shard, 8 * units),
            room(full, shard, 8 * units),
            room(full, 8 * part, width),
            dma(7),
        ],
        name="place",
    )(units_all, columns_all)
    layer = layer.reshape(1, local_rows, width)
    return (layer, grad_rows[None]) + tuple(weights) + (gains_sum[0], gains_sum[1])


def solution(mesh):
    if mesh.shape["ctx"] == 8 and mesh.shape["fsdp"] == 4:
        per_device = heads_plan
    else:
        per_device = rows_plan
    placed = (
        P("fsdp", "ctx", None),
        P("fsdp", "ctx", None),
        P(),
        P("fsdp"),
        P("fsdp", None),
        P("fsdp", None),
        P("fsdp", None),
        P("fsdp", None),
        P("fsdp", None),
        P("fsdp", None),
        P("fsdp", None),
        P("fsdp"),
        P("fsdp"),
    )
    return jax.shard_map(
        per_device,
        mesh=mesh,
        in_specs=placed,
        out_specs=(
            P("fsdp", "ctx", None),
            P("fsdp", "ctx", None),
            P("fsdp", None),
            P("fsdp", None),
            P("fsdp", None),
            P("fsdp", None),
            P("fsdp", None),
            P("fsdp", None),
            P("fsdp", None),
            P("fsdp"),
            P("fsdp"),
        ),
        check_vma=False,
    )
```

```python
import functools
import math

import jax
import jax.numpy as jnp
from jax import lax
from jax.experimental import pallas as pl
from jax.experimental.pallas import tpu as pltpu
from jax.sharding import PartitionSpec as P

HEADS = 16
HEAD = 64
CONT_LEN = 1024


epsilon = 1e-05
score_scale = 0.125
masked_value = -1e30


def rms_forward(values, gain):
    factor = lax.rsqrt(jnp.mean(values * values, axis=-1, keepdims=True) + epsilon)
    return (values * factor * gain, factor)


def rms_backward(values, factor, gain, grad_normed):
    scaled = grad_normed * gain
    grad_gain = jnp.sum(grad_normed * values * factor, axis=0)
    cubed = factor * factor * factor
    grad_values = factor * scaled - values * cubed * jnp.mean(
        scaled * values, axis=-1, keepdims=True
    )
    return (grad_values, grad_gain)


def segment_of(position, prompt):
    return jnp.where(position < prompt, -1, (position - prompt) // CONT_LEN)


def visible(query_pos, key_pos, prompt, length):
    same = (segment_of(query_pos, prompt)[:, None] == segment_of(key_pos, prompt)[None, :]) & (
        key_pos[None, :] <= query_pos[:, None]
    )
    shared = (query_pos[:, None] >= prompt) & (key_pos[None, :] < length)
    return same | shared


def rows_plan(
    patches,
    cotangent,
    deal_table,
    prompt_len,
    w_query,
    w_key,
    w_value,
    w_output,
    w_gate,
    w_up,
    w_down,
    gain_attn,
    gain_ffn,
):
    local_rows = patches.shape[1]
    width = patches.shape[2]
    devices_ctx = lax.axis_size("ctx")
    group_tok = local_rows * devices_ctx
    cont_count = group_tok // (2 * CONT_LEN)
    prompt = group_tok - cont_count * CONT_LEN
    block_len = local_rows // 2
    slot_count = 2 * devices_ctx
    key_rows = math.gcd(512, group_tok)
    block_count = group_tok // key_rows
    length = prompt_len[0]

    def positions_of(first_row, count):
        stored = first_row + jnp.arange(count, dtype=jnp.int32)
        slot_ids = stored // block_len
        picked = jnp.where(
            slot_ids[:, None] == jnp.arange(slot_count, dtype=jnp.int32)[None, :],
            deal_table[None, :],
            0,
        )
        return jnp.sum(picked, axis=1) * block_len + stored % block_len

    query_pos = positions_of(lax.axis_index("ctx") * local_rows, local_rows)
    key_pos = positions_of(0, group_tok).reshape(block_count, key_rows)
    (
        full_query,
        full_key,
        full_value,
        full_output,
        full_gate,
        full_up,
        full_down,
        full_gain_attn,
        full_gain_ffn,
    ) = (
        lax.all_gather(w_query, "fsdp", axis=0, tiled=True),
        lax.all_gather(w_key, "fsdp", axis=0, tiled=True),
        lax.all_gather(w_value, "fsdp", axis=0, tiled=True),
        lax.all_gather(w_output, "fsdp", axis=0, tiled=True),
        lax.all_gather(w_gate, "fsdp", axis=0, tiled=True),
        lax.all_gather(w_up, "fsdp", axis=0, tiled=True),
        lax.all_gather(w_down, "fsdp", axis=0, tiled=True),
        lax.all_gather(gain_attn, "fsdp", axis=0, tiled=True),
        lax.all_gather(gain_ffn, "fsdp", axis=0, tiled=True),
    )
    rows_f32 = patches[0].astype(jnp.float32)
    gain_one = full_gain_attn.astype(jnp.float32)
    normed, factor_attn = rms_forward(rows_f32, gain_one)
    normed_low = normed.astype(jnp.bfloat16)
    queries = jnp.dot(normed_low, full_query, preferred_element_type=jnp.float32).astype(
        jnp.bfloat16
    )
    keys_local = jnp.dot(normed_low, full_key, preferred_element_type=jnp.float32).astype(
        jnp.bfloat16
    )
    values_local = jnp.dot(normed_low, full_value, preferred_element_type=jnp.float32).astype(
        jnp.bfloat16
    )
    key_all, value_all = (
        lax.all_gather(keys_local, "ctx", axis=0, tiled=True),
        lax.all_gather(values_local, "ctx", axis=0, tiled=True),
    )
    query_heads = queries.reshape(local_rows, HEADS, HEAD)

    def split_blocks(array):
        return array.reshape(block_count, key_rows, HEADS, HEAD)

    def forward_block(state, block):
        key_block, value_block, block_pos = block
        visible_mask = visible(query_pos, block_pos, prompt, length)

        def forward_update(inner_state):
            maxima, totals, accum = inner_state
            scores = (
                jnp.einsum(
                    "qhe,khe->hqk", query_heads, key_block, preferred_element_type=jnp.float32
                )
                * score_scale
            )
            scores = jnp.where(visible_mask[None], scores, masked_value)
            new_max = jnp.maximum(maxima, jnp.max(scores, axis=-1))
            rescale = jnp.exp(maxima - new_max)
            probs = jnp.where(visible_mask[None], jnp.exp(scores - new_max[:, :, None]), 0.0)
            totals = totals * rescale + jnp.sum(probs, axis=-1)
            accum = accum * rescale.T[:, :, None] + jnp.einsum(
                "hqk,khe->qhe",
                probs.astype(jnp.bfloat16),
                value_block,
                preferred_element_type=jnp.float32,
            )
            return (new_max, totals, accum)

        return (
            lax.cond(jnp.any(visible_mask), forward_update, lambda inner_state: inner_state, state),
            None,
        )

    start_state = (
        jnp.full((HEADS, local_rows), masked_value, jnp.float32),
        jnp.zeros((HEADS, local_rows), jnp.float32),
        jnp.zeros((local_rows, HEADS, HEAD), jnp.float32),
    )
    (maxima, totals, accum), unused = lax.scan(
        forward_block, start_state, (split_blocks(key_all), split_blocks(value_all), key_pos)
    )
    attn_f32 = accum / totals.T[:, :, None]
    log_total = maxima + jnp.log(totals)
    attn_low = attn_f32.astype(jnp.bfloat16).reshape(local_rows, width)
    hidden = rows_f32 + jnp.dot(attn_low, full_output, preferred_element_type=jnp.float32)
    gain_two = full_gain_ffn.astype(jnp.float32)
    normed_ffn, factor_ffn = rms_forward(hidden, gain_two)
    ffn_low = normed_ffn.astype(jnp.bfloat16)
    gate = jnp.dot(ffn_low, full_gate, preferred_element_type=jnp.float32)
    up_proj = jnp.dot(ffn_low, full_up, preferred_element_type=jnp.float32)
    sigmoid = jax.nn.sigmoid(gate)
    activated = gate * sigmoid
    inner_low = (activated * up_proj).astype(jnp.bfloat16)
    layer = hidden + jnp.dot(inner_low, full_down, preferred_element_type=jnp.float32)
    grad_out = cotangent[0].astype(jnp.float32)
    grad_down_in = cotangent[0]
    grad_w_down = jnp.dot(inner_low.T, grad_down_in, preferred_element_type=jnp.float32)
    grad_inner = jnp.dot(grad_down_in, full_down.T, preferred_element_type=jnp.float32)
    grad_gate = (grad_inner * up_proj * sigmoid * (1.0 + gate * (1.0 - sigmoid))).astype(
        jnp.bfloat16
    )
    grad_up = (grad_inner * activated).astype(jnp.bfloat16)
    grad_w_gate = jnp.dot(ffn_low.T, grad_gate, preferred_element_type=jnp.float32)
    grad_w_up = jnp.dot(ffn_low.T, grad_up, preferred_element_type=jnp.float32)
    grad_normed_ffn = jnp.dot(grad_gate, full_gate.T, preferred_element_type=jnp.float32) + jnp.dot(
        grad_up, full_up.T, preferred_element_type=jnp.float32
    )
    grad_hidden_norm, grad_gain_ffn = rms_backward(hidden, factor_ffn, gain_two, grad_normed_ffn)
    grad_hidden = grad_out + grad_hidden_norm
    grad_branch = grad_hidden.astype(jnp.bfloat16)
    grad_w_output = jnp.dot(attn_low.T, grad_branch, preferred_element_type=jnp.float32)
    grad_attn = (
        jnp.dot(grad_branch, full_output.T, preferred_element_type=jnp.float32)
        .astype(jnp.bfloat16)
        .reshape(local_rows, HEADS, HEAD)
    )
    delta = jnp.einsum("qhe,qhe->hq", grad_attn.astype(jnp.float32), attn_f32)
    key_back, value_back = (key_all, value_all)

    def backward_block(grad_query, block):
        key_block, value_block, block_pos = block
        visible_mask = visible(query_pos, block_pos, prompt, length)

        def backward_update(grad_state):
            scores = (
                jnp.einsum(
                    "qhe,khe->hqk", query_heads, key_block, preferred_element_type=jnp.float32
                )
                * score_scale
            )
            probs = jnp.where(visible_mask[None], jnp.exp(scores - log_total[:, :, None]), 0.0)
            grad_probs = jnp.einsum(
                "qhe,khe->hqk", grad_attn, value_block, preferred_element_type=jnp.float32
            )
            grad_scores = (probs * (grad_probs - delta[:, :, None])).astype(jnp.bfloat16)
            grad_state = (
                grad_state
                + jnp.einsum(
                    "hqk,khe->qhe", grad_scores, key_block, preferred_element_type=jnp.float32
                )
                * score_scale
            )
            grad_keys = (
                jnp.einsum(
                    "hqk,qhe->khe", grad_scores, query_heads, preferred_element_type=jnp.float32
                )
                * score_scale
            )
            grad_values = jnp.einsum(
                "hqk,qhe->khe",
                probs.astype(jnp.bfloat16),
                grad_attn,
                preferred_element_type=jnp.float32,
            )
            return (grad_state, (grad_keys, grad_values))

        def skipped(grad_state):
            empty = jnp.zeros((key_rows, HEADS, HEAD), jnp.float32)
            return (grad_state, (empty, empty))

        return lax.cond(jnp.any(visible_mask), backward_update, skipped, grad_query)

    zero_query = jnp.zeros((local_rows, HEADS, HEAD), jnp.float32)
    grad_query, (grad_key_blocks, grad_value_blocks) = lax.scan(
        backward_block, zero_query, (split_blocks(key_back), split_blocks(value_back), key_pos)
    )
    grad_key_sum, grad_value_sum = (
        lax.psum_scatter(
            grad_key_blocks.reshape(group_tok, width).astype(jnp.bfloat16),
            "ctx",
            scatter_dimension=0,
            tiled=True,
        ).astype(jnp.float32),
        lax.psum_scatter(
            grad_value_blocks.reshape(group_tok, width).astype(jnp.bfloat16),
            "ctx",
            scatter_dimension=0,
            tiled=True,
        ).astype(jnp.float32),
    )
    grad_key_low = grad_key_sum.astype(jnp.bfloat16)
    grad_value_low = grad_value_sum.astype(jnp.bfloat16)
    grad_query_low = grad_query.reshape(local_rows, width).astype(jnp.bfloat16)
    grad_w_query = jnp.dot(normed_low.T, grad_query_low, preferred_element_type=jnp.float32)
    grad_w_key = jnp.dot(normed_low.T, grad_key_low, preferred_element_type=jnp.float32)
    grad_w_value = jnp.dot(normed_low.T, grad_value_low, preferred_element_type=jnp.float32)
    grad_normed = (
        jnp.dot(grad_query_low, full_query.T, preferred_element_type=jnp.float32)
        + jnp.dot(grad_key_low, full_key.T, preferred_element_type=jnp.float32)
        + jnp.dot(grad_value_low, full_value.T, preferred_element_type=jnp.float32)
    )
    grad_rows_norm, grad_gain_attn = rms_backward(rows_f32, factor_attn, gain_one, grad_normed)
    grad_rows = grad_hidden + grad_rows_norm
    shards = (
        lax.psum_scatter(
            grad_w_query.astype(jnp.bfloat16), "fsdp", scatter_dimension=0, tiled=True
        ).astype(jnp.float32),
        lax.psum_scatter(
            grad_w_key.astype(jnp.bfloat16), "fsdp", scatter_dimension=0, tiled=True
        ).astype(jnp.float32),
        lax.psum_scatter(
            grad_w_value.astype(jnp.bfloat16), "fsdp", scatter_dimension=0, tiled=True
        ).astype(jnp.float32),
        lax.psum_scatter(
            grad_w_output.astype(jnp.bfloat16), "fsdp", scatter_dimension=0, tiled=True
        ).astype(jnp.float32),
        lax.psum_scatter(
            grad_w_gate.astype(jnp.bfloat16), "fsdp", scatter_dimension=0, tiled=True
        ).astype(jnp.float32),
        lax.psum_scatter(
            grad_w_up.astype(jnp.bfloat16), "fsdp", scatter_dimension=0, tiled=True
        ).astype(jnp.float32),
        lax.psum_scatter(
            grad_w_down.astype(jnp.bfloat16), "fsdp", scatter_dimension=0, tiled=True
        ).astype(jnp.float32),
        lax.psum_scatter(
            grad_gain_attn.astype(jnp.bfloat16), "fsdp", scatter_dimension=0, tiled=True
        ).astype(jnp.float32),
        lax.psum_scatter(
            grad_gain_ffn.astype(jnp.bfloat16), "fsdp", scatter_dimension=0, tiled=True
        ).astype(jnp.float32),
    )
    summed = (
        lax.psum(shards[0].astype(jnp.bfloat16), "ctx").astype(jnp.float32),
        lax.psum(shards[1].astype(jnp.bfloat16), "ctx").astype(jnp.float32),
        lax.psum(shards[2].astype(jnp.bfloat16), "ctx").astype(jnp.float32),
        lax.psum(shards[3].astype(jnp.bfloat16), "ctx").astype(jnp.float32),
        lax.psum(shards[4].astype(jnp.bfloat16), "ctx").astype(jnp.float32),
        lax.psum(shards[5].astype(jnp.bfloat16), "ctx").astype(jnp.float32),
        lax.psum(shards[6].astype(jnp.bfloat16), "ctx").astype(jnp.float32),
        lax.psum(shards[7].astype(jnp.bfloat16), "ctx").astype(jnp.float32),
        lax.psum(shards[8].astype(jnp.bfloat16), "ctx").astype(jnp.float32),
    )
    return (
        layer.astype(jnp.bfloat16)[None],
        grad_rows[None],
        summed[0],
        summed[1],
        summed[2],
        summed[3],
        summed[4],
        summed[5],
        summed[6],
        summed[7],
        summed[8],
    )


TILE = 256


def dot_f32(left, right, left_dim, right_dim):
    return lax.dot_general(
        left,
        right,
        (((left_dim,), (right_dim,)), ((), ())),
        preferred_element_type=jnp.float32,
    )


def head_masks():
    lane = lax.broadcasted_iota(jnp.int32, (TILE, 2 * HEAD), 1)
    first = (lane < HEAD).astype(jnp.bfloat16)
    return first, (1 - first).astype(jnp.bfloat16)


def stack_heads(tile, masks):
    return jnp.concatenate([tile * masks[0], tile * masks[1]], axis=0)


def tile_mask(kind, tile, length):
    row = lax.broadcasted_iota(jnp.int32, (TILE, 2 * TILE), 0)
    if kind == "diagonal":
        column = lax.broadcasted_iota(jnp.int32, (TILE, 2 * TILE), 1)
        return row <= jnp.where(column < TILE, column, column - TILE)
    return row + tile * TILE < length


def over_keys(tile, per_segment, step, state):
    base = tile // per_segment * per_segment
    state = lax.fori_loop(0, base, lambda key, kept: step(key, kept, "prompt"), state)
    state = lax.fori_loop(base, tile, lambda key, kept: step(key, kept, "full"), state)
    return step(tile, state, "diagonal")


def load_tile(ref, tile):
    held = TILE // ref.shape[1]
    return ref[pl.ds(tile * held, held)].reshape(TILE, ref.shape[2])


def store_tile(ref, tile, values):
    held = TILE // ref.shape[1]
    ref[pl.ds(tile * held, held)] = values.reshape(held, ref.shape[1], ref.shape[2])


def to_logical(slot_of, source, column, target, scale=None):
    for block in range(target.shape[0]):
        picked = source[slot_of[block], :, column : column + 2 * HEAD]
        if scale is not None:
            picked = picked * scale
        target[block] = picked


def to_stored(block_of, source, target, column):
    block_len = source.shape[1]
    for slot in range(source.shape[0]):
        target[slot * block_len : (slot + 1) * block_len, column : column + 2 * HEAD] = source[
            block_of[slot]
        ]


def tiles_between(count, one_tile, between):
    first = 0
    for stop in sorted(between):
        lax.fori_loop(first, stop, one_tile, 0)
        between[stop]()
        first = stop
    lax.fori_loop(first, count, one_tile, 0)


def attend_forward(
    per_segment,
    slot_of,
    length_ref,
    qkv,
    attn_t,
    lse,
    query,
    key,
    value_t,
    kept,
    between,
):
    rows = qkv.shape[0] * qkv.shape[1]
    length = length_ref[0]
    to_logical(slot_of, qkv, 0, query, jnp.bfloat16(score_scale))
    to_logical(slot_of, qkv, 2 * HEAD, key)
    to_logical(slot_of, qkv, 4 * HEAD, kept)
    for tile in range(rows // TILE):
        value_t[tile] = load_tile(kept, tile).T
    masks = head_masks()

    def one_tile(tile, unused):
        both = stack_heads(load_tile(query, tile), masks)

        def step(key_tile, state, kind):
            maxima, totals, accum = state
            scores = dot_f32(load_tile(key, key_tile), both, 1, 1)
            if kind != "full":
                scores = jnp.where(tile_mask(kind, key_tile, length), scores, masked_value)
            new_max = jnp.maximum(maxima, jnp.max(scores, axis=0, keepdims=True))
            probs = jnp.exp(scores - new_max)
            rescale = jnp.exp(maxima - new_max)
            totals = totals * rescale + jnp.sum(probs, axis=0, keepdims=True)
            accum = accum * rescale + dot_f32(
                value_t[key_tile], probs.astype(jnp.bfloat16), 1, 0
            )
            return new_max, totals, accum

        maxima, totals, accum = over_keys(
            tile,
            per_segment,
            step,
            (
                jnp.full((1, 2 * TILE), masked_value, jnp.float32),
                jnp.zeros((1, 2 * TILE), jnp.float32),
                jnp.zeros((2 * HEAD, 2 * TILE), jnp.float32),
            ),
        )
        accum = accum / totals
        feature = lax.broadcasted_iota(jnp.int32, (2 * HEAD, TILE), 0)
        picked = jnp.where(feature < HEAD, accum[:, :TILE], accum[:, TILE:])
        attn_t[tile] = picked
        lse[tile] = maxima + jnp.log(totals)
        store_tile(kept, tile, picked.T.astype(jnp.bfloat16))
        return unused

    tiles_between(rows // TILE, one_tile, between)


def attend_backward(
    per_segment,
    slot_of,
    block_of,
    length_ref,
    qkv,
    grad_attn,
    attn_t,
    lse,
    grad_qkv,
    query,
    key,
    value,
    grad,
    key_t,
    grad_sums,
    between,
):
    rows = qkv.shape[0] * qkv.shape[1]
    length = length_ref[0]
    to_logical(slot_of, qkv, 0, query, jnp.bfloat16(score_scale))
    to_logical(slot_of, qkv, 2 * HEAD, key)
    to_logical(slot_of, qkv, 4 * HEAD, value)
    to_logical(slot_of, grad_attn, 0, grad)
    for tile in range(rows // TILE):
        key_t[tile] = load_tile(key, tile).T
    grad_sums[...] = jnp.zeros_like(grad_sums)
    masks = head_masks()

    def one_tile(tile, unused):
        both = stack_heads(load_tile(query, tile), masks)
        grad_tile = load_tile(grad, tile)
        both_grad = stack_heads(grad_tile, masks)
        product = grad_tile.astype(jnp.float32).T * attn_t[tile]
        delta = jnp.concatenate(
            [
                jnp.sum(product[:HEAD], axis=0, keepdims=True),
                jnp.sum(product[HEAD:], axis=0, keepdims=True),
            ],
            axis=1,
        )
        log_total = lse[tile]

        def step(key_tile, grad_query, kind):
            keys_at = pl.ds(pl.multiple_of(key_tile * 2 * HEAD, 2 * HEAD), 2 * HEAD)
            scores = dot_f32(load_tile(key, key_tile), both, 1, 1)
            if kind != "full":
                scores = jnp.where(tile_mask(kind, key_tile, length), scores, masked_value)
            probs = jnp.exp(scores - log_total)
            grad_probs = dot_f32(load_tile(value, key_tile), both_grad, 1, 1)
            grad_scores = (probs * (grad_probs - delta)).astype(jnp.bfloat16)
            grad_sums[1, :, keys_at] += dot_f32(probs.astype(jnp.bfloat16), both_grad, 1, 0)
            grad_sums[0, :, keys_at] += dot_f32(grad_scores, both, 1, 0)
            return grad_query + dot_f32(key_t[key_tile], grad_scores, 1, 0)

        grad_query = over_keys(
            tile, per_segment, step, jnp.zeros((2 * HEAD, 2 * TILE), jnp.float32)
        )
        feature = lax.broadcasted_iota(jnp.int32, (2 * HEAD, TILE), 0)
        picked = jnp.where(feature < HEAD, grad_query[:, :TILE], grad_query[:, TILE:])
        store_tile(query, tile, (picked * score_scale).T.astype(jnp.bfloat16))
        return unused

    tiles_between(rows // TILE, one_tile, between)
    for tile in range(rows // TILE):
        at = slice(tile * 2 * HEAD, (tile + 1) * 2 * HEAD)
        store_tile(key, tile, grad_sums[0, :, at].astype(jnp.bfloat16))
        store_tile(value, tile, grad_sums[1, :, at].astype(jnp.bfloat16))
    to_stored(block_of, query, grad_qkv, 0)
    to_stored(block_of, key, grad_qkv, 2 * HEAD)
    to_stored(block_of, value, grad_qkv, 4 * HEAD)


def dma(count):
    return pltpu.SemaphoreType.DMA((count,))


def flipped(bit, flip):
    return bit + flip - 2 * bit * flip


class Place:
    def __init__(self, devices_fsdp):
        self.me = lax.axis_index("ctx")
        self.core = lax.rem(self.me, 2)
        self.column = lax.rem(self.me // 2, 2)
        self.row = self.me // 4
        self.group = lax.axis_index("fsdp")
        self.groups = devices_fsdp

    def peer(self, flip):
        low, middle, high = flip % 2, flip // 2 % 2, flip // 4
        return (
            flipped(self.row, high) * 4
            + flipped(self.column, middle) * 2
            + flipped(self.core, low)
        )

    def other_group(self, step):
        return lax.rem(self.group + step, self.groups)

    def at_end(self):
        return lax.rem(self.group, 3) == 0

    def between(self):
        return lax.rem(self.group, 3) != 0

    def near(self, step):
        return self.group != {1: 3, 2: 4, 3: 0}[step]

    def heard(self, step):
        return self.group != {1: 0, 2: 4, 3: 3}[step]

    def meet(self):
        barrier = pltpu.get_barrier_semaphore()
        for flip in range(1, 8):
            pl.semaphore_signal(barrier, inc=1, device_id={"ctx": self.peer(flip)})
        for step in range(1, self.groups):
            pl.semaphore_signal(barrier, inc=1, device_id={"fsdp": self.other_group(step)})
        pl.semaphore_wait(barrier, 7 + self.groups - 1)


def remote(source, target, send, recv, device):
    return pltpu.make_async_remote_copy(
        src_ref=source,
        dst_ref=target,
        send_sem=send,
        recv_sem=recv,
        device_id=device,
        device_id_type=pl.DeviceIdType.MESH,
    )


class Spread:
    def __init__(self, place, own, region, send, recv):
        me, peer = place.me, place.peer

        def copy(index, source, target, flip):
            return remote(source, target, send.at[index], recv.at[index], {"ctx": peer(flip)})

        self.copies = [
            copy(0, own(None), region(me, None), 1),
            copy(1, own(0), region(me, 0), 2),
            copy(2, own(1), region(me, 1), 2),
            copy(3, own(1), region(me, 1), 4),
            copy(4, own(0), region(me, 0), 4),
            copy(5, region(peer(2), 0), region(peer(2), 0), 4),
            copy(6, region(peer(4), 1), region(peer(4), 1), 2),
            copy(7, region(peer(2), None), region(peer(2), None), 1),
            copy(8, region(peer(4), None), region(peer(4), None), 1),
            copy(9, region(peer(6), None), region(peer(6), None), 1),
        ]

    def start(self):
        for index in (1, 3, 0, 2, 4):
            self.copies[index].start()

    def arrived(self, *indices):
        for index in indices:
            self.copies[index].wait_recv()

    def relay_first(self):
        self.arrived(1)
        self.copies[5].start()
        self.arrived(3)
        self.copies[6].start()

    def relay_second(self):
        self.arrived(2)
        self.copies[7].start()
        self.arrived(4)
        self.copies[8].start()

    def relay_third(self):
        self.arrived(5, 6)
        self.copies[9].start()

    def sent(self):
        for copy in self.copies:
            copy.wait_send()


class PairSum:
    def __init__(self, place, stage, landed, sums, received, send, recv, out_send, out_recv):
        self.place = place
        self.slot = lambda pair: pair
        self.stage, self.landed, self.sums, self.received = stage, landed, sums, received
        self.send, self.recv, self.out_send, self.out_recv = send, recv, out_send, out_recv

    def mine(self, pair):
        place = self.place
        return (
            flipped(place.row, pair // 2) * 4
            + flipped(place.column, lax.rem(pair, 2)) * 2
            + place.core
        )

    def theirs(self, pair):
        return self.mine(pair) + 1 - 2 * self.place.core

    def staged(self, pair):
        return self.stage.at[self.slot(pair)]

    def exchange(self, pair):
        return remote(
            self.staged(pair),
            self.landed.at[self.slot(pair)],
            self.send.at[pair],
            self.recv.at[pair],
            {"ctx": self.place.peer(1)},
        )

    def deliver(self, pair):
        return remote(
            self.sums.at[pair],
            self.received.at[pair],
            self.out_send.at[pair],
            self.out_recv.at[pair],
            {"ctx": self.mine(pair)},
        )

    def sent(self):
        for pair in range(4):
            self.exchange(pair).wait_send()
            if pair:
                self.deliver(pair).wait_send()


class OutputSum(PairSum):
    def staged(self, pair):
        return self.stage.at[:, self.theirs(pair)]


class CrossSum(PairSum):
    def __init__(
        self, place, slot, stage, landed, sums, received, passed, send, recv, out_send, out_recv
    ):
        super().__init__(place, stage, landed, sums, received, send, recv, out_send, out_recv)
        self.slot = slot
        self.passed = passed

    def half(self, which):
        count = self.sums.shape[1] // 2
        return slice(which * count, (which + 1) * count)

    def far(self, which):
        slot = 3 * which
        return remote(
            self.sums.at[3, self.half(which)],
            self.passed.at[which],
            self.out_send.at[slot],
            self.out_recv.at[slot],
            {"ctx": self.place.peer(2 + 2 * which)},
        )

    def deliver(self, pair):
        return remote(
            self.sums.at[pair],
            self.received.at[pair - 1],
            self.out_send.at[pair],
            self.out_recv.at[pair],
            {"ctx": self.place.peer(2 * pair)},
        )

    def finish(self, pair, total):
        self.sums[pair] = total.astype(jnp.bfloat16)

        @pl.when(pair == 3)
        def _():
            self.far(0).start()
            self.far(1).start()

        for axis in (1, 2):
            which = 2 - axis

            @pl.when(pair == axis)
            def _(axis=axis, which=which):
                at = self.half(which)
                self.far(which).wait_recv()
                self.sums[axis, at, :] = (
                    total[at] + self.passed[which].astype(jnp.float32)
                ).astype(jnp.bfloat16)
                self.deliver(axis).start()

    def collect(self):
        total = self.sums[0].astype(jnp.float32)
        for pair in (1, 2):
            self.deliver(pair).wait_recv()
            total = total + self.received[pair - 1].astype(jnp.float32)
        return total

    def sent(self):
        for which in (0, 1):
            self.far(which).wait_send()
            self.deliver(which + 1).wait_send()


def halves(count):
    return lambda half: pl.ds(0 if half in (None, 0) else count // 2, count if half is None else count // 2)


def layer_kernel(
    per_segment,
    devices_fsdp,
    slot_of,
    block_of,
    length_ref,
    patches,
    cotangent,
    w_query,
    w_key,
    w_value,
    w_output,
    w_gate,
    w_up,
    w_down,
    gain_attn,
    gain_ffn,
    normed_out,
    layer,
    grad_patches,
    units_out,
    columns_out,
    gains_out,
    qkv,
    attn_t,
    lse,
    grad_units,
    grad_output,
    layer_sums,
    hidden,
    grad_hidden,
    rows_all,
    grads,
    normed_ffn,
    attn_all,
    w_qkv,
    output_all,
    gate_t,
    up_t,
    down,
    down_parts,
    gate_stage,
    up_stage,
    gain_stage,
    gains,
    query,
    key,
    value_t,
    kept,
    grad,
    attn_rows,
    units_t,
    stage,
    landed,
    own_sum,
    norm_sums,
    norm_received,
    norm_passed,
    grad_branch,
    grad_rows,
    grad_attn,
    units_landed,
    units_far,
    units_near,
    units_stage,
    output_landed,
    output_sums,
    output_received,
    output_total,
    output_group,
    qkv_landed,
    columns_stage,
    gain_parts,
    gain_landed,
    gain_total,
    gain_all,
    local_sem,
    save_sem,
    unit_sem,
    group_send,
    group_recv,
    pass_send,
    x_send,
    x_recv,
    g_send,
    g_recv,
    o_send,
    o_recv,
    first_send,
    first_recv,
    second_send,
    second_recv,
    third_send,
    third_recv,
    u_send,
    u_recv,
    c_send,
    c_recv,
    b_send,
    b_recv,
    gain_out_send,
    gain_out_recv,
    pair_send,
    pair_recv,
    out_send,
    out_recv,
    back_pair_send,
    back_pair_recv,
    back_out_send,
    back_out_recv,
    wo_send,
    wo_recv,
    wo_out_send,
    wo_out_recv,
    layer_send,
    layer_recv,
    units_send,
    units_recv,
    gain_send,
    gain_recv,
    far_sem,
    late_send,
    late_recv,
):
    place = Place(devices_fsdp)
    me, group = place.me, place.group
    local_rows, width = patches.shape
    cols = width // 8
    shard = w_query.shape[0]
    part = w_down.shape[1]
    units = part * devices_fsdp
    span = part * 8
    held = qkv.shape[0] // 8

    def unit_range(index):
        return span * index // 128 * 128, -(-span * (index + 1) // 128) * 128

    def unit_copies(weight, target, first):
        copies = []
        for index in range(devices_fsdp):
            low, high = unit_range(index)
            copies.append(
                pltpu.make_async_copy(
                    weight.at[:, low:high],
                    target.at[index // 2, index % 2, :, 0 : high - low],
                    unit_sem.at[first + index],
                )
            )
        return copies

    gate_copies = unit_copies(w_gate, stage, 0)
    up_copies = unit_copies(w_up, landed, devices_fsdp)
    for copy in gate_copies + up_copies:
        copy.start()
    place.meet()

    def rows_of(block, count=local_rows):
        return pl.ds(pl.multiple_of(block * count, count), count)

    def rows_half(ref):
        def region(block, half):
            start = block * local_rows + (local_rows // 2 if half == 1 else 0)
            count = local_rows if half is None else local_rows // 2
            return ref.at[pl.ds(pl.multiple_of(start, local_rows // 2), count)]

        return region

    def own_half(ref):
        return lambda half: ref.at[halves(local_rows)(half)]

    spread_x = Spread(place, own_half(patches), rows_half(rows_all), x_send, x_recv)
    spread_x.start()

    my_cols = rows_of(me, cols)
    def shard_of(index):
        return rows_of(index, shard)

    group_items = [
        (w_query.at[:, my_cols], lambda to: w_qkv.at[shard_of(to), 0:cols]),
        (w_key.at[:, my_cols], lambda to: w_qkv.at[shard_of(to), cols : 2 * cols]),
        (w_value.at[:, my_cols], lambda to: w_qkv.at[shard_of(to), 2 * cols : 3 * cols]),
        (gain_stage, lambda to: gains.at[:, shard_of(to)]),
        (w_output.at[me], lambda to: output_all.at[to, me]),
        (gate_stage, lambda to: gate_t.at[:, shard_of(to)]),
        (up_stage, lambda to: up_t.at[:, shard_of(to)]),
        (w_down.at[me], lambda to: down_parts.at[to]),
    ]

    def group_copy(index, step):
        source, target = group_items[index]
        return remote(
            source,
            target(group),
            group_send.at[index, step - 1],
            group_recv.at[index, step - 1],
            {"fsdp": place.other_group(step)},
        )

    def passed_copy(index):
        whose = place.other_group(2)
        held = group_items[index][1](whose)
        return remote(
            held,
            held,
            pass_send.at[index],
            group_recv.at[index, 2 * (group // 2)],
            {"fsdp": devices_fsdp - 1 - whose},
        )

    def local_copy(index):
        source, target = group_items[index]
        return pltpu.make_async_copy(source, target(group), local_sem.at[index])

    def send_group(index):
        group_copy(index, 2).start()
        for step in (1, 3):
            pl.when(place.near(step))(group_copy(index, step).start)
        local_copy(index).start()

    def pass_group(index):
        @pl.when(place.between())
        def _():
            group_copy(index, 2).wait_recv()
            passed_copy(index).start()

    def group_arrived(index):
        pl.when(place.at_end())(group_copy(index, 2).wait_recv)
        for step in (1, 3):
            group_copy(index, step).wait_recv()
        local_copy(index).wait()

    def group_sent(index):
        group_copy(index, 2).wait_send()
        for step in (1, 3):
            pl.when(place.near(step))(group_copy(index, step).wait_send)
        pl.when(place.between())(passed_copy(index).wait_send)

    for index in (0, 1, 2):
        send_group(index)
    gain_stage[0:8, :] = jnp.broadcast_to(gain_attn[...].astype(jnp.float32), (8, shard))
    gain_stage[8:16, :] = jnp.broadcast_to(gain_ffn[...].astype(jnp.float32), (8, shard))
    send_group(3)
    send_group(4)

    def pick_units(copies, source, target):
        pieces = []
        for index in range(devices_fsdp):
            low, high = unit_range(index)
            unit = lax.broadcasted_iota(jnp.int32, (part, high - low), 0)
            column = lax.broadcasted_iota(jnp.int32, (part, high - low), 1)
            chosen = (column + low == unit + span * index + part * me).astype(jnp.bfloat16)
            copies[index].wait()
            pieces.append(
                dot_f32(chosen, source[index // 2, index % 2, :, 0 : high - low], 1, 1)
            )
        target[...] = jnp.concatenate(pieces, axis=0).astype(jnp.bfloat16)

    pick_units(gate_copies, stage, gate_stage)
    pick_units(up_copies, landed, up_stage)
    send_group(5)
    send_group(6)
    send_group(7)

    rows_all[rows_of(me), :] = patches[...]
    load_grads = pltpu.make_async_copy(cotangent, grads.at[rows_of(me)], save_sem.at[0])
    load_grads.start()
    spread_x.relay_first()
    for index in (0, 1, 2, 3):
        pass_group(index)
    spread_x.relay_second()
    spread_g = Spread(place, own_half(cotangent), rows_half(grads), g_send, g_recv)
    spread_g.start()
    spread_x.relay_third()
    pass_group(4)
    spread_x.arrived(0, 7, 8, 9)
    for index in (0, 1, 2, 3):
        group_arrived(index)
    gain_one = gains[0:1, :]

    def output_half(block, half):
        if half is None:
            return output_all.at[:, block]
        lines = output_all.shape[2]
        return output_all.at[:, block, halves(lines)(half)]

    group_arrived(4)
    spread_o = Spread(place, lambda half: output_half(me, half), output_half, o_send, o_recv)
    spread_o.start()

    def project(block, unused):
        at = rows_of(block)
        values = rows_all[at, :].astype(jnp.float32)
        low = rms_forward(values, gain_one)[0].astype(jnp.bfloat16)
        normed_ffn[at, :] = low
        store_tile(qkv, block, dot_f32(low, w_qkv[...], 1, 0).astype(jnp.bfloat16))
        return unused

    spread_x.sent()
    lax.fori_loop(0, 8, project, 0)
    save_normed = pltpu.make_async_copy(normed_ffn, normed_out, local_sem.at[8])
    save_normed.start()
    spread_g.relay_first()

    def attn_spread(first, count, send, recv):
        def part(half):
            return slice(
                first + (count // 2 if half == 1 else 0),
                first + (count // 2 if half == 0 else count),
            )

        return Spread(
            place,
            lambda half: kept.at[part(half)],
            lambda block, half: attn_all.at[part(half), :, rows_of(block, cols)],
            send,
            recv,
        )

    half_blocks = kept.shape[0] // 2
    attn_first = attn_spread(0, half_blocks, first_send, first_recv)
    attn_second = attn_spread(half_blocks, half_blocks // 2, second_send, second_recv)
    attn_third = attn_spread(half_blocks * 3 // 2, half_blocks // 2, third_send, third_recv)

    def after_two():
        pass_group(5)

    def after_more():
        spread_g.relay_second()
        pass_group(6)

    def after_half():
        attn_second.start()
        spread_o.relay_first()

    def after_most():
        pass_group(7)
        spread_o.relay_second()

    attend_forward(
        per_segment,
        slot_of,
        length_ref,
        qkv,
        attn_t,
        lse,
        query,
        key,
        value_t,
        kept,
        {
            per_segment // 2: after_two,
            per_segment: attn_first.start,
            per_segment + 1: after_more,
            per_segment + per_segment // 2: after_half,
            2 * per_segment - 1: after_most,
        },
    )
    attn_third.start()
    attn_all[:, :, my_cols] = kept[...]
    spread_g.relay_third()
    attn_first.relay_first()
    attn_first.relay_second()
    spread_o.relay_third()
    for index in (5, 6, 7):
        group_arrived(index)
    down[...] = jnp.concatenate(
        [down_parts[index].astype(jnp.float32) for index in range(devices_fsdp)], axis=0
    ).astype(jnp.bfloat16)
    attn_second.relay_first()
    attn_second.relay_second()
    attn_first.relay_third()
    attn_third.relay_first()
    attn_third.relay_second()
    attn_second.relay_third()
    save_normed.wait()
    load_grads.wait()
    spread_g.arrived(0, 7, 8, 9)
    spread_o.arrived(0, 7, 8, 9)
    attn_third.relay_third()
    for spread in (attn_first, attn_second, attn_third):
        spread.arrived(0, 7, 8, 9)

    def swap(source, target, send, recv):
        return [
            remote(source(flip), target, send.at[flip - 1], recv.at[flip - 1], {"ctx": place.peer(flip)})
            for flip in range(1, 8)
        ]

    def attn_of(block):
        return jnp.concatenate(
            [attn_all[block_of[block * held + index]] for index in range(held)], axis=0
        )

    gain_two = gains[8:9, :]
    sums = CrossSum(
        place,
        lambda pair: lax.rem(pair, 2),
        stage,
        landed,
        norm_sums,
        norm_received,
        norm_passed,
        pair_send,
        pair_recv,
        out_send,
        out_recv,
    )

    def hidden_of(block, attn):
        return rows_all[rows_of(block), :].astype(jnp.float32) + dot_f32(
            attn, output_all[...].reshape(width, width), 1, 0
        )

    def feed(block):
        at = rows_of(block)
        low = rms_forward(hidden_of(block, attn_of(block)), gain_two)[0].astype(jnp.bfloat16)
        normed_ffn[at, :] = low
        grad_out = grads[at, :]
        gate = dot_f32(low, gate_t[...], 1, 1)
        up_proj = dot_f32(low, up_t[...], 1, 1)
        grad_inner = dot_f32(grad_out, down[...], 1, 1)
        sigmoid = jax.nn.sigmoid(gate)
        activated = gate * sigmoid
        inner = activated * up_proj
        inner_low = inner.astype(jnp.bfloat16)
        grad_gate = grad_inner * up_proj * sigmoid * (1.0 + gate * (1.0 - sigmoid))
        grad_up = grad_inner * activated
        gate_low = grad_gate.astype(jnp.bfloat16)
        up_low = grad_up.astype(jnp.bfloat16)
        units_t[0:units, at] = inner.T.astype(jnp.bfloat16)
        units_t[units : 2 * units, at] = grad_gate.T.astype(jnp.bfloat16)
        units_t[2 * units : 3 * units, at] = grad_up.T.astype(jnp.bfloat16)
        return (
            dot_f32(inner_low, down[...], 1, 0),
            dot_f32(gate_low, gate_t[...], 1, 0) + dot_f32(up_low, up_t[...], 1, 0),
        )

    def one_pair(step, unused):
        pair = 3 - step
        slot = lax.rem(pair, 2)
        layer, norm = feed(sums.theirs(pair))

        @pl.when(step > 1)
        def _():
            sums.exchange(pair + 2).wait_send()

        stage[slot, 0] = layer.astype(jnp.bfloat16)
        stage[slot, 1] = norm.astype(jnp.bfloat16)
        sums.exchange(pair).start()
        layer, norm = feed(sums.mine(pair))
        own_sum[0] = layer
        own_sum[1] = norm
        sums.exchange(pair).wait_recv()
        layer_sums[pair] = (
            (own_sum[0] + landed[slot, 0].astype(jnp.float32))
            .astype(jnp.bfloat16)
            .reshape(layer_sums.shape[1:])
        )
        sums.finish(pair, own_sum[1] + landed[slot, 1].astype(jnp.float32))
        return unused

    lax.fori_loop(0, 4, one_pair, 0)
    for pair in (1, 0):
        sums.exchange(pair).wait_send()
    attn_rows[...] = attn_of(me)
    hidden[...] = hidden_of(me, attn_rows[...])
    load_normed = pltpu.make_async_copy(normed_out, rows_all, local_sem.at[8])
    load_normed.start()

    def down_part(tile, unused):
        at = rows_of(tile, shard)
        down_tile = dot_f32(units_t[0:units, :], grads[:, at], 1, 0)
        for half in (0, 1):
            own_sum[half, 0 : units // 2, at] = down_tile[half * units // 2 : (half + 1) * units // 2]
        return unused

    lax.fori_loop(0, devices_fsdp, down_part, 0)
    for index in range(devices_fsdp):
        first = index % 2 * part
        grad_units[index, 2 * units : 3 * units, :] = jnp.concatenate(
            [
                own_sum[index // 2, first : first + part, tile * shard : (tile + 1) * shard]
                for tile in range(devices_fsdp)
            ],
            axis=0,
        ).astype(jnp.bfloat16)

    def units_copy(step, source):
        return remote(
            source,
            units_landed.at[group],
            units_send.at[step - 1],
            units_recv.at[step - 1],
            {"fsdp": place.other_group(step)},
        )

    def units_direct(step):
        return units_copy(step, grad_units.at[place.other_group(step)])

    units_far_copy = remote(
        grad_units.at[devices_fsdp - 1 - group],
        units_far,
        far_sem.at[0],
        far_sem.at[1],
        {"fsdp": 1 + group // 3},
    )
    units_sum_copy = units_copy(2, units_near)

    def units_tile(turn, unused):
        step = jnp.where(turn < 2, 3 - 2 * turn, 6 - 2 * turn)
        tile = place.other_group(step)
        grad_units[tile, 0 : 2 * units, :] = dot_f32(
            units_t[units : 3 * units, :], normed_ffn[:, rows_of(tile, shard)], 1, 0
        ).astype(jnp.bfloat16)

        for at, step in ((0, 3), (1, 1)):
            pl.when((turn == at) & place.near(step))(units_direct(step).start)
            pl.when((turn == at) & (group == 3 - step // 2 * 3))(units_far_copy.start)
        pl.when((turn == 2) & place.at_end())(units_direct(2).start)
        return unused

    lax.fori_loop(0, devices_fsdp, units_tile, 0)

    total = sums.collect()
    values = hidden[...]
    factor = lax.rsqrt(jnp.mean(values * values, axis=-1, keepdims=True) + epsilon)
    scaled = total * gain_two
    gain_part = jnp.sum(total * values * factor, axis=0, keepdims=True)
    whole = (
        grads[rows_of(me), :].astype(jnp.float32)
        + factor * scaled
        - values * (factor * factor * factor) * jnp.mean(scaled * values, axis=-1, keepdims=True)
    )
    grad_hidden[...] = whole
    grad_branch[...] = whole.astype(jnp.bfloat16)
    grad_rows[...] = (
        dot_f32(grad_branch[...], output_all[...].reshape(width, width), 1, 1)
        .astype(jnp.bfloat16)
        .reshape(grad_rows.shape)
    )
    to_heads = swap(
        lambda flip: grad_rows.at[:, :, rows_of(place.peer(flip), cols)],
        grad_attn.at[pl.ds(me * held, held)],
        b_send,
        b_recv,
    )
    for spread in (spread_g, spread_o, attn_first, attn_second, attn_third):
        spread.sent()
    sums.sent()
    for copy in to_heads:
        copy.start()
    grad_attn[pl.ds(me * held, held)] = grad_rows[:, :, my_cols]

    for index in range(devices_fsdp):
        piece = attn_rows[:, index * shard : (index + 1) * shard].T
        grad_output[index] = (
            dot_f32(piece, grad_branch[...], 1, 0)
            .astype(jnp.bfloat16)
            .reshape(8, shard // 8, width)
        )
    for copy in to_heads:
        copy.wait_recv()
    for index in range(8):
        group_sent(index)
    for copy in to_heads:
        copy.wait_send()

    def over_groups(source, target, send, recv):
        return [
            remote(
                source(place.other_group(step)),
                target.at[group],
                send.at[step - 1],
                recv.at[step - 1],
                {"fsdp": place.other_group(step)},
            )
            for step in range(1, devices_fsdp)
        ]

    def units_between():
        @pl.when(place.between())
        def _():
            units_far_copy.wait_recv()
            units_near[...] = (
                grad_units[place.other_group(2)].astype(jnp.float32)
                + units_far[...].astype(jnp.float32)
            ).astype(jnp.bfloat16)
            units_sum_copy.start()

    sums = CrossSum(
        place,
        lambda pair: (pair // 2, lax.rem(pair, 2)),
        stage,
        landed,
        norm_sums,
        norm_received,
        norm_passed,
        back_pair_send,
        back_pair_recv,
        back_out_send,
        back_out_recv,
    )
    output_pairs = OutputSum(
        place,
        grad_output,
        output_landed,
        output_sums,
        output_received,
        wo_send,
        wo_recv,
        wo_out_send,
        wo_out_recv,
    )
    for pair in range(4):
        output_pairs.exchange(pair).start()
    layer_copies = [
        remote(
            layer_sums.at[pair],
            attn_all.at[pair * held : (pair + 1) * held],
            layer_send.at[pair],
            layer_recv.at[pair],
            {"ctx": sums.mine(pair)},
        )
        for pair in range(1, 4)
    ]
    for copy in layer_copies:
        copy.start()

    def after_prompt():
        for pair in range(4):
            output_pairs.exchange(pair).wait_recv()
            output_sums[pair] = (
                grad_output[:, output_pairs.mine(pair)].astype(jnp.float32)
                + output_landed[pair].astype(jnp.float32)
            ).astype(jnp.bfloat16)
            if pair:
                output_pairs.deliver(pair).start()

    def half_of(ref, lines):
        def region(block, half):
            return ref.at[block] if half is None else ref.at[block, halves(lines)(half)]

        return region

    def own_of(ref, lines):
        return lambda half: ref if half is None else ref.at[halves(lines)(half)]

    spread_u = Spread(
        place,
        own_of(units_stage, 3 * units),
        half_of(units_out, 3 * units),
        u_send,
        u_recv,
    )
    save_units = pltpu.make_async_copy(units_stage, units_out.at[me], save_sem.at[0])
    output_copies = over_groups(
        lambda to: output_total.at[to], output_group, late_send.at[1], late_recv.at[1]
    )

    def before_last():
        total = output_sums[0].astype(jnp.float32)
        for pair in range(1, 4):
            output_pairs.deliver(pair).wait_recv()
            total = total + output_received[pair].astype(jnp.float32)
        output_total[...] = total.astype(jnp.bfloat16)
        for copy in output_copies:
            copy.start()
        units_landed[group] = grad_units[group]

        @pl.when(place.at_end())
        def _():
            units_landed[devices_fsdp - 1 - group] = jnp.zeros_like(grad_units[group])

        units_direct(2).wait_recv()
        for step in (1, 3):
            pl.when(place.heard(step))(units_direct(step).wait_recv)
        units_total = units_landed[0].astype(jnp.float32)
        for index in range(1, devices_fsdp):
            units_total = units_total + units_landed[index].astype(jnp.float32)
        units_stage[...] = units_total.astype(jnp.bfloat16)

        spread_u.start()
        save_units.start()

    attend_backward(
        per_segment,
        slot_of,
        block_of,
        length_ref,
        qkv,
        grad_attn,
        attn_t,
        lse,
        grads,
        query,
        key,
        kept,
        grad,
        value_t,
        own_sum,
        {
            per_segment // 2: units_between,
            per_segment: after_prompt,
            2 * per_segment - 1: before_last,
        },
    )

    def turn(tile, unused):
        at = rows_of(tile, TILE)
        units_t[0 : 3 * cols, at] = grads[at, 0 : 3 * cols].T
        return unused

    lax.fori_loop(0, grads.shape[0] // TILE, turn, 0)
    load_normed.wait()

    def weight_tile(tile, unused):
        at = rows_of(tile, shard)
        normed_ffn[0 : 3 * cols, at] = dot_f32(
            units_t[0 : 3 * cols, :], rows_all[:, at], 1, 0
        ).astype(jnp.bfloat16)
        return unused

    def qkv_parts(to):
        return normed_ffn.at[0 : 3 * cols, rows_of(to, shard)]

    lax.fori_loop(0, devices_fsdp, weight_tile, 0)
    qkv_copies = over_groups(
        qkv_parts, qkv_landed, late_send.at[0], late_recv.at[0]
    )
    for copy in qkv_copies:
        copy.start()
    spread_u.relay_first()

    def one_pair(step, unused):
        pair = 3 - step
        stage[pair // 2, lax.rem(pair, 2)] = dot_f32(
            grads[rows_of(sums.theirs(pair)), 0 : 3 * cols], w_qkv[...], 1, 1
        ).astype(jnp.bfloat16)
        sums.exchange(pair).start()
        return unused

    lax.fori_loop(0, 4, one_pair, 0)
    spread_u.relay_second()

    def sum_pair(step, unused):
        pair = 3 - step
        own_sum[0] = dot_f32(grads[rows_of(sums.mine(pair)), 0 : 3 * cols], w_qkv[...], 1, 1)
        sums.exchange(pair).wait_recv()
        sums.finish(
            pair, own_sum[0] + landed[pair // 2, lax.rem(pair, 2)].astype(jnp.float32)
        )
        return unused

    lax.fori_loop(0, 4, sum_pair, 0)

    def group_sum(own, landed_ref, copies):
        landed_ref[group] = own
        for copy in copies:
            copy.wait_recv()
        total = landed_ref[0].astype(jnp.float32)
        for index in range(1, devices_fsdp):
            total = total + landed_ref[index].astype(jnp.float32)
        return total

    total = layer_sums[0].astype(jnp.float32)
    for pair, copy in enumerate(layer_copies):
        copy.wait_recv()
        at = slice((pair + 1) * held, (pair + 2) * held)
        total = total + attn_all[at].astype(jnp.float32)
    grad_rows[...] = (hidden[...].reshape(total.shape) + total).astype(jnp.bfloat16)
    save_layer = pltpu.make_async_copy(grad_rows, layer, save_sem.at[2])
    save_layer.start()

    spread_u.relay_third()
    turned = group_sum(qkv_parts(group)[...], qkv_landed, qkv_copies).T.astype(jnp.bfloat16)
    for index in range(3):
        columns_stage[index * shard : (index + 1) * shard, :] = turned[
            :, index * cols : (index + 1) * cols
        ]
    summed = group_sum(output_total[group], output_group, output_copies).astype(jnp.bfloat16)
    lines = shard // 8
    for index in range(8):
        columns_stage[3 * shard + index * lines : 3 * shard + (index + 1) * lines, :] = summed[
            :, index * cols : (index + 1) * cols
        ]
    spread_c = Spread(
        place, own_of(columns_stage, 4 * shard), half_of(columns_out, 4 * shard), c_send, c_recv
    )
    spread_c.start()
    save_columns = pltpu.make_async_copy(columns_stage, columns_out.at[me], save_sem.at[1])
    save_columns.start()
    total = sums.collect()
    values = patches[...].astype(jnp.float32)
    factor = lax.rsqrt(jnp.mean(values * values, axis=-1, keepdims=True) + epsilon)
    scaled = total * gain_one
    gain_parts[...] = jnp.zeros_like(gain_parts)
    attn_part = jnp.sum(total * values * factor, axis=0, keepdims=True)
    ffn_part = gain_part
    for index in range(devices_fsdp):
        at = slice(index * shard, (index + 1) * shard)
        gain_parts[index, 0:1, :] = attn_part[:, at]
        gain_parts[index, 1:2, :] = ffn_part[:, at]
    gain_copies = over_groups(lambda to: gain_parts.at[to], gain_landed, gain_send, gain_recv)
    for copy in gain_copies:
        copy.start()
    spread_c.relay_first()
    grad_hidden[...] = (
        grad_hidden[...]
        + factor * scaled
        - values * (factor * factor * factor) * jnp.mean(scaled * values, axis=-1, keepdims=True)
    )
    save_rows = pltpu.make_async_copy(grad_hidden, grad_patches, save_sem.at[3])
    save_rows.start()
    spread_c.relay_second()
    gain_total[...] = group_sum(gain_parts[group], gain_landed, gain_copies)
    gain_out = [
        remote(
            gain_total,
            gain_all.at[me],
            gain_out_send.at[flip - 1],
            gain_out_recv.at[flip - 1],
            {"ctx": place.peer(flip)},
        )
        for flip in range(1, 8)
    ]
    for copy in gain_out:
        copy.start()
    gain_all[me] = gain_total[...]

    spread_c.relay_third()
    for copy in gain_out:
        copy.wait_recv()
    gain_sum = gain_all[0]
    for index in range(1, 8):
        gain_sum = gain_sum + gain_all[index]
    gains_out[...] = gain_sum
    spread_u.arrived(0, 7, 8, 9)
    spread_c.arrived(0, 7, 8, 9)
    for step in (1, 3):
        pl.when(place.near(step))(units_direct(step).wait_send)
    units_direct(2).wait_send()
    pl.when(place.at_end())(units_far_copy.wait_send)
    for copy in layer_copies + qkv_copies + output_copies + gain_copies + gain_out:
        copy.wait_send()
    for pair in range(4):
        sums.exchange(pair).wait_send()
    sums.sent()
    output_pairs.sent()
    save_layer.wait()
    save_rows.wait()
    spread_u.sent()
    spread_c.sent()
    save_units.wait()
    save_columns.wait()


def place_kernel(
    devices_fsdp,
    units_all,
    columns_all,
    out_query,
    out_key,
    out_value,
    out_output,
    out_gate,
    out_up,
    out_down,
    columns,
    outputs,
    natural,
    gate,
    up,
    down,
    sems,
):
    shard = out_query.shape[0]
    cols = columns_all.shape[2]
    lines = shard // 8
    units = units_all.shape[1] // 3
    part = units // devices_fsdp
    span = part * 8
    saves = []

    def save(source, target):
        copy = pltpu.make_async_copy(source, target, sems.at[len(saves)])
        copy.start()
        saves.append(copy)

    for index in range(8):
        piece = units_all[index, 2 * units : 3 * units, :].astype(jnp.float32)
        for tile in range(devices_fsdp):
            down[index * part : (index + 1) * part, tile * shard : (tile + 1) * shard] = piece[
                tile * part : (tile + 1) * part, :
            ]
    save(down, out_down)
    for which, (target, out) in enumerate(((gate, out_gate), (up, out_up))):
        for index in range(8):
            piece = units_all[index, which * units : (which + 1) * units, :].astype(jnp.float32)
            for tile in range(devices_fsdp):
                first = tile * span + index * part
                natural[first : first + part, :] = piece[tile * part : (tile + 1) * part, :]
        for first in range(0, span * devices_fsdp, 128):
            target[:, first : first + 128] = natural[first : first + 128, :].T
        save(target, out)
    for index in range(8):
        at = slice(index * cols, (index + 1) * cols)
        for which in range(3):
            columns[which, :, at] = columns_all[
                index, which * shard : (which + 1) * shard, :
            ].astype(jnp.float32)
        for tile in range(8):
            first = 3 * shard + tile * lines
            outputs[index * lines : (index + 1) * lines, tile * cols : (tile + 1) * cols] = (
                columns_all[index, first : first + lines, :].astype(jnp.float32)
            )
    save(columns.at[0], out_query)
    save(columns.at[1], out_key)
    save(columns.at[2], out_value)
    save(outputs, out_output)
    for copy in saves:
        copy.wait()


def heads_plan(
    patches,
    cotangent,
    deal_table,
    prompt_len,
    w_query,
    w_key,
    w_value,
    w_output,
    w_gate,
    w_up,
    w_down,
    gain_attn,
    gain_ffn,
):
    local_rows = patches.shape[1]
    width = patches.shape[2]
    groups = lax.axis_size("fsdp")
    rows = local_rows * 8
    cols = width // 8
    shard = width // groups
    part = w_down.shape[0] // 8
    units = part * groups
    tiles = rows // TILE
    blocks = deal_table.shape[0]
    block_len = rows // blocks
    per_segment = CONT_LEN // TILE
    slots = jnp.arange(deal_table.shape[0], dtype=jnp.int32)
    slot_of = jnp.sum(
        jnp.where(deal_table[None, :] == slots[:, None], slots[None, :], 0), axis=1
    ).astype(jnp.int32)
    smem = pl.BlockSpec(memory_space=pltpu.SMEM)
    vmem = pl.BlockSpec(memory_space=pltpu.VMEM)
    anywhere = pl.BlockSpec(memory_space=pl.ANY)
    low, full = jnp.bfloat16, jnp.float32

    def shaped(kind, *dims):
        return jax.ShapeDtypeStruct(dims, kind)

    def room(kind, *dims):
        return pltpu.VMEM(dims, kind)

    unused, layer, grad_rows, units_all, columns_all, gains_sum = pl.pallas_call(
        functools.partial(layer_kernel, per_segment, groups),
        out_shape=(
            shaped(low, rows, width),
            shaped(low, blocks // 8, block_len, width),
            shaped(full, local_rows, width),
            shaped(low, 8, 3 * units, shard),
            shaped(low, 8, 4 * shard, cols),
            shaped(full, 8, shard),
        ),
        in_specs=[smem] * 3 + [vmem] + [anywhere] * 8 + [vmem] * 2,
        out_specs=(anywhere,) * 5 + (vmem,),
        scratch_shapes=[
            room(low, blocks, block_len, 3 * cols),
            room(full, tiles, cols, TILE),
            room(full, tiles, 1, 2 * TILE),
            room(low, groups, 3 * units, shard),
            room(low, groups, 8, shard // 8, width),
            room(low, 4, blocks // 8, block_len, width),
            room(full, local_rows, width),
            room(full, local_rows, width),
            room(low, rows, width),
            room(low, rows, width),
            room(low, rows, width),
            room(low, blocks, block_len, width),
            room(low, width, 3 * cols),
            room(low, groups, 8, shard // 8, width),
            room(low, units, width),
            room(low, units, width),
            room(low, units, width),
            room(low, groups, part, width),
            room(low, units, shard),
            room(low, units, shard),
            room(full, 16, shard),
            room(full, 16, width),
            room(low, blocks, block_len, cols),
            room(low, blocks, block_len, cols),
            room(low, tiles, cols, TILE),
            room(low, blocks, block_len, cols),
            room(low, blocks, block_len, cols),
            room(low, local_rows, width),
            room(low, 3 * units, rows),
            room(low, 2, 2, local_rows, width),
            room(low, 2, 2, local_rows, width),
            room(full, 2, local_rows, width),
            room(low, 4, local_rows, width),
            room(low, 2, local_rows, width),
            room(low, 2, local_rows // 2, width),
            room(low, local_rows, width),
            room(low, blocks // 8, block_len, width),
            room(low, blocks, block_len, cols),
            room(low, groups, 3 * units, shard),
            room(low, 3 * units, shard),
            room(low, 3 * units, shard),
            room(low, 3 * units, shard),
            room(low, 4, groups, shard // 8, width),
            room(low, 4, groups, shard // 8, width),
            room(low, 4, groups, shard // 8, width),
            room(low, groups, shard // 8, width),
            room(low, groups, shard // 8, width),
            room(low, groups, 3 * cols, shard),
            room(low, 4 * shard, cols),
            room(full, groups, 8, shard),
            room(full, groups, 8, shard),
            room(full, 8, shard),
            room(full, 8, 8, shard),
            dma(9),
            dma(4),
            dma(2 * groups),
            pltpu.SemaphoreType.DMA((8, groups - 1)),
            pltpu.SemaphoreType.DMA((8, groups - 1)),
            dma(8),
            dma(10),
            dma(10),
            dma(10),
            dma(10),
            dma(10),
            dma(10),
            dma(10),
            dma(10),
            dma(10),
            dma(10),
            dma(10),
            dma(10),
            dma(10),
            dma(10),
            dma(10),
            dma(10),
            dma(7),
            dma(7),
            dma(7),
            dma(7),
            dma(4),
            dma(4),
            dma(4),
            dma(4),
            dma(4),
            dma(4),
            dma(4),
            dma(4),
            dma(4),
            dma(4),
            dma(4),
            dma(4),
            dma(4),
            dma(4),
            dma(groups - 1),
            dma(groups - 1),
            dma(groups - 1),
            dma(groups - 1),
            dma(2),
            pltpu.SemaphoreType.DMA((2, groups - 1)),
            pltpu.SemaphoreType.DMA((2, groups - 1)),
        ],
        compiler_params=pltpu.CompilerParams(
            collective_id=0, has_side_effects=True, vmem_limit_bytes=67_000_000
        ),
        name="layer",
    )(
        slot_of,
        deal_table,
        prompt_len,
        patches[0],
        cotangent[0],
        w_query,
        w_key,
        w_value,
        w_output.reshape(8, shard // 8, width),
        w_gate,
        w_up,
        w_down.reshape(8, part, width),
        gain_attn[None],
        gain_ffn[None],
    )

    weights = pl.pallas_call(
        functools.partial(place_kernel, groups),
        out_shape=tuple(shaped(full, shard, width) for _ in range(4))
        + tuple(shaped(full, shard, 8 * units) for _ in range(2))
        + (shaped(full, 8 * part, width),),
        in_specs=[vmem, vmem],
        out_specs=(anywhere,) * 7,
        scratch_shapes=[
            room(full, 3, shard, width),
            room(full, shard, width),
            room(full, 8 * units, shard),
            room(full, shard, 8 * units),
            room(full, shard, 8 * units),
            room(full, 8 * part, width),
            dma(7),
        ],
        name="place",
    )(units_all, columns_all)
    layer = layer.reshape(1, local_rows, width)
    return (layer, grad_rows[None]) + tuple(weights) + (gains_sum[0], gains_sum[1])


def solution(mesh):
    if mesh.shape["ctx"] == 8 and mesh.shape["fsdp"] == 4:
        per_device = heads_plan
    else:
        per_device = rows_plan
    placed = (
        P("fsdp", "ctx", None),
        P("fsdp", "ctx", None),
        P(),
        P("fsdp"),
        P("fsdp", None),
        P("fsdp", None),
        P("fsdp", None),
        P("fsdp", None),
        P("fsdp", None),
        P("fsdp", None),
        P("fsdp", None),
        P("fsdp"),
        P("fsdp"),
    )
    return jax.shard_map(
        per_device,
        mesh=mesh,
        in_specs=placed,
        out_specs=(
            P("fsdp", "ctx", None),
            P("fsdp", "ctx", None),
            P("fsdp", None),
            P("fsdp", None),
            P("fsdp", None),
            P("fsdp", None),
            P("fsdp", None),
            P("fsdp", None),
            P("fsdp", None),
            P("fsdp"),
            P("fsdp"),
        ),
        check_vma=False,
    )
```

```python
import functools
import math

import jax
import jax.numpy as jnp
from jax import lax
from jax.experimental import pallas as pl
from jax.experimental.pallas import tpu as pltpu
from jax.sharding import PartitionSpec as P

HEADS = 16
HEAD = 64
CONT_LEN = 1024


epsilon = 1e-05
score_scale = 0.125
masked_value = -1e30


def rms_forward(values, gain):
    factor = lax.rsqrt(jnp.mean(values * values, axis=-1, keepdims=True) + epsilon)
    return (values * factor * gain, factor)


def rms_backward(values, factor, gain, grad_normed):
    scaled = grad_normed * gain
    grad_gain = jnp.sum(grad_normed * values * factor, axis=0)
    cubed = factor * factor * factor
    grad_values = factor * scaled - values * cubed * jnp.mean(
        scaled * values, axis=-1, keepdims=True
    )
    return (grad_values, grad_gain)


def segment_of(position, prompt):
    return jnp.where(position < prompt, -1, (position - prompt) // CONT_LEN)


def visible(query_pos, key_pos, prompt, length):
    same = (segment_of(query_pos, prompt)[:, None] == segment_of(key_pos, prompt)[None, :]) & (
        key_pos[None, :] <= query_pos[:, None]
    )
    shared = (query_pos[:, None] >= prompt) & (key_pos[None, :] < length)
    return same | shared


def rows_plan(
    patches,
    cotangent,
    deal_table,
    prompt_len,
    w_query,
    w_key,
    w_value,
    w_output,
    w_gate,
    w_up,
    w_down,
    gain_attn,
    gain_ffn,
):
    local_rows = patches.shape[1]
    width = patches.shape[2]
    devices_ctx = lax.axis_size("ctx")
    group_tok = local_rows * devices_ctx
    cont_count = group_tok // (2 * CONT_LEN)
    prompt = group_tok - cont_count * CONT_LEN
    block_len = local_rows // 2
    slot_count = 2 * devices_ctx
    key_rows = math.gcd(512, group_tok)
    block_count = group_tok // key_rows
    length = prompt_len[0]

    def positions_of(first_row, count):
        stored = first_row + jnp.arange(count, dtype=jnp.int32)
        slot_ids = stored // block_len
        picked = jnp.where(
            slot_ids[:, None] == jnp.arange(slot_count, dtype=jnp.int32)[None, :],
            deal_table[None, :],
            0,
        )
        return jnp.sum(picked, axis=1) * block_len + stored % block_len

    query_pos = positions_of(lax.axis_index("ctx") * local_rows, local_rows)
    key_pos = positions_of(0, group_tok).reshape(block_count, key_rows)
    (
        full_query,
        full_key,
        full_value,
        full_output,
        full_gate,
        full_up,
        full_down,
        full_gain_attn,
        full_gain_ffn,
    ) = (
        lax.all_gather(w_query, "fsdp", axis=0, tiled=True),
        lax.all_gather(w_key, "fsdp", axis=0, tiled=True),
        lax.all_gather(w_value, "fsdp", axis=0, tiled=True),
        lax.all_gather(w_output, "fsdp", axis=0, tiled=True),
        lax.all_gather(w_gate, "fsdp", axis=0, tiled=True),
        lax.all_gather(w_up, "fsdp", axis=0, tiled=True),
        lax.all_gather(w_down, "fsdp", axis=0, tiled=True),
        lax.all_gather(gain_attn, "fsdp", axis=0, tiled=True),
        lax.all_gather(gain_ffn, "fsdp", axis=0, tiled=True),
    )
    rows_f32 = patches[0].astype(jnp.float32)
    gain_one = full_gain_attn.astype(jnp.float32)
    normed, factor_attn = rms_forward(rows_f32, gain_one)
    normed_low = normed.astype(jnp.bfloat16)
    queries = jnp.dot(normed_low, full_query, preferred_element_type=jnp.float32).astype(
        jnp.bfloat16
    )
    keys_local = jnp.dot(normed_low, full_key, preferred_element_type=jnp.float32).astype(
        jnp.bfloat16
    )
    values_local = jnp.dot(normed_low, full_value, preferred_element_type=jnp.float32).astype(
        jnp.bfloat16
    )
    key_all, value_all = (
        lax.all_gather(keys_local, "ctx", axis=0, tiled=True),
        lax.all_gather(values_local, "ctx", axis=0, tiled=True),
    )
    query_heads = queries.reshape(local_rows, HEADS, HEAD)

    def split_blocks(array):
        return array.reshape(block_count, key_rows, HEADS, HEAD)

    def forward_block(state, block):
        key_block, value_block, block_pos = block
        visible_mask = visible(query_pos, block_pos, prompt, length)

        def forward_update(inner_state):
            maxima, totals, accum = inner_state
            scores = (
                jnp.einsum(
                    "qhe,khe->hqk", query_heads, key_block, preferred_element_type=jnp.float32
                )
                * score_scale
            )
            scores = jnp.where(visible_mask[None], scores, masked_value)
            new_max = jnp.maximum(maxima, jnp.max(scores, axis=-1))
            rescale = jnp.exp(maxima - new_max)
            probs = jnp.where(visible_mask[None], jnp.exp(scores - new_max[:, :, None]), 0.0)
            totals = totals * rescale + jnp.sum(probs, axis=-1)
            accum = accum * rescale.T[:, :, None] + jnp.einsum(
                "hqk,khe->qhe",
                probs.astype(jnp.bfloat16),
                value_block,
                preferred_element_type=jnp.float32,
            )
            return (new_max, totals, accum)

        return (
            lax.cond(jnp.any(visible_mask), forward_update, lambda inner_state: inner_state, state),
            None,
        )

    start_state = (
        jnp.full((HEADS, local_rows), masked_value, jnp.float32),
        jnp.zeros((HEADS, local_rows), jnp.float32),
        jnp.zeros((local_rows, HEADS, HEAD), jnp.float32),
    )
    (maxima, totals, accum), unused = lax.scan(
        forward_block, start_state, (split_blocks(key_all), split_blocks(value_all), key_pos)
    )
    attn_f32 = accum / totals.T[:, :, None]
    log_total = maxima + jnp.log(totals)
    attn_low = attn_f32.astype(jnp.bfloat16).reshape(local_rows, width)
    hidden = rows_f32 + jnp.dot(attn_low, full_output, preferred_element_type=jnp.float32)
    gain_two = full_gain_ffn.astype(jnp.float32)
    normed_ffn, factor_ffn = rms_forward(hidden, gain_two)
    ffn_low = normed_ffn.astype(jnp.bfloat16)
    gate = jnp.dot(ffn_low, full_gate, preferred_element_type=jnp.float32)
    up_proj = jnp.dot(ffn_low, full_up, preferred_element_type=jnp.float32)
    sigmoid = jax.nn.sigmoid(gate)
    activated = gate * sigmoid
    inner_low = (activated * up_proj).astype(jnp.bfloat16)
    layer = hidden + jnp.dot(inner_low, full_down, preferred_element_type=jnp.float32)
    grad_out = cotangent[0].astype(jnp.float32)
    grad_down_in = cotangent[0]
    grad_w_down = jnp.dot(inner_low.T, grad_down_in, preferred_element_type=jnp.float32)
    grad_inner = jnp.dot(grad_down_in, full_down.T, preferred_element_type=jnp.float32)
    grad_gate = (grad_inner * up_proj * sigmoid * (1.0 + gate * (1.0 - sigmoid))).astype(
        jnp.bfloat16
    )
    grad_up = (grad_inner * activated).astype(jnp.bfloat16)
    grad_w_gate = jnp.dot(ffn_low.T, grad_gate, preferred_element_type=jnp.float32)
    grad_w_up = jnp.dot(ffn_low.T, grad_up, preferred_element_type=jnp.float32)
    grad_normed_ffn = jnp.dot(grad_gate, full_gate.T, preferred_element_type=jnp.float32) + jnp.dot(
        grad_up, full_up.T, preferred_element_type=jnp.float32
    )
    grad_hidden_norm, grad_gain_ffn = rms_backward(hidden, factor_ffn, gain_two, grad_normed_ffn)
    grad_hidden = grad_out + grad_hidden_norm
    grad_branch = grad_hidden.astype(jnp.bfloat16)
    grad_w_output = jnp.dot(attn_low.T, grad_branch, preferred_element_type=jnp.float32)
    grad_attn = (
        jnp.dot(grad_branch, full_output.T, preferred_element_type=jnp.float32)
        .astype(jnp.bfloat16)
        .reshape(local_rows, HEADS, HEAD)
    )
    delta = jnp.einsum("qhe,qhe->hq", grad_attn.astype(jnp.float32), attn_f32)
    key_back, value_back = (key_all, value_all)

    def backward_block(grad_query, block):
        key_block, value_block, block_pos = block
        visible_mask = visible(query_pos, block_pos, prompt, length)

        def backward_update(grad_state):
            scores = (
                jnp.einsum(
                    "qhe,khe->hqk", query_heads, key_block, preferred_element_type=jnp.float32
                )
                * score_scale
            )
            probs = jnp.where(visible_mask[None], jnp.exp(scores - log_total[:, :, None]), 0.0)
            grad_probs = jnp.einsum(
                "qhe,khe->hqk", grad_attn, value_block, preferred_element_type=jnp.float32
            )
            grad_scores = (probs * (grad_probs - delta[:, :, None])).astype(jnp.bfloat16)
            grad_state = (
                grad_state
                + jnp.einsum(
                    "hqk,khe->qhe", grad_scores, key_block, preferred_element_type=jnp.float32
                )
                * score_scale
            )
            grad_keys = (
                jnp.einsum(
                    "hqk,qhe->khe", grad_scores, query_heads, preferred_element_type=jnp.float32
                )
                * score_scale
            )
            grad_values = jnp.einsum(
                "hqk,qhe->khe",
                probs.astype(jnp.bfloat16),
                grad_attn,
                preferred_element_type=jnp.float32,
            )
            return (grad_state, (grad_keys, grad_values))

        def skipped(grad_state):
            empty = jnp.zeros((key_rows, HEADS, HEAD), jnp.float32)
            return (grad_state, (empty, empty))

        return lax.cond(jnp.any(visible_mask), backward_update, skipped, grad_query)

    zero_query = jnp.zeros((local_rows, HEADS, HEAD), jnp.float32)
    grad_query, (grad_key_blocks, grad_value_blocks) = lax.scan(
        backward_block, zero_query, (split_blocks(key_back), split_blocks(value_back), key_pos)
    )
    grad_key_sum, grad_value_sum = (
        lax.psum_scatter(
            grad_key_blocks.reshape(group_tok, width).astype(jnp.bfloat16),
            "ctx",
            scatter_dimension=0,
            tiled=True,
        ).astype(jnp.float32),
        lax.psum_scatter(
            grad_value_blocks.reshape(group_tok, width).astype(jnp.bfloat16),
            "ctx",
            scatter_dimension=0,
            tiled=True,
        ).astype(jnp.float32),
    )
    grad_key_low = grad_key_sum.astype(jnp.bfloat16)
    grad_value_low = grad_value_sum.astype(jnp.bfloat16)
    grad_query_low = grad_query.reshape(local_rows, width).astype(jnp.bfloat16)
    grad_w_query = jnp.dot(normed_low.T, grad_query_low, preferred_element_type=jnp.float32)
    grad_w_key = jnp.dot(normed_low.T, grad_key_low, preferred_element_type=jnp.float32)
    grad_w_value = jnp.dot(normed_low.T, grad_value_low, preferred_element_type=jnp.float32)
    grad_normed = (
        jnp.dot(grad_query_low, full_query.T, preferred_element_type=jnp.float32)
        + jnp.dot(grad_key_low, full_key.T, preferred_element_type=jnp.float32)
        + jnp.dot(grad_value_low, full_value.T, preferred_element_type=jnp.float32)
    )
    grad_rows_norm, grad_gain_attn = rms_backward(rows_f32, factor_attn, gain_one, grad_normed)
    grad_rows = grad_hidden + grad_rows_norm
    shards = (
        lax.psum_scatter(
            grad_w_query.astype(jnp.bfloat16), "fsdp", scatter_dimension=0, tiled=True
        ).astype(jnp.float32),
        lax.psum_scatter(
            grad_w_key.astype(jnp.bfloat16), "fsdp", scatter_dimension=0, tiled=True
        ).astype(jnp.float32),
        lax.psum_scatter(
            grad_w_value.astype(jnp.bfloat16), "fsdp", scatter_dimension=0, tiled=True
        ).astype(jnp.float32),
        lax.psum_scatter(
            grad_w_output.astype(jnp.bfloat16), "fsdp", scatter_dimension=0, tiled=True
        ).astype(jnp.float32),
        lax.psum_scatter(
            grad_w_gate.astype(jnp.bfloat16), "fsdp", scatter_dimension=0, tiled=True
        ).astype(jnp.float32),
        lax.psum_scatter(
            grad_w_up.astype(jnp.bfloat16), "fsdp", scatter_dimension=0, tiled=True
        ).astype(jnp.float32),
        lax.psum_scatter(
            grad_w_down.astype(jnp.bfloat16), "fsdp", scatter_dimension=0, tiled=True
        ).astype(jnp.float32),
        lax.psum_scatter(
            grad_gain_attn.astype(jnp.bfloat16), "fsdp", scatter_dimension=0, tiled=True
        ).astype(jnp.float32),
        lax.psum_scatter(
            grad_gain_ffn.astype(jnp.bfloat16), "fsdp", scatter_dimension=0, tiled=True
        ).astype(jnp.float32),
    )
    summed = (
        lax.psum(shards[0].astype(jnp.bfloat16), "ctx").astype(jnp.float32),
        lax.psum(shards[1].astype(jnp.bfloat16), "ctx").astype(jnp.float32),
        lax.psum(shards[2].astype(jnp.bfloat16), "ctx").astype(jnp.float32),
        lax.psum(shards[3].astype(jnp.bfloat16), "ctx").astype(jnp.float32),
        lax.psum(shards[4].astype(jnp.bfloat16), "ctx").astype(jnp.float32),
        lax.psum(shards[5].astype(jnp.bfloat16), "ctx").astype(jnp.float32),
        lax.psum(shards[6].astype(jnp.bfloat16), "ctx").astype(jnp.float32),
        lax.psum(shards[7].astype(jnp.bfloat16), "ctx").astype(jnp.float32),
        lax.psum(shards[8].astype(jnp.bfloat16), "ctx").astype(jnp.float32),
    )
    return (
        layer.astype(jnp.bfloat16)[None],
        grad_rows[None],
        summed[0],
        summed[1],
        summed[2],
        summed[3],
        summed[4],
        summed[5],
        summed[6],
        summed[7],
        summed[8],
    )


TILE = 256


def dot_f32(left, right, left_dim, right_dim):
    return lax.dot_general(
        left,
        right,
        (((left_dim,), (right_dim,)), ((), ())),
        preferred_element_type=jnp.float32,
    )


def head_masks():
    lane = lax.broadcasted_iota(jnp.int32, (TILE, 2 * HEAD), 1)
    first = (lane < HEAD).astype(jnp.bfloat16)
    return first, (1 - first).astype(jnp.bfloat16)


def stack_heads(tile, masks):
    return jnp.concatenate([tile * masks[0], tile * masks[1]], axis=0)


def tile_mask(kind, tile, length):
    row = lax.broadcasted_iota(jnp.int32, (TILE, 2 * TILE), 0)
    if kind == "diagonal":
        column = lax.broadcasted_iota(jnp.int32, (TILE, 2 * TILE), 1)
        return row <= jnp.where(column < TILE, column, column - TILE)
    return row + tile * TILE < length


def over_keys(tile, per_segment, step, state):
    base = tile // per_segment * per_segment
    state = lax.fori_loop(0, base, lambda key, kept: step(key, kept, "prompt"), state)
    state = lax.fori_loop(base, tile, lambda key, kept: step(key, kept, "full"), state)
    return step(tile, state, "diagonal")


def load_tile(ref, tile):
    held = TILE // ref.shape[1]
    return ref[pl.ds(tile * held, held)].reshape(TILE, ref.shape[2])


def store_tile(ref, tile, values):
    held = TILE // ref.shape[1]
    ref[pl.ds(tile * held, held)] = values.reshape(held, ref.shape[1], ref.shape[2])


def to_logical(slot_of, source, column, target, scale=None):
    for block in range(target.shape[0]):
        picked = source[slot_of[block], :, column : column + 2 * HEAD]
        if scale is not None:
            picked = picked * scale
        target[block] = picked


def to_stored(block_of, source, target, column):
    block_len = source.shape[1]
    for slot in range(source.shape[0]):
        target[slot * block_len : (slot + 1) * block_len, column : column + 2 * HEAD] = source[
            block_of[slot]
        ]


def tiles_between(count, one_tile, between):
    first = 0
    for stop in sorted(between):
        lax.fori_loop(first, stop, one_tile, 0)
        between[stop]()
        first = stop
    lax.fori_loop(first, count, one_tile, 0)


def attend_forward(
    per_segment,
    slot_of,
    length_ref,
    qkv,
    attn_t,
    lse,
    query,
    key,
    value_t,
    kept,
    between,
):
    rows = qkv.shape[0] * qkv.shape[1]
    length = length_ref[0]
    to_logical(slot_of, qkv, 0, query, jnp.bfloat16(score_scale))
    to_logical(slot_of, qkv, 2 * HEAD, key)
    to_logical(slot_of, qkv, 4 * HEAD, kept)
    for tile in range(rows // TILE):
        value_t[tile] = load_tile(kept, tile).T
    masks = head_masks()

    def one_tile(tile, unused):
        both = stack_heads(load_tile(query, tile), masks)

        def step(key_tile, state, kind):
            maxima, totals, accum = state
            scores = dot_f32(load_tile(key, key_tile), both, 1, 1)
            if kind != "full":
                scores = jnp.where(tile_mask(kind, key_tile, length), scores, masked_value)
            new_max = jnp.maximum(maxima, jnp.max(scores, axis=0, keepdims=True))
            probs = jnp.exp(scores - new_max)
            rescale = jnp.exp(maxima - new_max)
            totals = totals * rescale + jnp.sum(probs, axis=0, keepdims=True)
            accum = accum * rescale + dot_f32(
                value_t[key_tile], probs.astype(jnp.bfloat16), 1, 0
            )
            return new_max, totals, accum

        maxima, totals, accum = over_keys(
            tile,
            per_segment,
            step,
            (
                jnp.full((1, 2 * TILE), masked_value, jnp.float32),
                jnp.zeros((1, 2 * TILE), jnp.float32),
                jnp.zeros((2 * HEAD, 2 * TILE), jnp.float32),
            ),
        )
        accum = accum / totals
        feature = lax.broadcasted_iota(jnp.int32, (2 * HEAD, TILE), 0)
        picked = jnp.where(feature < HEAD, accum[:, :TILE], accum[:, TILE:])
        attn_t[tile] = picked
        lse[tile] = maxima + jnp.log(totals)
        store_tile(kept, tile, picked.T.astype(jnp.bfloat16))
        return unused

    tiles_between(rows // TILE, one_tile, between)


def attend_backward(
    per_segment,
    slot_of,
    block_of,
    length_ref,
    qkv,
    grad_attn,
    attn_t,
    lse,
    grad_qkv,
    query,
    key,
    value,
    grad,
    key_t,
    grad_sums,
    between,
):
    rows = qkv.shape[0] * qkv.shape[1]
    length = length_ref[0]
    to_logical(slot_of, qkv, 0, query, jnp.bfloat16(score_scale))
    to_logical(slot_of, qkv, 2 * HEAD, key)
    to_logical(slot_of, qkv, 4 * HEAD, value)
    to_logical(slot_of, grad_attn, 0, grad)
    for tile in range(rows // TILE):
        key_t[tile] = load_tile(key, tile).T
    grad_sums[...] = jnp.zeros_like(grad_sums)
    masks = head_masks()

    def one_tile(tile, unused):
        both = stack_heads(load_tile(query, tile), masks)
        grad_tile = load_tile(grad, tile)
        both_grad = stack_heads(grad_tile, masks)
        product = grad_tile.astype(jnp.float32).T * attn_t[tile]
        delta = jnp.concatenate(
            [
                jnp.sum(product[:HEAD], axis=0, keepdims=True),
                jnp.sum(product[HEAD:], axis=0, keepdims=True),
            ],
            axis=1,
        )
        log_total = lse[tile]

        def step(key_tile, grad_query, kind):
            keys_at = pl.ds(pl.multiple_of(key_tile * 2 * HEAD, 2 * HEAD), 2 * HEAD)
            scores = dot_f32(load_tile(key, key_tile), both, 1, 1)
            if kind != "full":
                scores = jnp.where(tile_mask(kind, key_tile, length), scores, masked_value)
            probs = jnp.exp(scores - log_total)
            grad_probs = dot_f32(load_tile(value, key_tile), both_grad, 1, 1)
            grad_scores = (probs * (grad_probs - delta)).astype(jnp.bfloat16)
            grad_sums[1, :, keys_at] += dot_f32(probs.astype(jnp.bfloat16), both_grad, 1, 0)
            grad_sums[0, :, keys_at] += dot_f32(grad_scores, both, 1, 0)
            return grad_query + dot_f32(key_t[key_tile], grad_scores, 1, 0)

        grad_query = over_keys(
            tile, per_segment, step, jnp.zeros((2 * HEAD, 2 * TILE), jnp.float32)
        )
        feature = lax.broadcasted_iota(jnp.int32, (2 * HEAD, TILE), 0)
        picked = jnp.where(feature < HEAD, grad_query[:, :TILE], grad_query[:, TILE:])
        store_tile(query, tile, (picked * score_scale).T.astype(jnp.bfloat16))
        return unused

    tiles_between(rows // TILE, one_tile, between)
    for tile in range(rows // TILE):
        at = slice(tile * 2 * HEAD, (tile + 1) * 2 * HEAD)
        store_tile(key, tile, grad_sums[0, :, at].astype(jnp.bfloat16))
        store_tile(value, tile, grad_sums[1, :, at].astype(jnp.bfloat16))
    to_stored(block_of, query, grad_qkv, 0)
    to_stored(block_of, key, grad_qkv, 2 * HEAD)
    to_stored(block_of, value, grad_qkv, 4 * HEAD)


def dma(count):
    return pltpu.SemaphoreType.DMA((count,))


def flipped(bit, flip):
    return bit + flip - 2 * bit * flip


class Place:
    def __init__(self, devices_fsdp):
        self.me = lax.axis_index("ctx")
        self.core = lax.rem(self.me, 2)
        self.column = lax.rem(self.me // 2, 2)
        self.row = self.me // 4
        self.group = lax.axis_index("fsdp")
        self.groups = devices_fsdp

    def peer(self, flip):
        low, middle, high = flip % 2, flip // 2 % 2, flip // 4
        return (
            flipped(self.row, high) * 4
            + flipped(self.column, middle) * 2
            + flipped(self.core, low)
        )

    def other_group(self, step):
        return lax.rem(self.group + step, self.groups)

    def at_end(self):
        return lax.rem(self.group, 3) == 0

    def between(self):
        return lax.rem(self.group, 3) != 0

    def near(self, step):
        return self.group != {1: 3, 2: 4, 3: 0}[step]

    def heard(self, step):
        return self.group != {1: 0, 2: 4, 3: 3}[step]

    def meet(self):
        barrier = pltpu.get_barrier_semaphore()
        for flip in range(1, 8):
            pl.semaphore_signal(barrier, inc=1, device_id={"ctx": self.peer(flip)})
        for step in range(1, self.groups):
            pl.semaphore_signal(barrier, inc=1, device_id={"fsdp": self.other_group(step)})
        pl.semaphore_wait(barrier, 7 + self.groups - 1)


def remote(source, target, send, recv, device):
    return pltpu.make_async_remote_copy(
        src_ref=source,
        dst_ref=target,
        send_sem=send,
        recv_sem=recv,
        device_id=device,
        device_id_type=pl.DeviceIdType.MESH,
    )


class Spread:
    def __init__(self, place, own, region, send, recv):
        me, peer = place.me, place.peer

        def copy(index, source, target, flip):
            return remote(source, target, send.at[index], recv.at[index], {"ctx": peer(flip)})

        self.copies = [
            copy(0, own(None), region(me, None), 1),
            copy(1, own(0), region(me, 0), 2),
            copy(2, own(1), region(me, 1), 2),
            copy(3, own(1), region(me, 1), 4),
            copy(4, own(0), region(me, 0), 4),
            copy(5, region(peer(2), 0), region(peer(2), 0), 4),
            copy(6, region(peer(4), 1), region(peer(4), 1), 2),
            copy(7, region(peer(2), None), region(peer(2), None), 1),
            copy(8, region(peer(4), None), region(peer(4), None), 1),
            copy(9, region(peer(6), None), region(peer(6), None), 1),
        ]

    def start(self):
        for index in (1, 3, 0, 2, 4):
            self.copies[index].start()

    def arrived(self, *indices):
        for index in indices:
            self.copies[index].wait_recv()

    def relay_first(self):
        self.arrived(1)
        self.copies[5].start()
        self.arrived(3)
        self.copies[6].start()

    def relay_second(self):
        self.arrived(2)
        self.copies[7].start()
        self.arrived(4)
        self.copies[8].start()

    def relay_third(self):
        self.arrived(5, 6)
        self.copies[9].start()

    def sent(self):
        for copy in self.copies:
            copy.wait_send()


class PairSum:
    def __init__(self, place, stage, landed, sums, received, send, recv, out_send, out_recv):
        self.place = place
        self.slot = lambda pair: pair
        self.stage, self.landed, self.sums, self.received = stage, landed, sums, received
        self.send, self.recv, self.out_send, self.out_recv = send, recv, out_send, out_recv

    def mine(self, pair):
        place = self.place
        return (
            flipped(place.row, pair // 2) * 4
            + flipped(place.column, lax.rem(pair, 2)) * 2
            + place.core
        )

    def theirs(self, pair):
        return self.mine(pair) + 1 - 2 * self.place.core

    def staged(self, pair):
        return self.stage.at[self.slot(pair)]

    def exchange(self, pair):
        return remote(
            self.staged(pair),
            self.landed.at[self.slot(pair)],
            self.send.at[pair],
            self.recv.at[pair],
            {"ctx": self.place.peer(1)},
        )

    def deliver(self, pair):
        return remote(
            self.sums.at[pair],
            self.received.at[pair],
            self.out_send.at[pair],
            self.out_recv.at[pair],
            {"ctx": self.mine(pair)},
        )

    def sent(self):
        for pair in range(4):
            self.exchange(pair).wait_send()
            if pair:
                self.deliver(pair).wait_send()


class OutputSum(PairSum):
    def staged(self, pair):
        return self.stage.at[:, self.theirs(pair)]


class CrossSum(PairSum):
    def __init__(
        self, place, slot, stage, landed, sums, received, passed, send, recv, out_send, out_recv
    ):
        super().__init__(place, stage, landed, sums, received, send, recv, out_send, out_recv)
        self.slot = slot
        self.passed = passed

    def half(self, which):
        count = self.sums.shape[1] // 2
        return slice(which * count, (which + 1) * count)

    def far(self, which):
        slot = 3 * which
        return remote(
            self.sums.at[3, self.half(which)],
            self.passed.at[which],
            self.out_send.at[slot],
            self.out_recv.at[slot],
            {"ctx": self.place.peer(2 + 2 * which)},
        )

    def deliver(self, pair):
        return remote(
            self.sums.at[pair],
            self.received.at[pair - 1],
            self.out_send.at[pair],
            self.out_recv.at[pair],
            {"ctx": self.place.peer(2 * pair)},
        )

    def finish(self, pair, total):
        self.sums[pair] = total.astype(jnp.bfloat16)

        @pl.when(pair == 3)
        def _():
            self.far(0).start()
            self.far(1).start()

        for axis in (1, 2):
            which = 2 - axis

            @pl.when(pair == axis)
            def _(axis=axis, which=which):
                at = self.half(which)
                self.far(which).wait_recv()
                self.sums[axis, at, :] = (
                    total[at] + self.passed[which].astype(jnp.float32)
                ).astype(jnp.bfloat16)
                self.deliver(axis).start()

    def collect(self):
        total = self.sums[0].astype(jnp.float32)
        for pair in (1, 2):
            self.deliver(pair).wait_recv()
            total = total + self.received[pair - 1].astype(jnp.float32)
        return total

    def sent(self):
        for which in (0, 1):
            self.far(which).wait_send()
            self.deliver(which + 1).wait_send()


def halves(count):
    return lambda half: pl.ds(0 if half in (None, 0) else count // 2, count if half is None else count // 2)


def slots_of(block_of):
    count = block_of.shape[0]
    held = [block_of[slot] for slot in range(count)]
    slots = []
    for block in range(count):
        found = jnp.int32(0)
        for slot in range(1, count):
            found = jnp.where(held[slot] == block, jnp.int32(slot), found)
        slots.append(found)
    return slots


def layer_kernel(
    per_segment,
    devices_fsdp,
    block_of,
    length_ref,
    patches,
    cotangent,
    w_query,
    w_key,
    w_value,
    w_output,
    w_gate,
    w_up,
    w_down,
    gain_attn,
    gain_ffn,
    normed_out,
    layer,
    grad_patches,
    units_out,
    columns_out,
    gains_out,
    qkv,
    attn_t,
    lse,
    grad_units,
    grad_output,
    layer_sums,
    hidden,
    grad_hidden,
    rows_all,
    grads,
    normed_ffn,
    attn_all,
    w_qkv,
    output_all,
    gate_t,
    up_t,
    down,
    down_parts,
    gate_stage,
    up_stage,
    gain_stage,
    gains,
    query,
    key,
    value_t,
    kept,
    grad,
    attn_rows,
    units_t,
    stage,
    landed,
    own_sum,
    norm_sums,
    norm_received,
    norm_passed,
    grad_branch,
    grad_rows,
    grad_attn,
    units_landed,
    units_far,
    units_near,
    units_stage,
    output_landed,
    output_sums,
    output_received,
    output_total,
    output_group,
    qkv_landed,
    columns_stage,
    gain_parts,
    gain_landed,
    gain_total,
    gain_all,
    local_sem,
    save_sem,
    unit_sem,
    group_send,
    group_recv,
    pass_send,
    x_send,
    x_recv,
    g_send,
    g_recv,
    o_send,
    o_recv,
    first_send,
    first_recv,
    second_send,
    second_recv,
    third_send,
    third_recv,
    u_send,
    u_recv,
    c_send,
    c_recv,
    b_send,
    b_recv,
    gain_out_send,
    gain_out_recv,
    pair_send,
    pair_recv,
    out_send,
    out_recv,
    back_pair_send,
    back_pair_recv,
    back_out_send,
    back_out_recv,
    wo_send,
    wo_recv,
    wo_out_send,
    wo_out_recv,
    layer_send,
    layer_recv,
    units_send,
    units_recv,
    gain_send,
    gain_recv,
    far_sem,
    late_send,
    late_recv,
):
    place = Place(devices_fsdp)
    slot_of = slots_of(block_of)
    me, group = place.me, place.group
    local_rows, width = patches.shape
    cols = width // 8
    shard = w_query.shape[0]
    part = w_down.shape[1]
    units = part * devices_fsdp
    span = part * 8
    held = qkv.shape[0] // 8

    def unit_range(index):
        return span * index // 128 * 128, -(-span * (index + 1) // 128) * 128

    def unit_copies(weight, target, first):
        copies = []
        for index in range(devices_fsdp):
            low, high = unit_range(index)
            copies.append(
                pltpu.make_async_copy(
                    weight.at[:, low:high],
                    target.at[index // 2, index % 2, :, 0 : high - low],
                    unit_sem.at[first + index],
                )
            )
        return copies

    gate_copies = unit_copies(w_gate, stage, 0)
    up_copies = unit_copies(w_up, landed, devices_fsdp)
    for copy in gate_copies + up_copies:
        copy.start()
    place.meet()

    def rows_of(block, count=local_rows):
        return pl.ds(pl.multiple_of(block * count, count), count)

    def rows_half(ref):
        def region(block, half):
            start = block * local_rows + (local_rows // 2 if half == 1 else 0)
            count = local_rows if half is None else local_rows // 2
            return ref.at[pl.ds(pl.multiple_of(start, local_rows // 2), count)]

        return region

    def own_half(ref):
        return lambda half: ref.at[halves(local_rows)(half)]

    spread_x = Spread(place, own_half(patches), rows_half(rows_all), x_send, x_recv)
    spread_x.start()

    my_cols = rows_of(me, cols)
    def shard_of(index):
        return rows_of(index, shard)

    group_items = [
        (w_query.at[:, my_cols], lambda to: w_qkv.at[shard_of(to), 0:cols]),
        (w_key.at[:, my_cols], lambda to: w_qkv.at[shard_of(to), cols : 2 * cols]),
        (w_value.at[:, my_cols], lambda to: w_qkv.at[shard_of(to), 2 * cols : 3 * cols]),
        (gain_stage, lambda to: gains.at[:, shard_of(to)]),
        (w_output.at[me], lambda to: output_all.at[to, me]),
        (gate_stage, lambda to: gate_t.at[:, shard_of(to)]),
        (up_stage, lambda to: up_t.at[:, shard_of(to)]),
        (w_down.at[me], lambda to: down_parts.at[to]),
    ]

    def group_copy(index, step):
        source, target = group_items[index]
        return remote(
            source,
            target(group),
            group_send.at[index, step - 1],
            group_recv.at[index, step - 1],
            {"fsdp": place.other_group(step)},
        )

    def passed_copy(index):
        whose = place.other_group(2)
        held = group_items[index][1](whose)
        return remote(
            held,
            held,
            pass_send.at[index],
            group_recv.at[index, 2 * (group // 2)],
            {"fsdp": devices_fsdp - 1 - whose},
        )

    def local_copy(index):
        source, target = group_items[index]
        return pltpu.make_async_copy(source, target(group), local_sem.at[index])

    def send_group(index):
        group_copy(index, 2).start()
        for step in (1, 3):
            pl.when(place.near(step))(group_copy(index, step).start)
        local_copy(index).start()

    def pass_group(index):
        @pl.when(place.between())
        def _():
            group_copy(index, 2).wait_recv()
            passed_copy(index).start()

    def group_arrived(index):
        pl.when(place.at_end())(group_copy(index, 2).wait_recv)
        for step in (1, 3):
            group_copy(index, step).wait_recv()
        local_copy(index).wait()

    def group_sent(index):
        group_copy(index, 2).wait_send()
        for step in (1, 3):
            pl.when(place.near(step))(group_copy(index, step).wait_send)
        pl.when(place.between())(passed_copy(index).wait_send)

    for index in (0, 1, 2):
        send_group(index)
    gain_stage[0:8, :] = jnp.broadcast_to(gain_attn[...].astype(jnp.float32)[None], (8, shard))
    gain_stage[8:16, :] = jnp.broadcast_to(gain_ffn[...].astype(jnp.float32)[None], (8, shard))
    send_group(3)
    send_group(4)

    def pick_units(copies, source, target):
        pieces = []
        for index in range(devices_fsdp):
            low, high = unit_range(index)
            unit = lax.broadcasted_iota(jnp.int32, (part, high - low), 0)
            column = lax.broadcasted_iota(jnp.int32, (part, high - low), 1)
            chosen = (column + low == unit + span * index + part * me).astype(jnp.bfloat16)
            copies[index].wait()
            pieces.append(
                dot_f32(chosen, source[index // 2, index % 2, :, 0 : high - low], 1, 1)
            )
        target[...] = jnp.concatenate(pieces, axis=0).astype(jnp.bfloat16)

    pick_units(gate_copies, stage, gate_stage)
    pick_units(up_copies, landed, up_stage)
    send_group(5)
    send_group(6)
    send_group(7)

    rows_all[rows_of(me), :] = patches[...]
    load_grads = pltpu.make_async_copy(cotangent, grads.at[rows_of(me)], save_sem.at[0])
    load_grads.start()
    spread_x.relay_first()
    for index in (0, 1, 2, 3):
        pass_group(index)
    spread_x.relay_second()
    spread_g = Spread(place, own_half(cotangent), rows_half(grads), g_send, g_recv)
    spread_g.start()
    spread_x.relay_third()
    pass_group(4)
    spread_x.arrived(0, 7, 8, 9)
    for index in (0, 1, 2, 3):
        group_arrived(index)
    gain_one = gains[0:1, :]

    def output_half(block, half):
        if half is None:
            return output_all.at[:, block]
        lines = output_all.shape[2]
        return output_all.at[:, block, halves(lines)(half)]

    group_arrived(4)
    spread_o = Spread(place, lambda half: output_half(me, half), output_half, o_send, o_recv)
    spread_o.start()

    def project(block, unused):
        at = rows_of(block)
        values = rows_all[at, :].astype(jnp.float32)
        low = rms_forward(values, gain_one)[0].astype(jnp.bfloat16)
        normed_ffn[at, :] = low
        store_tile(qkv, block, dot_f32(low, w_qkv[...], 1, 0).astype(jnp.bfloat16))
        return unused

    spread_x.sent()
    lax.fori_loop(0, 8, project, 0)
    save_normed = pltpu.make_async_copy(normed_ffn, normed_out, local_sem.at[8])
    save_normed.start()
    spread_g.relay_first()

    def attn_spread(first, count, send, recv):
        def part(half):
            return slice(
                first + (count // 2 if half == 1 else 0),
                first + (count // 2 if half == 0 else count),
            )

        return Spread(
            place,
            lambda half: kept.at[part(half)],
            lambda block, half: attn_all.at[part(half), :, rows_of(block, cols)],
            send,
            recv,
        )

    half_blocks = kept.shape[0] // 2
    attn_first = attn_spread(0, half_blocks, first_send, first_recv)
    attn_second = attn_spread(half_blocks, half_blocks // 2, second_send, second_recv)
    attn_third = attn_spread(half_blocks * 3 // 2, half_blocks // 2, third_send, third_recv)

    def after_two():
        pass_group(5)

    def after_more():
        spread_g.relay_second()
        pass_group(6)

    def after_half():
        attn_second.start()
        spread_o.relay_first()

    def after_most():
        pass_group(7)
        spread_o.relay_second()

    attend_forward(
        per_segment,
        slot_of,
        length_ref,
        qkv,
        attn_t,
        lse,
        query,
        key,
        value_t,
        kept,
        {
            per_segment // 2: after_two,
            per_segment: attn_first.start,
            per_segment + 1: after_more,
            per_segment + per_segment // 2: after_half,
            2 * per_segment - 1: after_most,
        },
    )
    attn_third.start()
    attn_all[:, :, my_cols] = kept[...]
    spread_g.relay_third()
    attn_first.relay_first()
    attn_first.relay_second()
    spread_o.relay_third()
    for index in (5, 6, 7):
        group_arrived(index)
    down[...] = jnp.concatenate(
        [down_parts[index].astype(jnp.float32) for index in range(devices_fsdp)], axis=0
    ).astype(jnp.bfloat16)
    attn_second.relay_first()
    attn_second.relay_second()
    attn_first.relay_third()
    attn_third.relay_first()
    attn_third.relay_second()
    attn_second.relay_third()
    save_normed.wait()
    load_grads.wait()
    spread_g.arrived(0, 7, 8, 9)
    spread_o.arrived(0, 7, 8, 9)
    attn_third.relay_third()
    for spread in (attn_first, attn_second, attn_third):
        spread.arrived(0, 7, 8, 9)

    def swap(source, target, send, recv):
        return [
            remote(source(flip), target, send.at[flip - 1], recv.at[flip - 1], {"ctx": place.peer(flip)})
            for flip in range(1, 8)
        ]

    def attn_of(block):
        return jnp.concatenate(
            [attn_all[block_of[block * held + index]] for index in range(held)], axis=0
        )

    gain_two = gains[8:9, :]
    sums = CrossSum(
        place,
        lambda pair: lax.rem(pair, 2),
        stage,
        landed,
        norm_sums,
        norm_received,
        norm_passed,
        pair_send,
        pair_recv,
        out_send,
        out_recv,
    )

    def hidden_of(block, attn):
        return rows_all[rows_of(block), :].astype(jnp.float32) + dot_f32(
            attn, output_all[...].reshape(width, width), 1, 0
        )

    def feed(block):
        at = rows_of(block)
        low = rms_forward(hidden_of(block, attn_of(block)), gain_two)[0].astype(jnp.bfloat16)
        normed_ffn[at, :] = low
        grad_out = grads[at, :]
        gate = dot_f32(low, gate_t[...], 1, 1)
        up_proj = dot_f32(low, up_t[...], 1, 1)
        grad_inner = dot_f32(grad_out, down[...], 1, 1)
        sigmoid = jax.nn.sigmoid(gate)
        activated = gate * sigmoid
        inner = activated * up_proj
        inner_low = inner.astype(jnp.bfloat16)
        grad_gate = grad_inner * up_proj * sigmoid * (1.0 + gate * (1.0 - sigmoid))
        grad_up = grad_inner * activated
        gate_low = grad_gate.astype(jnp.bfloat16)
        up_low = grad_up.astype(jnp.bfloat16)
        units_t[0:units, at] = inner.T.astype(jnp.bfloat16)
        units_t[units : 2 * units, at] = grad_gate.T.astype(jnp.bfloat16)
        units_t[2 * units : 3 * units, at] = grad_up.T.astype(jnp.bfloat16)
        return (
            dot_f32(inner_low, down[...], 1, 0),
            dot_f32(gate_low, gate_t[...], 1, 0) + dot_f32(up_low, up_t[...], 1, 0),
        )

    def one_pair(step, unused):
        pair = 3 - step
        slot = lax.rem(pair, 2)
        layer, norm = feed(sums.theirs(pair))

        @pl.when(step > 1)
        def _():
            sums.exchange(pair + 2).wait_send()

        stage[slot, 0] = layer.astype(jnp.bfloat16)
        stage[slot, 1] = norm.astype(jnp.bfloat16)
        sums.exchange(pair).start()
        layer, norm = feed(sums.mine(pair))
        own_sum[0] = layer
        own_sum[1] = norm
        sums.exchange(pair).wait_recv()
        layer_sums[pair] = (
            (own_sum[0] + landed[slot, 0].astype(jnp.float32))
            .astype(jnp.bfloat16)
            .reshape(layer_sums.shape[1:])
        )
        sums.finish(pair, own_sum[1] + landed[slot, 1].astype(jnp.float32))
        return unused

    lax.fori_loop(0, 4, one_pair, 0)
    for pair in (1, 0):
        sums.exchange(pair).wait_send()
    attn_rows[...] = attn_of(me)
    hidden[...] = hidden_of(me, attn_rows[...])
    load_normed = pltpu.make_async_copy(normed_out, rows_all, local_sem.at[8])
    load_normed.start()

    def down_part(tile, unused):
        at = rows_of(tile, shard)
        down_tile = dot_f32(units_t[0:units, :], grads[:, at], 1, 0)
        for half in (0, 1):
            own_sum[half, 0 : units // 2, at] = down_tile[half * units // 2 : (half + 1) * units // 2]
        return unused

    lax.fori_loop(0, devices_fsdp, down_part, 0)
    for index in range(devices_fsdp):
        first = index % 2 * part
        grad_units[index, 2 * units : 3 * units, :] = jnp.concatenate(
            [
                own_sum[index // 2, first : first + part, tile * shard : (tile + 1) * shard]
                for tile in range(devices_fsdp)
            ],
            axis=0,
        ).astype(jnp.bfloat16)

    def units_copy(step, source):
        return remote(
            source,
            units_landed.at[group],
            units_send.at[step - 1],
            units_recv.at[step - 1],
            {"fsdp": place.other_group(step)},
        )

    def units_direct(step):
        return units_copy(step, grad_units.at[place.other_group(step)])

    units_far_copy = remote(
        grad_units.at[devices_fsdp - 1 - group],
        units_far,
        far_sem.at[0],
        far_sem.at[1],
        {"fsdp": 1 + group // 3},
    )
    units_sum_copy = units_copy(2, units_near)

    def units_tile(turn, unused):
        step = jnp.where(turn < 2, 3 - 2 * turn, 6 - 2 * turn)
        tile = place.other_group(step)
        grad_units[tile, 0 : 2 * units, :] = dot_f32(
            units_t[units : 3 * units, :], normed_ffn[:, rows_of(tile, shard)], 1, 0
        ).astype(jnp.bfloat16)

        for at, step in ((0, 3), (1, 1)):
            pl.when((turn == at) & place.near(step))(units_direct(step).start)
            pl.when((turn == at) & (group == 3 - step // 2 * 3))(units_far_copy.start)
        pl.when((turn == 2) & place.at_end())(units_direct(2).start)
        return unused

    lax.fori_loop(0, devices_fsdp, units_tile, 0)

    total = sums.collect()
    values = hidden[...]
    factor = lax.rsqrt(jnp.mean(values * values, axis=-1, keepdims=True) + epsilon)
    scaled = total * gain_two
    gain_part = jnp.sum(total * values * factor, axis=0, keepdims=True)
    whole = (
        grads[rows_of(me), :].astype(jnp.float32)
        + factor * scaled
        - values * (factor * factor * factor) * jnp.mean(scaled * values, axis=-1, keepdims=True)
    )
    grad_hidden[...] = whole
    grad_branch[...] = whole.astype(jnp.bfloat16)
    grad_rows[...] = (
        dot_f32(grad_branch[...], output_all[...].reshape(width, width), 1, 1)
        .astype(jnp.bfloat16)
        .reshape(grad_rows.shape)
    )
    to_heads = swap(
        lambda flip: grad_rows.at[:, :, rows_of(place.peer(flip), cols)],
        grad_attn.at[pl.ds(me * held, held)],
        b_send,
        b_recv,
    )
    for spread in (spread_g, spread_o, attn_first, attn_second, attn_third):
        spread.sent()
    sums.sent()
    for copy in to_heads:
        copy.start()
    grad_attn[pl.ds(me * held, held)] = grad_rows[:, :, my_cols]

    for index in range(devices_fsdp):
        piece = attn_rows[:, index * shard : (index + 1) * shard].T
        grad_output[index] = (
            dot_f32(piece, grad_branch[...], 1, 0)
            .astype(jnp.bfloat16)
            .reshape(8, shard // 8, width)
        )
    for copy in to_heads:
        copy.wait_recv()
    for index in range(8):
        group_sent(index)
    for copy in to_heads:
        copy.wait_send()

    def over_groups(source, target, send, recv):
        return [
            remote(
                source(place.other_group(step)),
                target.at[group],
                send.at[step - 1],
                recv.at[step - 1],
                {"fsdp": place.other_group(step)},
            )
            for step in range(1, devices_fsdp)
        ]

    def units_between():
        @pl.when(place.between())
        def _():
            units_far_copy.wait_recv()
            units_near[...] = (
                grad_units[place.other_group(2)].astype(jnp.float32)
                + units_far[...].astype(jnp.float32)
            ).astype(jnp.bfloat16)
            units_sum_copy.start()

    sums = CrossSum(
        place,
        lambda pair: (pair // 2, lax.rem(pair, 2)),
        stage,
        landed,
        norm_sums,
        norm_received,
        norm_passed,
        back_pair_send,
        back_pair_recv,
        back_out_send,
        back_out_recv,
    )
    output_pairs = OutputSum(
        place,
        grad_output,
        output_landed,
        output_sums,
        output_received,
        wo_send,
        wo_recv,
        wo_out_send,
        wo_out_recv,
    )
    for pair in range(4):
        output_pairs.exchange(pair).start()
    layer_copies = [
        remote(
            layer_sums.at[pair],
            attn_all.at[pair * held : (pair + 1) * held],
            layer_send.at[pair],
            layer_recv.at[pair],
            {"ctx": sums.mine(pair)},
        )
        for pair in range(1, 4)
    ]
    for copy in layer_copies:
        copy.start()

    def after_prompt():
        for pair in range(4):
            output_pairs.exchange(pair).wait_recv()
            output_sums[pair] = (
                grad_output[:, output_pairs.mine(pair)].astype(jnp.float32)
                + output_landed[pair].astype(jnp.float32)
            ).astype(jnp.bfloat16)
            if pair:
                output_pairs.deliver(pair).start()

    def half_of(ref, lines):
        def region(block, half):
            return ref.at[block] if half is None else ref.at[block, halves(lines)(half)]

        return region

    def own_of(ref, lines):
        return lambda half: ref if half is None else ref.at[halves(lines)(half)]

    spread_u = Spread(
        place,
        own_of(units_stage, 3 * units),
        half_of(units_out, 3 * units),
        u_send,
        u_recv,
    )
    save_units = pltpu.make_async_copy(units_stage, units_out.at[me], save_sem.at[0])
    output_copies = over_groups(
        lambda to: output_total.at[to], output_group, late_send.at[1], late_recv.at[1]
    )

    def before_last():
        total = output_sums[0].astype(jnp.float32)
        for pair in range(1, 4):
            output_pairs.deliver(pair).wait_recv()
            total = total + output_received[pair].astype(jnp.float32)
        output_total[...] = total.astype(jnp.bfloat16)
        for copy in output_copies:
            copy.start()
        units_landed[group] = grad_units[group]

        @pl.when(place.at_end())
        def _():
            units_landed[devices_fsdp - 1 - group] = jnp.zeros_like(grad_units[group])

        units_direct(2).wait_recv()
        for step in (1, 3):
            pl.when(place.heard(step))(units_direct(step).wait_recv)
        units_total = units_landed[0].astype(jnp.float32)
        for index in range(1, devices_fsdp):
            units_total = units_total + units_landed[index].astype(jnp.float32)
        units_stage[...] = units_total.astype(jnp.bfloat16)

        spread_u.start()
        save_units.start()

    attend_backward(
        per_segment,
        slot_of,
        block_of,
        length_ref,
        qkv,
        grad_attn,
        attn_t,
        lse,
        grads,
        query,
        key,
        kept,
        grad,
        value_t,
        own_sum,
        {
            per_segment // 2: units_between,
            per_segment: after_prompt,
            2 * per_segment - 1: before_last,
        },
    )

    def turn(tile, unused):
        at = rows_of(tile, TILE)
        units_t[0 : 3 * cols, at] = grads[at, 0 : 3 * cols].T
        return unused

    lax.fori_loop(0, grads.shape[0] // TILE, turn, 0)
    load_normed.wait()

    def weight_tile(tile, unused):
        at = rows_of(tile, shard)
        normed_ffn[0 : 3 * cols, at] = dot_f32(
            units_t[0 : 3 * cols, :], rows_all[:, at], 1, 0
        ).astype(jnp.bfloat16)
        return unused

    def qkv_parts(to):
        return normed_ffn.at[0 : 3 * cols, rows_of(to, shard)]

    lax.fori_loop(0, devices_fsdp, weight_tile, 0)
    qkv_copies = over_groups(
        qkv_parts, qkv_landed, late_send.at[0], late_recv.at[0]
    )
    for copy in qkv_copies:
        copy.start()
    spread_u.relay_first()

    def one_pair(step, unused):
        pair = 3 - step
        stage[pair // 2, lax.rem(pair, 2)] = dot_f32(
            grads[rows_of(sums.theirs(pair)), 0 : 3 * cols], w_qkv[...], 1, 1
        ).astype(jnp.bfloat16)
        sums.exchange(pair).start()
        return unused

    lax.fori_loop(0, 4, one_pair, 0)
    spread_u.relay_second()

    def sum_pair(step, unused):
        pair = 3 - step
        own_sum[0] = dot_f32(grads[rows_of(sums.mine(pair)), 0 : 3 * cols], w_qkv[...], 1, 1)
        sums.exchange(pair).wait_recv()
        sums.finish(
            pair, own_sum[0] + landed[pair // 2, lax.rem(pair, 2)].astype(jnp.float32)
        )
        return unused

    lax.fori_loop(0, 4, sum_pair, 0)

    def group_sum(own, landed_ref, copies):
        landed_ref[group] = own
        for copy in copies:
            copy.wait_recv()
        total = landed_ref[0].astype(jnp.float32)
        for index in range(1, devices_fsdp):
            total = total + landed_ref[index].astype(jnp.float32)
        return total

    total = layer_sums[0].astype(jnp.float32)
    for pair, copy in enumerate(layer_copies):
        copy.wait_recv()
        at = slice((pair + 1) * held, (pair + 2) * held)
        total = total + attn_all[at].astype(jnp.float32)
    grad_rows[...] = (hidden[...].reshape(total.shape) + total).astype(jnp.bfloat16)
    save_layer = pltpu.make_async_copy(grad_rows, layer, save_sem.at[2])
    save_layer.start()

    spread_u.relay_third()
    turned = group_sum(qkv_parts(group)[...], qkv_landed, qkv_copies).T.astype(jnp.bfloat16)
    for index in range(3):
        columns_stage[index * shard : (index + 1) * shard, :] = turned[
            :, index * cols : (index + 1) * cols
        ]
    summed = group_sum(output_total[group], output_group, output_copies).astype(jnp.bfloat16)
    lines = shard // 8
    for index in range(8):
        columns_stage[3 * shard + index * lines : 3 * shard + (index + 1) * lines, :] = summed[
            :, index * cols : (index + 1) * cols
        ]
    spread_c = Spread(
        place, own_of(columns_stage, 4 * shard), half_of(columns_out, 4 * shard), c_send, c_recv
    )
    spread_c.start()
    save_columns = pltpu.make_async_copy(columns_stage, columns_out.at[me], save_sem.at[1])
    save_columns.start()
    total = sums.collect()
    values = patches[...].astype(jnp.float32)
    factor = lax.rsqrt(jnp.mean(values * values, axis=-1, keepdims=True) + epsilon)
    scaled = total * gain_one
    gain_parts[...] = jnp.zeros_like(gain_parts)
    attn_part = jnp.sum(total * values * factor, axis=0, keepdims=True)
    ffn_part = gain_part
    for index in range(devices_fsdp):
        at = slice(index * shard, (index + 1) * shard)
        gain_parts[index, 0:1, :] = attn_part[:, at]
        gain_parts[index, 1:2, :] = ffn_part[:, at]
    gain_copies = over_groups(lambda to: gain_parts.at[to], gain_landed, gain_send, gain_recv)
    for copy in gain_copies:
        copy.start()
    spread_c.relay_first()
    grad_hidden[...] = (
        grad_hidden[...]
        + factor * scaled
        - values * (factor * factor * factor) * jnp.mean(scaled * values, axis=-1, keepdims=True)
    )
    save_rows = pltpu.make_async_copy(grad_hidden, grad_patches, save_sem.at[3])
    save_rows.start()
    spread_c.relay_second()
    gain_total[...] = group_sum(gain_parts[group], gain_landed, gain_copies)
    gain_out = [
        remote(
            gain_total,
            gain_all.at[me],
            gain_out_send.at[flip - 1],
            gain_out_recv.at[flip - 1],
            {"ctx": place.peer(flip)},
        )
        for flip in range(1, 8)
    ]
    for copy in gain_out:
        copy.start()
    gain_all[me] = gain_total[...]

    spread_c.relay_third()
    for copy in gain_out:
        copy.wait_recv()
    gain_sum = gain_all[0]
    for index in range(1, 8):
        gain_sum = gain_sum + gain_all[index]
    gains_out[...] = gain_sum
    spread_u.arrived(0, 7, 8, 9)
    spread_c.arrived(0, 7, 8, 9)
    for step in (1, 3):
        pl.when(place.near(step))(units_direct(step).wait_send)
    units_direct(2).wait_send()
    pl.when(place.at_end())(units_far_copy.wait_send)
    for copy in layer_copies + qkv_copies + output_copies + gain_copies + gain_out:
        copy.wait_send()
    for pair in range(4):
        sums.exchange(pair).wait_send()
    sums.sent()
    output_pairs.sent()
    save_layer.wait()
    save_rows.wait()
    spread_u.sent()
    spread_c.sent()
    save_units.wait()
    save_columns.wait()


def place_kernel(
    devices_fsdp,
    units_all,
    columns_all,
    layer,
    grad_rows,
    gains,
    out_layer,
    out_rows,
    out_query,
    out_key,
    out_value,
    out_output,
    out_gate,
    out_up,
    out_down,
    out_gain_attn,
    out_gain_ffn,
    units_held,
    columns_held,
    layer_held,
    rows_held,
    columns,
    outputs,
    natural,
    gate,
    up,
    down,
    load_sems,
    sems,
):
    shard = out_query.shape[0]
    cols = columns_all.shape[2]
    lines = shard // 8
    units = units_all.shape[1] // 3
    part = units // devices_fsdp
    span = part * 8
    loads = []
    saves = []

    def load(source, target):
        copy = pltpu.make_async_copy(source, target, load_sems.at[len(loads)])
        copy.start()
        loads.append(copy)

    def save(source, target):
        copy = pltpu.make_async_copy(source, target, sems.at[len(saves)])
        copy.start()
        saves.append(copy)

    for which in (2, 0, 1):
        load(units_all.at[:, which * units : (which + 1) * units], units_held.at[which])
    load(columns_all, columns_held)
    load(grad_rows, rows_held)
    load(layer, layer_held)
    out_gain_attn[...] = gains[0, :]
    out_gain_ffn[...] = gains[1, :]
    loads[0].wait()
    for index in range(8):
        piece = units_held[2, index].astype(jnp.float32)
        for tile in range(devices_fsdp):
            down[index * part : (index + 1) * part, tile * shard : (tile + 1) * shard] = piece[
                tile * part : (tile + 1) * part, :
            ]
    save(down, out_down)
    for which, (target, out) in enumerate(((gate, out_gate), (up, out_up))):
        loads[1 + which].wait()
        for index in range(8):
            piece = units_held[which, index].astype(jnp.float32)
            for tile in range(devices_fsdp):
                first = tile * span + index * part
                natural[first : first + part, :] = piece[tile * part : (tile + 1) * part, :]
        for first in range(0, span * devices_fsdp, 128):
            target[:, first : first + 128] = natural[first : first + 128, :].T
        save(target, out)
    loads[4].wait()
    save(rows_held, out_rows)
    loads[5].wait()
    save(layer_held, out_layer)
    loads[3].wait()
    for index in range(8):
        at = slice(index * cols, (index + 1) * cols)
        for which in range(3):
            columns[which, :, at] = columns_held[
                index, which * shard : (which + 1) * shard, :
            ].astype(jnp.float32)
        for tile in range(8):
            first = 3 * shard + tile * lines
            outputs[index * lines : (index + 1) * lines, tile * cols : (tile + 1) * cols] = (
                columns_held[index, first : first + lines, :].astype(jnp.float32)
            )
    save(columns.at[0], out_query)
    save(columns.at[1], out_key)
    save(columns.at[2], out_value)
    save(outputs, out_output)
    for copy in saves:
        copy.wait()


def heads_plan(
    patches,
    cotangent,
    deal_table,
    prompt_len,
    w_query,
    w_key,
    w_value,
    w_output,
    w_gate,
    w_up,
    w_down,
    gain_attn,
    gain_ffn,
):
    local_rows = patches.shape[1]
    width = patches.shape[2]
    groups = lax.axis_size("fsdp")
    rows = local_rows * 8
    cols = width // 8
    shard = width // groups
    part = w_down.shape[0] // 8
    units = part * groups
    tiles = rows // TILE
    blocks = deal_table.shape[0]
    block_len = rows // blocks
    per_segment = CONT_LEN // TILE
    smem = pl.BlockSpec(memory_space=pltpu.SMEM)
    vmem = pl.BlockSpec(memory_space=pltpu.VMEM)
    anywhere = pl.BlockSpec(memory_space=pl.ANY)
    low, full = jnp.bfloat16, jnp.float32

    def shaped(kind, *dims):
        return jax.ShapeDtypeStruct(dims, kind)

    def room(kind, *dims):
        return pltpu.VMEM(dims, kind)

    unused, layer, grad_rows, units_all, columns_all, gains_sum = pl.pallas_call(
        functools.partial(layer_kernel, per_segment, groups),
        out_shape=(
            shaped(low, rows, width),
            shaped(low, blocks // 8, block_len, width),
            shaped(full, local_rows, width),
            shaped(low, 8, 3 * units, shard),
            shaped(low, 8, 4 * shard, cols),
            shaped(full, 8, shard),
        ),
        in_specs=[smem] * 2 + [vmem] + [anywhere] * 8 + [vmem] * 2,
        out_specs=(anywhere,) * 5 + (vmem,),
        scratch_shapes=[
            room(low, blocks, block_len, 3 * cols),
            room(full, tiles, cols, TILE),
            room(full, tiles, 1, 2 * TILE),
            room(low, groups, 3 * units, shard),
            room(low, groups, 8, shard // 8, width),
            room(low, 4, blocks // 8, block_len, width),
            room(full, local_rows, width),
            room(full, local_rows, width),
            room(low, rows, width),
            room(low, rows, width),
            room(low, rows, width),
            room(low, blocks, block_len, width),
            room(low, width, 3 * cols),
            room(low, groups, 8, shard // 8, width),
            room(low, units, width),
            room(low, units, width),
            room(low, units, width),
            room(low, groups, part, width),
            room(low, units, shard),
            room(low, units, shard),
            room(full, 16, shard),
            room(full, 16, width),
            room(low, blocks, block_len, cols),
            room(low, blocks, block_len, cols),
            room(low, tiles, cols, TILE),
            room(low, blocks, block_len, cols),
            room(low, blocks, block_len, cols),
            room(low, local_rows, width),
            room(low, 3 * units, rows),
            room(low, 2, 2, local_rows, width),
            room(low, 2, 2, local_rows, width),
            room(full, 2, local_rows, width),
            room(low, 4, local_rows, width),
            room(low, 2, local_rows, width),
            room(low, 2, local_rows // 2, width),
            room(low, local_rows, width),
            room(low, blocks // 8, block_len, width),
            room(low, blocks, block_len, cols),
            room(low, groups, 3 * units, shard),
            room(low, 3 * units, shard),
            room(low, 3 * units, shard),
            room(low, 3 * units, shard),
            room(low, 4, groups, shard // 8, width),
            room(low, 4, groups, shard // 8, width),
            room(low, 4, groups, shard // 8, width),
            room(low, groups, shard // 8, width),
            room(low, groups, shard // 8, width),
            room(low, groups, 3 * cols, shard),
            room(low, 4 * shard, cols),
            room(full, groups, 8, shard),
            room(full, groups, 8, shard),
            room(full, 8, shard),
            room(full, 8, 8, shard),
            dma(9),
            dma(4),
            dma(2 * groups),
            pltpu.SemaphoreType.DMA((8, groups - 1)),
            pltpu.SemaphoreType.DMA((8, groups - 1)),
            dma(8),
            dma(10),
            dma(10),
            dma(10),
            dma(10),
            dma(10),
            dma(10),
            dma(10),
            dma(10),
            dma(10),
            dma(10),
            dma(10),
            dma(10),
            dma(10),
            dma(10),
            dma(10),
            dma(10),
            dma(7),
            dma(7),
            dma(7),
            dma(7),
            dma(4),
            dma(4),
            dma(4),
            dma(4),
            dma(4),
            dma(4),
            dma(4),
            dma(4),
            dma(4),
            dma(4),
            dma(4),
            dma(4),
            dma(4),
            dma(4),
            dma(groups - 1),
            dma(groups - 1),
            dma(groups - 1),
            dma(groups - 1),
            dma(2),
            pltpu.SemaphoreType.DMA((2, groups - 1)),
            pltpu.SemaphoreType.DMA((2, groups - 1)),
        ],
        compiler_params=pltpu.CompilerParams(
            collective_id=0, has_side_effects=True, vmem_limit_bytes=67_000_000
        ),
        name="layer",
    )(
        deal_table,
        prompt_len,
        patches[0],
        cotangent[0],
        w_query,
        w_key,
        w_value,
        w_output.reshape(8, shard // 8, width),
        w_gate,
        w_up,
        w_down.reshape(8, part, width),
        gain_attn,
        gain_ffn,
    )

    results = pl.pallas_call(
        functools.partial(place_kernel, groups),
        out_shape=(
            shaped(low, blocks // 8, block_len, width),
            shaped(full, local_rows, width),
        )
        + tuple(shaped(full, shard, width) for _ in range(4))
        + tuple(shaped(full, shard, 8 * units) for _ in range(2))
        + (shaped(full, 8 * part, width), shaped(full, shard), shaped(full, shard)),
        in_specs=[anywhere] * 4 + [vmem],
        out_specs=(anywhere,) * 9 + (vmem,) * 2,
        scratch_shapes=[
            room(low, 3, 8, units, shard),
            room(low, 8, 4 * shard, cols),
            room(low, blocks // 8, block_len, width),
            room(full, local_rows, width),
            room(full, 3, shard, width),
            room(full, shard, width),
            room(full, 8 * units, shard),
            room(full, shard, 8 * units),
            room(full, shard, 8 * units),
            room(full, 8 * part, width),
            dma(6),
            dma(9),
        ],
        name="place",
    )(units_all, columns_all, layer, grad_rows, gains_sum)
    return (results[0].reshape(1, local_rows, width), results[1][None]) + tuple(results[2:])


def solution(mesh):
    if mesh.shape["ctx"] == 8 and mesh.shape["fsdp"] == 4:
        per_device = heads_plan
    else:
        per_device = rows_plan
    placed = (
        P("fsdp", "ctx", None),
        P("fsdp", "ctx", None),
        P(),
        P("fsdp"),
        P("fsdp", None),
        P("fsdp", None),
        P("fsdp", None),
        P("fsdp", None),
        P("fsdp", None),
        P("fsdp", None),
        P("fsdp", None),
        P("fsdp"),
        P("fsdp"),
    )
    return jax.shard_map(
        per_device,
        mesh=mesh,
        in_specs=placed,
        out_specs=(
            P("fsdp", "ctx", None),
            P("fsdp", "ctx", None),
            P("fsdp", None),
            P("fsdp", None),
            P("fsdp", None),
            P("fsdp", None),
            P("fsdp", None),
            P("fsdp", None),
            P("fsdp", None),
            P("fsdp"),
            P("fsdp"),
        ),
        check_vma=False,
    )
```

```python
import functools
import math

import jax
import jax.numpy as jnp
from jax import lax
from jax.experimental import pallas as pl
from jax.experimental.pallas import tpu as pltpu
from jax.sharding import PartitionSpec as P

HEADS = 16
HEAD = 64
CONT_LEN = 1024


epsilon = 1e-05
score_scale = 0.125
masked_value = -1e30


def rms_forward(values, gain):
    factor = lax.rsqrt(jnp.mean(values * values, axis=-1, keepdims=True) + epsilon)
    return (values * factor * gain, factor)


def rms_backward(values, factor, gain, grad_normed):
    scaled = grad_normed * gain
    grad_gain = jnp.sum(grad_normed * values * factor, axis=0)
    cubed = factor * factor * factor
    grad_values = factor * scaled - values * cubed * jnp.mean(
        scaled * values, axis=-1, keepdims=True
    )
    return (grad_values, grad_gain)


def segment_of(position, prompt):
    return jnp.where(position < prompt, -1, (position - prompt) // CONT_LEN)


def visible(query_pos, key_pos, prompt, length):
    same = (segment_of(query_pos, prompt)[:, None] == segment_of(key_pos, prompt)[None, :]) & (
        key_pos[None, :] <= query_pos[:, None]
    )
    shared = (query_pos[:, None] >= prompt) & (key_pos[None, :] < length)
    return same | shared


def rows_plan(
    patches,
    cotangent,
    deal_table,
    prompt_len,
    w_query,
    w_key,
    w_value,
    w_output,
    w_gate,
    w_up,
    w_down,
    gain_attn,
    gain_ffn,
):
    local_rows = patches.shape[1]
    width = patches.shape[2]
    devices_ctx = lax.axis_size("ctx")
    group_tok = local_rows * devices_ctx
    cont_count = group_tok // (2 * CONT_LEN)
    prompt = group_tok - cont_count * CONT_LEN
    block_len = local_rows // 2
    slot_count = 2 * devices_ctx
    key_rows = math.gcd(512, group_tok)
    block_count = group_tok // key_rows
    length = prompt_len[0]

    def positions_of(first_row, count):
        stored = first_row + jnp.arange(count, dtype=jnp.int32)
        slot_ids = stored // block_len
        picked = jnp.where(
            slot_ids[:, None] == jnp.arange(slot_count, dtype=jnp.int32)[None, :],
            deal_table[None, :],
            0,
        )
        return jnp.sum(picked, axis=1) * block_len + stored % block_len

    query_pos = positions_of(lax.axis_index("ctx") * local_rows, local_rows)
    key_pos = positions_of(0, group_tok).reshape(block_count, key_rows)
    (
        full_query,
        full_key,
        full_value,
        full_output,
        full_gate,
        full_up,
        full_down,
        full_gain_attn,
        full_gain_ffn,
    ) = (
        lax.all_gather(w_query, "fsdp", axis=0, tiled=True),
        lax.all_gather(w_key, "fsdp", axis=0, tiled=True),
        lax.all_gather(w_value, "fsdp", axis=0, tiled=True),
        lax.all_gather(w_output, "fsdp", axis=0, tiled=True),
        lax.all_gather(w_gate, "fsdp", axis=0, tiled=True),
        lax.all_gather(w_up, "fsdp", axis=0, tiled=True),
        lax.all_gather(w_down, "fsdp", axis=0, tiled=True),
        lax.all_gather(gain_attn, "fsdp", axis=0, tiled=True),
        lax.all_gather(gain_ffn, "fsdp", axis=0, tiled=True),
    )
    rows_f32 = patches[0].astype(jnp.float32)
    gain_one = full_gain_attn.astype(jnp.float32)
    normed, factor_attn = rms_forward(rows_f32, gain_one)
    normed_low = normed.astype(jnp.bfloat16)
    queries = jnp.dot(normed_low, full_query, preferred_element_type=jnp.float32).astype(
        jnp.bfloat16
    )
    keys_local = jnp.dot(normed_low, full_key, preferred_element_type=jnp.float32).astype(
        jnp.bfloat16
    )
    values_local = jnp.dot(normed_low, full_value, preferred_element_type=jnp.float32).astype(
        jnp.bfloat16
    )
    key_all, value_all = (
        lax.all_gather(keys_local, "ctx", axis=0, tiled=True),
        lax.all_gather(values_local, "ctx", axis=0, tiled=True),
    )
    query_heads = queries.reshape(local_rows, HEADS, HEAD)

    def split_blocks(array):
        return array.reshape(block_count, key_rows, HEADS, HEAD)

    def forward_block(state, block):
        key_block, value_block, block_pos = block
        visible_mask = visible(query_pos, block_pos, prompt, length)

        def forward_update(inner_state):
            maxima, totals, accum = inner_state
            scores = (
                jnp.einsum(
                    "qhe,khe->hqk", query_heads, key_block, preferred_element_type=jnp.float32
                )
                * score_scale
            )
            scores = jnp.where(visible_mask[None], scores, masked_value)
            new_max = jnp.maximum(maxima, jnp.max(scores, axis=-1))
            rescale = jnp.exp(maxima - new_max)
            probs = jnp.where(visible_mask[None], jnp.exp(scores - new_max[:, :, None]), 0.0)
            totals = totals * rescale + jnp.sum(probs, axis=-1)
            accum = accum * rescale.T[:, :, None] + jnp.einsum(
                "hqk,khe->qhe",
                probs.astype(jnp.bfloat16),
                value_block,
                preferred_element_type=jnp.float32,
            )
            return (new_max, totals, accum)

        return (
            lax.cond(jnp.any(visible_mask), forward_update, lambda inner_state: inner_state, state),
            None,
        )

    start_state = (
        jnp.full((HEADS, local_rows), masked_value, jnp.float32),
        jnp.zeros((HEADS, local_rows), jnp.float32),
        jnp.zeros((local_rows, HEADS, HEAD), jnp.float32),
    )
    (maxima, totals, accum), unused = lax.scan(
        forward_block, start_state, (split_blocks(key_all), split_blocks(value_all), key_pos)
    )
    attn_f32 = accum / totals.T[:, :, None]
    log_total = maxima + jnp.log(totals)
    attn_low = attn_f32.astype(jnp.bfloat16).reshape(local_rows, width)
    hidden = rows_f32 + jnp.dot(attn_low, full_output, preferred_element_type=jnp.float32)
    gain_two = full_gain_ffn.astype(jnp.float32)
    normed_ffn, factor_ffn = rms_forward(hidden, gain_two)
    ffn_low = normed_ffn.astype(jnp.bfloat16)
    gate = jnp.dot(ffn_low, full_gate, preferred_element_type=jnp.float32)
    up_proj = jnp.dot(ffn_low, full_up, preferred_element_type=jnp.float32)
    sigmoid = jax.nn.sigmoid(gate)
    activated = gate * sigmoid
    inner_low = (activated * up_proj).astype(jnp.bfloat16)
    layer = hidden + jnp.dot(inner_low, full_down, preferred_element_type=jnp.float32)
    grad_out = cotangent[0].astype(jnp.float32)
    grad_down_in = cotangent[0]
    grad_w_down = jnp.dot(inner_low.T, grad_down_in, preferred_element_type=jnp.float32)
    grad_inner = jnp.dot(grad_down_in, full_down.T, preferred_element_type=jnp.float32)
    grad_gate = (grad_inner * up_proj * sigmoid * (1.0 + gate * (1.0 - sigmoid))).astype(
        jnp.bfloat16
    )
    grad_up = (grad_inner * activated).astype(jnp.bfloat16)
    grad_w_gate = jnp.dot(ffn_low.T, grad_gate, preferred_element_type=jnp.float32)
    grad_w_up = jnp.dot(ffn_low.T, grad_up, preferred_element_type=jnp.float32)
    grad_normed_ffn = jnp.dot(grad_gate, full_gate.T, preferred_element_type=jnp.float32) + jnp.dot(
        grad_up, full_up.T, preferred_element_type=jnp.float32
    )
    grad_hidden_norm, grad_gain_ffn = rms_backward(hidden, factor_ffn, gain_two, grad_normed_ffn)
    grad_hidden = grad_out + grad_hidden_norm
    grad_branch = grad_hidden.astype(jnp.bfloat16)
    grad_w_output = jnp.dot(attn_low.T, grad_branch, preferred_element_type=jnp.float32)
    grad_attn = (
        jnp.dot(grad_branch, full_output.T, preferred_element_type=jnp.float32)
        .astype(jnp.bfloat16)
        .reshape(local_rows, HEADS, HEAD)
    )
    delta = jnp.einsum("qhe,qhe->hq", grad_attn.astype(jnp.float32), attn_f32)
    key_back, value_back = (key_all, value_all)

    def backward_block(grad_query, block):
        key_block, value_block, block_pos = block
        visible_mask = visible(query_pos, block_pos, prompt, length)

        def backward_update(grad_state):
            scores = (
                jnp.einsum(
                    "qhe,khe->hqk", query_heads, key_block, preferred_element_type=jnp.float32
                )
                * score_scale
            )
            probs = jnp.where(visible_mask[None], jnp.exp(scores - log_total[:, :, None]), 0.0)
            grad_probs = jnp.einsum(
                "qhe,khe->hqk", grad_attn, value_block, preferred_element_type=jnp.float32
            )
            grad_scores = (probs * (grad_probs - delta[:, :, None])).astype(jnp.bfloat16)
            grad_state = (
                grad_state
                + jnp.einsum(
                    "hqk,khe->qhe", grad_scores, key_block, preferred_element_type=jnp.float32
                )
                * score_scale
            )
            grad_keys = (
                jnp.einsum(
                    "hqk,qhe->khe", grad_scores, query_heads, preferred_element_type=jnp.float32
                )
                * score_scale
            )
            grad_values = jnp.einsum(
                "hqk,qhe->khe",
                probs.astype(jnp.bfloat16),
                grad_attn,
                preferred_element_type=jnp.float32,
            )
            return (grad_state, (grad_keys, grad_values))

        def skipped(grad_state):
            empty = jnp.zeros((key_rows, HEADS, HEAD), jnp.float32)
            return (grad_state, (empty, empty))

        return lax.cond(jnp.any(visible_mask), backward_update, skipped, grad_query)

    zero_query = jnp.zeros((local_rows, HEADS, HEAD), jnp.float32)
    grad_query, (grad_key_blocks, grad_value_blocks) = lax.scan(
        backward_block, zero_query, (split_blocks(key_back), split_blocks(value_back), key_pos)
    )
    grad_key_sum, grad_value_sum = (
        lax.psum_scatter(
            grad_key_blocks.reshape(group_tok, width).astype(jnp.bfloat16),
            "ctx",
            scatter_dimension=0,
            tiled=True,
        ).astype(jnp.float32),
        lax.psum_scatter(
            grad_value_blocks.reshape(group_tok, width).astype(jnp.bfloat16),
            "ctx",
            scatter_dimension=0,
            tiled=True,
        ).astype(jnp.float32),
    )
    grad_key_low = grad_key_sum.astype(jnp.bfloat16)
    grad_value_low = grad_value_sum.astype(jnp.bfloat16)
    grad_query_low = grad_query.reshape(local_rows, width).astype(jnp.bfloat16)
    grad_w_query = jnp.dot(normed_low.T, grad_query_low, preferred_element_type=jnp.float32)
    grad_w_key = jnp.dot(normed_low.T, grad_key_low, preferred_element_type=jnp.float32)
    grad_w_value = jnp.dot(normed_low.T, grad_value_low, preferred_element_type=jnp.float32)
    grad_normed = (
        jnp.dot(grad_query_low, full_query.T, preferred_element_type=jnp.float32)
        + jnp.dot(grad_key_low, full_key.T, preferred_element_type=jnp.float32)
        + jnp.dot(grad_value_low, full_value.T, preferred_element_type=jnp.float32)
    )
    grad_rows_norm, grad_gain_attn = rms_backward(rows_f32, factor_attn, gain_one, grad_normed)
    grad_rows = grad_hidden + grad_rows_norm
    shards = (
        lax.psum_scatter(
            grad_w_query.astype(jnp.bfloat16), "fsdp", scatter_dimension=0, tiled=True
        ).astype(jnp.float32),
        lax.psum_scatter(
            grad_w_key.astype(jnp.bfloat16), "fsdp", scatter_dimension=0, tiled=True
        ).astype(jnp.float32),
        lax.psum_scatter(
            grad_w_value.astype(jnp.bfloat16), "fsdp", scatter_dimension=0, tiled=True
        ).astype(jnp.float32),
        lax.psum_scatter(
            grad_w_output.astype(jnp.bfloat16), "fsdp", scatter_dimension=0, tiled=True
        ).astype(jnp.float32),
        lax.psum_scatter(
            grad_w_gate.astype(jnp.bfloat16), "fsdp", scatter_dimension=0, tiled=True
        ).astype(jnp.float32),
        lax.psum_scatter(
            grad_w_up.astype(jnp.bfloat16), "fsdp", scatter_dimension=0, tiled=True
        ).astype(jnp.float32),
        lax.psum_scatter(
            grad_w_down.astype(jnp.bfloat16), "fsdp", scatter_dimension=0, tiled=True
        ).astype(jnp.float32),
        lax.psum_scatter(
            grad_gain_attn.astype(jnp.bfloat16), "fsdp", scatter_dimension=0, tiled=True
        ).astype(jnp.float32),
        lax.psum_scatter(
            grad_gain_ffn.astype(jnp.bfloat16), "fsdp", scatter_dimension=0, tiled=True
        ).astype(jnp.float32),
    )
    summed = (
        lax.psum(shards[0].astype(jnp.bfloat16), "ctx").astype(jnp.float32),
        lax.psum(shards[1].astype(jnp.bfloat16), "ctx").astype(jnp.float32),
        lax.psum(shards[2].astype(jnp.bfloat16), "ctx").astype(jnp.float32),
        lax.psum(shards[3].astype(jnp.bfloat16), "ctx").astype(jnp.float32),
        lax.psum(shards[4].astype(jnp.bfloat16), "ctx").astype(jnp.float32),
        lax.psum(shards[5].astype(jnp.bfloat16), "ctx").astype(jnp.float32),
        lax.psum(shards[6].astype(jnp.bfloat16), "ctx").astype(jnp.float32),
        lax.psum(shards[7].astype(jnp.bfloat16), "ctx").astype(jnp.float32),
        lax.psum(shards[8].astype(jnp.bfloat16), "ctx").astype(jnp.float32),
    )
    return (
        layer.astype(jnp.bfloat16)[None],
        grad_rows[None],
        summed[0],
        summed[1],
        summed[2],
        summed[3],
        summed[4],
        summed[5],
        summed[6],
        summed[7],
        summed[8],
    )


TILE = 256


def dot_f32(left, right, left_dim, right_dim):
    return lax.dot_general(
        left,
        right,
        (((left_dim,), (right_dim,)), ((), ())),
        preferred_element_type=jnp.float32,
    )


def head_masks():
    lane = lax.broadcasted_iota(jnp.int32, (TILE, 2 * HEAD), 1)
    first = (lane < HEAD).astype(jnp.bfloat16)
    return first, (1 - first).astype(jnp.bfloat16)


def stack_heads(tile, masks):
    return jnp.concatenate([tile * masks[0], tile * masks[1]], axis=0)


def tile_mask(kind, tile, length):
    row = lax.broadcasted_iota(jnp.int32, (TILE, 2 * TILE), 0)
    if kind == "diagonal":
        column = lax.broadcasted_iota(jnp.int32, (TILE, 2 * TILE), 1)
        return row <= jnp.where(column < TILE, column, column - TILE)
    return row + tile * TILE < length


def over_keys(tile, per_segment, step, state):
    base = tile // per_segment * per_segment
    state = lax.fori_loop(0, base, lambda key, kept: step(key, kept, "prompt"), state)
    state = lax.fori_loop(base, tile, lambda key, kept: step(key, kept, "full"), state)
    return step(tile, state, "diagonal")


def load_tile(ref, tile):
    held = TILE // ref.shape[1]
    return ref[pl.ds(tile * held, held)].reshape(TILE, ref.shape[2])


def store_tile(ref, tile, values):
    held = TILE // ref.shape[1]
    ref[pl.ds(tile * held, held)] = values.reshape(held, ref.shape[1], ref.shape[2])


def to_logical(slot_of, source, column, target, scale=None):
    for block in range(target.shape[0]):
        picked = source[slot_of[block], :, column : column + 2 * HEAD]
        if scale is not None:
            picked = picked * scale
        target[block] = picked


def to_stored(block_of, source, target, column):
    block_len = source.shape[1]
    for slot in range(source.shape[0]):
        target[slot * block_len : (slot + 1) * block_len, column : column + 2 * HEAD] = source[
            block_of[slot]
        ]


def tiles_between(count, one_tile, between):
    first = 0
    for stop in sorted(between):
        lax.fori_loop(first, stop, one_tile, 0)
        between[stop]()
        first = stop
    lax.fori_loop(first, count, one_tile, 0)


def attend_forward(
    per_segment,
    slot_of,
    length_ref,
    qkv,
    attn_t,
    lse,
    query,
    key,
    value_t,
    kept,
    between,
):
    rows = qkv.shape[0] * qkv.shape[1]
    length = length_ref[0]
    to_logical(slot_of, qkv, 0, query, jnp.bfloat16(score_scale))
    to_logical(slot_of, qkv, 2 * HEAD, key)
    to_logical(slot_of, qkv, 4 * HEAD, kept)
    for tile in range(rows // TILE):
        value_t[tile] = load_tile(kept, tile).T
    masks = head_masks()

    def one_tile(tile, unused):
        both = stack_heads(load_tile(query, tile), masks)

        def step(key_tile, state, kind):
            maxima, totals, accum = state
            scores = dot_f32(load_tile(key, key_tile), both, 1, 1)
            if kind != "full":
                scores = jnp.where(tile_mask(kind, key_tile, length), scores, masked_value)
            new_max = jnp.maximum(maxima, jnp.max(scores, axis=0, keepdims=True))
            probs = jnp.exp(scores - new_max)
            rescale = jnp.exp(maxima - new_max)
            totals = totals * rescale + jnp.sum(probs, axis=0, keepdims=True)
            accum = accum * rescale + dot_f32(
                value_t[key_tile], probs.astype(jnp.bfloat16), 1, 0
            )
            return new_max, totals, accum

        maxima, totals, accum = over_keys(
            tile,
            per_segment,
            step,
            (
                jnp.full((1, 2 * TILE), masked_value, jnp.float32),
                jnp.zeros((1, 2 * TILE), jnp.float32),
                jnp.zeros((2 * HEAD, 2 * TILE), jnp.float32),
            ),
        )
        accum = accum / totals
        feature = lax.broadcasted_iota(jnp.int32, (2 * HEAD, TILE), 0)
        picked = jnp.where(feature < HEAD, accum[:, :TILE], accum[:, TILE:])
        attn_t[tile] = picked
        lse[tile] = maxima + jnp.log(totals)
        store_tile(kept, tile, picked.T.astype(jnp.bfloat16))
        return unused

    tiles_between(rows // TILE, one_tile, between)


def attend_backward(
    per_segment,
    slot_of,
    block_of,
    length_ref,
    qkv,
    grad_attn,
    attn_t,
    lse,
    grad_qkv,
    query,
    key,
    value,
    grad,
    key_t,
    grad_sums,
    between,
):
    rows = qkv.shape[0] * qkv.shape[1]
    length = length_ref[0]
    to_logical(slot_of, qkv, 0, query, jnp.bfloat16(score_scale))
    to_logical(slot_of, qkv, 2 * HEAD, key)
    to_logical(slot_of, qkv, 4 * HEAD, value)
    to_logical(slot_of, grad_attn, 0, grad)
    for tile in range(rows // TILE):
        key_t[tile] = load_tile(key, tile).T
    grad_sums[...] = jnp.zeros_like(grad_sums)
    masks = head_masks()

    def one_tile(tile, unused):
        both = stack_heads(load_tile(query, tile), masks)
        grad_tile = load_tile(grad, tile)
        both_grad = stack_heads(grad_tile, masks)
        product = grad_tile.astype(jnp.float32).T * attn_t[tile]
        delta = jnp.concatenate(
            [
                jnp.sum(product[:HEAD], axis=0, keepdims=True),
                jnp.sum(product[HEAD:], axis=0, keepdims=True),
            ],
            axis=1,
        )
        log_total = lse[tile]

        def step(key_tile, grad_query, kind):
            keys_at = pl.ds(pl.multiple_of(key_tile * 2 * HEAD, 2 * HEAD), 2 * HEAD)
            scores = dot_f32(load_tile(key, key_tile), both, 1, 1)
            if kind != "full":
                scores = jnp.where(tile_mask(kind, key_tile, length), scores, masked_value)
            probs = jnp.exp(scores - log_total)
            grad_probs = dot_f32(load_tile(value, key_tile), both_grad, 1, 1)
            grad_scores = (probs * (grad_probs - delta)).astype(jnp.bfloat16)
            grad_sums[1, :, keys_at] += dot_f32(probs.astype(jnp.bfloat16), both_grad, 1, 0)
            grad_sums[0, :, keys_at] += dot_f32(grad_scores, both, 1, 0)
            return grad_query + dot_f32(key_t[key_tile], grad_scores, 1, 0)

        grad_query = over_keys(
            tile, per_segment, step, jnp.zeros((2 * HEAD, 2 * TILE), jnp.float32)
        )
        feature = lax.broadcasted_iota(jnp.int32, (2 * HEAD, TILE), 0)
        picked = jnp.where(feature < HEAD, grad_query[:, :TILE], grad_query[:, TILE:])
        store_tile(query, tile, (picked * score_scale).T.astype(jnp.bfloat16))
        return unused

    tiles_between(rows // TILE, one_tile, between)
    for tile in range(rows // TILE):
        at = slice(tile * 2 * HEAD, (tile + 1) * 2 * HEAD)
        store_tile(key, tile, grad_sums[0, :, at].astype(jnp.bfloat16))
        store_tile(value, tile, grad_sums[1, :, at].astype(jnp.bfloat16))
    to_stored(block_of, query, grad_qkv, 0)
    to_stored(block_of, key, grad_qkv, 2 * HEAD)
    to_stored(block_of, value, grad_qkv, 4 * HEAD)


def dma(count):
    return pltpu.SemaphoreType.DMA((count,))


def flipped(bit, flip):
    return bit + flip - 2 * bit * flip


class Place:
    def __init__(self, devices_fsdp):
        self.me = lax.axis_index("ctx")
        self.core = lax.rem(self.me, 2)
        self.column = lax.rem(self.me // 2, 2)
        self.row = self.me // 4
        self.group = lax.axis_index("fsdp")
        self.groups = devices_fsdp

    def peer(self, flip):
        low, middle, high = flip % 2, flip // 2 % 2, flip // 4
        return (
            flipped(self.row, high) * 4
            + flipped(self.column, middle) * 2
            + flipped(self.core, low)
        )

    def other_group(self, step):
        return lax.rem(self.group + step, self.groups)

    def at_end(self):
        return lax.rem(self.group, 3) == 0

    def between(self):
        return lax.rem(self.group, 3) != 0

    def near(self, step):
        return self.group != {1: 3, 2: 4, 3: 0}[step]

    def heard(self, step):
        return self.group != {1: 0, 2: 4, 3: 3}[step]

    def meet(self):
        barrier = pltpu.get_barrier_semaphore()
        for flip in range(1, 8):
            pl.semaphore_signal(barrier, inc=1, device_id={"ctx": self.peer(flip)})
        for step in range(1, self.groups):
            pl.semaphore_signal(barrier, inc=1, device_id={"fsdp": self.other_group(step)})
        pl.semaphore_wait(barrier, 7 + self.groups - 1)


def remote(source, target, send, recv, device):
    return pltpu.make_async_remote_copy(
        src_ref=source,
        dst_ref=target,
        send_sem=send,
        recv_sem=recv,
        device_id=device,
        device_id_type=pl.DeviceIdType.MESH,
    )


class Spread:
    def __init__(self, place, own, region, send, recv):
        me, peer = place.me, place.peer

        def copy(index, source, target, flip):
            return remote(source, target, send.at[index], recv.at[index], {"ctx": peer(flip)})

        self.copies = [
            copy(0, own(None), region(me, None), 1),
            copy(1, own(0), region(me, 0), 2),
            copy(2, own(1), region(me, 1), 2),
            copy(3, own(1), region(me, 1), 4),
            copy(4, own(0), region(me, 0), 4),
            copy(5, region(peer(2), 0), region(peer(2), 0), 4),
            copy(6, region(peer(4), 1), region(peer(4), 1), 2),
            copy(7, region(peer(2), None), region(peer(2), None), 1),
            copy(8, region(peer(4), None), region(peer(4), None), 1),
            copy(9, region(peer(6), None), region(peer(6), None), 1),
        ]

    def start(self):
        for index in (1, 3, 0, 2, 4):
            self.copies[index].start()

    def arrived(self, *indices):
        for index in indices:
            self.copies[index].wait_recv()

    def relay_first(self):
        self.arrived(1)
        self.copies[5].start()
        self.arrived(3)
        self.copies[6].start()

    def relay_second(self):
        self.arrived(2)
        self.copies[7].start()
        self.arrived(4)
        self.copies[8].start()

    def relay_third(self):
        self.arrived(5, 6)
        self.copies[9].start()

    def sent(self):
        for copy in self.copies:
            copy.wait_send()


class PairSum:
    def __init__(self, place, stage, landed, sums, received, send, recv, out_send, out_recv):
        self.place = place
        self.slot = lambda pair: pair
        self.stage, self.landed, self.sums, self.received = stage, landed, sums, received
        self.send, self.recv, self.out_send, self.out_recv = send, recv, out_send, out_recv

    def mine(self, pair):
        place = self.place
        return (
            flipped(place.row, pair // 2) * 4
            + flipped(place.column, lax.rem(pair, 2)) * 2
            + place.core
        )

    def theirs(self, pair):
        return self.mine(pair) + 1 - 2 * self.place.core

    def staged(self, pair):
        return self.stage.at[self.slot(pair)]

    def exchange(self, pair):
        return remote(
            self.staged(pair),
            self.landed.at[self.slot(pair)],
            self.send.at[pair],
            self.recv.at[pair],
            {"ctx": self.place.peer(1)},
        )

    def deliver(self, pair):
        return remote(
            self.sums.at[pair],
            self.received.at[pair],
            self.out_send.at[pair],
            self.out_recv.at[pair],
            {"ctx": self.mine(pair)},
        )

    def sent(self):
        for pair in range(4):
            self.exchange(pair).wait_send()
            if pair:
                self.deliver(pair).wait_send()


class OutputSum(PairSum):
    def staged(self, pair):
        return self.stage.at[:, self.theirs(pair)]


class CrossSum(PairSum):
    def __init__(
        self, place, slot, stage, landed, sums, received, passed, send, recv, out_send, out_recv
    ):
        super().__init__(place, stage, landed, sums, received, send, recv, out_send, out_recv)
        self.slot = slot
        self.passed = passed

    def half(self, which):
        count = self.sums.shape[1] // 2
        return slice(which * count, (which + 1) * count)

    def far(self, which):
        slot = 3 * which
        return remote(
            self.sums.at[3, self.half(which)],
            self.passed.at[which],
            self.out_send.at[slot],
            self.out_recv.at[slot],
            {"ctx": self.place.peer(2 + 2 * which)},
        )

    def deliver(self, pair):
        return remote(
            self.sums.at[pair],
            self.received.at[pair - 1],
            self.out_send.at[pair],
            self.out_recv.at[pair],
            {"ctx": self.place.peer(2 * pair)},
        )

    def finish(self, pair, total):
        self.sums[pair] = total.astype(jnp.bfloat16)

        @pl.when(pair == 3)
        def _():
            self.far(0).start()
            self.far(1).start()

        for axis in (1, 2):
            which = 2 - axis

            @pl.when(pair == axis)
            def _(axis=axis, which=which):
                at = self.half(which)
                self.far(which).wait_recv()
                self.sums[axis, at, :] = (
                    total[at] + self.passed[which].astype(jnp.float32)
                ).astype(jnp.bfloat16)
                self.deliver(axis).start()

    def collect(self):
        total = self.sums[0].astype(jnp.float32)
        for pair in (1, 2):
            self.deliver(pair).wait_recv()
            total = total + self.received[pair - 1].astype(jnp.float32)
        return total

    def sent(self):
        for which in (0, 1):
            self.far(which).wait_send()
            self.deliver(which + 1).wait_send()


def halves(count):
    return lambda half: pl.ds(0 if half in (None, 0) else count // 2, count if half is None else count // 2)


def slots_of(block_of):
    count = block_of.shape[0]
    held = [block_of[slot] for slot in range(count)]
    slots = []
    for block in range(count):
        found = jnp.int32(0)
        for slot in range(1, count):
            found = jnp.where(held[slot] == block, jnp.int32(slot), found)
        slots.append(found)
    return slots


def layer_kernel(
    per_segment,
    devices_fsdp,
    block_of,
    length_ref,
    patches,
    cotangent,
    w_query,
    w_key,
    w_value,
    w_output,
    w_gate,
    w_up,
    w_down,
    gain_attn,
    gain_ffn,
    normed_out,
    layer,
    grad_patches,
    units_out,
    columns_out,
    gains_out,
    qkv,
    attn_t,
    lse,
    grad_units,
    grad_output,
    layer_sums,
    hidden,
    grad_hidden,
    rows_all,
    grads,
    normed_ffn,
    attn_all,
    w_qkv,
    output_all,
    gate_t,
    up_t,
    down,
    down_parts,
    gate_stage,
    up_stage,
    gain_stage,
    gains,
    query,
    key,
    value_t,
    kept,
    grad,
    attn_rows,
    units_t,
    stage,
    landed,
    own_sum,
    norm_sums,
    norm_received,
    norm_passed,
    grad_branch,
    grad_rows,
    grad_attn,
    units_landed,
    units_far,
    units_near,
    units_stage,
    output_landed,
    output_sums,
    output_received,
    output_total,
    output_group,
    qkv_landed,
    columns_stage,
    gain_parts,
    gain_landed,
    gain_total,
    gain_all,
    local_sem,
    save_sem,
    unit_sem,
    group_send,
    group_recv,
    pass_send,
    x_send,
    x_recv,
    g_send,
    g_recv,
    o_send,
    o_recv,
    first_send,
    first_recv,
    second_send,
    second_recv,
    third_send,
    third_recv,
    u_send,
    u_recv,
    c_send,
    c_recv,
    b_send,
    b_recv,
    gain_out_send,
    gain_out_recv,
    pair_send,
    pair_recv,
    out_send,
    out_recv,
    back_pair_send,
    back_pair_recv,
    back_out_send,
    back_out_recv,
    wo_send,
    wo_recv,
    wo_out_send,
    wo_out_recv,
    layer_send,
    layer_recv,
    units_send,
    units_recv,
    gain_send,
    gain_recv,
    far_sem,
    late_send,
    late_recv,
):
    place = Place(devices_fsdp)
    slot_of = slots_of(block_of)
    me, group = place.me, place.group
    local_rows, width = patches.shape
    cols = width // 8
    shard = w_query.shape[0]
    part = w_down.shape[1]
    units = part * devices_fsdp
    span = part * 8
    held = qkv.shape[0] // 8

    def unit_range(index):
        return span * index // 128 * 128, -(-span * (index + 1) // 128) * 128

    def unit_copies(weight, target, first):
        copies = []
        for index in range(devices_fsdp):
            low, high = unit_range(index)
            copies.append(
                pltpu.make_async_copy(
                    weight.at[:, low:high],
                    target.at[index // 2, index % 2, :, 0 : high - low],
                    unit_sem.at[first + index],
                )
            )
        return copies

    gate_copies = unit_copies(w_gate, stage, 0)
    up_copies = unit_copies(w_up, landed, devices_fsdp)
    for copy in gate_copies + up_copies:
        copy.start()
    place.meet()

    def rows_of(block, count=local_rows):
        return pl.ds(pl.multiple_of(block * count, count), count)

    def rows_half(ref):
        def region(block, half):
            start = block * local_rows + (local_rows // 2 if half == 1 else 0)
            count = local_rows if half is None else local_rows // 2
            return ref.at[pl.ds(pl.multiple_of(start, local_rows // 2), count)]

        return region

    def own_half(ref):
        return lambda half: ref.at[halves(local_rows)(half)]

    spread_x = Spread(place, own_half(patches), rows_half(rows_all), x_send, x_recv)
    spread_x.start()

    my_cols = rows_of(me, cols)
    def shard_of(index):
        return rows_of(index, shard)

    group_items = [
        (w_query.at[:, my_cols], lambda to: w_qkv.at[shard_of(to), 0:cols]),
        (w_key.at[:, my_cols], lambda to: w_qkv.at[shard_of(to), cols : 2 * cols]),
        (w_value.at[:, my_cols], lambda to: w_qkv.at[shard_of(to), 2 * cols : 3 * cols]),
        (gain_stage, lambda to: gains.at[:, shard_of(to)]),
        (w_output.at[me], lambda to: output_all.at[to, me]),
        (gate_stage, lambda to: gate_t.at[:, shard_of(to)]),
        (up_stage, lambda to: up_t.at[:, shard_of(to)]),
        (w_down.at[me], lambda to: down_parts.at[to]),
    ]

    def group_copy(index, step):
        source, target = group_items[index]
        return remote(
            source,
            target(group),
            group_send.at[index, step - 1],
            group_recv.at[index, step - 1],
            {"fsdp": place.other_group(step)},
        )

    def passed_copy(index):
        whose = place.other_group(2)
        held = group_items[index][1](whose)
        return remote(
            held,
            held,
            pass_send.at[index],
            group_recv.at[index, 2 * (group // 2)],
            {"fsdp": devices_fsdp - 1 - whose},
        )

    def local_copy(index):
        source, target = group_items[index]
        return pltpu.make_async_copy(source, target(group), local_sem.at[index])

    def send_group(index):
        group_copy(index, 2).start()
        for step in (1, 3):
            pl.when(place.near(step))(group_copy(index, step).start)
        local_copy(index).start()

    def pass_group(index):
        @pl.when(place.between())
        def _():
            group_copy(index, 2).wait_recv()
            passed_copy(index).start()

    def group_arrived(index):
        pl.when(place.at_end())(group_copy(index, 2).wait_recv)
        for step in (1, 3):
            group_copy(index, step).wait_recv()
        local_copy(index).wait()

    def group_sent(index):
        group_copy(index, 2).wait_send()
        for step in (1, 3):
            pl.when(place.near(step))(group_copy(index, step).wait_send)
        pl.when(place.between())(passed_copy(index).wait_send)

    for index in (0, 1, 2):
        send_group(index)
    gain_stage[0:8, :] = jnp.broadcast_to(gain_attn[...].astype(jnp.float32)[None], (8, shard))
    gain_stage[8:16, :] = jnp.broadcast_to(gain_ffn[...].astype(jnp.float32)[None], (8, shard))
    send_group(3)
    send_group(4)

    def pick_units(copies, source, target):
        pieces = []
        for index in range(devices_fsdp):
            low, high = unit_range(index)
            unit = lax.broadcasted_iota(jnp.int32, (part, high - low), 0)
            column = lax.broadcasted_iota(jnp.int32, (part, high - low), 1)
            chosen = (column + low == unit + span * index + part * me).astype(jnp.bfloat16)
            copies[index].wait()
            pieces.append(
                dot_f32(chosen, source[index // 2, index % 2, :, 0 : high - low], 1, 1)
            )
        target[...] = jnp.concatenate(pieces, axis=0).astype(jnp.bfloat16)

    pick_units(gate_copies, stage, gate_stage)
    pick_units(up_copies, landed, up_stage)
    send_group(5)
    send_group(6)
    send_group(7)

    rows_all[rows_of(me), :] = patches[...]
    load_grads = pltpu.make_async_copy(cotangent, grads.at[rows_of(me)], save_sem.at[0])
    load_grads.start()
    spread_x.relay_first()
    for index in (0, 1, 2, 3):
        pass_group(index)
    spread_x.relay_second()
    spread_g = Spread(place, own_half(cotangent), rows_half(grads), g_send, g_recv)
    spread_g.start()
    for index in (0, 1, 2, 3):
        group_arrived(index)
    gain_one = gains[0:1, :]

    def project(flip, unused):
        block = place.peer(flip)
        at = rows_of(block)
        values = rows_all[at, :].astype(jnp.float32)
        low = rms_forward(values, gain_one)[0].astype(jnp.bfloat16)
        normed_ffn[at, :] = low
        store_tile(qkv, block, dot_f32(low, w_qkv[...], 1, 0).astype(jnp.bfloat16))
        return unused

    lax.fori_loop(0, 3, lambda index, kept: project(2 * index, kept), 0)
    spread_x.relay_third()
    pass_group(4)

    def output_half(block, half):
        if half is None:
            return output_all.at[:, block]
        lines = output_all.shape[2]
        return output_all.at[:, block, halves(lines)(half)]

    group_arrived(4)
    spread_o = Spread(place, lambda half: output_half(me, half), output_half, o_send, o_recv)
    spread_o.start()

    spread_x.arrived(0, 7, 8)
    lax.fori_loop(0, 3, lambda index, kept: project(2 * index + 1, kept), 0)
    spread_x.arrived(9)
    lax.fori_loop(6, 8, project, 0)
    spread_x.sent()
    save_normed = pltpu.make_async_copy(normed_ffn, normed_out, local_sem.at[8])
    save_normed.start()
    spread_g.relay_first()

    def attn_spread(first, count, send, recv):
        def part(half):
            return slice(
                first + (count // 2 if half == 1 else 0),
                first + (count // 2 if half == 0 else count),
            )

        return Spread(
            place,
            lambda half: kept.at[part(half)],
            lambda block, half: attn_all.at[part(half), :, rows_of(block, cols)],
            send,
            recv,
        )

    half_blocks = kept.shape[0] // 2
    attn_first = attn_spread(0, half_blocks, first_send, first_recv)
    attn_second = attn_spread(half_blocks, half_blocks // 2, second_send, second_recv)
    attn_third = attn_spread(half_blocks * 3 // 2, half_blocks // 2, third_send, third_recv)

    def after_two():
        pass_group(5)

    def after_more():
        spread_g.relay_second()
        pass_group(6)

    def after_half():
        attn_second.start()
        spread_o.relay_first()

    def after_most():
        pass_group(7)
        spread_o.relay_second()

    attend_forward(
        per_segment,
        slot_of,
        length_ref,
        qkv,
        attn_t,
        lse,
        query,
        key,
        value_t,
        kept,
        {
            per_segment // 2: after_two,
            per_segment: attn_first.start,
            per_segment + 1: after_more,
            per_segment + per_segment // 2: after_half,
            2 * per_segment - 1: after_most,
        },
    )
    attn_third.start()
    attn_all[:, :, my_cols] = kept[...]
    spread_g.relay_third()
    attn_first.relay_first()
    attn_first.relay_second()
    spread_o.relay_third()
    for index in (5, 6, 7):
        group_arrived(index)
    down[...] = jnp.concatenate(
        [down_parts[index].astype(jnp.float32) for index in range(devices_fsdp)], axis=0
    ).astype(jnp.bfloat16)
    attn_second.relay_first()
    attn_second.relay_second()
    attn_first.relay_third()
    attn_third.relay_first()
    attn_third.relay_second()
    attn_second.relay_third()
    save_normed.wait()
    load_grads.wait()
    spread_g.arrived(0, 7, 8, 9)
    spread_o.arrived(0, 7, 8, 9)
    attn_third.relay_third()
    for spread in (attn_first, attn_second, attn_third):
        spread.arrived(0, 7, 8, 9)

    def swap(source, target, send, recv):
        return [
            remote(source(flip), target, send.at[flip - 1], recv.at[flip - 1], {"ctx": place.peer(flip)})
            for flip in range(1, 8)
        ]

    def attn_of(block):
        return jnp.concatenate(
            [attn_all[block_of[block * held + index]] for index in range(held)], axis=0
        )

    gain_two = gains[8:9, :]
    sums = CrossSum(
        place,
        lambda pair: lax.rem(pair, 2),
        stage,
        landed,
        norm_sums,
        norm_received,
        norm_passed,
        pair_send,
        pair_recv,
        out_send,
        out_recv,
    )

    def hidden_of(block, attn):
        return rows_all[rows_of(block), :].astype(jnp.float32) + dot_f32(
            attn, output_all[...].reshape(width, width), 1, 0
        )

    def feed(block):
        at = rows_of(block)
        low = rms_forward(hidden_of(block, attn_of(block)), gain_two)[0].astype(jnp.bfloat16)
        normed_ffn[at, :] = low
        grad_out = grads[at, :]
        gate = dot_f32(low, gate_t[...], 1, 1)
        up_proj = dot_f32(low, up_t[...], 1, 1)
        grad_inner = dot_f32(grad_out, down[...], 1, 1)
        sigmoid = jax.nn.sigmoid(gate)
        activated = gate * sigmoid
        inner = activated * up_proj
        inner_low = inner.astype(jnp.bfloat16)
        grad_gate = grad_inner * up_proj * sigmoid * (1.0 + gate * (1.0 - sigmoid))
        grad_up = grad_inner * activated
        gate_low = grad_gate.astype(jnp.bfloat16)
        up_low = grad_up.astype(jnp.bfloat16)
        units_t[0:units, at] = inner.T.astype(jnp.bfloat16)
        units_t[units : 2 * units, at] = grad_gate.T.astype(jnp.bfloat16)
        units_t[2 * units : 3 * units, at] = grad_up.T.astype(jnp.bfloat16)
        return (
            dot_f32(inner_low, down[...], 1, 0),
            dot_f32(gate_low, gate_t[...], 1, 0) + dot_f32(up_low, up_t[...], 1, 0),
        )

    def one_pair(step, unused):
        pair = 3 - step
        slot = lax.rem(pair, 2)
        layer, norm = feed(sums.theirs(pair))

        @pl.when(step > 1)
        def _():
            sums.exchange(pair + 2).wait_send()

        stage[slot, 0] = layer.astype(jnp.bfloat16)
        stage[slot, 1] = norm.astype(jnp.bfloat16)
        sums.exchange(pair).start()
        layer, norm = feed(sums.mine(pair))
        own_sum[0] = layer
        own_sum[1] = norm
        sums.exchange(pair).wait_recv()
        layer_sums[pair] = (
            (own_sum[0] + landed[slot, 0].astype(jnp.float32))
            .astype(jnp.bfloat16)
            .reshape(layer_sums.shape[1:])
        )
        sums.finish(pair, own_sum[1] + landed[slot, 1].astype(jnp.float32))
        return unused

    lax.fori_loop(0, 4, one_pair, 0)
    for pair in (1, 0):
        sums.exchange(pair).wait_send()
    attn_rows[...] = attn_of(me)
    hidden[...] = hidden_of(me, attn_rows[...])
    load_normed = pltpu.make_async_copy(normed_out, rows_all, local_sem.at[8])
    load_normed.start()

    def down_part(tile, unused):
        at = rows_of(tile, shard)
        down_tile = dot_f32(units_t[0:units, :], grads[:, at], 1, 0)
        for half in (0, 1):
            own_sum[half, 0 : units // 2, at] = down_tile[half * units // 2 : (half + 1) * units // 2]
        return unused

    lax.fori_loop(0, devices_fsdp, down_part, 0)
    for index in range(devices_fsdp):
        first = index % 2 * part
        grad_units[index, 2 * units : 3 * units, :] = jnp.concatenate(
            [
                own_sum[index // 2, first : first + part, tile * shard : (tile + 1) * shard]
                for tile in range(devices_fsdp)
            ],
            axis=0,
        ).astype(jnp.bfloat16)

    def units_copy(step, source):
        return remote(
            source,
            units_landed.at[group],
            units_send.at[step - 1],
            units_recv.at[step - 1],
            {"fsdp": place.other_group(step)},
        )

    def units_direct(step):
        return units_copy(step, grad_units.at[place.other_group(step)])

    units_far_copy = remote(
        grad_units.at[devices_fsdp - 1 - group],
        units_far,
        far_sem.at[0],
        far_sem.at[1],
        {"fsdp": 1 + group // 3},
    )
    units_sum_copy = units_copy(2, units_near)

    def units_tile(turn, unused):
        step = jnp.where(turn < 2, 3 - 2 * turn, 6 - 2 * turn)
        tile = place.other_group(step)
        grad_units[tile, 0 : 2 * units, :] = dot_f32(
            units_t[units : 3 * units, :], normed_ffn[:, rows_of(tile, shard)], 1, 0
        ).astype(jnp.bfloat16)

        for at, step in ((0, 3), (1, 1)):
            pl.when((turn == at) & place.near(step))(units_direct(step).start)
            pl.when((turn == at) & (group == 3 - step // 2 * 3))(units_far_copy.start)
        pl.when((turn == 2) & place.at_end())(units_direct(2).start)
        return unused

    lax.fori_loop(0, devices_fsdp, units_tile, 0)

    total = sums.collect()
    values = hidden[...]
    factor = lax.rsqrt(jnp.mean(values * values, axis=-1, keepdims=True) + epsilon)
    scaled = total * gain_two
    gain_part = jnp.sum(total * values * factor, axis=0, keepdims=True)
    whole = (
        grads[rows_of(me), :].astype(jnp.float32)
        + factor * scaled
        - values * (factor * factor * factor) * jnp.mean(scaled * values, axis=-1, keepdims=True)
    )
    grad_hidden[...] = whole
    grad_branch[...] = whole.astype(jnp.bfloat16)
    grad_rows[...] = (
        dot_f32(grad_branch[...], output_all[...].reshape(width, width), 1, 1)
        .astype(jnp.bfloat16)
        .reshape(grad_rows.shape)
    )
    to_heads = swap(
        lambda flip: grad_rows.at[:, :, rows_of(place.peer(flip), cols)],
        grad_attn.at[pl.ds(me * held, held)],
        b_send,
        b_recv,
    )
    for spread in (spread_g, spread_o, attn_first, attn_second, attn_third):
        spread.sent()
    sums.sent()
    for copy in to_heads:
        copy.start()
    grad_attn[pl.ds(me * held, held)] = grad_rows[:, :, my_cols]

    for index in range(devices_fsdp):
        piece = attn_rows[:, index * shard : (index + 1) * shard].T
        grad_output[index] = (
            dot_f32(piece, grad_branch[...], 1, 0)
            .astype(jnp.bfloat16)
            .reshape(8, shard // 8, width)
        )
    for copy in to_heads:
        copy.wait_recv()
    for index in range(8):
        group_sent(index)
    for copy in to_heads:
        copy.wait_send()

    def over_groups(source, target, send, recv):
        return [
            remote(
                source(place.other_group(step)),
                target.at[group],
                send.at[step - 1],
                recv.at[step - 1],
                {"fsdp": place.other_group(step)},
            )
            for step in range(1, devices_fsdp)
        ]

    def units_between():
        @pl.when(place.between())
        def _():
            units_far_copy.wait_recv()
            units_near[...] = (
                grad_units[place.other_group(2)].astype(jnp.float32)
                + units_far[...].astype(jnp.float32)
            ).astype(jnp.bfloat16)
            units_sum_copy.start()

    sums = CrossSum(
        place,
        lambda pair: (pair // 2, lax.rem(pair, 2)),
        stage,
        landed,
        norm_sums,
        norm_received,
        norm_passed,
        back_pair_send,
        back_pair_recv,
        back_out_send,
        back_out_recv,
    )
    output_pairs = OutputSum(
        place,
        grad_output,
        output_landed,
        output_sums,
        output_received,
        wo_send,
        wo_recv,
        wo_out_send,
        wo_out_recv,
    )
    for pair in range(4):
        output_pairs.exchange(pair).start()
    layer_copies = [
        remote(
            layer_sums.at[pair],
            attn_all.at[pair * held : (pair + 1) * held],
            layer_send.at[pair],
            layer_recv.at[pair],
            {"ctx": sums.mine(pair)},
        )
        for pair in range(1, 4)
    ]
    for copy in layer_copies:
        copy.start()

    def after_prompt():
        for pair in range(4):
            output_pairs.exchange(pair).wait_recv()
            output_sums[pair] = (
                grad_output[:, output_pairs.mine(pair)].astype(jnp.float32)
                + output_landed[pair].astype(jnp.float32)
            ).astype(jnp.bfloat16)
            if pair:
                output_pairs.deliver(pair).start()

    def half_of(ref, lines):
        def region(block, half):
            return ref.at[block] if half is None else ref.at[block, halves(lines)(half)]

        return region

    def own_of(ref, lines):
        return lambda half: ref if half is None else ref.at[halves(lines)(half)]

    spread_u = Spread(
        place,
        own_of(units_stage, 3 * units),
        half_of(units_out, 3 * units),
        u_send,
        u_recv,
    )
    save_units = pltpu.make_async_copy(units_stage, units_out.at[me], save_sem.at[0])
    output_copies = over_groups(
        lambda to: output_total.at[to], output_group, late_send.at[1], late_recv.at[1]
    )

    def before_last():
        total = output_sums[0].astype(jnp.float32)
        for pair in range(1, 4):
            output_pairs.deliver(pair).wait_recv()
            total = total + output_received[pair].astype(jnp.float32)
        output_total[...] = total.astype(jnp.bfloat16)
        for copy in output_copies:
            copy.start()
        units_landed[group] = grad_units[group]

        @pl.when(place.at_end())
        def _():
            units_landed[devices_fsdp - 1 - group] = jnp.zeros_like(grad_units[group])

        units_direct(2).wait_recv()
        for step in (1, 3):
            pl.when(place.heard(step))(units_direct(step).wait_recv)
        units_total = units_landed[0].astype(jnp.float32)
        for index in range(1, devices_fsdp):
            units_total = units_total + units_landed[index].astype(jnp.float32)
        units_stage[...] = units_total.astype(jnp.bfloat16)

        spread_u.start()
        save_units.start()

    attend_backward(
        per_segment,
        slot_of,
        block_of,
        length_ref,
        qkv,
        grad_attn,
        attn_t,
        lse,
        grads,
        query,
        key,
        kept,
        grad,
        value_t,
        own_sum,
        {
            per_segment // 2: units_between,
            per_segment: after_prompt,
            2 * per_segment - 1: before_last,
        },
    )

    def turn(tile, unused):
        at = rows_of(tile, TILE)
        units_t[0 : 3 * cols, at] = grads[at, 0 : 3 * cols].T
        return unused

    lax.fori_loop(0, grads.shape[0] // TILE, turn, 0)
    load_normed.wait()

    def weight_tile(tile, unused):
        at = rows_of(tile, shard)
        normed_ffn[0 : 3 * cols, at] = dot_f32(
            units_t[0 : 3 * cols, :], rows_all[:, at], 1, 0
        ).astype(jnp.bfloat16)
        return unused

    def qkv_parts(to):
        return normed_ffn.at[0 : 3 * cols, rows_of(to, shard)]

    lax.fori_loop(0, devices_fsdp, weight_tile, 0)
    qkv_copies = over_groups(
        qkv_parts, qkv_landed, late_send.at[0], late_recv.at[0]
    )
    for copy in qkv_copies:
        copy.start()
    spread_u.relay_first()

    def one_pair(step, unused):
        pair = 3 - step
        stage[pair // 2, lax.rem(pair, 2)] = dot_f32(
            grads[rows_of(sums.theirs(pair)), 0 : 3 * cols], w_qkv[...], 1, 1
        ).astype(jnp.bfloat16)
        sums.exchange(pair).start()
        return unused

    lax.fori_loop(0, 4, one_pair, 0)
    spread_u.relay_second()

    def sum_pair(step, unused):
        pair = 3 - step
        own_sum[0] = dot_f32(grads[rows_of(sums.mine(pair)), 0 : 3 * cols], w_qkv[...], 1, 1)
        sums.exchange(pair).wait_recv()
        sums.finish(
            pair, own_sum[0] + landed[pair // 2, lax.rem(pair, 2)].astype(jnp.float32)
        )
        return unused

    lax.fori_loop(0, 4, sum_pair, 0)

    def group_sum(own, landed_ref, copies):
        landed_ref[group] = own
        for copy in copies:
            copy.wait_recv()
        total = landed_ref[0].astype(jnp.float32)
        for index in range(1, devices_fsdp):
            total = total + landed_ref[index].astype(jnp.float32)
        return total

    total = layer_sums[0].astype(jnp.float32)
    for pair, copy in enumerate(layer_copies):
        copy.wait_recv()
        at = slice((pair + 1) * held, (pair + 2) * held)
        total = total + attn_all[at].astype(jnp.float32)
    grad_rows[...] = (hidden[...].reshape(total.shape) + total).astype(jnp.bfloat16)
    save_layer = pltpu.make_async_copy(grad_rows, layer, save_sem.at[2])
    save_layer.start()

    spread_u.relay_third()
    turned = group_sum(qkv_parts(group)[...], qkv_landed, qkv_copies).T.astype(jnp.bfloat16)
    for index in range(3):
        columns_stage[index * shard : (index + 1) * shard, :] = turned[
            :, index * cols : (index + 1) * cols
        ]
    summed = group_sum(output_total[group], output_group, output_copies).astype(jnp.bfloat16)
    lines = shard // 8
    for index in range(8):
        columns_stage[3 * shard + index * lines : 3 * shard + (index + 1) * lines, :] = summed[
            :, index * cols : (index + 1) * cols
        ]
    spread_c = Spread(
        place, own_of(columns_stage, 4 * shard), half_of(columns_out, 4 * shard), c_send, c_recv
    )
    spread_c.start()
    save_columns = pltpu.make_async_copy(columns_stage, columns_out.at[me], save_sem.at[1])
    save_columns.start()
    total = sums.collect()
    values = patches[...].astype(jnp.float32)
    factor = lax.rsqrt(jnp.mean(values * values, axis=-1, keepdims=True) + epsilon)
    scaled = total * gain_one
    gain_parts[...] = jnp.zeros_like(gain_parts)
    attn_part = jnp.sum(total * values * factor, axis=0, keepdims=True)
    ffn_part = gain_part
    for index in range(devices_fsdp):
        at = slice(index * shard, (index + 1) * shard)
        gain_parts[index, 0:1, :] = attn_part[:, at]
        gain_parts[index, 1:2, :] = ffn_part[:, at]
    gain_copies = over_groups(lambda to: gain_parts.at[to], gain_landed, gain_send, gain_recv)
    for copy in gain_copies:
        copy.start()
    spread_c.relay_first()
    grad_hidden[...] = (
        grad_hidden[...]
        + factor * scaled
        - values * (factor * factor * factor) * jnp.mean(scaled * values, axis=-1, keepdims=True)
    )
    save_rows = pltpu.make_async_copy(grad_hidden, grad_patches, save_sem.at[3])
    save_rows.start()
    spread_c.relay_second()
    gain_total[...] = group_sum(gain_parts[group], gain_landed, gain_copies)
    gain_out = [
        remote(
            gain_total,
            gain_all.at[me],
            gain_out_send.at[flip - 1],
            gain_out_recv.at[flip - 1],
            {"ctx": place.peer(flip)},
        )
        for flip in range(1, 8)
    ]
    for copy in gain_out:
        copy.start()
    gain_all[me] = gain_total[...]

    spread_c.relay_third()
    for copy in gain_out:
        copy.wait_recv()
    gain_sum = gain_all[0]
    for index in range(1, 8):
        gain_sum = gain_sum + gain_all[index]
    gains_out[...] = gain_sum
    spread_u.arrived(0, 7, 8, 9)
    spread_c.arrived(0, 7, 8, 9)
    for step in (1, 3):
        pl.when(place.near(step))(units_direct(step).wait_send)
    units_direct(2).wait_send()
    pl.when(place.at_end())(units_far_copy.wait_send)
    for copy in layer_copies + qkv_copies + output_copies + gain_copies + gain_out:
        copy.wait_send()
    for pair in range(4):
        sums.exchange(pair).wait_send()
    sums.sent()
    output_pairs.sent()
    save_layer.wait()
    save_rows.wait()
    spread_u.sent()
    spread_c.sent()
    save_units.wait()
    save_columns.wait()


def place_kernel(
    devices_fsdp,
    units_all,
    columns_all,
    layer,
    grad_rows,
    gains,
    out_layer,
    out_rows,
    out_query,
    out_key,
    out_value,
    out_output,
    out_gate,
    out_up,
    out_down,
    out_gain_attn,
    out_gain_ffn,
    units_held,
    columns_held,
    layer_held,
    rows_held,
    columns,
    outputs,
    natural,
    gate,
    up,
    down,
    load_sems,
    sems,
):
    shard = out_query.shape[0]
    cols = columns_all.shape[2]
    lines = shard // 8
    units = units_all.shape[1] // 3
    part = units // devices_fsdp
    span = part * 8
    loads = []
    saves = []

    def load(source, target):
        copy = pltpu.make_async_copy(source, target, load_sems.at[len(loads)])
        copy.start()
        loads.append(copy)

    def save(source, target):
        copy = pltpu.make_async_copy(source, target, sems.at[len(saves)])
        copy.start()
        saves.append(copy)

    for which in (2, 0, 1):
        load(units_all.at[:, which * units : (which + 1) * units], units_held.at[which])
    load(columns_all, columns_held)
    load(grad_rows, rows_held)
    load(layer, layer_held)
    out_gain_attn[...] = gains[0, :]
    out_gain_ffn[...] = gains[1, :]
    loads[0].wait()
    for index in range(8):
        piece = units_held[2, index].astype(jnp.float32)
        for tile in range(devices_fsdp):
            down[index * part : (index + 1) * part, tile * shard : (tile + 1) * shard] = piece[
                tile * part : (tile + 1) * part, :
            ]
    save(down, out_down)
    for which, (target, out) in enumerate(((gate, out_gate), (up, out_up))):
        loads[1 + which].wait()
        for index in range(8):
            piece = units_held[which, index].astype(jnp.float32)
            for tile in range(devices_fsdp):
                first = tile * span + index * part
                natural[first : first + part, :] = piece[tile * part : (tile + 1) * part, :]
        for first in range(0, span * devices_fsdp, 128):
            target[:, first : first + 128] = natural[first : first + 128, :].T
        save(target, out)
    loads[4].wait()
    save(rows_held, out_rows)
    loads[5].wait()
    save(layer_held, out_layer)
    loads[3].wait()
    for index in range(8):
        at = slice(index * cols, (index + 1) * cols)
        for which in range(3):
            columns[which, :, at] = columns_held[
                index, which * shard : (which + 1) * shard, :
            ].astype(jnp.float32)
        for tile in range(8):
            first = 3 * shard + tile * lines
            outputs[index * lines : (index + 1) * lines, tile * cols : (tile + 1) * cols] = (
                columns_held[index, first : first + lines, :].astype(jnp.float32)
            )
    save(columns.at[0], out_query)
    save(columns.at[1], out_key)
    save(columns.at[2], out_value)
    save(outputs, out_output)
    for copy in saves:
        copy.wait()


def heads_plan(
    patches,
    cotangent,
    deal_table,
    prompt_len,
    w_query,
    w_key,
    w_value,
    w_output,
    w_gate,
    w_up,
    w_down,
    gain_attn,
    gain_ffn,
):
    local_rows = patches.shape[1]
    width = patches.shape[2]
    groups = lax.axis_size("fsdp")
    rows = local_rows * 8
    cols = width // 8
    shard = width // groups
    part = w_down.shape[0] // 8
    units = part * groups
    tiles = rows // TILE
    blocks = deal_table.shape[0]
    block_len = rows // blocks
    per_segment = CONT_LEN // TILE
    smem = pl.BlockSpec(memory_space=pltpu.SMEM)
    vmem = pl.BlockSpec(memory_space=pltpu.VMEM)
    anywhere = pl.BlockSpec(memory_space=pl.ANY)
    low, full = jnp.bfloat16, jnp.float32

    def shaped(kind, *dims):
        return jax.ShapeDtypeStruct(dims, kind)

    def room(kind, *dims):
        return pltpu.VMEM(dims, kind)

    unused, layer, grad_rows, units_all, columns_all, gains_sum = pl.pallas_call(
        functools.partial(layer_kernel, per_segment, groups),
        out_shape=(
            shaped(low, rows, width),
            shaped(low, blocks // 8, block_len, width),
            shaped(full, local_rows, width),
            shaped(low, 8, 3 * units, shard),
            shaped(low, 8, 4 * shard, cols),
            shaped(full, 8, shard),
        ),
        in_specs=[smem] * 2 + [vmem] + [anywhere] * 8 + [vmem] * 2,
        out_specs=(anywhere,) * 5 + (vmem,),
        scratch_shapes=[
            room(low, blocks, block_len, 3 * cols),
            room(full, tiles, cols, TILE),
            room(full, tiles, 1, 2 * TILE),
            room(low, groups, 3 * units, shard),
            room(low, groups, 8, shard // 8, width),
            room(low, 4, blocks // 8, block_len, width),
            room(full, local_rows, width),
            room(full, local_rows, width),
            room(low, rows, width),
            room(low, rows, width),
            room(low, rows, width),
            room(low, blocks, block_len, width),
            room(low, width, 3 * cols),
            room(low, groups, 8, shard // 8, width),
            room(low, units, width),
            room(low, units, width),
            room(low, units, width),
            room(low, groups, part, width),
            room(low, units, shard),
            room(low, units, shard),
            room(full, 16, shard),
            room(full, 16, width),
            room(low, blocks, block_len, cols),
            room(low, blocks, block_len, cols),
            room(low, tiles, cols, TILE),
            room(low, blocks, block_len, cols),
            room(low, blocks, block_len, cols),
            room(low, local_rows, width),
            room(low, 3 * units, rows),
            room(low, 2, 2, local_rows, width),
            room(low, 2, 2, local_rows, width),
            room(full, 2, local_rows, width),
            room(low, 4, local_rows, width),
            room(low, 2, local_rows, width),
            room(low, 2, local_rows // 2, width),
            room(low, local_rows, width),
            room(low, blocks // 8, block_len, width),
            room(low, blocks, block_len, cols),
            room(low, groups, 3 * units, shard),
            room(low, 3 * units, shard),
            room(low, 3 * units, shard),
            room(low, 3 * units, shard),
            room(low, 4, groups, shard // 8, width),
            room(low, 4, groups, shard // 8, width),
            room(low, 4, groups, shard // 8, width),
            room(low, groups, shard // 8, width),
            room(low, groups, shard // 8, width),
            room(low, groups, 3 * cols, shard),
            room(low, 4 * shard, cols),
            room(full, groups, 8, shard),
            room(full, groups, 8, shard),
            room(full, 8, shard),
            room(full, 8, 8, shard),
            dma(9),
            dma(4),
            dma(2 * groups),
            pltpu.SemaphoreType.DMA((8, groups - 1)),
            pltpu.SemaphoreType.DMA((8, groups - 1)),
            dma(8),
            dma(10),
            dma(10),
            dma(10),
            dma(10),
            dma(10),
            dma(10),
            dma(10),
            dma(10),
            dma(10),
            dma(10),
            dma(10),
            dma(10),
            dma(10),
            dma(10),
            dma(10),
            dma(10),
            dma(7),
            dma(7),
            dma(7),
            dma(7),
            dma(4),
            dma(4),
            dma(4),
            dma(4),
            dma(4),
            dma(4),
            dma(4),
            dma(4),
            dma(4),
            dma(4),
            dma(4),
            dma(4),
            dma(4),
            dma(4),
            dma(groups - 1),
            dma(groups - 1),
            dma(groups - 1),
            dma(groups - 1),
            dma(2),
            pltpu.SemaphoreType.DMA((2, groups - 1)),
            pltpu.SemaphoreType.DMA((2, groups - 1)),
        ],
        compiler_params=pltpu.CompilerParams(
            collective_id=0, has_side_effects=True, vmem_limit_bytes=67_000_000
        ),
        name="layer",
    )(
        deal_table,
        prompt_len,
        patches[0],
        cotangent[0],
        w_query,
        w_key,
        w_value,
        w_output.reshape(8, shard // 8, width),
        w_gate,
        w_up,
        w_down.reshape(8, part, width),
        gain_attn,
        gain_ffn,
    )

    results = pl.pallas_call(
        functools.partial(place_kernel, groups),
        out_shape=(
            shaped(low, blocks // 8, block_len, width),
            shaped(full, local_rows, width),
        )
        + tuple(shaped(full, shard, width) for _ in range(4))
        + tuple(shaped(full, shard, 8 * units) for _ in range(2))
        + (shaped(full, 8 * part, width), shaped(full, shard), shaped(full, shard)),
        in_specs=[anywhere] * 4 + [vmem],
        out_specs=(anywhere,) * 9 + (vmem,) * 2,
        scratch_shapes=[
            room(low, 3, 8, units, shard),
            room(low, 8, 4 * shard, cols),
            room(low, blocks // 8, block_len, width),
            room(full, local_rows, width),
            room(full, 3, shard, width),
            room(full, shard, width),
            room(full, 8 * units, shard),
            room(full, shard, 8 * units),
            room(full, shard, 8 * units),
            room(full, 8 * part, width),
            dma(6),
            dma(9),
        ],
        name="place",
    )(units_all, columns_all, layer, grad_rows, gains_sum)
    return (results[0].reshape(1, local_rows, width), results[1][None]) + tuple(results[2:])


def solution(mesh):
    if mesh.shape["ctx"] == 8 and mesh.shape["fsdp"] == 4:
        per_device = heads_plan
    else:
        per_device = rows_plan
    placed = (
        P("fsdp", "ctx", None),
        P("fsdp", "ctx", None),
        P(),
        P("fsdp"),
        P("fsdp", None),
        P("fsdp", None),
        P("fsdp", None),
        P("fsdp", None),
        P("fsdp", None),
        P("fsdp", None),
        P("fsdp", None),
        P("fsdp"),
        P("fsdp"),
    )
    return jax.shard_map(
        per_device,
        mesh=mesh,
        in_specs=placed,
        out_specs=(
            P("fsdp", "ctx", None),
            P("fsdp", "ctx", None),
            P("fsdp", None),
            P("fsdp", None),
            P("fsdp", None),
            P("fsdp", None),
            P("fsdp", None),
            P("fsdp", None),
            P("fsdp", None),
            P("fsdp"),
            P("fsdp"),
        ),
        check_vma=False,
    )
```
